32 devices in a mesh: dp: 8 (over z, y), tensor: 4 (over x, core).
Axes of the slice: x: 2, y: 2, z: 4, core: 2. Of those that a mesh axis runs over, the one named last changes fastest.
Arguments:
- tokens: bfloat16 [16384, 512], P(('dp', 'tensor')), may hold values from -6 to 6
- encoder_states: bfloat16 [16384, 512], P(('dp', 'tensor')), may hold values from -6 to 6
- output_grad: bfloat16 [16384, 512], P(('dp', 'tensor')), may hold values from -6 to 6
- valid_mask: int32 [16384], P(('dp', 'tensor')), may hold values 0 or 1
- segment_ids: int32 [16, 1024], P('dp'), may hold values from 0 to 15, never falling along the last dimension, each value on 1 to 512 neighbouring positions
- context_ranks: int32 [16, 8], P('dp'), may hold values from 0 to 7, each once within a row
- self_query: bfloat16 [512, 512], P('dp', 'tensor'), may hold values from -0.25 to 0.25
- self_key: bfloat16 [512, 512], P('dp', 'tensor'), may hold values from -0.25 to 0.25
- self_value: bfloat16 [512, 512], P('dp', 'tensor'), may hold values from -0.25 to 0.25
- self_output: bfloat16 [512, 512], P('tensor', 'dp'), may hold values from -1.5 to 1.5
- cross_query: bfloat16 [512, 512], P('dp', 'tensor'), may hold values from -0.25 to 0.25
- cross_key: bfloat16 [512, 512], P('dp', 'tensor'), may hold values from -0.25 to 0.25
- cross_value: bfloat16 [512, 512], P('dp', 'tensor'), may hold values from -0.25 to 0.25
- cross_output: bfloat16 [512, 512], P('tensor', 'dp'), may hold values from -4 to 4
- hidden_up: bfloat16 [512, 2048], P('dp', 'tensor'), may hold values from -0.25 to 0.25
- hidden_down: bfloat16 [2048, 512], P('tensor', 'dp'), may hold values from -0.1875 to 0.1875
- norm1_gain: float32 [512], replicated, may hold values from 0.5 to 1.5
- norm1_bias: float32 [512], replicated, may hold values from -1.2 to 1.2
- norm2_gain: float32 [512], replicated, may hold values from 0.5 to 1.5
- norm2_bias: float32 [512], replicated, may hold values from -1.2 to 1.2
- norm3_gain: float32 [512], replicated, may hold values from 0.5 to 1.5
- norm3_bias: float32 [512], replicated, may hold values from -1.2 to 1.2
Outputs:
- layer_output: float32 [16384, 512], P(('dp', 'tensor'))
- tokens_grad: float32 [16384, 512], P(('dp', 'tensor'))
- encoder_grad: float32 [16384, 512], P(('dp', 'tensor'))
- grad_self_query: float32 [512, 512], P('dp', 'tensor')
- grad_self_key: float32 [512, 512], P('dp', 'tensor')
- grad_self_value: float32 [512, 512], P('dp', 'tensor')
- grad_self_output: float32 [512, 512], P('tensor', 'dp')
- grad_cross_query: float32 [512, 512], P('dp', 'tensor')
- grad_cross_key: float32 [512, 512], P('dp', 'tensor')
- grad_cross_value: float32 [512, 512], P('dp', 'tensor')
- grad_cross_output: float32 [512, 512], P('tensor', 'dp')
- grad_hidden_up: float32 [512, 2048], P('dp', 'tensor')
- grad_hidden_down: float32 [2048, 512], P('tensor', 'dp')
- norm_grads: float32 [6, 512], replicated
- valid_scales: float32 [2, 512], replicated
The draws below stay inside these ranges and needn't reach their ends.
Inputs may be any that keep to these rules, and one draw needn't show every extreme that they name: `segment_ids`: within a sequence the ids never fall; each document has 1 to 512 tokens and one has exactly 512. `context_ranks`: each sequence's row holds every block rank once.
All inputs are finite; a program needn't handle non-finite values. No bound on the sum of `valid_mask` on one device may be relied on, other than what follows from the above.
Results may differ from the reference program's by a relative error of at most 0.024.
The reference program's roundings to bfloat16 on the way count: a program that leaves them out, or rounds other values in their place, can miss the bound.
Values may be sent and summed in bfloat16 or wider, within the bound.
A program may use at most 128 MiB of HBM per device.

```python
import math
import jax
import jax.numpy as jnp
import numpy as np
from jax import lax

D = 512
HEADS = 8
HEAD = 64
FF = 2048
LEN = 1024
BLK = 128
DOCS = 16
NBLK = 8
SEQS = 16
TOKENS = 16384


def touch_ends(values, key, low, top_value):
    extent = values.shape
    place = [jax.random.randint(jax.random.fold_in(key, axis), (), 0, extent[axis]) for axis in range(len(extent))]
    values = values.at[tuple(place)].set(low)
    longest = extent.index(max(extent))
    place[longest] = (place[longest] + 1) % extent[longest]
    return values.at[tuple(place)].set(top_value)


def steps_of(rng, shape, cuts, low, largest):
    factor_of = 1.0
    for axis_at, shards_of in cuts:
        steps = jax.random.uniform(jax.random.fold_in(jax.random.fold_in(rng, 6), axis_at), (shards_of,), jnp.float32, low / len(cuts), largest / len(cuts))
        factor_of = factor_of * jnp.repeat(jnp.exp(steps), shape[axis_at] // shards_of).reshape((-1,) + (1,) * (len(shape) - 1 - axis_at))
    return factor_of


def split_up(number_of, total, reach, skew):
    portions = [(1 << 20) // math.isqrt(standing ** skew) + 1 for standing in range(2, number_of + 1)]
    spare, given = total - reach - (number_of - 1), [1] * (number_of - 1)
    while spare > 0:
        free = [i for i in range(number_of - 1) if given[i] < reach]
        pool, remaining = sum([portions[i] for i in free]), spare
        for i in free:
            addition = min(reach - given[i], max(1, remaining * portions[i] // pool), spare)
            given[i] = given[i] + addition
            spare = spare - addition
    return np.array([reach] + given)


def ragged(key, amount, total, most, slope):
    if amount == 2:
        one = jax.random.randint(key, (), max(1, total - most), min(most, total - 1) + 1)
        return jnp.stack([one, total - one])
    sizes = jnp.asarray(split_up(amount, total, most, slope), jnp.int32)
    couples = (amount - 1) // 2
    source_of, receiver = sizes[1:1 + 2 * couples:2], sizes[2:2 + 2 * couples:2]
    margin = jnp.minimum(source_of - 1, most - receiver)
    moved = jax.random.randint(jax.random.fold_in(key, 1), (couples,), 0, 1 << 20) % (margin + 1)
    sizes = sizes.at[1:1 + 2 * couples:2].set(source_of - moved).at[2:2 + 2 * couples:2].set(receiver + moved)
    return sizes[jax.random.permutation(jax.random.fold_in(key, 2), amount)]


def scatter_about(key, shape, deviation, most, shards=(), held_as=jnp.bfloat16):
    level = steps_of(key, shape, shards, -0.22, 0.18) if shards else 1.0
    values = jax.random.normal(key, shape, jnp.float32) * deviation * level
    return jnp.minimum(jnp.maximum(values, -most), most).astype(held_as)


def setup_inputs(seed: int = 0) -> dict:
    arg_keys = jax.random.split(jax.random.key(seed), 23)
    tokens = scatter_about(arg_keys[0], (TOKENS, D), 1.0, 6.0, ((0, 32),))
    encoder_states = scatter_about(arg_keys[1], (TOKENS, D), 1.0, 6.0, ((0, 32),))
    output_grad = scatter_about(arg_keys[2], (TOKENS, D), 1.0, 6.0, ((0, 32),))
    valid_mask = touch_ends((jax.random.randint(arg_keys[3], (TOKENS,), 0, 8) < 7).astype(jnp.int32), jax.random.fold_in(arg_keys[3], 1), 0, 1)
    segment_ids = jax.vmap(lambda own: jnp.searchsorted(jnp.cumsum(ragged(own, DOCS, LEN, LEN // 2, 2)), jnp.arange(LEN), side="right"))(jax.random.split(arg_keys[4], SEQS)).reshape((SEQS, LEN)).astype(jnp.int32)
    context_ranks = jax.vmap(lambda own: jax.random.permutation(own, NBLK))(jax.random.split(arg_keys[5], SEQS)).reshape((SEQS, NBLK)).astype(jnp.int32)
    self_query = scatter_about(arg_keys[6], (D, D), D ** -0.5, 0.25, ((0, 8), (1, 4)))
    self_key = scatter_about(arg_keys[7], (D, D), D ** -0.5, 0.25, ((0, 8), (1, 4)))
    self_value = scatter_about(arg_keys[8], (D, D), D ** -0.5, 0.25, ((0, 8), (1, 4)))
    self_output = scatter_about(arg_keys[9], (D, D), (max(D // 32, 1)) ** -0.5, 1.5, ((0, 4), (1, 8)))
    cross_query = scatter_about(arg_keys[10], (D, D), D ** -0.5, 0.25, ((0, 8), (1, 4)))
    cross_key = scatter_about(arg_keys[11], (D, D), D ** -0.5, 0.25, ((0, 8), (1, 4)))
    cross_value = scatter_about(arg_keys[12], (D, D), D ** -0.5, 0.25, ((0, 8), (1, 4)))
    cross_output = scatter_about(arg_keys[13], (D, D), (max(D // 256, 1)) ** -0.5, 4.0, ((0, 4), (1, 8)))
    hidden_up = scatter_about(arg_keys[14], (D, FF), D ** -0.5, 0.25, ((0, 8), (1, 4)))
    hidden_down = scatter_about(arg_keys[15], (FF, D), (FF // 2) ** -0.5, 0.1875, ((0, 4), (1, 8)))
    norm1_gain = jnp.clip(1.0 + 0.1 * jax.random.normal(arg_keys[16], (D,), jnp.float32), 0.5, 1.5)
    norm1_bias = scatter_about(arg_keys[17], (D,), 0.2, 1.2, (), jnp.float32)
    norm2_gain = jnp.clip(1.0 + 0.1 * jax.random.normal(arg_keys[18], (D,), jnp.float32), 0.5, 1.5)
    norm2_bias = scatter_about(arg_keys[19], (D,), 0.2, 1.2, (), jnp.float32)
    norm3_gain = jnp.clip(1.0 + 0.1 * jax.random.normal(arg_keys[20], (D,), jnp.float32), 0.5, 1.5)
    norm3_bias = scatter_about(arg_keys[21], (D,), 0.2, 1.2, (), jnp.float32)
    return dict(tokens=tokens, encoder_states=encoder_states, output_grad=output_grad, valid_mask=valid_mask, segment_ids=segment_ids, context_ranks=context_ranks, self_query=self_query, self_key=self_key, self_value=self_value, self_output=self_output, cross_query=cross_query, cross_key=cross_key, cross_value=cross_value, cross_output=cross_output, hidden_up=hidden_up, hidden_down=hidden_down, norm1_gain=norm1_gain, norm1_bias=norm1_bias, norm2_gain=norm2_gain, norm2_bias=norm2_bias, norm3_gain=norm3_gain, norm3_bias=norm3_bias)


@jax.custom_vjp
def low(v):
    return lax.optimization_barrier(v.astype(jnp.bfloat16)).astype(jnp.float32)

@jax.custom_vjp
def low_back(v):
    return v

def low_keep(v):
    return (low(v), None)

def low_pass(kept, grad):
    return (grad,)

def back_keep(v):
    return (v, None)

def back_low(kept, grad):
    return (low(grad),)
low.defvjp(low_keep, low_pass)
low_back.defvjp(back_keep, back_low)
norm_eps = 1e-05
mask_fill = -1000000000.0

def project(left, right):
    return jnp.dot(left, right, precision=lax.Precision.HIGHEST)

def layer_norm(value, gain, bias):
    mean = lax.optimization_barrier(jnp.mean(value, axis=-1, keepdims=True))
    centred = value - mean
    spread = lax.optimization_barrier(jnp.mean(centred * centred, axis=-1, keepdims=True))
    return centred * lax.rsqrt(spread + norm_eps) * gain + bias

def context_allowed(segments, ranks, first, count):
    length = segments.shape[0]
    key_block = jnp.arange(length, dtype=jnp.int32) // BLK
    key_rank = jnp.broadcast_to(ranks[:, None], (ranks.shape[0], BLK)).reshape(length)
    query_segment = lax.dynamic_slice_in_dim(segments, first, count)
    query_rank = lax.dynamic_slice_in_dim(key_rank, first, count)
    query_block = (first + jnp.arange(count, dtype=jnp.int32)) // BLK
    same_doc = query_segment[:, None] == segments[None, :]
    earlier = key_rank[None, :] < query_rank[:, None]
    same_block = query_block[:, None] == key_block[None, :]
    return same_doc & (earlier | same_block)

def attention(query, keys, values, allowed):
    length = query.shape[0]
    query = query.reshape(length, HEADS, HEAD)
    keys = keys.reshape(keys.shape[0], HEADS, HEAD)
    values = values.reshape(values.shape[0], HEADS, HEAD)
    scores = low_back(jnp.einsum('qhd,khd->hqk', query, keys, precision=lax.Precision.HIGHEST) * 0.125)
    if allowed is not None:
        scores = jnp.where(allowed[None], scores, mask_fill)
    top = lax.optimization_barrier(jnp.max(scores, axis=-1, keepdims=True))
    raised = jnp.exp(scores - top)
    shares = low(raised / lax.optimization_barrier(jnp.sum(raised, axis=-1, keepdims=True)))
    mixed = jnp.einsum('hqk,khd->qhd', shares, values, precision=lax.Precision.HIGHEST)
    return low(low_back(mixed.reshape(length, HEADS * HEAD)))

def layer(weights, tokens, encoder, segments, ranks):
    self_query, self_key, self_value, self_output, cross_query, cross_key, cross_value, cross_output, hidden_up, hidden_down, norm1_gain, norm1_bias, norm2_gain, norm2_bias, norm3_gain, norm3_bias = weights
    count = tokens.shape[0] // LEN

    def shaped(value):
        return value.reshape(count, LEN, D)
    query = low(low_back(project(tokens, self_query)))
    keys = low(low_back(project(tokens, self_key)))
    values = low(low_back(project(tokens, self_value)))

    def self_one(items):
        return attention(items[0], items[1], items[2], context_allowed(items[3], items[4], 0, LEN))
    mixed = lax.map(jax.checkpoint(self_one), (shaped(query), shaped(keys), shaped(values), segments, ranks))
    attended = low_back(project(mixed.reshape(tokens.shape[0], D), self_output))
    first_out = layer_norm(tokens + attended, norm1_gain, norm1_bias)
    first_low = low(first_out)
    second_query = low(low_back(project(first_low, cross_query)))
    encoder_keys = low(low_back(project(encoder, cross_key)))
    encoder_values = low(low_back(project(encoder, cross_value)))

    def cross_one(items):
        return attention(items[0], items[1], items[2], None)
    cross_mixed = lax.map(jax.checkpoint(cross_one), (shaped(second_query), shaped(encoder_keys), shaped(encoder_values)))
    crossed = low_back(project(cross_mixed.reshape(tokens.shape[0], D), cross_output))
    second_out = layer_norm(first_out + crossed, norm2_gain, norm2_bias)
    preact = low_back(project(low(second_out), hidden_up))
    activated = low(jax.nn.gelu(preact, approximate=False))
    feed_out = low_back(project(activated, hidden_down))
    return layer_norm(second_out + feed_out, norm3_gain, norm3_bias)

def reference(tokens, encoder_states, output_grad, valid_mask, segment_ids, context_ranks, self_query, self_key, self_value, self_output, cross_query, cross_key, cross_value, cross_output, hidden_up, hidden_down, norm1_gain, norm1_bias, norm2_gain, norm2_bias, norm3_gain, norm3_bias):
    weights = tuple((item.astype(jnp.float32) for item in (self_query, self_key, self_value, self_output, cross_query, cross_key, cross_value, cross_output, hidden_up, hidden_down, norm1_gain, norm1_bias, norm2_gain, norm2_bias, norm3_gain, norm3_bias)))
    group = math.gcd(SEQS, max(1, 4096 // LEN))
    rows = group * LEN
    steps_count = SEQS // group

    def one(carry, index):
        grads, sums = carry
        first = (index * rows).astype(jnp.int32)
        first_sequence = (index * group).astype(jnp.int32)
        part_tokens = lax.dynamic_slice_in_dim(tokens, first, rows).astype(jnp.float32)
        part_encoder = lax.dynamic_slice_in_dim(encoder_states, first, rows).astype(jnp.float32)
        part_segments = lax.dynamic_slice_in_dim(segment_ids, first_sequence, group)
        part_ranks = lax.dynamic_slice_in_dim(context_ranks, first_sequence, group)

        def forward(inner_weights, inputs, encoder):
            return layer(inner_weights, inputs, encoder, part_segments, part_ranks)
        result, pullback = jax.vjp(forward, weights, part_tokens, part_encoder)
        valid = lax.dynamic_slice_in_dim(valid_mask, first, rows).astype(jnp.float32)[:, None]
        grad_layer = lax.dynamic_slice_in_dim(output_grad, first, rows).astype(jnp.float32) * valid
        grad_weights, grad_tokens, grad_encoder = pullback(grad_layer)
        grads = jax.tree.map(jnp.add, grads, grad_weights)
        sums = sums + jnp.stack([lax.optimization_barrier(jnp.sum(valid * result * result, axis=0)), lax.optimization_barrier(jnp.sum(valid * grad_tokens * grad_tokens, axis=0))])
        return ((grads, sums), (result, grad_tokens, grad_encoder))
    zero_grads = jax.tree.map(jnp.zeros_like, weights)
    (grads, sums), (outputs, grad_inputs, grad_encoders) = lax.scan(one, (zero_grads, jnp.zeros((2, D), jnp.float32)), jnp.arange(steps_count, dtype=jnp.int32))
    return (outputs.reshape(TOKENS, D), grad_inputs.reshape(TOKENS, D), grad_encoders.reshape(TOKENS, D), grads[0], grads[1], grads[2], grads[3], grads[4], grads[5], grads[6], grads[7], grads[8], grads[9], jnp.stack(grads[10:16]), jnp.sqrt(sums / TOKENS))
```

```python
import jax
import jax.numpy as jnp
from jax import lax
from jax.experimental import pallas as pl
from jax.experimental.pallas import tpu as pltpu
from jax.sharding import PartitionSpec as P

HEAD = 64
LEN = 1024
BLK = 128


norm_eps = 1e-05
mask_fill = -1000000000.0


def gelu_exact(value):
    return jax.nn.gelu(value, approximate=False)


def gelu_back(preact, upstream):
    return jax.vjp(gelu_exact, preact)[1](upstream)[0]


def layer_norm(value, gain, bias):
    mean = jnp.mean(value, axis=-1, keepdims=True)
    centred = value - mean
    scale = lax.rsqrt(jnp.mean(centred * centred, axis=-1, keepdims=True) + norm_eps)
    normal = centred * scale
    return (normal * gain + bias, normal, scale)


def norm_back(upstream, normal, scale, gain):
    scaled = upstream * gain
    mean_grad = jnp.mean(scaled, axis=-1, keepdims=True)
    mean_cross = jnp.mean(scaled * normal, axis=-1, keepdims=True)
    inward = scale * (scaled - mean_grad - normal * mean_cross)
    return (inward, jnp.sum(upstream * normal, axis=0), jnp.sum(upstream, axis=0))


def context_allowed(segments, ranks, first, count):
    length = segments.shape[0]
    key_block = jnp.arange(length, dtype=jnp.int32) // BLK
    key_rank = jnp.broadcast_to(ranks[:, None], (ranks.shape[0], BLK)).reshape(length)
    query_segment = lax.dynamic_slice_in_dim(segments, first, count)
    query_rank = lax.dynamic_slice_in_dim(key_rank, first, count)
    query_block = (first + jnp.arange(count, dtype=jnp.int32)) // BLK
    same_doc = query_segment[:, None] == segments[None, :]
    earlier = key_rank[None, :] < query_rank[:, None]
    same_block = query_block[:, None] == key_block[None, :]
    return same_doc & (earlier | same_block)


def full_rows(value):
    return lax.all_gather(value, "tensor", axis=0, tiled=True)


def grad_rows(value):
    return lax.all_gather(value, "tensor", axis=0, tiled=True)


def branch_sum(mixed, weight):
    return lax.psum_scatter(
        jnp.dot(mixed, weight, preferred_element_type=jnp.float32),
        "tensor",
        scatter_dimension=0,
        tiled=True,
    )


def back_product(left, weight):
    return lax.dot_general(
        left, weight, (((1,), (1,)), ((), ())), preferred_element_type=jnp.float32
    )


def row_product(left, right):
    return lax.dot_general(
        left, right, (((0,), (0,)), ((), ())), preferred_element_type=jnp.float32
    )


def input_sum(pairs):
    total = None
    for left, weight in pairs:
        portion = back_product(left, weight)
        total = portion if total is None else total + portion
    return lax.psum_scatter(total, "tensor", scatter_dimension=0, tiled=True)


def split_heads(value, count):
    return value.reshape(count, LEN, value.shape[1] // HEAD, HEAD)


def attend_sequence(query, keys, values, segments, ranks, masked):
    length = query.shape[0]
    width = min(length, 512)

    def one_block(index):
        first = index * width
        piece = lax.dynamic_slice_in_dim(query, first, width, 0)
        scores = jnp.einsum("qhd,khd->hqk", piece, keys, preferred_element_type=jnp.float32) * 0.125
        if masked:
            scores = jnp.where(
                context_allowed(segments, ranks, first, width)[None], scores, mask_fill
            )
        top = jnp.max(scores, axis=-1, keepdims=True)
        raised = jnp.exp(scores - top)
        total = jnp.sum(raised, axis=-1, keepdims=True)
        shares = (raised / total).astype(jnp.bfloat16)
        mixed = jnp.einsum("hqk,khd->qhd", shares, values, preferred_element_type=jnp.float32)
        return (mixed.astype(jnp.bfloat16), (top + jnp.log(total))[..., 0])

    mixed, log_total = lax.map(one_block, jnp.arange(length // width, dtype=jnp.int32))
    return (mixed.reshape(query.shape), log_total)


def attend_sequence_back(query, keys, values, segments, ranks, masked, log_total, grad_mixed):
    length = query.shape[0]
    width = min(length, 512)

    def one_block(carry, index):
        key_sum, value_sum = carry
        first = index * width
        piece = lax.dynamic_slice_in_dim(query, first, width, 0)
        grad_piece = lax.dynamic_slice_in_dim(grad_mixed, first, width, 0)
        scores = jnp.einsum("qhd,khd->hqk", piece, keys, preferred_element_type=jnp.float32) * 0.125
        if masked:
            scores = jnp.where(
                context_allowed(segments, ranks, first, width)[None], scores, mask_fill
            )
        shares = jnp.exp(scores - log_total[index][..., None])
        grad_shares = jnp.einsum(
            "qhd,khd->hqk", grad_piece, values, preferred_element_type=jnp.float32
        )
        inner = jnp.sum(shares * grad_shares, axis=-1, keepdims=True)
        grad_scores = (shares * (grad_shares - inner)).astype(jnp.bfloat16)
        grad_query = (
            jnp.einsum("hqk,khd->qhd", grad_scores, keys, preferred_element_type=jnp.float32)
            * 0.125
        )
        key_sum = (
            key_sum
            + jnp.einsum("hqk,qhd->khd", grad_scores, piece, preferred_element_type=jnp.float32)
            * 0.125
        )
        value_sum = value_sum + jnp.einsum(
            "hqk,qhd->khd",
            shares.astype(jnp.bfloat16),
            grad_piece,
            preferred_element_type=jnp.float32,
        )
        return ((key_sum, value_sum), grad_query.astype(jnp.bfloat16))

    zeros = jnp.zeros(keys.shape, jnp.float32)
    (key_sum, value_sum), grad_query = lax.scan(
        one_block, (zeros, zeros), jnp.arange(length // width, dtype=jnp.int32)
    )
    return (
        grad_query.reshape(query.shape),
        key_sum.astype(jnp.bfloat16),
        value_sum.astype(jnp.bfloat16),
    )


def attend_all(query, keys, values, segments, ranks, masked):
    count = query.shape[0] // LEN

    def one_sequence(items):
        return attend_sequence(items[0], items[1], items[2], items[3], items[4], masked)

    mixed, log_total = lax.map(
        one_sequence,
        (
            split_heads(query, count),
            split_heads(keys, count),
            split_heads(values, count),
            segments,
            ranks,
        ),
    )
    return (mixed.reshape(query.shape), log_total)


def attend_back_all(query, keys, values, segments, ranks, masked, log_total, grad_mixed):
    count = query.shape[0] // LEN

    def one_sequence(items):
        return attend_sequence_back(
            items[0], items[1], items[2], items[3], items[4], masked, items[5], items[6]
        )

    grad_query, grad_keys, grad_values = lax.map(
        one_sequence,
        (
            split_heads(query, count),
            split_heads(keys, count),
            split_heads(values, count),
            segments,
            ranks,
            log_total,
            split_heads(grad_mixed, count),
        ),
    )
    return (
        grad_query.reshape(query.shape),
        grad_keys.reshape(keys.shape),
        grad_values.reshape(values.shape),
    )


def shards(
    tokens,
    encoder_states,
    output_grad,
    valid_mask,
    segment_ids,
    context_ranks,
    self_query,
    self_key,
    self_value,
    self_output,
    cross_query,
    cross_key,
    cross_value,
    cross_output,
    hidden_up,
    hidden_down,
    norm1_gain,
    norm1_bias,
    norm2_gain,
    norm2_bias,
    norm3_gain,
    norm3_bias,
):
    (
        self_query,
        self_key,
        self_value,
        self_output,
        cross_query,
        cross_key,
        cross_value,
        cross_output,
        hidden_up,
        hidden_down,
    ) = (
        lax.all_gather(self_query, "dp", axis=0, tiled=True),
        lax.all_gather(self_key, "dp", axis=0, tiled=True),
        lax.all_gather(self_value, "dp", axis=0, tiled=True),
        lax.all_gather(self_output, "dp", axis=1, tiled=True),
        lax.all_gather(cross_query, "dp", axis=0, tiled=True),
        lax.all_gather(cross_key, "dp", axis=0, tiled=True),
        lax.all_gather(cross_value, "dp", axis=0, tiled=True),
        lax.all_gather(cross_output, "dp", axis=1, tiled=True),
        lax.all_gather(hidden_up, "dp", axis=0, tiled=True),
        lax.all_gather(hidden_down, "dp", axis=1, tiled=True),
    )
    tokens_full = full_rows(tokens)
    query = jnp.dot(tokens_full, self_query, preferred_element_type=jnp.float32).astype(
        jnp.bfloat16
    )
    keys = jnp.dot(tokens_full, self_key, preferred_element_type=jnp.float32).astype(jnp.bfloat16)
    values = jnp.dot(tokens_full, self_value, preferred_element_type=jnp.float32).astype(
        jnp.bfloat16
    )
    self_mixed, self_log = attend_all(query, keys, values, segment_ids, context_ranks, True)
    attended = branch_sum(self_mixed, self_output)
    first_out, first_normal, first_scale = layer_norm(
        tokens.astype(jnp.float32) + attended, norm1_gain, norm1_bias
    )
    first_full = full_rows(first_out.astype(jnp.bfloat16))
    encoder_full = full_rows(encoder_states)
    second_query = jnp.dot(first_full, cross_query, preferred_element_type=jnp.float32).astype(
        jnp.bfloat16
    )
    encoder_keys = jnp.dot(encoder_full, cross_key, preferred_element_type=jnp.float32).astype(
        jnp.bfloat16
    )
    encoder_values = jnp.dot(encoder_full, cross_value, preferred_element_type=jnp.float32).astype(
        jnp.bfloat16
    )
    cross_mixed, cross_log = attend_all(
        second_query, encoder_keys, encoder_values, segment_ids, context_ranks, False
    )
    crossed = branch_sum(cross_mixed, cross_output)
    second_out, second_normal, second_scale = layer_norm(
        first_out + crossed, norm2_gain, norm2_bias
    )
    second_low = second_out.astype(jnp.bfloat16)
    feed_input = full_rows(second_low)
    preact = jnp.dot(feed_input, hidden_up, preferred_element_type=jnp.float32)
    activated = gelu_exact(preact).astype(jnp.bfloat16)
    feed_out = branch_sum(activated, hidden_down)
    third_out, third_normal, third_scale = layer_norm(second_out + feed_out, norm3_gain, norm3_bias)
    valid_rows = valid_mask.astype(jnp.float32)[:, None]
    grad_layer = output_grad.astype(jnp.float32) * valid_rows
    grad_third, gain3_grad, bias3_grad = norm_back(
        grad_layer, third_normal, third_scale, norm3_gain
    )
    grad_third_low = grad_third.astype(jnp.bfloat16)
    grad_feed = grad_rows(grad_third_low)
    grad_active = back_product(grad_feed, hidden_down)
    grad_preact = gelu_back(preact, grad_active).astype(jnp.bfloat16)
    up_grad = row_product(feed_input, grad_preact)
    down_grad = row_product(activated, grad_feed)
    grad_second = grad_third + input_sum([(grad_preact, hidden_up)])
    grad_second_in, gain2_grad, bias2_grad = norm_back(
        grad_second, second_normal, second_scale, norm2_gain
    )
    grad_crossed = grad_rows(grad_second_in.astype(jnp.bfloat16))
    cross_output_grad = row_product(cross_mixed, grad_crossed)
    grad_cross_mixed = back_product(grad_crossed, cross_output).astype(jnp.bfloat16)
    grad_second_query, grad_encoder_keys, grad_encoder_values = attend_back_all(
        second_query,
        encoder_keys,
        encoder_values,
        segment_ids,
        context_ranks,
        False,
        cross_log,
        grad_cross_mixed,
    )
    cross_query_grad = row_product(first_full, grad_second_query)
    cross_key_grad = row_product(encoder_full, grad_encoder_keys)
    cross_value_grad = row_product(encoder_full, grad_encoder_values)
    grad_first = grad_second_in + input_sum([(grad_second_query, cross_query)])
    encoder_grad = input_sum([(grad_encoder_keys, cross_key), (grad_encoder_values, cross_value)])
    grad_first_in, gain1_grad, bias1_grad = norm_back(
        grad_first, first_normal, first_scale, norm1_gain
    )
    grad_attended = grad_rows(grad_first_in.astype(jnp.bfloat16))
    self_output_grad = row_product(self_mixed, grad_attended)
    grad_self_mixed = back_product(grad_attended, self_output).astype(jnp.bfloat16)
    grad_query, grad_keys, grad_values = attend_back_all(
        query, keys, values, segment_ids, context_ranks, True, self_log, grad_self_mixed
    )
    self_query_grad = row_product(tokens_full, grad_query)
    self_key_grad = row_product(tokens_full, grad_keys)
    self_value_grad = row_product(tokens_full, grad_values)
    tokens_grad = grad_first_in + input_sum(
        [(grad_query, self_query), (grad_keys, self_key), (grad_values, self_value)]
    )
    (
        self_query_grad,
        self_key_grad,
        self_value_grad,
        self_output_grad,
        cross_query_grad,
        cross_key_grad,
        cross_value_grad,
        cross_output_grad,
        up_grad,
        down_grad,
    ) = (
        lax.psum_scatter(self_query_grad, "dp", scatter_dimension=0, tiled=True),
        lax.psum_scatter(self_key_grad, "dp", scatter_dimension=0, tiled=True),
        lax.psum_scatter(self_value_grad, "dp", scatter_dimension=0, tiled=True),
        lax.psum_scatter(self_output_grad, "dp", scatter_dimension=1, tiled=True),
        lax.psum_scatter(cross_query_grad, "dp", scatter_dimension=0, tiled=True),
        lax.psum_scatter(cross_key_grad, "dp", scatter_dimension=0, tiled=True),
        lax.psum_scatter(cross_value_grad, "dp", scatter_dimension=0, tiled=True),
        lax.psum_scatter(cross_output_grad, "dp", scatter_dimension=1, tiled=True),
        lax.psum_scatter(up_grad, "dp", scatter_dimension=0, tiled=True),
        lax.psum_scatter(down_grad, "dp", scatter_dimension=1, tiled=True),
    )
    norm_sums, square_sums = lax.psum(
        (
            jnp.stack([gain1_grad, bias1_grad, gain2_grad, bias2_grad, gain3_grad, bias3_grad]),
            jnp.stack(
                [
                    jnp.sum(valid_rows * third_out * third_out, axis=0),
                    jnp.sum(valid_rows * tokens_grad * tokens_grad, axis=0),
                ]
            ),
        ),
        ("dp", "tensor"),
    )
    total_tokens = tokens.shape[0] * lax.axis_size("dp") * lax.axis_size("tensor")
    valid_scales = jnp.sqrt(square_sums / total_tokens)
    return (
        third_out,
        tokens_grad,
        encoder_grad,
        self_query_grad,
        self_key_grad,
        self_value_grad,
        self_output_grad,
        cross_query_grad,
        cross_key_grad,
        cross_value_grad,
        cross_output_grad,
        up_grad,
        down_grad,
        norm_sums,
        valid_scales,
    )


MESH = pl.DeviceIdType.MESH
BF = jnp.bfloat16
F32 = jnp.float32
LOG2E = 1.4426950408889634
SCALE = 0.125 * LOG2E
CH = 128


def nn(a, b):
    return lax.dot_general(a, b, (((1,), (0,)), ((), ())), preferred_element_type=F32)


def nt(a, b):
    return lax.dot_general(a, b, (((1,), (1,)), ((), ())), preferred_element_type=F32)


def turn(x):
    return x.T


class Place:
    def __init__(self):
        self.d = lax.axis_index("dp")
        self.t = lax.axis_index("tensor")
        self.z, self.y = self.d // 2, self.d % 2
        self.x, self.c = self.t // 2, self.t % 2
        self.xt = (1 - self.x) * 2 + self.c
        self.xn = (self.d, self.xt)
        self.yn = (self.z * 2 + 1 - self.y, self.t)
        self.pair = (self.d, self.x * 2 + 1 - self.c)
        self.zn = [None] + [((((self.z + k) % 4) * 2 + self.y), self.t) for k in (1, 2, 3)]

    def barrier(self):
        sem = pltpu.get_barrier_semaphore()
        for dev in [self.xn, self.yn, self.pair] + self.zn[1:]:
            pl.semaphore_signal(sem, inc=1, device_id=dev, device_id_type=MESH)
        pl.semaphore_wait(sem, 6)


def remote(src, dst, send, recv, dev):
    return pltpu.make_async_remote_copy(
        src_ref=src, dst_ref=dst, send_sem=send, recv_sem=recv, device_id=dev, device_id_type=MESH
    )


class Gather:
    def __init__(self, p, w, cols, ss, rs):
        self.p, self.w, self.cols, self.ss, self.rs = p, w, cols, ss, rs

    def col(self, t):
        return pl.ds(pl.multiple_of(t * self.cols, 128), self.cols)

    def blk(self, k, y, t):
        zs = (self.p.z - k + 4) % 4
        return self.w.at[:, zs, y, :, self.col(t)]

    def cp(self, ref, i, dev):
        return remote(ref, ref, self.ss.at[i], self.rs.at[i], dev)

    def own(self):
        return self.blk(0, self.p.y, self.p.t)

    def z_send(self, k):
        return self.cp(self.own(), k - 1, self.p.zn[k])

    def z_recv(self, k):
        return self.cp(self.blk(k, self.p.y, self.p.t), k - 1, self.p.zn[k])

    def x_send(self, k):
        return self.cp(self.blk(k, self.p.y, self.p.t), 3 + k, self.p.xn)

    def x_recv(self, k):
        return self.cp(self.blk(k, self.p.y, self.p.xt), 3 + k, self.p.xn)

    def y_send(self, k):
        return self.cp(self.blk(k, self.p.y, self.p.t), 7 + k, self.p.yn)

    def y_recv(self, k):
        return self.cp(self.blk(k, 1 - self.p.y, self.p.t), 7 + k, self.p.yn)

    def q_send(self, k):
        if k < 2:
            return self.cp(self.blk(k, self.p.y, self.p.xt), 11 + k, self.p.yn)
        return self.cp(self.blk(k, 1 - self.p.y, self.p.t), 11 + k, self.p.xn)

    def q_recv(self, k):
        return self.cp(self.blk(k, 1 - self.p.y, self.p.xt), 11 + k, self.p.xn)

    def rail(self, i, core):
        x = self.p.x if i == 0 else 1 - self.p.x
        return self.w.at[:, :, :, :, self.col(x * 2 + core)]

    def p_send(self, i):
        return self.cp(self.rail(i, self.p.c), 15 + i, self.p.pair)

    def p_recv(self, i):
        return self.cp(self.rail(i, 1 - self.p.c), 15 + i, self.p.pair)

    def start(self):
        for k in (1, 2, 3):
            self.z_send(k).start()
        self.x_send(0).start()
        self.y_send(0).start()

    def plane(self):
        for k in (1, 2, 3):
            self.z_recv(k).wait_recv()
            self.x_send(k).start()
            self.y_send(k).start()

    def corner(self):
        for k in range(4):
            self.x_recv(k).wait_recv()
            if k < 2:
                self.q_send(k).start()
            self.y_recv(k).wait_recv()
            if k >= 2:
                self.q_send(k).start()

    def cross(self):
        self.p_send(0).start() if False else None
        for k in range(4):
            self.q_recv(k).wait_recv()
        self.p_send(0).start()
        self.p_send(1).start()

    def finish(self):
        self.p_recv(0).wait_recv()
        self.p_recv(1).wait_recv()

    def drain(self):
        for k in (1, 2, 3):
            self.z_send(k).wait_send()
        for k in range(4):
            self.x_send(k).wait_send()
            self.y_send(k).wait_send()
            self.q_send(k).wait_send()
        self.p_send(0).wait_send()
        self.p_send(1).wait_send()


class Reduce:
    def __init__(self, p, g, cols, held, r1, r2, r3, out, ss, rs):
        self.p, self.g, self.cols, self.held = p, g, cols, held
        self.r1, self.r2, self.r3, self.out, self.ss, self.rs = r1, r2, r3, out, ss, rs
        self.n = g.shape[0]

    def col(self, t):
        return pl.ds(pl.multiple_of(t * self.cols, 128), self.cols)

    def cp(self, src, dst, i, dev):
        return remote(src, dst, self.ss.at[i], self.rs.at[i], dev)

    def pair_copy(self, x):
        src = self.g.at[:, :, :, :, self.col(x * 2 + 1 - self.p.c)]
        return self.cp(src, self.held.at[x], x, self.p.pair)

    def corner_copy(self, i):
        p = self.p
        src = self.held.at[1 - p.x, :, pl.ds(2 * i, 2), 1 - p.y]
        return self.cp(src, self.r1.at[i], 2 + i, p.yn if i == 0 else p.xn)

    def plane_copy(self, i):
        p = self.p
        src = self.held.at[1 - p.x, :, :, p.y] if i == 0 else self.held.at[p.x, :, :, 1 - p.y]
        return self.cp(src, self.r2.at[i], 4 + i, p.xn if i == 0 else p.yn)

    def z_copy(self, k):
        p = self.p
        src = self.held.at[p.x, :, (p.z + k) % 4, p.y]
        return self.cp(src, self.r3.at[k - 1], 5 + k, p.zn[k])

    def start(self):
        self.pair_copy(0).start()
        self.pair_copy(1).start()

    def corner(self):
        for x in (0, 1):
            self.pair_copy(x).wait_recv()
        for x in (0, 1):
            col = self.col(x * 2 + self.p.c)

            def one(j, _, x=x, col=col):
                i, d = j // 8, j % 8
                mine = self.g[i, d // 2, d % 2, :, col].astype(F32)
                theirs = self.held[x, i, d // 2, d % 2].astype(F32)
                self.held[x, i, d // 2, d % 2] = (mine + theirs).astype(BF)
                return 0

            lax.fori_loop(0, self.n * 8, one, 0)
        self.corner_copy(0).start()
        self.corner_copy(1).start()

    def plane(self):
        p = self.p
        self.corner_copy(0).wait_recv()
        self.corner_copy(1).wait_recv()
        for i in range(self.n):
            for j in range(2):
                a = self.held[1 - p.x, i, j, p.y].astype(F32) + self.r1[0, i, j].astype(F32)
                self.held[1 - p.x, i, j, p.y] = a.astype(BF)
                b = self.held[p.x, i, 2 + j, 1 - p.y].astype(F32) + self.r1[1, i, j].astype(F32)
                self.held[p.x, i, 2 + j, 1 - p.y] = b.astype(BF)
        self.plane_copy(0).start()
        self.plane_copy(1).start()

    def along(self):
        p = self.p
        self.plane_copy(0).wait_recv()
        self.plane_copy(1).wait_recv()
        for k in (1, 2, 3):
            zt = (p.z + k) % 4
            for i in range(self.n):
                a = (
                    self.held[p.x, i, zt, p.y].astype(F32)
                    + self.r2[0, i, zt].astype(F32)
                    + self.r2[1, i, zt].astype(F32)
                )
                self.held[p.x, i, zt, p.y] = a.astype(BF)
            self.z_copy(k).start()

    def finish(self):
        p = self.p
        for k in (1, 2, 3):
            self.z_copy(k).wait_recv()
        for i in range(self.n):
            a = (
                self.held[p.x, i, p.z, p.y].astype(F32)
                + self.r2[0, i, p.z].astype(F32)
                + self.r2[1, i, p.z].astype(F32)
            )
            for k in range(3):
                a = a + self.r3[k, i].astype(F32)
            self.out[i] = a

    def drain(self):
        for i in (0, 1):
            self.pair_copy(i).wait_send()
            self.corner_copy(i).wait_send()
            self.plane_copy(i).wait_send()
        for k in (1, 2, 3):
            self.z_copy(k).wait_send()


def row_steps(count, one):
    def body(i, _):
        one(pl.ds(pl.multiple_of(i * CH, CH), CH))
        return 0

    lax.fori_loop(0, count // CH, body, 0)


def head_half(shape, axis, h):
    return (lax.broadcasted_iota(jnp.int32, shape, axis) // HEAD) == h


def keep_half(value, axis, h):
    return jnp.where(head_half(value.shape, axis, h), value.astype(F32), 0.0).astype(BF)


def attend(qt, k, vt, bias, ot, lse, temp, hooks):
    def pair(p, _):
        lanes = pl.ds(pl.multiple_of(p * 128, 128), 128)
        kp = k[:, lanes]
        qp = qt[lanes, :]
        for h in (0, 1):
            qm = keep_half(qp, 0, h)
            top = None
            for i in range(4):
                rows = slice(i * 256, i * 256 + 256)
                s = nn(kp[rows], qm) * SCALE
                if bias is not None:
                    s = s + bias[rows, :]
                temp[rows, :] = s
                m = jnp.max(s, axis=0, keepdims=True)
                top = m if top is None else jnp.maximum(top, m)
            total, mixed = None, None
            vh = vt[pl.ds(pl.multiple_of(p * 128 + h * 64, 64), 64), :]
            for i in range(4):
                rows = slice(i * 256, i * 256 + 256)
                e = jnp.exp2(temp[rows, :] - top)
                part = jnp.sum(e, axis=0, keepdims=True)
                total = part if total is None else total + part
                o = nn(vh[:, rows], e.astype(BF))
                mixed = o if mixed is None else mixed + o
            ot[pl.ds(pl.multiple_of(p * 128 + h * 64, 64), 64), :] = mixed * (1.0 / total)
            lse[pl.ds(p * 2 + h, 1), :] = top + jnp.log2(total)
        for at, hook in hooks.items():
            pl.when(p == at)(hook)
        return 0

    lax.fori_loop(0, 4, pair, 0)


def attend_back(q, qt, k, kt, v, do, dot_, ot, bias, lse, dqt, dk_own, dv_own, dkv_send, hooks):
    def pair(p, _):
        lanes = pl.ds(pl.multiple_of(p * 128, 128), 128)
        kp, vp = k[:, lanes], v[:, lanes]
        qp, dop = qt[lanes, :], dot_[lanes, :]
        inner = dop.astype(F32) * ot[lanes, :]
        qms = [keep_half(qp, 0, h) for h in (0, 1)]
        doms = [keep_half(dop, 0, h) for h in (0, 1)]
        qr = jnp.concatenate([keep_half(q[:, lanes], 1, h) for h in (0, 1)], axis=0)
        dor = jnp.concatenate([keep_half(do[:, lanes], 1, h) for h in (0, 1)], axis=0)
        ds_sum = [jnp.sum(inner[h * 64 : h * 64 + 64], axis=0, keepdims=True) for h in (0, 1)]
        logs = [lse[pl.ds(p * 2 + h, 1), :] for h in (0, 1)]
        dq = [None, None]
        for i in range(4):
            rows = slice(i * 256, i * 256 + 256)
            shares, grads = [], []
            for h in (0, 1):
                s = nn(kp[rows], qms[h]) * SCALE
                if bias is not None:
                    s = s + bias[rows, :]
                e = jnp.exp2(s - logs[h])
                dp = nn(vp[rows], doms[h])
                g = (e * (dp - ds_sum[h])).astype(BF)
                shares.append(e.astype(BF))
                grads.append(g)
                kh = kt[pl.ds(pl.multiple_of(p * 128 + h * 64, 64), 64), rows]
                part = nn(kh, g)
                dq[h] = part if dq[h] is None else dq[h] + part
            dv = nn(jnp.concatenate(shares, axis=1), dor)
            dk = nn(jnp.concatenate(grads, axis=1), qr) * 0.125
            if i < 2:
                dk_own[rows, lanes] = dk
                dv_own[rows, lanes] = dv
            else:
                back = slice(i * 256 - 512, i * 256 - 256)
                dkv_send[0, back, lanes] = dk.astype(BF)
                dkv_send[1, back, lanes] = dv.astype(BF)
        for h in (0, 1):
            dqt[pl.ds(pl.multiple_of(p * 128 + h * 64, 64), 64), :] = (dq[h] * 0.125).astype(BF)
        for at, hook in hooks.items():
            pl.when(p == at)(hook)
        return 0

    lax.fori_loop(0, 4, pair, 0)


def norm_rows(z):
    mean = jnp.mean(z, axis=-1, keepdims=True)
    centred = z - mean
    r = lax.rsqrt(jnp.mean(centred * centred, axis=-1, keepdims=True) + norm_eps)
    return centred * r, r


def norm_back_rows(e, n, r, gain):
    s = e * gain
    a = jnp.mean(s, axis=-1, keepdims=True)
    b = jnp.mean(s * n, axis=-1, keepdims=True)
    return r * (s - a - n * b)


def fast_kernel(
    x, enc, og, valid, seg, rank,
    sq, sk, sv, so, cq, ck, cv, co, up, down,
    g1, b1, g2, b2, g3, b3,
    y_o, dx_o, eg_o, ga_o, gb_o, gf_o, ns_o, vs_o,
    wa, wb, wf, ga,
    q1, qt1, k1, v1, vt1, o1, ot1, l1,
    q2, qt2, k2, v2, vt2, o2, ot2, l2,
    bias, n1, n2, r1, r2, h1b, h2b, u, gp, dg, dz, low, lowt, do, dot_,
    dqt, dq, kvs, kvr1, kvr2, dkv, tt, yb, vcol, st,
    ha, hb, hf, a1, a2, a3, m1, m2, m3, f1, f2, f3,
    st_r, gss, grs, rss, rrs, ess, ers, tss, trs, ls,
):
    p = Place()
    p.barrier()
    G = [
        Gather(p, w, cols, gss.at[i], grs.at[i])
        for i, (w, cols) in enumerate(((wa, 128), (wb, 128), (wf, 512)))
    ]
    GA, GB, GF = G
    loads = []
    for i, (src, w, j, cols) in enumerate(
        (
            (sq, wa, 0, 128), (sk, wa, 1, 128), (sv, wa, 2, 128),
            (ck, wb, 1, 128), (cv, wb, 2, 128), (cq, wb, 3, 128), (up, wf, 0, 512),
        )
    ):
        col = pl.ds(pl.multiple_of(p.t * cols, 128), cols)
        cp = pltpu.make_async_copy(src, w.at[j, p.z, p.y, :, col], ls.at[i])
        cp.start()
        loads.append(cp)
    for src, w, j, cols in ((so, wb, 0, 128), (co, wb, 4, 128), (down, wf, 1, 512)):
        col = pl.ds(pl.multiple_of(p.t * cols, 128), cols)
        w[j, p.z, p.y, :, col] = src[...].astype(F32).T.astype(BF)
    for cp in loads:
        cp.wait()
    GA.start()
    GB.start()
    GF.start()

    def mat(w, j):
        return w[j].reshape(512, w.shape[4])

    st[...] = jnp.zeros_like(st)
    vcol[...] = jnp.broadcast_to(valid[...].astype(F32), (128, 512)).T
    own = pl.ds(pl.multiple_of(p.c * 512, 128), 512)
    other = pl.ds(pl.multiple_of((1 - p.c) * 512, 128), 512)
    sx = pl.ds(p.x, 1)
    base = seg[sx, own] * 8
    high = base + rank[sx, own]
    for i, half in enumerate((own, other)):
        code = jnp.broadcast_to(seg[sx, half] * 8 + rank[sx, half], (128, 512)).T
        for j in range(4):
            c = code[j * 128 : j * 128 + 128, :1]
            ok = (c >= base) & (c <= high)
            bias[i * 512 + j * 128 : i * 512 + j * 128 + 128, :] = jnp.where(ok, 0.0, -2.0e9)

    GA.plane()
    GA.corner()
    GA.cross()
    GB.plane()
    GA.finish()

    xv = x[...]
    k1[0:512, :] = nn(xv, mat(wa, 1)).astype(BF)
    v1[0:512, :] = nn(xv, mat(wa, 2)).astype(BF)

    def swap(buf, i):
        return remote(buf.at[pl.ds(0, 512)], buf.at[pl.ds(512, 512)], ess.at[i], ers.at[i], p.pair)

    swap(k1, 0).start()
    swap(v1, 1).start()
    qv = nn(xv, mat(wa, 0)).astype(BF)
    q1[...] = qv
    qt1[...] = turn(qv)
    GB.corner()
    GF.plane()
    swap(k1, 0).wait_recv()
    swap(v1, 1).wait_recv()
    vt1[...] = turn(v1[...])
    attend(qt1, k1, vt1, bias, ot1, l1, gp, {0: GB.cross, 2: GF.corner})
    o1[...] = turn(ot1[...].astype(BF))
    GB.finish()
    ev = enc[...]
    k2[0:512, :] = nn(ev, mat(wb, 1)).astype(BF)
    v2[0:512, :] = nn(ev, mat(wb, 2)).astype(BF)
    swap(k2, 2).start()
    swap(v2, 3).start()
    yb[...] = nt(o1[...], mat(wb, 0))

    def first(r):
        n, s = norm_rows(x[r, :].astype(F32) + yb[r, :])
        n1[r, :] = n
        r1[r, :] = s
        h1b[r, :] = (n * g1[...] + b1[...]).astype(BF)

    row_steps(512, first)
    qv = nn(h1b[...], mat(wb, 3)).astype(BF)
    q2[...] = qv
    qt2[...] = turn(qv)
    swap(k2, 2).wait_recv()
    swap(v2, 3).wait_recv()
    vt2[...] = turn(v2[...])
    attend(qt2, k2, vt2, None, ot2, l2, gp, {0: GF.cross})
    o2[...] = turn(ot2[...].astype(BF))
    yb[...] = nt(o2[...], mat(wb, 4))

    def second(r):
        n, s = norm_rows(n1[r, :] * g1[...] + b1[...] + yb[r, :])
        n2[r, :] = n
        r2[r, :] = s
        h2b[r, :] = (n * g2[...] + b2[...]).astype(BF)

    row_steps(512, second)
    GF.finish()
    hv = h2b[...]
    for j in range(4):
        cols = slice(j * 512, j * 512 + 512)
        gp[cols, :] = nn(hv, wf[0, :, :, :, cols].reshape(512, 512))

        def gelu(r, j=j, cols=cols):
            at = pl.ds(pl.multiple_of(r.start + j * 512, CH), CH)
            v = gp[at, :]
            cdf = 0.5 * (1.0 + lax.erf(v * 0.7071067811865476))
            u[r, cols] = (v * cdf).astype(BF)
            gp[at, :] = cdf + v * (jnp.exp2(v * v * (-0.5 * LOG2E)) * 0.3989422804014327)

        row_steps(512, gelu)
    yb[...] = nt(u[...], mat(wf, 1))

    def third(r):
        n, s = norm_rows(n2[r, :] * g2[...] + b2[...] + yb[r, :])
        out = n * g3[...] + b3[...]
        vc = vcol[r, :1]
        yb[r, :] = out
        e = og[r, :].astype(F32) * vc
        st[4:5, :] += jnp.sum(e * n, axis=0, keepdims=True)
        st[5:6, :] += jnp.sum(e, axis=0, keepdims=True)
        st[6:7, :] += jnp.sum(vc * out * out, axis=0, keepdims=True)
        back = norm_back_rows(e, n, s, g3[...])
        dz[r, :] = back
        low[r, :] = back.astype(BF)

    row_steps(512, third)
    y_copy = pltpu.make_async_copy(yb, y_o, ls.at[7])
    y_copy.start()
    lv = low[...]
    lowt[...] = turn(lv)
    for j in range(4):
        cols = slice(j * 512, j * 512 + 512)
        dg[:, cols] = (nn(lv, wf[1, :, :, :, cols].reshape(512, 512)) * gp[cols, :]).astype(BF)
    dz[...] += nt(dg[...], mat(wf, 0))
    for g in G:
        g.drain()
    tt[...] = turn(h2b[...])
    for j in range(4):
        cols = slice(j * 512, j * 512 + 512)
        wf[0, :, :, :, cols] = nn(tt[...], dg[:, cols]).astype(BF).reshape(4, 2, 64, 512)
        wf[1, :, :, :, cols] = nn(lowt[...], u[:, cols]).astype(BF).reshape(4, 2, 64, 512)
    R = [
        Reduce(p, *args, rss.at[i], rrs.at[i])
        for i, args in enumerate(
            (
                (ga, 128, ha, a1, a2, a3, ga_o),
                (wb, 128, hb, m1, m2, m3, gb_o),
                (wf, 512, hf, f1, f2, f3, gf_o),
            )
        )
    ]
    RA, RB, RF = R
    RF.start()

    def back2(r):
        e = dz[r, :]
        n = n2[r, :]
        st[2:3, :] += jnp.sum(e * n, axis=0, keepdims=True)
        st[3:4, :] += jnp.sum(e, axis=0, keepdims=True)
        back = norm_back_rows(e, n, r2[r, :], g2[...])
        dz[r, :] = back
        low[r, :] = back.astype(BF)

    row_steps(512, back2)
    dov = nn(low[...], mat(wb, 4)).astype(BF)
    do[...] = dov
    dot_[...] = turn(dov)
    lowt[...] = turn(low[...])
    wb[4] = nn(lowt[...], o2[...]).astype(BF).reshape(4, 2, 64, 512)
    vt2[...] = turn(k2[...])
    attend_back(
        q2, qt2, k2, vt2, v2, do, dot_, ot2, None, l2, dqt,
        gp.at[pl.ds(0, 512)], gp.at[pl.ds(512, 512)], kvs,
        {0: RF.corner, 1: RF.plane, 3: RF.along},
    )

    def swap_back(buf, i):
        return remote(kvs, buf, ess.at[i], ers.at[i], p.pair)

    swap_back(kvr2, 4).start()
    dqv = turn(dqt[...])
    dz[...] += nt(dqv, mat(wb, 3))
    tt[...] = turn(h1b[...])
    wb[3] = nn(tt[...], dqv).astype(BF).reshape(4, 2, 64, 512)

    def back1(r):
        e = dz[r, :]
        n = n1[r, :]
        st[0:1, :] += jnp.sum(e * n, axis=0, keepdims=True)
        st[1:2, :] += jnp.sum(e, axis=0, keepdims=True)
        back = norm_back_rows(e, n, r1[r, :], g1[...])
        dz[r, :] = back
        low[r, :] = back.astype(BF)

    row_steps(512, back1)
    dov = nn(low[...], mat(wb, 0)).astype(BF)
    do[...] = dov
    dot_[...] = turn(dov)
    lowt[...] = turn(low[...])
    wb[0] = nn(lowt[...], o1[...]).astype(BF).reshape(4, 2, 64, 512)
    vt1[...] = turn(k1[...])
    swap_back(kvr2, 4).wait()

    def join(recv, at):
        def one(r):
            for i in (0, 1):
                own_rows = pl.ds(pl.multiple_of(r.start + at + i * 512, CH), CH)
                dkv[i, r, :] = (gp[own_rows, :] + recv[i, r, :].astype(F32)).astype(BF)

        row_steps(512, one)

    join(kvr2, 0)
    y_copy.wait()
    yb[...] = nt(dkv[0], mat(wb, 1)) + nt(dkv[1], mat(wb, 2))
    e_copy = pltpu.make_async_copy(yb, eg_o, ls.at[7])
    e_copy.start()
    tt[...] = turn(enc[...])
    wb[1] = nn(tt[...], dkv[0]).astype(BF).reshape(4, 2, 64, 512)
    wb[2] = nn(tt[...], dkv[1]).astype(BF).reshape(4, 2, 64, 512)
    RB.start()
    attend_back(
        q1, qt1, k1, vt1, v1, do, dot_, ot1, bias, l1, dqt,
        gp.at[pl.ds(1024, 512)], gp.at[pl.ds(1536, 512)], kvs,
        {0: RB.corner, 1: RB.plane, 2: RF.finish, 3: RB.along},
    )
    swap_back(kvr1, 5).start()
    tt[...] = turn(x[...])
    dqv = turn(dqt[...])
    ga[0] = nn(tt[...], dqv).astype(BF).reshape(4, 2, 64, 512)
    dz[...] += nt(dqv, mat(wa, 0))
    swap_back(kvr1, 5).wait()
    join(kvr1, 1024)
    ga[1] = nn(tt[...], dkv[0]).astype(BF).reshape(4, 2, 64, 512)
    ga[2] = nn(tt[...], dkv[1]).astype(BF).reshape(4, 2, 64, 512)
    RA.start()
    dz[...] += nt(dkv[0], mat(wa, 1)) + nt(dkv[1], mat(wa, 2))
    RA.corner()
    x_copy = pltpu.make_async_copy(dz, dx_o, ls.at[8])
    x_copy.start()

    def squares(r):
        st[7:8, :] += jnp.sum(vcol[r, :1] * dz[r, :] * dz[r, :], axis=0, keepdims=True)

    row_steps(512, squares)

    def stat(i, src, dev):
        return remote(src, st_r.at[i], tss.at[i], trs.at[i], dev)

    stat(0, st, p.pair).start()
    RA.plane()
    RB.finish()
    stat(0, st, p.pair).wait()
    st_r[6] = st[...] + st_r[0]
    stat(1, st_r.at[6], p.xn).start()
    stat(1, st_r.at[6], p.xn).wait()
    st_r[7] = st_r[6] + st_r[1]
    stat(2, st_r.at[7], p.yn).start()
    RA.along()
    stat(2, st_r.at[7], p.yn).wait()
    st_r[8] = st_r[7] + st_r[2]
    for k in (1, 2, 3):
        stat(2 + k, st_r.at[8], p.zn[k]).start()
    RA.finish()
    for k in (1, 2, 3):
        stat(2 + k, st_r.at[8], p.zn[k]).wait()
    total = None
    for zs in range(4):
        part = None
        for k in range(4):
            got = st_r[8] if k == 0 else st_r[2 + k]
            got = jnp.where((p.z - k + 4) % 4 == zs, got, 0.0)
            part = got if part is None else part + got
        total = part if total is None else total + part
    ns_o[...] = total[0:6]
    vs_o[...] = jnp.sqrt(total[6:8] * (1.0 / 16384.0))
    for i in range(4):
        swap((k1, v1, k2, v2)[i], i).wait_send()
    for r in R:
        r.drain()
    e_copy.wait()
    x_copy.wait()


def fast_shards(
    tokens, encoder_states, output_grad, valid_mask, segment_ids, context_ranks,
    self_query, self_key, self_value, self_output,
    cross_query, cross_key, cross_value, cross_output, hidden_up, hidden_down,
    norm1_gain, norm1_bias, norm2_gain, norm2_bias, norm3_gain, norm3_bias,
):
    vm = pl.BlockSpec(memory_space=pltpu.VMEM)
    hbm = pl.BlockSpec(memory_space=pl.ANY)
    ranks = jnp.repeat(context_ranks, BLK, axis=1)
    rows = [
        v.reshape(1, 512)
        for v in (norm1_gain, norm1_bias, norm2_gain, norm2_bias, norm3_gain, norm3_bias)
    ]

    def V(*shape, dtype=BF):
        return pltpu.VMEM(shape, dtype)

    def S(*shape):
        return pltpu.SemaphoreType.DMA(shape)

    def group(n, cols):
        return [
            V(2, n, 4, 2, 64, cols),
            [V(2, n, 2, 64, cols), V(2, n, 4, 64, cols), V(3, n, 64, cols)],
        ]

    ra, rb, rf = group(3, 128), group(5, 128), group(2, 512)

    def attention():
        return [
            V(512, 512), V(512, 512), V(1024, 512), V(1024, 512), V(512, 1024), V(512, 512),
            V(512, 512, dtype=F32), V(8, 512, dtype=F32),
        ]

    scratch = (
        [V(3, 4, 2, 64, 512), V(5, 4, 2, 64, 512), V(2, 4, 2, 64, 2048), V(3, 4, 2, 64, 512)]
        + attention()
        + attention()
        + [V(1024, 512, dtype=F32), V(512, 512, dtype=F32), V(512, 512, dtype=F32)]
        + [V(512, 1, dtype=F32), V(512, 1, dtype=F32), V(512, 512), V(512, 512)]
        + [V(512, 2048), V(2048, 512, dtype=F32), V(512, 2048), V(512, 512, dtype=F32)]
        + [V(512, 512)] * 4
        + [V(512, 512), V(512, 512), V(2, 512, 512), V(2, 512, 512), V(2, 512, 512), V(2, 512, 512)]
        + [V(512, 512), V(512, 512, dtype=F32), V(512, 128, dtype=F32), V(8, 512, dtype=F32)]
        + [ra[0], rb[0], rf[0]]
        + ra[1] + rb[1] + rf[1]
        + [V(9, 8, 512, dtype=F32)]
        + [S(3, 17), S(3, 17), S(3, 9), S(3, 9), S(6), S(6), S(6), S(6), S(9)]
    )
    big = jax.ShapeDtypeStruct((512, 512), F32)
    outs = pl.pallas_call(
        fast_kernel,
        out_shape=[big, big, big]
        + [jax.ShapeDtypeStruct(s, F32) for s in ((3, 64, 128), (5, 64, 128), (2, 64, 512), (6, 512), (2, 512))],
        in_specs=[vm] * 6 + [hbm] * 3 + [vm] + [hbm] * 3 + [vm] + [hbm] + [vm] + [vm] * 6,
        out_specs=[hbm] * 3 + [vm] * 5,
        scratch_shapes=scratch,
        compiler_params=pltpu.CompilerParams(
            collective_id=0, has_side_effects=True, vmem_limit_bytes=60 << 20
        ),
        name="layer",
    )(
        tokens, encoder_states, output_grad, valid_mask.reshape(1, 512), segment_ids, ranks,
        self_query, self_key, self_value, self_output,
        cross_query, cross_key, cross_value, cross_output, hidden_up, hidden_down, *rows,
    )
    y, dx, eg, ga, gb, gf, ns, vs = outs
    return (
        y, dx, eg, ga[0], ga[1], ga[2], gb[0].T, gb[3], gb[1], gb[2], gb[4].T, gf[0], gf[1].T, ns, vs,
    )


def solution(mesh):
    in_specs = (
        P(("dp", "tensor"), None),
        P(("dp", "tensor"), None),
        P(("dp", "tensor"), None),
        P(("dp", "tensor")),
        P("dp", None),
        P("dp", None),
        P("dp", "tensor"),
        P("dp", "tensor"),
        P("dp", "tensor"),
        P("tensor", "dp"),
        P("dp", "tensor"),
        P("dp", "tensor"),
        P("dp", "tensor"),
        P("tensor", "dp"),
        P("dp", "tensor"),
        P("tensor", "dp"),
        P(),
        P(),
        P(),
        P(),
        P(),
        P(),
    )
    out_specs = (
        P(("dp", "tensor"), None),
        P(("dp", "tensor"), None),
        P(("dp", "tensor"), None),
        P("dp", "tensor"),
        P("dp", "tensor"),
        P("dp", "tensor"),
        P("tensor", "dp"),
        P("dp", "tensor"),
        P("dp", "tensor"),
        P("dp", "tensor"),
        P("tensor", "dp"),
        P("dp", "tensor"),
        P("tensor", "dp"),
        P(),
        P(),
    )
    body = fast_shards if dict(mesh.shape) == {"dp": 8, "tensor": 4} else shards
    return jax.shard_map(body, mesh=mesh, in_specs=in_specs, out_specs=out_specs, check_vma=False)
```

```python
import jax
import jax.numpy as jnp
from jax import lax
from jax.experimental import pallas as pl
from jax.experimental.pallas import tpu as pltpu
from jax.sharding import PartitionSpec as P

HEAD = 64
LEN = 1024
BLK = 128


norm_eps = 1e-05
mask_fill = -1000000000.0


def gelu_exact(value):
    return jax.nn.gelu(value, approximate=False)


def gelu_back(preact, upstream):
    return jax.vjp(gelu_exact, preact)[1](upstream)[0]


def layer_norm(value, gain, bias):
    mean = jnp.mean(value, axis=-1, keepdims=True)
    centred = value - mean
    scale = lax.rsqrt(jnp.mean(centred * centred, axis=-1, keepdims=True) + norm_eps)
    normal = centred * scale
    return (normal * gain + bias, normal, scale)


def norm_back(upstream, normal, scale, gain):
    scaled = upstream * gain
    mean_grad = jnp.mean(scaled, axis=-1, keepdims=True)
    mean_cross = jnp.mean(scaled * normal, axis=-1, keepdims=True)
    inward = scale * (scaled - mean_grad - normal * mean_cross)
    return (inward, jnp.sum(upstream * normal, axis=0), jnp.sum(upstream, axis=0))


def context_allowed(segments, ranks, first, count):
    length = segments.shape[0]
    key_block = jnp.arange(length, dtype=jnp.int32) // BLK
    key_rank = jnp.broadcast_to(ranks[:, None], (ranks.shape[0], BLK)).reshape(length)
    query_segment = lax.dynamic_slice_in_dim(segments, first, count)
    query_rank = lax.dynamic_slice_in_dim(key_rank, first, count)
    query_block = (first + jnp.arange(count, dtype=jnp.int32)) // BLK
    same_doc = query_segment[:, None] == segments[None, :]
    earlier = key_rank[None, :] < query_rank[:, None]
    same_block = query_block[:, None] == key_block[None, :]
    return same_doc & (earlier | same_block)


def full_rows(value):
    return lax.all_gather(value, "tensor", axis=0, tiled=True)


def grad_rows(value):
    return lax.all_gather(value, "tensor", axis=0, tiled=True)


def branch_sum(mixed, weight):
    return lax.psum_scatter(
        jnp.dot(mixed, weight, preferred_element_type=jnp.float32),
        "tensor",
        scatter_dimension=0,
        tiled=True,
    )


def back_product(left, weight):
    return lax.dot_general(
        left, weight, (((1,), (1,)), ((), ())), preferred_element_type=jnp.float32
    )


def row_product(left, right):
    return lax.dot_general(
        left, right, (((0,), (0,)), ((), ())), preferred_element_type=jnp.float32
    )


def input_sum(pairs):
    total = None
    for left, weight in pairs:
        portion = back_product(left, weight)
        total = portion if total is None else total + portion
    return lax.psum_scatter(total, "tensor", scatter_dimension=0, tiled=True)


def split_heads(value, count):
    return value.reshape(count, LEN, value.shape[1] // HEAD, HEAD)


def attend_sequence(query, keys, values, segments, ranks, masked):
    length = query.shape[0]
    width = min(length, 512)

    def one_block(index):
        first = index * width
        piece = lax.dynamic_slice_in_dim(query, first, width, 0)
        scores = jnp.einsum("qhd,khd->hqk", piece, keys, preferred_element_type=jnp.float32) * 0.125
        if masked:
            scores = jnp.where(
                context_allowed(segments, ranks, first, width)[None], scores, mask_fill
            )
        top = jnp.max(scores, axis=-1, keepdims=True)
        raised = jnp.exp(scores - top)
        total = jnp.sum(raised, axis=-1, keepdims=True)
        shares = (raised / total).astype(jnp.bfloat16)
        mixed = jnp.einsum("hqk,khd->qhd", shares, values, preferred_element_type=jnp.float32)
        return (mixed.astype(jnp.bfloat16), (top + jnp.log(total))[..., 0])

    mixed, log_total = lax.map(one_block, jnp.arange(length // width, dtype=jnp.int32))
    return (mixed.reshape(query.shape), log_total)


def attend_sequence_back(query, keys, values, segments, ranks, masked, log_total, grad_mixed):
    length = query.shape[0]
    width = min(length, 512)

    def one_block(carry, index):
        key_sum, value_sum = carry
        first = index * width
        piece = lax.dynamic_slice_in_dim(query, first, width, 0)
        grad_piece = lax.dynamic_slice_in_dim(grad_mixed, first, width, 0)
        scores = jnp.einsum("qhd,khd->hqk", piece, keys, preferred_element_type=jnp.float32) * 0.125
        if masked:
            scores = jnp.where(
                context_allowed(segments, ranks, first, width)[None], scores, mask_fill
            )
        shares = jnp.exp(scores - log_total[index][..., None])
        grad_shares = jnp.einsum(
            "qhd,khd->hqk", grad_piece, values, preferred_element_type=jnp.float32
        )
        inner = jnp.sum(shares * grad_shares, axis=-1, keepdims=True)
        grad_scores = (shares * (grad_shares - inner)).astype(jnp.bfloat16)
        grad_query = (
            jnp.einsum("hqk,khd->qhd", grad_scores, keys, preferred_element_type=jnp.float32)
            * 0.125
        )
        key_sum = (
            key_sum
            + jnp.einsum("hqk,qhd->khd", grad_scores, piece, preferred_element_type=jnp.float32)
            * 0.125
        )
        value_sum = value_sum + jnp.einsum(
            "hqk,qhd->khd",
            shares.astype(jnp.bfloat16),
            grad_piece,
            preferred_element_type=jnp.float32,
        )
        return ((key_sum, value_sum), grad_query.astype(jnp.bfloat16))

    zeros = jnp.zeros(keys.shape, jnp.float32)
    (key_sum, value_sum), grad_query = lax.scan(
        one_block, (zeros, zeros), jnp.arange(length // width, dtype=jnp.int32)
    )
    return (
        grad_query.reshape(query.shape),
        key_sum.astype(jnp.bfloat16),
        value_sum.astype(jnp.bfloat16),
    )


def attend_all(query, keys, values, segments, ranks, masked):
    count = query.shape[0] // LEN

    def one_sequence(items):
        return attend_sequence(items[0], items[1], items[2], items[3], items[4], masked)

    mixed, log_total = lax.map(
        one_sequence,
        (
            split_heads(query, count),
            split_heads(keys, count),
            split_heads(values, count),
            segments,
            ranks,
        ),
    )
    return (mixed.reshape(query.shape), log_total)


def attend_back_all(query, keys, values, segments, ranks, masked, log_total, grad_mixed):
    count = query.shape[0] // LEN

    def one_sequence(items):
        return attend_sequence_back(
            items[0], items[1], items[2], items[3], items[4], masked, items[5], items[6]
        )

    grad_query, grad_keys, grad_values = lax.map(
        one_sequence,
        (
            split_heads(query, count),
            split_heads(keys, count),
            split_heads(values, count),
            segments,
            ranks,
            log_total,
            split_heads(grad_mixed, count),
        ),
    )
    return (
        grad_query.reshape(query.shape),
        grad_keys.reshape(keys.shape),
        grad_values.reshape(values.shape),
    )


def shards(
    tokens,
    encoder_states,
    output_grad,
    valid_mask,
    segment_ids,
    context_ranks,
    self_query,
    self_key,
    self_value,
    self_output,
    cross_query,
    cross_key,
    cross_value,
    cross_output,
    hidden_up,
    hidden_down,
    norm1_gain,
    norm1_bias,
    norm2_gain,
    norm2_bias,
    norm3_gain,
    norm3_bias,
):
    (
        self_query,
        self_key,
        self_value,
        self_output,
        cross_query,
        cross_key,
        cross_value,
        cross_output,
        hidden_up,
        hidden_down,
    ) = (
        lax.all_gather(self_query, "dp", axis=0, tiled=True),
        lax.all_gather(self_key, "dp", axis=0, tiled=True),
        lax.all_gather(self_value, "dp", axis=0, tiled=True),
        lax.all_gather(self_output, "dp", axis=1, tiled=True),
        lax.all_gather(cross_query, "dp", axis=0, tiled=True),
        lax.all_gather(cross_key, "dp", axis=0, tiled=True),
        lax.all_gather(cross_value, "dp", axis=0, tiled=True),
        lax.all_gather(cross_output, "dp", axis=1, tiled=True),
        lax.all_gather(hidden_up, "dp", axis=0, tiled=True),
        lax.all_gather(hidden_down, "dp", axis=1, tiled=True),
    )
    tokens_full = full_rows(tokens)
    query = jnp.dot(tokens_full, self_query, preferred_element_type=jnp.float32).astype(
        jnp.bfloat16
    )
    keys = jnp.dot(tokens_full, self_key, preferred_element_type=jnp.float32).astype(jnp.bfloat16)
    values = jnp.dot(tokens_full, self_value, preferred_element_type=jnp.float32).astype(
        jnp.bfloat16
    )
    self_mixed, self_log = attend_all(query, keys, values, segment_ids, context_ranks, True)
    attended = branch_sum(self_mixed, self_output)
    first_out, first_normal, first_scale = layer_norm(
        tokens.astype(jnp.float32) + attended, norm1_gain, norm1_bias
    )
    first_full = full_rows(first_out.astype(jnp.bfloat16))
    encoder_full = full_rows(encoder_states)
    second_query = jnp.dot(first_full, cross_query, preferred_element_type=jnp.float32).astype(
        jnp.bfloat16
    )
    encoder_keys = jnp.dot(encoder_full, cross_key, preferred_element_type=jnp.float32).astype(
        jnp.bfloat16
    )
    encoder_values = jnp.dot(encoder_full, cross_value, preferred_element_type=jnp.float32).astype(
        jnp.bfloat16
    )
    cross_mixed, cross_log = attend_all(
        second_query, encoder_keys, encoder_values, segment_ids, context_ranks, False
    )
    crossed = branch_sum(cross_mixed, cross_output)
    second_out, second_normal, second_scale = layer_norm(
        first_out + crossed, norm2_gain, norm2_bias
    )
    second_low = second_out.astype(jnp.bfloat16)
    feed_input = full_rows(second_low)
    preact = jnp.dot(feed_input, hidden_up, preferred_element_type=jnp.float32)
    activated = gelu_exact(preact).astype(jnp.bfloat16)
    feed_out = branch_sum(activated, hidden_down)
    third_out, third_normal, third_scale = layer_norm(second_out + feed_out, norm3_gain, norm3_bias)
    valid_rows = valid_mask.astype(jnp.float32)[:, None]
    grad_layer = output_grad.astype(jnp.float32) * valid_rows
    grad_third, gain3_grad, bias3_grad = norm_back(
        grad_layer, third_normal, third_scale, norm3_gain
    )
    grad_third_low = grad_third.astype(jnp.bfloat16)
    grad_feed = grad_rows(grad_third_low)
    grad_active = back_product(grad_feed, hidden_down)
    grad_preact = gelu_back(preact, grad_active).astype(jnp.bfloat16)
    up_grad = row_product(feed_input, grad_preact)
    down_grad = row_product(activated, grad_feed)
    grad_second = grad_third + input_sum([(grad_preact, hidden_up)])
    grad_second_in, gain2_grad, bias2_grad = norm_back(
        grad_second, second_normal, second_scale, norm2_gain
    )
    grad_crossed = grad_rows(grad_second_in.astype(jnp.bfloat16))
    cross_output_grad = row_product(cross_mixed, grad_crossed)
    grad_cross_mixed = back_product(grad_crossed, cross_output).astype(jnp.bfloat16)
    grad_second_query, grad_encoder_keys, grad_encoder_values = attend_back_all(
        second_query,
        encoder_keys,
        encoder_values,
        segment_ids,
        context_ranks,
        False,
        cross_log,
        grad_cross_mixed,
    )
    cross_query_grad = row_product(first_full, grad_second_query)
    cross_key_grad = row_product(encoder_full, grad_encoder_keys)
    cross_value_grad = row_product(encoder_full, grad_encoder_values)
    grad_first = grad_second_in + input_sum([(grad_second_query, cross_query)])
    encoder_grad = input_sum([(grad_encoder_keys, cross_key), (grad_encoder_values, cross_value)])
    grad_first_in, gain1_grad, bias1_grad = norm_back(
        grad_first, first_normal, first_scale, norm1_gain
    )
    grad_attended = grad_rows(grad_first_in.astype(jnp.bfloat16))
    self_output_grad = row_product(self_mixed, grad_attended)
    grad_self_mixed = back_product(grad_attended, self_output).astype(jnp.bfloat16)
    grad_query, grad_keys, grad_values = attend_back_all(
        query, keys, values, segment_ids, context_ranks, True, self_log, grad_self_mixed
    )
    self_query_grad = row_product(tokens_full, grad_query)
    self_key_grad = row_product(tokens_full, grad_keys)
    self_value_grad = row_product(tokens_full, grad_values)
    tokens_grad = grad_first_in + input_sum(
        [(grad_query, self_query), (grad_keys, self_key), (grad_values, self_value)]
    )
    (
        self_query_grad,
        self_key_grad,
        self_value_grad,
        self_output_grad,
        cross_query_grad,
        cross_key_grad,
        cross_value_grad,
        cross_output_grad,
        up_grad,
        down_grad,
    ) = (
        lax.psum_scatter(self_query_grad, "dp", scatter_dimension=0, tiled=True),
        lax.psum_scatter(self_key_grad, "dp", scatter_dimension=0, tiled=True),
        lax.psum_scatter(self_value_grad, "dp", scatter_dimension=0, tiled=True),
        lax.psum_scatter(self_output_grad, "dp", scatter_dimension=1, tiled=True),
        lax.psum_scatter(cross_query_grad, "dp", scatter_dimension=0, tiled=True),
        lax.psum_scatter(cross_key_grad, "dp", scatter_dimension=0, tiled=True),
        lax.psum_scatter(cross_value_grad, "dp", scatter_dimension=0, tiled=True),
        lax.psum_scatter(cross_output_grad, "dp", scatter_dimension=1, tiled=True),
        lax.psum_scatter(up_grad, "dp", scatter_dimension=0, tiled=True),
        lax.psum_scatter(down_grad, "dp", scatter_dimension=1, tiled=True),
    )
    norm_sums, square_sums = lax.psum(
        (
            jnp.stack([gain1_grad, bias1_grad, gain2_grad, bias2_grad, gain3_grad, bias3_grad]),
            jnp.stack(
                [
                    jnp.sum(valid_rows * third_out * third_out, axis=0),
                    jnp.sum(valid_rows * tokens_grad * tokens_grad, axis=0),
                ]
            ),
        ),
        ("dp", "tensor"),
    )
    total_tokens = tokens.shape[0] * lax.axis_size("dp") * lax.axis_size("tensor")
    valid_scales = jnp.sqrt(square_sums / total_tokens)
    return (
        third_out,
        tokens_grad,
        encoder_grad,
        self_query_grad,
        self_key_grad,
        self_value_grad,
        self_output_grad,
        cross_query_grad,
        cross_key_grad,
        cross_value_grad,
        cross_output_grad,
        up_grad,
        down_grad,
        norm_sums,
        valid_scales,
    )


MESH = pl.DeviceIdType.MESH
BF = jnp.bfloat16
F32 = jnp.float32
LOG2E = 1.4426950408889634
SCALE = 0.125 * LOG2E
CH = 128


def nn(a, b):
    return lax.dot_general(a, b, (((1,), (0,)), ((), ())), preferred_element_type=F32)


def nt(a, b):
    return lax.dot_general(a, b, (((1,), (1,)), ((), ())), preferred_element_type=F32)


def turn(x):
    return x.T


class Place:
    def __init__(self):
        self.d = lax.axis_index("dp")
        self.t = lax.axis_index("tensor")
        self.z, self.y = self.d // 2, self.d % 2
        self.x, self.c = self.t // 2, self.t % 2
        self.xt = (1 - self.x) * 2 + self.c
        self.xn = (self.d, self.xt)
        self.yn = (self.z * 2 + 1 - self.y, self.t)
        self.pair = (self.d, self.x * 2 + 1 - self.c)
        self.zn = [None] + [((((self.z + k) % 4) * 2 + self.y), self.t) for k in (1, 2, 3)]

    def barrier(self):
        sem = pltpu.get_barrier_semaphore()
        for dev in [self.xn, self.yn, self.pair] + self.zn[1:]:
            pl.semaphore_signal(sem, inc=1, device_id=dev, device_id_type=MESH)
        pl.semaphore_wait(sem, 6)


def remote(src, dst, send, recv, dev):
    return pltpu.make_async_remote_copy(
        src_ref=src, dst_ref=dst, send_sem=send, recv_sem=recv, device_id=dev, device_id_type=MESH
    )


class Gather:
    def __init__(self, p, w, cols, ss, rs):
        self.p, self.w, self.cols, self.ss, self.rs = p, w, cols, ss, rs

    def col(self, t):
        return pl.ds(pl.multiple_of(t * self.cols, 128), self.cols)

    def blk(self, k, y, t):
        zs = (self.p.z - k + 4) % 4
        return self.w.at[:, zs, y, :, self.col(t)]

    def cp(self, ref, i, dev):
        return remote(ref, ref, self.ss.at[i], self.rs.at[i], dev)

    def own(self):
        return self.blk(0, self.p.y, self.p.t)

    def z_send(self, k):
        return self.cp(self.own(), k - 1, self.p.zn[k])

    def z_recv(self, k):
        return self.cp(self.blk(k, self.p.y, self.p.t), k - 1, self.p.zn[k])

    def x_send(self, k):
        return self.cp(self.blk(k, self.p.y, self.p.t), 3 + k, self.p.xn)

    def x_recv(self, k):
        return self.cp(self.blk(k, self.p.y, self.p.xt), 3 + k, self.p.xn)

    def y_send(self, k):
        return self.cp(self.blk(k, self.p.y, self.p.t), 7 + k, self.p.yn)

    def y_recv(self, k):
        return self.cp(self.blk(k, 1 - self.p.y, self.p.t), 7 + k, self.p.yn)

    def q_send(self, k):
        if k < 2:
            return self.cp(self.blk(k, self.p.y, self.p.xt), 11 + k, self.p.yn)
        return self.cp(self.blk(k, 1 - self.p.y, self.p.t), 11 + k, self.p.xn)

    def q_recv(self, k):
        return self.cp(self.blk(k, 1 - self.p.y, self.p.xt), 11 + k, self.p.xn)

    def rail(self, i, core):
        x = self.p.x if i == 0 else 1 - self.p.x
        return self.w.at[:, :, :, :, self.col(x * 2 + core)]

    def p_send(self, i):
        return self.cp(self.rail(i, self.p.c), 15 + i, self.p.pair)

    def p_recv(self, i):
        return self.cp(self.rail(i, 1 - self.p.c), 15 + i, self.p.pair)

    def zs(self):
        for k in (1, 2, 3):
            self.z_send(k).start()

    def oxy(self):
        self.x_send(0).start()
        self.y_send(0).start()

    def plane(self, *between):
        for k in (1, 2, 3):
            self.z_recv(k).wait_recv()
            if k == 1:
                for fn in between:
                    fn()
            self.x_send(k).start()
            self.y_send(k).start()

    def corner(self):
        for k in range(4):
            self.x_recv(k).wait_recv()
            if k < 2:
                self.q_send(k).start()
            self.y_recv(k).wait_recv()
            if k >= 2:
                self.q_send(k).start()
        self.p_send(0).start()

    def cross(self):
        for k in range(4):
            self.q_recv(k).wait_recv()
        self.p_send(1).start()

    def finish(self):
        self.p_recv(0).wait_recv()
        self.p_recv(1).wait_recv()

    def drain(self):
        for k in (1, 2, 3):
            self.z_send(k).wait_send()
        for k in range(4):
            self.x_send(k).wait_send()
            self.y_send(k).wait_send()
            self.q_send(k).wait_send()
        self.p_send(0).wait_send()
        self.p_send(1).wait_send()


class Reduce:
    def __init__(self, p, g, cols, held, r1, r2, r3, out, ss, rs):
        self.p, self.g, self.cols, self.held = p, g, cols, held
        self.r1, self.r2, self.r3, self.out, self.ss, self.rs = r1, r2, r3, out, ss, rs
        self.n = g.shape[0]

    def col(self, t):
        return pl.ds(pl.multiple_of(t * self.cols, 128), self.cols)

    def cp(self, src, dst, i, dev):
        return remote(src, dst, self.ss.at[i], self.rs.at[i], dev)

    def pair_copy(self, x):
        src = self.g.at[:, :, :, :, self.col(x * 2 + 1 - self.p.c)]
        return self.cp(src, self.held.at[x], x, self.p.pair)

    def corner_copy(self, i):
        p = self.p
        src = self.held.at[1 - p.x, :, pl.ds(2 * i, 2), 1 - p.y]
        return self.cp(src, self.r1.at[i], 2 + i, p.yn if i == 0 else p.xn)

    def plane_copy(self, i):
        p = self.p
        src = self.held.at[1 - p.x, :, :, p.y] if i == 0 else self.held.at[p.x, :, :, 1 - p.y]
        return self.cp(src, self.r2.at[i], 4 + i, p.xn if i == 0 else p.yn)

    def z_copy(self, k):
        p = self.p
        src = self.held.at[p.x, :, (p.z + k) % 4, p.y]
        return self.cp(src, self.r3.at[k - 1], 5 + k, p.zn[k])

    def start(self):
        self.pair_copy(0).start()
        self.pair_copy(1).start()

    def corner(self):
        for x in (0, 1):
            self.pair_copy(x).wait_recv()
        for x in (0, 1):
            col = self.col(x * 2 + self.p.c)

            def one(j, _, x=x, col=col):
                i, d = j // 8, j % 8
                mine = self.g[i, d // 2, d % 2, :, col].astype(F32)
                theirs = self.held[x, i, d // 2, d % 2].astype(F32)
                self.held[x, i, d // 2, d % 2] = (mine + theirs).astype(BF)
                return 0

            lax.fori_loop(0, self.n * 8, one, 0)
        self.corner_copy(0).start()
        self.corner_copy(1).start()

    def plane(self):
        p = self.p
        self.corner_copy(0).wait_recv()
        self.corner_copy(1).wait_recv()
        for i in range(self.n):
            for j in range(2):
                a = self.held[1 - p.x, i, j, p.y].astype(F32) + self.r1[0, i, j].astype(F32)
                self.held[1 - p.x, i, j, p.y] = a.astype(BF)
                b = self.held[p.x, i, 2 + j, 1 - p.y].astype(F32) + self.r1[1, i, j].astype(F32)
                self.held[p.x, i, 2 + j, 1 - p.y] = b.astype(BF)
        self.plane_copy(0).start()
        self.plane_copy(1).start()

    def along(self):
        p = self.p
        self.plane_copy(0).wait_recv()
        self.plane_copy(1).wait_recv()
        for k in (1, 2, 3):
            zt = (p.z + k) % 4
            for i in range(self.n):
                a = (
                    self.held[p.x, i, zt, p.y].astype(F32)
                    + self.r2[0, i, zt].astype(F32)
                    + self.r2[1, i, zt].astype(F32)
                )
                self.held[p.x, i, zt, p.y] = a.astype(BF)
            self.z_copy(k).start()

    def finish(self):
        p = self.p
        for k in (1, 2, 3):
            self.z_copy(k).wait_recv()
        for i in range(self.n):
            a = (
                self.held[p.x, i, p.z, p.y].astype(F32)
                + self.r2[0, i, p.z].astype(F32)
                + self.r2[1, i, p.z].astype(F32)
            )
            for k in range(3):
                a = a + self.r3[k, i].astype(F32)
            self.out[i] = a

    def drain(self):
        for i in (0, 1):
            self.pair_copy(i).wait_send()
            self.corner_copy(i).wait_send()
            self.plane_copy(i).wait_send()
        for k in (1, 2, 3):
            self.z_copy(k).wait_send()


class Tail:
    def __init__(self, p, gt, hp, hx, hy, hz, out, ss, rs):
        self.p, self.gt, self.hp, self.hx, self.hy, self.hz = p, gt, hp, hx, hy, hz
        self.out, self.ss, self.rs = out, ss, rs

    def cp(self, src, dst, i, dev):
        return remote(src, dst, self.ss.at[i], self.rs.at[i], dev)

    def pair_copy(self, j):
        return self.cp(self.gt.at[j], self.hp.at[j // 2], j, self.p.pair)

    def x_copy(self, j):
        return self.cp(self.gt.at[j], self.hx, 4, self.p.xn)

    def y_copy(self, j):
        return self.cp(self.gt.at[j, :, :, 1 - self.p.y], self.hy, 5, self.p.yn)

    def z_copy(self, j, k):
        p = self.p
        return self.cp(self.gt.at[j, :, (p.z + k) % 4, p.y], self.hz.at[k - 1], 5 + k, p.zn[k])

    def mine(self, j, fn):
        pl.when(self.p.c == j % 2)(fn)

    def start(self, j):
        pl.when(self.p.c != j % 2)(lambda: self.pair_copy(j).start())

    def sum_pair(self, j):
        def do():
            self.pair_copy(j).wait_recv()
            if j >= 2:
                self.x_copy(j).wait_recv()

            def one(i, _):
                w, d = i // 8, i % 8
                at = (w, d // 2, d % 2)
                a = self.gt[(j,) + at].astype(F32) + self.hp[(j // 2,) + at].astype(F32)
                if j >= 2:
                    a = a + self.hx[at].astype(F32)
                self.gt[(j,) + at] = a.astype(BF)
                return 0

            lax.fori_loop(0, 24, one, 0)
            if j < 2:
                self.x_copy(j).start()
            else:
                self.y_copy(j).start()

        self.mine(j, do)

    def sum_y(self, j):
        def do():
            p = self.p
            self.y_copy(j).wait_recv()
            for i in range(3):
                for k in (1, 2, 3):
                    zt = (p.z + k) % 4
                    a = self.gt[j, i, zt, p.y].astype(F32) + self.hy[i, zt].astype(F32)
                    self.gt[j, i, zt, p.y] = a.astype(BF)
            for k in (1, 2, 3):
                self.z_copy(j, k).start()

        self.mine(j, do)

    def finish(self, j):
        def do():
            p = self.p
            for k in (1, 2, 3):
                self.z_copy(j, k).wait_recv()
            for i in range(3):
                a = self.gt[j, i, p.z, p.y].astype(F32) + self.hy[i, p.z].astype(F32)
                for k in range(3):
                    a = a + self.hz[k, i].astype(F32)
                self.out[i] = a

        self.mine(j, do)

    def drain(self):
        for j in range(4):
            pl.when(self.p.c != j % 2)(lambda j=j: self.pair_copy(j).wait_send())

        def sent(j):
            self.x_copy(j).wait_send()
            self.y_copy(j + 2).wait_send()
            for k in (1, 2, 3):
                self.z_copy(j + 2, k).wait_send()

        for j in (0, 1):
            self.mine(j, lambda j=j: sent(j))


def row_steps(count, one):
    def body(i, _):
        one(pl.ds(pl.multiple_of(i * CH, CH), CH))
        return 0

    lax.fori_loop(0, count // CH, body, 0)


def head_half(shape, axis, h):
    return (lax.broadcasted_iota(jnp.int32, shape, axis) // HEAD) == h


def keep_half(value, axis, h):
    return jnp.where(head_half(value.shape, axis, h), value.astype(F32), 0.0).astype(BF)


def run_hooks(hooks, step, half):
    for (at, part), hook in hooks.items():
        if part == half:
            pl.when(step == at)(hook)


def attend(qt, k, vt, bias, ot, lse, temp, hooks):
    def pair(p, _):
        lanes = pl.ds(pl.multiple_of(p * 128, 128), 128)
        kp = k[:, lanes]
        qp = qt[lanes, :]
        for h in (0, 1):
            qm = keep_half(qp, 0, h)
            top = None
            for i in range(4):
                rows = slice(i * 256, i * 256 + 256)
                s = nn(kp[rows], qm) * SCALE
                if bias is not None:
                    s = s + bias[rows, :]
                temp[rows, :] = s
                m = jnp.max(s, axis=0, keepdims=True)
                top = m if top is None else jnp.maximum(top, m)
            total, mixed = None, None
            vh = vt[pl.ds(pl.multiple_of(p * 128 + h * 64, 64), 64), :]
            for i in range(4):
                rows = slice(i * 256, i * 256 + 256)
                e = jnp.exp2(temp[rows, :] - top)
                part = jnp.sum(e, axis=0, keepdims=True)
                total = part if total is None else total + part
                o = nn(vh[:, rows], e.astype(BF))
                mixed = o if mixed is None else mixed + o
            ot[pl.ds(pl.multiple_of(p * 128 + h * 64, 64), 64), :] = mixed * (1.0 / total)
            lse[pl.ds(p * 2 + h, 1), :] = top + jnp.log2(total)
            run_hooks(hooks, p, h)
        return 0

    lax.fori_loop(0, 4, pair, 0)


def attend_back(q, qt, k, kt, v, do, dot_, ot, bias, lse, dqt, dk_own, dv_own, dkv_send, order, hooks):
    def pair(step, _):
        p = order(step)
        lanes = pl.ds(pl.multiple_of(p * 128, 128), 128)
        kp, vp = k[:, lanes], v[:, lanes]
        qp, dop = qt[lanes, :], dot_[lanes, :]
        inner = dop.astype(F32) * ot[lanes, :]
        qms = [keep_half(qp, 0, h) for h in (0, 1)]
        doms = [keep_half(dop, 0, h) for h in (0, 1)]
        qr = jnp.concatenate([keep_half(q[:, lanes], 1, h) for h in (0, 1)], axis=0)
        dor = jnp.concatenate([keep_half(do[:, lanes], 1, h) for h in (0, 1)], axis=0)
        ds_sum = [jnp.sum(inner[h * 64 : h * 64 + 64], axis=0, keepdims=True) for h in (0, 1)]
        logs = [lse[pl.ds(p * 2 + h, 1), :] for h in (0, 1)]
        dq = [None, None]
        for i in range(4):
            rows = slice(i * 256, i * 256 + 256)
            shares, grads = [], []
            for h in (0, 1):
                s = nn(kp[rows], qms[h]) * SCALE
                if bias is not None:
                    s = s + bias[rows, :]
                e = jnp.exp2(s - logs[h])
                dp = nn(vp[rows], doms[h])
                g = (e * (dp - ds_sum[h])).astype(BF)
                shares.append(e.astype(BF))
                grads.append(g)
                kh = kt[pl.ds(pl.multiple_of(p * 128 + h * 64, 64), 64), rows]
                part = nn(kh, g)
                dq[h] = part if dq[h] is None else dq[h] + part
            dv = nn(jnp.concatenate(shares, axis=1), dor)
            dk = nn(jnp.concatenate(grads, axis=1), qr) * 0.125
            if i < 2:
                dk_own[rows, lanes] = dk
                dv_own[rows, lanes] = dv
            else:
                back = slice(i * 256 - 512, i * 256 - 256)
                dkv_send[0, back, lanes] = dk.astype(BF)
                dkv_send[1, back, lanes] = dv.astype(BF)
            if i == 1:
                run_hooks(hooks, step, 0)
        for h in (0, 1):
            dqt[pl.ds(pl.multiple_of(p * 128 + h * 64, 64), 64), :] = (dq[h] * 0.125).astype(BF)
        run_hooks(hooks, step, 1)
        return 0

    lax.fori_loop(0, 4, pair, 0)


def norm_rows(z):
    mean = jnp.mean(z, axis=-1, keepdims=True)
    centred = z - mean
    r = lax.rsqrt(jnp.mean(centred * centred, axis=-1, keepdims=True) + norm_eps)
    return centred * r, r


def norm_back_rows(e, n, r, gain):
    s = e * gain
    a = jnp.mean(s, axis=-1, keepdims=True)
    b = jnp.mean(s * n, axis=-1, keepdims=True)
    return r * (s - a - n * b)


def fast_kernel(
    x_i, enc_i, og_i, valid, seg, rank,
    sq, sk, sv, so, cq, ck, cv, co, up, down,
    g1, b1, g2, b2, g3, b3,
    y_o, dx_o, eg_o, ga_o, gb_o, gf_o, ns_o, vs_o,
    x, enc, og, codes, wa, wb, wf, gt,
    q1, qt1, k1, v1, vt1, o1, ot1, l1,
    q2, qt2, k2, v2, vt2, o2, ot2, l2,
    bias, n1, n2, r1, r2, h1b, h2b, u, gp, dg, dz, low, lowt, do, dot_,
    dqt, dq, kvs, kvr1, kvr2, dkv, tt, yb, vcol, st,
    hb, hu, hd, m1, m2, m3, u1, u2, u3, d1, d2, d3, hp, hx, hy, hz,
    st_r, gss, grs, rss, rrs, aas, ars, ess, ers, tss, trs, ls,
):
    p = Place()
    loads = []
    for i, (src, w, j, cols) in enumerate(
        (
            (sq, wa, 0, 128), (sk, wa, 1, 128), (sv, wa, 2, 128),
            (so, wb, 0, 128), (ck, wb, 1, 128), (cv, wb, 2, 128), (cq, wb, 3, 128), (co, wb, 4, 128),
            (up, wf, 0, 512), (down, wf, 1, 512),
        )
    ):
        col = pl.ds(pl.multiple_of(p.t * cols, 128), cols)
        loads.append(pltpu.make_async_copy(src, w.at[j, p.z, p.y, :, col], ls.at[i]))
    for i, (src, dst) in enumerate(((x_i, x), (enc_i, enc), (og_i, og))):
        loads.append(pltpu.make_async_copy(src, dst, ls.at[10 + i]))
    for cp in loads:
        cp.start()
    p.barrier()
    GA, GB, GU, GD = G = [
        Gather(p, w, cols, gss.at[i], grs.at[i])
        for i, (w, cols) in enumerate(
            ((wa, 128), (wb, 128), (wf.at[pl.ds(0, 1)], 512), (wf.at[pl.ds(1, 1)], 512))
        )
    ]
    for cp in loads[:3]:
        cp.wait()
    GA.zs()
    GA.oxy()
    for cp in loads[3:]:
        cp.wait()
    GB.oxy()

    def mat(w, j):
        return w[j].reshape(512, w.shape[4])

    st[...] = jnp.zeros_like(st)
    vcol[...] = jnp.broadcast_to(valid[...].astype(F32), (128, 512)).T
    own = pl.ds(pl.multiple_of(p.c * 512, 128), 512)
    other = pl.ds(pl.multiple_of((1 - p.c) * 512, 128), 512)
    sx = pl.ds(p.x, 1)
    ranks = rank[sx, :]
    codes[1:2, :] = seg[sx, :] * 8
    codes[0:1, :] = seg[sx, :] * 8 + jnp.concatenate(
        [jnp.broadcast_to(ranks[:, b : b + 1], (1, 128)) for b in range(8)], axis=1
    )
    base, high = codes[1:2, own], codes[0:1, own]
    for i, half in enumerate((own, other)):
        code = jnp.broadcast_to(codes[0:1, half], (128, 512)).T
        for j in range(4):
            c = code[j * 128 : j * 128 + 128, :1]
            ok = (c >= base) & (c <= high)
            bias[i * 512 + j * 128 : i * 512 + j * 128 + 128, :] = jnp.where(ok, 0.0, -2.0e9)
    tt[...] = turn(x[...])

    GA.plane(GB.zs)
    GU.oxy()
    GA.corner()
    GU.zs()
    GD.oxy()
    GA.cross()
    GB.plane()
    GA.finish()
    GD.zs()

    xv = x[...]
    k1[0:512, :] = nn(xv, mat(wa, 1)).astype(BF)
    v1[0:512, :] = nn(xv, mat(wa, 2)).astype(BF)

    def swap(buf, i):
        return remote(buf.at[pl.ds(0, 512)], buf.at[pl.ds(512, 512)], ess.at[i], ers.at[i], p.pair)

    swap(k1, 0).start()
    swap(v1, 1).start()
    qv = nn(xv, mat(wa, 0)).astype(BF)
    q1[...] = qv
    qt1[...] = turn(qv)
    swap(k1, 0).wait_recv()
    swap(v1, 1).wait_recv()
    vt1[...] = turn(v1[...])
    attend(qt1, k1, vt1, bias, ot1, l1, gp, {(0, 1): GB.corner, (1, 0): GU.plane, (2, 1): GB.cross, (3, 1): GD.plane})
    o1[...] = turn(ot1[...].astype(BF))
    GB.finish()
    ev = enc[...]
    k2[0:512, :] = nn(ev, mat(wb, 1)).astype(BF)
    v2[0:512, :] = nn(ev, mat(wb, 2)).astype(BF)
    swap(k2, 2).start()
    swap(v2, 3).start()
    yb[...] = nt(o1[...], mat(wb, 0))

    def first(r):
        n, s = norm_rows(x[r, :].astype(F32) + yb[r, :])
        n1[r, :] = n
        r1[r, :] = s
        h1b[r, :] = (n * g1[...] + b1[...]).astype(BF)

    row_steps(512, first)
    GU.corner()
    qv = nn(h1b[...], mat(wb, 3)).astype(BF)
    q2[...] = qv
    qt2[...] = turn(qv)
    swap(k2, 2).wait_recv()
    swap(v2, 3).wait_recv()
    vt2[...] = turn(v2[...])
    attend(qt2, k2, vt2, None, ot2, l2, gp, {(0, 1): GU.cross, (3, 0): GD.corner})
    o2[...] = turn(ot2[...].astype(BF))
    yb[...] = nt(o2[...], mat(wb, 4))

    def second(r):
        n, s = norm_rows(n1[r, :] * g1[...] + b1[...] + yb[r, :])
        n2[r, :] = n
        r2[r, :] = s
        h2b[r, :] = (n * g2[...] + b2[...]).astype(BF)

    row_steps(512, second)
    GD.cross()
    GU.finish()
    hv = h2b[...]
    for j in range(4):
        cols = slice(j * 512, j * 512 + 512)
        gp[cols, :] = nn(hv, wf[0, :, :, :, cols].reshape(512, 512))

        def gelu(r, j=j, cols=cols):
            at = pl.ds(pl.multiple_of(r.start + j * 512, CH), CH)
            v = gp[at, :]
            cdf = 0.5 * (1.0 + lax.erf(v * 0.7071067811865476))
            u[r, cols] = (v * cdf).astype(BF)
            gp[at, :] = cdf + v * (jnp.exp2(v * v * (-0.5 * LOG2E)) * 0.3989422804014327)

        row_steps(512, gelu)
    GD.finish()
    yb[...] = nt(u[...], mat(wf, 1))

    def third(r):
        n, s = norm_rows(n2[r, :] * g2[...] + b2[...] + yb[r, :])
        out = n * g3[...] + b3[...]
        vc = vcol[r, :1]
        yb[r, :] = out
        e = og[r, :].astype(F32) * vc
        st[4:5, :] += jnp.sum(e * n, axis=0, keepdims=True)
        st[5:6, :] += jnp.sum(e, axis=0, keepdims=True)
        st[6:7, :] += jnp.sum(vc * out * out, axis=0, keepdims=True)
        back = norm_back_rows(e, n, s, g3[...])
        dz[r, :] = back
        low[r, :] = back.astype(BF)

    row_steps(512, third)
    y_copy = pltpu.make_async_copy(yb, y_o, ls.at[0])
    y_copy.start()
    lv = low[...]
    lowt[...] = turn(lv)
    for j in range(4):
        cols = slice(j * 512, j * 512 + 512)
        dg[:, cols] = (nn(lv, wf[1, :, :, :, cols].reshape(512, 512)) * gp[cols, :]).astype(BF)
    for g in G:
        g.drain()
    RB, RU, RD = R = [
        Reduce(p, *args, rss.at[i], rrs.at[i])
        for i, args in enumerate(
            (
                (wb, 128, hb, m1, m2, m3, gb_o),
                (wf.at[pl.ds(0, 1)], 512, hu, u1, u2, u3, gf_o.at[pl.ds(0, 1)]),
                (wf.at[pl.ds(1, 1)], 512, hd, d1, d2, d3, gf_o.at[pl.ds(1, 1)]),
            )
        )
    ]
    for j in range(4):
        cols = slice(j * 512, j * 512 + 512)
        wf[1, :, :, :, cols] = nn(lowt[...], u[:, cols]).astype(BF).reshape(4, 2, 64, 512)
    RD.start()
    dz[...] += nt(dg[...], mat(wf, 0))
    tt[...] = turn(h2b[...])
    for j in range(4):
        cols = slice(j * 512, j * 512 + 512)
        wf[0, :, :, :, cols] = nn(tt[...], dg[:, cols]).astype(BF).reshape(4, 2, 64, 512)
    RU.start()

    def back2(r):
        e = dz[r, :]
        n = n2[r, :]
        st[2:3, :] += jnp.sum(e * n, axis=0, keepdims=True)
        st[3:4, :] += jnp.sum(e, axis=0, keepdims=True)
        back = norm_back_rows(e, n, r2[r, :], g2[...])
        dz[r, :] = back
        low[r, :] = back.astype(BF)

    row_steps(512, back2)
    RD.corner()
    dov = nn(low[...], mat(wb, 4)).astype(BF)
    do[...] = dov
    dot_[...] = turn(dov)
    lowt[...] = turn(low[...])
    wb[4] = nn(lowt[...], o2[...]).astype(BF).reshape(4, 2, 64, 512)
    vt2[...] = turn(k2[...])
    attend_back(
        q2, qt2, k2, vt2, v2, do, dot_, ot2, None, l2, dqt,
        gp.at[pl.ds(0, 512)], gp.at[pl.ds(512, 512)], kvs, lambda step: step,
        {(0, 0): RU.corner, (0, 1): RD.plane, (1, 1): RU.plane, (3, 0): RD.along},
    )

    def swap_back(buf, i):
        return remote(kvs, buf, ess.at[i], ers.at[i], p.pair)

    swap_back(kvr2, 4).start()
    dqv = turn(dqt[...])
    dz[...] += nt(dqv, mat(wb, 3))
    tt[...] = turn(h1b[...])
    wb[3] = nn(tt[...], dqv).astype(BF).reshape(4, 2, 64, 512)

    def back1(r):
        e = dz[r, :]
        n = n1[r, :]
        st[0:1, :] += jnp.sum(e * n, axis=0, keepdims=True)
        st[1:2, :] += jnp.sum(e, axis=0, keepdims=True)
        back = norm_back_rows(e, n, r1[r, :], g1[...])
        dz[r, :] = back
        low[r, :] = back.astype(BF)

    row_steps(512, back1)
    RU.along()
    dov = nn(low[...], mat(wb, 0)).astype(BF)
    do[...] = dov
    dot_[...] = turn(dov)
    lowt[...] = turn(low[...])
    wb[0] = nn(lowt[...], o1[...]).astype(BF).reshape(4, 2, 64, 512)
    vt1[...] = turn(k1[...])
    swap_back(kvr2, 4).wait()

    def join(recv, at):
        def one(r):
            for i in (0, 1):
                own_rows = pl.ds(pl.multiple_of(r.start + at + i * 512, CH), CH)
                dkv[i, r, :] = (gp[own_rows, :] + recv[i, r, :].astype(F32)).astype(BF)

        row_steps(512, one)

    join(kvr2, 0)
    y_copy.wait()
    yb[...] = nt(dkv[0], mat(wb, 1)) + nt(dkv[1], mat(wb, 2))
    e_copy = pltpu.make_async_copy(yb, eg_o, ls.at[0])
    e_copy.start()
    tt[...] = turn(enc[...])
    wb[1] = nn(tt[...], dkv[0]).astype(BF).reshape(4, 2, 64, 512)
    wb[2] = nn(tt[...], dkv[1]).astype(BF).reshape(4, 2, 64, 512)
    RB.start()
    tt[...] = turn(x[...])
    T = Tail(p, gt, hp, hx, hy, hz, ga_o, aas, ars)

    def order(step):
        far = (step // 2) * p.x + (1 - step // 2) * (1 - p.x)
        return 2 * far + step % 2

    def lanes_of(step):
        return pl.ds(pl.multiple_of(order(step) * 128, 128), 128)

    def part_back(step):
        at = lanes_of(step)
        return remote(
            kvs.at[:, :, at], kvr1.at[:, :, at], ess.at[5 + step], ers.at[5 + step], p.pair
        )

    def grads(step):
        at = lanes_of(step)
        part_back(step).wait_recv()

        def one(r):
            for i in (0, 1):
                rows = pl.ds(pl.multiple_of(r.start + 1024 + i * 512, CH), CH)
                dkv[i, r, at] = (gp[rows, at] + kvr1[i, r, at].astype(F32)).astype(BF)

        row_steps(512, one)
        dqv = turn(dqt[at, :])
        dq[:, at] = dqv
        gt[step, 0] = nn(tt[...], dqv).astype(BF).reshape(4, 2, 64, 128)
        gt[step, 1] = nn(tt[...], dkv[0, :, at]).astype(BF).reshape(4, 2, 64, 128)
        gt[step, 2] = nn(tt[...], dkv[1, :, at]).astype(BF).reshape(4, 2, 64, 128)
        T.start(step)

    def both(*fns):
        def run():
            for fn in fns:
                fn()

        return run

    attend_back(
        q1, qt1, k1, vt1, v1, do, dot_, ot1, bias, l1, dqt,
        gp.at[pl.ds(1024, 512)], gp.at[pl.ds(1536, 512)], kvs, order,
        {
            (0, 0): RB.corner,
            (0, 1): lambda: part_back(0).start(),
            (1, 0): both(lambda: grads(0), RB.plane),
            (1, 1): both(lambda: part_back(1).start(), RD.finish),
            (2, 0): both(lambda: grads(1), lambda: T.sum_pair(0)),
            (2, 1): both(lambda: part_back(2).start(), RU.finish),
            (3, 0): both(lambda: grads(2), lambda: T.sum_pair(1), RB.along),
            (3, 1): lambda: part_back(3).start(),
        },
    )
    T.sum_pair(2)
    grads(3)
    T.sum_pair(3)
    T.sum_y(2)
    dz[...] += nt(dq[...], mat(wa, 0)) + nt(dkv[0], mat(wa, 1)) + nt(dkv[1], mat(wa, 2))
    x_copy = pltpu.make_async_copy(dz, dx_o, ls.at[1])
    x_copy.start()

    def squares(r):
        st[7:8, :] += jnp.sum(vcol[r, :1] * dz[r, :] * dz[r, :], axis=0, keepdims=True)

    row_steps(512, squares)

    def stat(i, src, dev):
        return remote(src, st_r.at[i], tss.at[i], trs.at[i], dev)

    stat(0, st, p.pair).start()
    T.sum_y(3)
    stat(0, st, p.pair).wait()
    st_r[6] = st[...] + st_r[0]
    stat(1, st_r.at[6], p.xn).start()
    T.finish(2)
    RB.finish()
    stat(1, st_r.at[6], p.xn).wait()
    st_r[7] = st_r[6] + st_r[1]
    stat(2, st_r.at[7], p.yn).start()
    stat(2, st_r.at[7], p.yn).wait()
    st_r[8] = st_r[7] + st_r[2]
    for k in (1, 2, 3):
        stat(2 + k, st_r.at[8], p.zn[k]).start()
    T.finish(3)
    for k in (1, 2, 3):
        stat(2 + k, st_r.at[8], p.zn[k]).wait()
    total = None
    for zs in range(4):
        part = None
        for k in range(4):
            got = st_r[8] if k == 0 else st_r[2 + k]
            got = jnp.where((p.z - k + 4) % 4 == zs, got, 0.0)
            part = got if part is None else part + got
        total = part if total is None else total + part
    ns_o[...] = total[0:6]
    vs_o[...] = jnp.sqrt(total[6:8] * (1.0 / 16384.0))
    for i in range(4):
        swap((k1, v1, k2, v2)[i], i).wait_send()
    for step in range(4):
        part_back(step).wait_send()
    for r in R:
        r.drain()
    T.drain()
    e_copy.wait()
    x_copy.wait()


def place_kernel(*refs):
    srcs, outs, held, sems = refs[:8], refs[8:23], refs[23:31], refs[31]
    parts = [held[0], held[1], held[2]] + [held[3].at[i] for i in range(3)]
    parts += [held[4].at[i] for i in range(5)] + [held[5].at[i] for i in range(2)] + [held[6], held[7]]
    first = [pltpu.make_async_copy(a, b, sems.at[i]) for i, (a, b) in enumerate(zip(srcs, held))]
    last = [pltpu.make_async_copy(a, b, sems.at[8 + i]) for i, (a, b) in enumerate(zip(parts, outs))]
    ends = [(0, 1), (1, 2), (2, 3), (3, 6), (6, 11), (11, 13), (13, 14), (14, 15)]
    order = (6, 7, 3, 4, 5, 0, 1, 2)
    for i in order:
        first[i].start()
    for i in order:
        first[i].wait()
        for cp in last[ends[i][0] : ends[i][1]]:
            cp.start()
    for cp in last:
        cp.wait()


def fast_shards(
    tokens, encoder_states, output_grad, valid_mask, segment_ids, context_ranks,
    self_query, self_key, self_value, self_output,
    cross_query, cross_key, cross_value, cross_output, hidden_up, hidden_down,
    norm1_gain, norm1_bias, norm2_gain, norm2_bias, norm3_gain, norm3_bias,
):
    vm = pl.BlockSpec(memory_space=pltpu.VMEM)
    hbm = pl.BlockSpec(memory_space=pl.ANY)
    rows = [
        v.reshape(1, 512)
        for v in (norm1_gain, norm1_bias, norm2_gain, norm2_bias, norm3_gain, norm3_bias)
    ]

    def V(*shape, dtype=BF):
        return pltpu.VMEM(shape, dtype)

    def S(*shape):
        return pltpu.SemaphoreType.DMA(shape)

    def group(n, cols):
        return [
            V(2, n, 4, 2, 64, cols),
            [V(2, n, 2, 64, cols), V(2, n, 4, 64, cols), V(3, n, 64, cols)],
        ]

    rb, ru, rd = group(5, 128), group(1, 512), group(1, 512)

    def attention():
        return [
            V(512, 512), V(512, 512), V(1024, 512), V(1024, 512), V(512, 1024), V(512, 512),
            V(512, 512, dtype=F32), V(8, 512, dtype=F32),
        ]

    scratch = (
        [V(512, 512)] * 3
        + [V(8, 1024, dtype=jnp.int32)]
        + [V(3, 4, 2, 64, 512), V(5, 4, 2, 64, 512), V(2, 4, 2, 64, 2048), V(4, 3, 4, 2, 64, 128)]
        + attention()
        + attention()
        + [V(1024, 512, dtype=F32), V(512, 512, dtype=F32), V(512, 512, dtype=F32)]
        + [V(512, 1, dtype=F32), V(512, 1, dtype=F32), V(512, 512), V(512, 512)]
        + [V(512, 2048), V(2048, 512, dtype=F32), V(512, 2048), V(512, 512, dtype=F32)]
        + [V(512, 512)] * 4
        + [V(512, 512), V(512, 512), V(2, 512, 512), V(2, 512, 512), V(2, 512, 512), V(2, 512, 512)]
        + [V(512, 512), V(512, 512, dtype=F32), V(512, 128, dtype=F32), V(8, 512, dtype=F32)]
        + [rb[0], ru[0], rd[0]]
        + rb[1] + ru[1] + rd[1]
        + [V(2, 3, 4, 2, 64, 128), V(3, 4, 2, 64, 128), V(3, 4, 64, 128), V(3, 3, 64, 128)]
        + [V(9, 8, 512, dtype=F32)]
        + [S(4, 17), S(4, 17), S(3, 9), S(3, 9), S(9), S(9), S(9), S(9), S(6), S(6), S(13)]
    )
    big = jax.ShapeDtypeStruct((512, 512), F32)
    outs = pl.pallas_call(
        fast_kernel,
        out_shape=[big, big, big]
        + [jax.ShapeDtypeStruct(s, F32) for s in ((3, 64, 128), (5, 64, 128), (2, 64, 512), (6, 512), (2, 512))],
        in_specs=[hbm] * 3 + [vm] * 3 + [hbm] * 10 + [vm] * 6,
        out_specs=[hbm] * 3 + [vm] * 5,
        scratch_shapes=scratch,
        compiler_params=pltpu.CompilerParams(
            collective_id=0, has_side_effects=True, vmem_limit_bytes=60 << 20
        ),
        name="layer",
    )(
        tokens, encoder_states, output_grad, valid_mask.reshape(1, 512), segment_ids, context_ranks,
        self_query, self_key, self_value, self_output.T,
        cross_query, cross_key, cross_value, cross_output.T, hidden_up, hidden_down.T, *rows,
    )
    ends = [big, big, big] + [jax.ShapeDtypeStruct((64, 128), F32)] * 8
    ends += [jax.ShapeDtypeStruct((64, 512), F32)] * 2
    ends += [jax.ShapeDtypeStruct(v, F32) for v in ((6, 512), (2, 512))]
    y, dx, eg, dsq, dsk, dsv, dso, dck, dcv, dcq, dco, dup, ddown, ns, vs = pl.pallas_call(
        place_kernel,
        out_shape=ends,
        in_specs=[hbm] * 8,
        out_specs=[hbm] * 15,
        scratch_shapes=[pltpu.VMEM(o.shape, F32) for o in outs] + [S(23)],
        name="place",
    )(*outs)
    return (
        y, dx, eg, dsq, dsk, dsv, dso.T, dcq, dck, dcv, dco.T, dup, ddown.T, ns, vs,
    )


def solution(mesh):
    in_specs = (
        P(("dp", "tensor"), None),
        P(("dp", "tensor"), None),
        P(("dp", "tensor"), None),
        P(("dp", "tensor")),
        P("dp", None),
        P("dp", None),
        P("dp", "tensor"),
        P("dp", "tensor"),
        P("dp", "tensor"),
        P("tensor", "dp"),
        P("dp", "tensor"),
        P("dp", "tensor"),
        P("dp", "tensor"),
        P("tensor", "dp"),
        P("dp", "tensor"),
        P("tensor", "dp"),
        P(),
        P(),
        P(),
        P(),
        P(),
        P(),
    )
    out_specs = (
        P(("dp", "tensor"), None),
        P(("dp", "tensor"), None),
        P(("dp", "tensor"), None),
        P("dp", "tensor"),
        P("dp", "tensor"),
        P("dp", "tensor"),
        P("tensor", "dp"),
        P("dp", "tensor"),
        P("dp", "tensor"),
        P("dp", "tensor"),
        P("tensor", "dp"),
        P("dp", "tensor"),
        P("tensor", "dp"),
        P(),
        P(),
    )
    body = fast_shards if dict(mesh.shape) == {"dp": 8, "tensor": 4} else shards
    return jax.shard_map(body, mesh=mesh, in_specs=in_specs, out_specs=out_specs, check_vma=False)
```

```python
import jax
import jax.numpy as jnp
from jax import lax
from jax.experimental import pallas as pl
from jax.experimental.pallas import tpu as pltpu
from jax.sharding import PartitionSpec as P

HEAD = 64
LEN = 1024
BLK = 128


norm_eps = 1e-05
mask_fill = -1000000000.0


def gelu_exact(value):
    return jax.nn.gelu(value, approximate=False)


def gelu_back(preact, upstream):
    return jax.vjp(gelu_exact, preact)[1](upstream)[0]


def layer_norm(value, gain, bias):
    mean = jnp.mean(value, axis=-1, keepdims=True)
    centred = value - mean
    scale = lax.rsqrt(jnp.mean(centred * centred, axis=-1, keepdims=True) + norm_eps)
    normal = centred * scale
    return (normal * gain + bias, normal, scale)


def norm_back(upstream, normal, scale, gain):
    scaled = upstream * gain
    mean_grad = jnp.mean(scaled, axis=-1, keepdims=True)
    mean_cross = jnp.mean(scaled * normal, axis=-1, keepdims=True)
    inward = scale * (scaled - mean_grad - normal * mean_cross)
    return (inward, jnp.sum(upstream * normal, axis=0), jnp.sum(upstream, axis=0))


def context_allowed(segments, ranks, first, count):
    length = segments.shape[0]
    key_block = jnp.arange(length, dtype=jnp.int32) // BLK
    key_rank = jnp.broadcast_to(ranks[:, None], (ranks.shape[0], BLK)).reshape(length)
    query_segment = lax.dynamic_slice_in_dim(segments, first, count)
    query_rank = lax.dynamic_slice_in_dim(key_rank, first, count)
    query_block = (first + jnp.arange(count, dtype=jnp.int32)) // BLK
    same_doc = query_segment[:, None] == segments[None, :]
    earlier = key_rank[None, :] < query_rank[:, None]
    same_block = query_block[:, None] == key_block[None, :]
    return same_doc & (earlier | same_block)


def full_rows(value):
    return lax.all_gather(value, "tensor", axis=0, tiled=True)


def grad_rows(value):
    return lax.all_gather(value, "tensor", axis=0, tiled=True)


def branch_sum(mixed, weight):
    return lax.psum_scatter(
        jnp.dot(mixed, weight, preferred_element_type=jnp.float32),
        "tensor",
        scatter_dimension=0,
        tiled=True,
    )


def back_product(left, weight):
    return lax.dot_general(
        left, weight, (((1,), (1,)), ((), ())), preferred_element_type=jnp.float32
    )


def row_product(left, right):
    return lax.dot_general(
        left, right, (((0,), (0,)), ((), ())), preferred_element_type=jnp.float32
    )


def input_sum(pairs):
    total = None
    for left, weight in pairs:
        portion = back_product(left, weight)
        total = portion if total is None else total + portion
    return lax.psum_scatter(total, "tensor", scatter_dimension=0, tiled=True)


def split_heads(value, count):
    return value.reshape(count, LEN, value.shape[1] // HEAD, HEAD)


def attend_sequence(query, keys, values, segments, ranks, masked):
    length = query.shape[0]
    width = min(length, 512)

    def one_block(index):
        first = index * width
        piece = lax.dynamic_slice_in_dim(query, first, width, 0)
        scores = jnp.einsum("qhd,khd->hqk", piece, keys, preferred_element_type=jnp.float32) * 0.125
        if masked:
            scores = jnp.where(
                context_allowed(segments, ranks, first, width)[None], scores, mask_fill
            )
        top = jnp.max(scores, axis=-1, keepdims=True)
        raised = jnp.exp(scores - top)
        total = jnp.sum(raised, axis=-1, keepdims=True)
        shares = (raised / total).astype(jnp.bfloat16)
        mixed = jnp.einsum("hqk,khd->qhd", shares, values, preferred_element_type=jnp.float32)
        return (mixed.astype(jnp.bfloat16), (top + jnp.log(total))[..., 0])

    mixed, log_total = lax.map(one_block, jnp.arange(length // width, dtype=jnp.int32))
    return (mixed.reshape(query.shape), log_total)


def attend_sequence_back(query, keys, values, segments, ranks, masked, log_total, grad_mixed):
    length = query.shape[0]
    width = min(length, 512)

    def one_block(carry, index):
        key_sum, value_sum = carry
        first = index * width
        piece = lax.dynamic_slice_in_dim(query, first, width, 0)
        grad_piece = lax.dynamic_slice_in_dim(grad_mixed, first, width, 0)
        scores = jnp.einsum("qhd,khd->hqk", piece, keys, preferred_element_type=jnp.float32) * 0.125
        if masked:
            scores = jnp.where(
                context_allowed(segments, ranks, first, width)[None], scores, mask_fill
            )
        shares = jnp.exp(scores - log_total[index][..., None])
        grad_shares = jnp.einsum(
            "qhd,khd->hqk", grad_piece, values, preferred_element_type=jnp.float32
        )
        inner = jnp.sum(shares * grad_shares, axis=-1, keepdims=True)
        grad_scores = (shares * (grad_shares - inner)).astype(jnp.bfloat16)
        grad_query = (
            jnp.einsum("hqk,khd->qhd", grad_scores, keys, preferred_element_type=jnp.float32)
            * 0.125
        )
        key_sum = (
            key_sum
            + jnp.einsum("hqk,qhd->khd", grad_scores, piece, preferred_element_type=jnp.float32)
            * 0.125
        )
        value_sum = value_sum + jnp.einsum(
            "hqk,qhd->khd",
            shares.astype(jnp.bfloat16),
            grad_piece,
            preferred_element_type=jnp.float32,
        )
        return ((key_sum, value_sum), grad_query.astype(jnp.bfloat16))

    zeros = jnp.zeros(keys.shape, jnp.float32)
    (key_sum, value_sum), grad_query = lax.scan(
        one_block, (zeros, zeros), jnp.arange(length // width, dtype=jnp.int32)
    )
    return (
        grad_query.reshape(query.shape),
        key_sum.astype(jnp.bfloat16),
        value_sum.astype(jnp.bfloat16),
    )


def attend_all(query, keys, values, segments, ranks, masked):
    count = query.shape[0] // LEN

    def one_sequence(items):
        return attend_sequence(items[0], items[1], items[2], items[3], items[4], masked)

    mixed, log_total = lax.map(
        one_sequence,
        (
            split_heads(query, count),
            split_heads(keys, count),
            split_heads(values, count),
            segments,
            ranks,
        ),
    )
    return (mixed.reshape(query.shape), log_total)


def attend_back_all(query, keys, values, segments, ranks, masked, log_total, grad_mixed):
    count = query.shape[0] // LEN

    def one_sequence(items):
        return attend_sequence_back(
            items[0], items[1], items[2], items[3], items[4], masked, items[5], items[6]
        )

    grad_query, grad_keys, grad_values = lax.map(
        one_sequence,
        (
            split_heads(query, count),
            split_heads(keys, count),
            split_heads(values, count),
            segments,
            ranks,
            log_total,
            split_heads(grad_mixed, count),
        ),
    )
    return (
        grad_query.reshape(query.shape),
        grad_keys.reshape(keys.shape),
        grad_values.reshape(values.shape),
    )


def shards(
    tokens,
    encoder_states,
    output_grad,
    valid_mask,
    segment_ids,
    context_ranks,
    self_query,
    self_key,
    self_value,
    self_output,
    cross_query,
    cross_key,
    cross_value,
    cross_output,
    hidden_up,
    hidden_down,
    norm1_gain,
    norm1_bias,
    norm2_gain,
    norm2_bias,
    norm3_gain,
    norm3_bias,
):
    (
        self_query,
        self_key,
        self_value,
        self_output,
        cross_query,
        cross_key,
        cross_value,
        cross_output,
        hidden_up,
        hidden_down,
    ) = (
        lax.all_gather(self_query, "dp", axis=0, tiled=True),
        lax.all_gather(self_key, "dp", axis=0, tiled=True),
        lax.all_gather(self_value, "dp", axis=0, tiled=True),
        lax.all_gather(self_output, "dp", axis=1, tiled=True),
        lax.all_gather(cross_query, "dp", axis=0, tiled=True),
        lax.all_gather(cross_key, "dp", axis=0, tiled=True),
        lax.all_gather(cross_value, "dp", axis=0, tiled=True),
        lax.all_gather(cross_output, "dp", axis=1, tiled=True),
        lax.all_gather(hidden_up, "dp", axis=0, tiled=True),
        lax.all_gather(hidden_down, "dp", axis=1, tiled=True),
    )
    tokens_full = full_rows(tokens)
    query = jnp.dot(tokens_full, self_query, preferred_element_type=jnp.float32).astype(
        jnp.bfloat16
    )
    keys = jnp.dot(tokens_full, self_key, preferred_element_type=jnp.float32).astype(jnp.bfloat16)
    values = jnp.dot(tokens_full, self_value, preferred_element_type=jnp.float32).astype(
        jnp.bfloat16
    )
    self_mixed, self_log = attend_all(query, keys, values, segment_ids, context_ranks, True)
    attended = branch_sum(self_mixed, self_output)
    first_out, first_normal, first_scale = layer_norm(
        tokens.astype(jnp.float32) + attended, norm1_gain, norm1_bias
    )
    first_full = full_rows(first_out.astype(jnp.bfloat16))
    encoder_full = full_rows(encoder_states)
    second_query = jnp.dot(first_full, cross_query, preferred_element_type=jnp.float32).astype(
        jnp.bfloat16
    )
    encoder_keys = jnp.dot(encoder_full, cross_key, preferred_element_type=jnp.float32).astype(
        jnp.bfloat16
    )
    encoder_values = jnp.dot(encoder_full, cross_value, preferred_element_type=jnp.float32).astype(
        jnp.bfloat16
    )
    cross_mixed, cross_log = attend_all(
        second_query, encoder_keys, encoder_values, segment_ids, context_ranks, False
    )
    crossed = branch_sum(cross_mixed, cross_output)
    second_out, second_normal, second_scale = layer_norm(
        first_out + crossed, norm2_gain, norm2_bias
    )
    second_low = second_out.astype(jnp.bfloat16)
    feed_input = full_rows(second_low)
    preact = jnp.dot(feed_input, hidden_up, preferred_element_type=jnp.float32)
    activated = gelu_exact(preact).astype(jnp.bfloat16)
    feed_out = branch_sum(activated, hidden_down)
    third_out, third_normal, third_scale = layer_norm(second_out + feed_out, norm3_gain, norm3_bias)
    valid_rows = valid_mask.astype(jnp.float32)[:, None]
    grad_layer = output_grad.astype(jnp.float32) * valid_rows
    grad_third, gain3_grad, bias3_grad = norm_back(
        grad_layer, third_normal, third_scale, norm3_gain
    )
    grad_third_low = grad_third.astype(jnp.bfloat16)
    grad_feed = grad_rows(grad_third_low)
    grad_active = back_product(grad_feed, hidden_down)
    grad_preact = gelu_back(preact, grad_active).astype(jnp.bfloat16)
    up_grad = row_product(feed_input, grad_preact)
    down_grad = row_product(activated, grad_feed)
    grad_second = grad_third + input_sum([(grad_preact, hidden_up)])
    grad_second_in, gain2_grad, bias2_grad = norm_back(
        grad_second, second_normal, second_scale, norm2_gain
    )
    grad_crossed = grad_rows(grad_second_in.astype(jnp.bfloat16))
    cross_output_grad = row_product(cross_mixed, grad_crossed)
    grad_cross_mixed = back_product(grad_crossed, cross_output).astype(jnp.bfloat16)
    grad_second_query, grad_encoder_keys, grad_encoder_values = attend_back_all(
        second_query,
        encoder_keys,
        encoder_values,
        segment_ids,
        context_ranks,
        False,
        cross_log,
        grad_cross_mixed,
    )
    cross_query_grad = row_product(first_full, grad_second_query)
    cross_key_grad = row_product(encoder_full, grad_encoder_keys)
    cross_value_grad = row_product(encoder_full, grad_encoder_values)
    grad_first = grad_second_in + input_sum([(grad_second_query, cross_query)])
    encoder_grad = input_sum([(grad_encoder_keys, cross_key), (grad_encoder_values, cross_value)])
    grad_first_in, gain1_grad, bias1_grad = norm_back(
        grad_first, first_normal, first_scale, norm1_gain
    )
    grad_attended = grad_rows(grad_first_in.astype(jnp.bfloat16))
    self_output_grad = row_product(self_mixed, grad_attended)
    grad_self_mixed = back_product(grad_attended, self_output).astype(jnp.bfloat16)
    grad_query, grad_keys, grad_values = attend_back_all(
        query, keys, values, segment_ids, context_ranks, True, self_log, grad_self_mixed
    )
    self_query_grad = row_product(tokens_full, grad_query)
    self_key_grad = row_product(tokens_full, grad_keys)
    self_value_grad = row_product(tokens_full, grad_values)
    tokens_grad = grad_first_in + input_sum(
        [(grad_query, self_query), (grad_keys, self_key), (grad_values, self_value)]
    )
    (
        self_query_grad,
        self_key_grad,
        self_value_grad,
        self_output_grad,
        cross_query_grad,
        cross_key_grad,
        cross_value_grad,
        cross_output_grad,
        up_grad,
        down_grad,
    ) = (
        lax.psum_scatter(self_query_grad, "dp", scatter_dimension=0, tiled=True),
        lax.psum_scatter(self_key_grad, "dp", scatter_dimension=0, tiled=True),
        lax.psum_scatter(self_value_grad, "dp", scatter_dimension=0, tiled=True),
        lax.psum_scatter(self_output_grad, "dp", scatter_dimension=1, tiled=True),
        lax.psum_scatter(cross_query_grad, "dp", scatter_dimension=0, tiled=True),
        lax.psum_scatter(cross_key_grad, "dp", scatter_dimension=0, tiled=True),
        lax.psum_scatter(cross_value_grad, "dp", scatter_dimension=0, tiled=True),
        lax.psum_scatter(cross_output_grad, "dp", scatter_dimension=1, tiled=True),
        lax.psum_scatter(up_grad, "dp", scatter_dimension=0, tiled=True),
        lax.psum_scatter(down_grad, "dp", scatter_dimension=1, tiled=True),
    )
    norm_sums, square_sums = lax.psum(
        (
            jnp.stack([gain1_grad, bias1_grad, gain2_grad, bias2_grad, gain3_grad, bias3_grad]),
            jnp.stack(
                [
                    jnp.sum(valid_rows * third_out * third_out, axis=0),
                    jnp.sum(valid_rows * tokens_grad * tokens_grad, axis=0),
                ]
            ),
        ),
        ("dp", "tensor"),
    )
    total_tokens = tokens.shape[0] * lax.axis_size("dp") * lax.axis_size("tensor")
    valid_scales = jnp.sqrt(square_sums / total_tokens)
    return (
        third_out,
        tokens_grad,
        encoder_grad,
        self_query_grad,
        self_key_grad,
        self_value_grad,
        self_output_grad,
        cross_query_grad,
        cross_key_grad,
        cross_value_grad,
        cross_output_grad,
        up_grad,
        down_grad,
        norm_sums,
        valid_scales,
    )


MESH = pl.DeviceIdType.MESH
BF = jnp.bfloat16
F32 = jnp.float32
LOG2E = 1.4426950408889634
SCALE = 0.125 * LOG2E
CH = 256


def nn(a, b):
    return lax.dot_general(a, b, (((1,), (0,)), ((), ())), preferred_element_type=F32)


def nt(a, b):
    return lax.dot_general(a, b, (((1,), (1,)), ((), ())), preferred_element_type=F32)


def turn(x):
    return x.T


class Place:
    def __init__(self):
        self.d = lax.axis_index("dp")
        self.t = lax.axis_index("tensor")
        self.z, self.y = self.d // 2, self.d % 2
        self.x, self.c = self.t // 2, self.t % 2
        self.xt = (1 - self.x) * 2 + self.c
        self.xn = (self.d, self.xt)
        self.yn = (self.z * 2 + 1 - self.y, self.t)
        self.pair = (self.d, self.x * 2 + 1 - self.c)
        self.zn = [None] + [((((self.z + k) % 4) * 2 + self.y), self.t) for k in (1, 2, 3)]
        top = self.z // 2
        self.near = [self.z, top * (5 - self.z) + (1 - top) * (1 - self.z), 2 - top, 3 * (1 - top)]

    def barrier(self):
        sem = pltpu.get_barrier_semaphore()
        for dev in [self.xn, self.yn, self.pair] + self.zn[1:]:
            pl.semaphore_signal(sem, inc=1, device_id=dev, device_id_type=MESH)
        pl.semaphore_wait(sem, 6)


def remote(src, dst, send, recv, dev):
    return pltpu.make_async_remote_copy(
        src_ref=src, dst_ref=dst, send_sem=send, recv_sem=recv, device_id=dev, device_id_type=MESH
    )


class Gather:
    def __init__(self, p, w, cols, ss, rs):
        self.p, self.w, self.cols, self.ss, self.rs = p, w, cols, ss, rs

    def col(self, t):
        return pl.ds(pl.multiple_of(t * self.cols, 128), self.cols)

    def blk(self, k, y, t):
        return self.w.at[:, self.p.near[k], y, :, self.col(t)]

    def cp(self, ref, i, dev, send=None):
        return remote(ref, ref, self.ss.at[i if send is None else send], self.rs.at[i], dev)

    def own(self):
        return self.blk(0, self.p.y, self.p.t)

    def z_send(self, k):
        p = self.p
        dev = (p.near[k] * 2 + p.y, p.t)
        return self.cp(self.own(), 15 + p.z, dev, k - 1)

    def z_recv(self, k):
        p = self.p
        ref = self.blk(k, p.y, p.t)
        return self.cp(ref, 15 + p.near[k], (p.near[k] * 2 + p.y, p.t), k - 1)

    def x_send(self, k):
        return self.cp(self.blk(k, self.p.y, self.p.t), 3 + k, self.p.xn)

    def x_recv(self, k):
        return self.cp(self.blk(k, self.p.y, self.p.xt), 3 + k, self.p.xn)

    def y_send(self, k):
        return self.cp(self.blk(k, self.p.y, self.p.t), 7 + k, self.p.yn)

    def y_recv(self, k):
        return self.cp(self.blk(k, 1 - self.p.y, self.p.t), 7 + k, self.p.yn)

    def q_send(self, k):
        if k < 2:
            return self.cp(self.blk(k, self.p.y, self.p.xt), 11 + k, self.p.yn)
        return self.cp(self.blk(k, 1 - self.p.y, self.p.t), 11 + k, self.p.xn)

    def q_recv(self, k):
        return self.cp(self.blk(k, 1 - self.p.y, self.p.xt), 11 + k, self.p.xn)

    def rail(self, i, core):
        x = self.p.x if i == 0 else 1 - self.p.x
        return self.w.at[:, :, :, :, self.col(x * 2 + core)]

    def p_send(self, i):
        return self.cp(self.rail(i, self.p.c), 1 + i, self.p.pair, 17 + i)

    def p_recv(self, i):
        return self.cp(self.rail(i, 1 - self.p.c), 1 + i, self.p.pair, 17 + i)

    def zs(self):
        for k in (1, 2, 3):
            self.z_send(k).start()

    def oxy(self):
        self.x_send(0).start()
        self.y_send(0).start()

    def plane(self, *between):
        for k in (1, 2, 3):
            self.z_recv(k).wait_recv()
            if k == 1:
                for fn in between:
                    fn()
            self.x_send(k).start()
            self.y_send(k).start()

    def corner(self):
        for k in range(4):
            self.x_recv(k).wait_recv()
            if k < 2:
                self.q_send(k).start()
            self.y_recv(k).wait_recv()
            if k >= 2:
                self.q_send(k).start()
        self.p_send(0).start()

    def cross(self):
        for k in range(4):
            self.q_recv(k).wait_recv()
        self.p_send(1).start()

    def finish(self):
        self.p_recv(0).wait_recv()
        self.p_recv(1).wait_recv()

    def drain(self):
        for k in (1, 2, 3):
            self.z_send(k).wait_send()
        for k in range(4):
            self.x_send(k).wait_send()
            self.y_send(k).wait_send()
            self.q_send(k).wait_send()
        self.p_send(0).wait_send()
        self.p_send(1).wait_send()


class Reduce:
    def __init__(self, p, g, cols, held, r1, r2, r3, out, ss, rs):
        self.p, self.g, self.cols, self.held = p, g, cols, held
        self.r1, self.r2, self.r3, self.out, self.ss, self.rs = r1, r2, r3, out, ss, rs
        self.n = g.shape[0]

    def col(self, t):
        return pl.ds(pl.multiple_of(t * self.cols, 128), self.cols)

    def cp(self, src, dst, i, dev):
        return remote(src, dst, self.ss.at[i], self.rs.at[i], dev)

    def pair_copy(self, x):
        src = self.g.at[:, :, :, :, self.col(x * 2 + 1 - self.p.c)]
        return self.cp(src, self.held.at[x], x, self.p.pair)

    def corner_copy(self, i):
        p = self.p
        src = self.held.at[1 - p.x, :, pl.ds(2 * i, 2), 1 - p.y]
        return self.cp(src, self.r1.at[i], 2 + i, p.yn if i == 0 else p.xn)

    def plane_copy(self, i):
        p = self.p
        src = self.held.at[1 - p.x, :, :, p.y] if i == 0 else self.held.at[p.x, :, :, 1 - p.y]
        return self.cp(src, self.r2.at[i], 4 + i, p.xn if i == 0 else p.yn)

    def z_copy(self, k):
        p = self.p
        src = self.held.at[p.x, :, (p.z + k) % 4, p.y]
        return self.cp(src, self.r3.at[k - 1], 5 + k, p.zn[k])

    def start(self):
        self.pair_copy(0).start()
        self.pair_copy(1).start()

    def corner(self):
        for x in (0, 1):
            self.pair_copy(x).wait_recv()
        for x in (0, 1):
            col = self.col(x * 2 + self.p.c)

            def one(j, _, x=x, col=col):
                i, d = j // 8, j % 8
                mine = self.g[i, d // 2, d % 2, :, col].astype(F32)
                theirs = self.held[x, i, d // 2, d % 2].astype(F32)
                self.held[x, i, d // 2, d % 2] = (mine + theirs).astype(BF)
                return 0

            lax.fori_loop(0, self.n * 8, one, 0)
        self.corner_copy(0).start()
        self.corner_copy(1).start()

    def plane(self):
        p = self.p
        self.corner_copy(0).wait_recv()
        self.corner_copy(1).wait_recv()
        for i in range(self.n):
            for j in range(2):
                a = self.held[1 - p.x, i, j, p.y].astype(F32) + self.r1[0, i, j].astype(F32)
                self.held[1 - p.x, i, j, p.y] = a.astype(BF)
                b = self.held[p.x, i, 2 + j, 1 - p.y].astype(F32) + self.r1[1, i, j].astype(F32)
                self.held[p.x, i, 2 + j, 1 - p.y] = b.astype(BF)
        self.plane_copy(0).start()
        self.plane_copy(1).start()

    def along(self):
        p = self.p
        self.plane_copy(0).wait_recv()
        self.plane_copy(1).wait_recv()
        for k in (1, 2, 3):
            zt = (p.z + k) % 4
            for i in range(self.n):
                a = (
                    self.held[p.x, i, zt, p.y].astype(F32)
                    + self.r2[0, i, zt].astype(F32)
                    + self.r2[1, i, zt].astype(F32)
                )
                self.held[p.x, i, zt, p.y] = a.astype(BF)
            self.z_copy(k).start()

    def finish(self):
        p = self.p
        for k in (1, 2, 3):
            self.z_copy(k).wait_recv()
        for i in range(self.n):
            a = (
                self.held[p.x, i, p.z, p.y].astype(F32)
                + self.r2[0, i, p.z].astype(F32)
                + self.r2[1, i, p.z].astype(F32)
            )
            for k in range(3):
                a = a + self.r3[k, i].astype(F32)
            self.out[i] = a

    def drain(self):
        for i in (0, 1):
            self.pair_copy(i).wait_send()
            self.corner_copy(i).wait_send()
            self.plane_copy(i).wait_send()
        for k in (1, 2, 3):
            self.z_copy(k).wait_send()


class Tail:
    def __init__(self, p, gt, hp, hx, hy, hz, out, ss, rs):
        self.p, self.gt, self.hp, self.hx, self.hy, self.hz = p, gt, hp, hx, hy, hz
        self.out, self.ss, self.rs = out, ss, rs

    def cp(self, src, dst, i, dev):
        return remote(src, dst, self.ss.at[i], self.rs.at[i], dev)

    def pair_copy(self, j):
        return self.cp(self.gt.at[j], self.hp.at[j // 2], j, self.p.pair)

    def x_copy(self, j):
        return self.cp(self.gt.at[j], self.hx, 4, self.p.xn)

    def y_copy(self, j):
        return self.cp(self.gt.at[j, :, :, 1 - self.p.y], self.hy, 5, self.p.yn)

    def z_copy(self, j, k):
        p = self.p
        return self.cp(self.gt.at[j, :, (p.z + k) % 4, p.y], self.hz.at[k - 1], 5 + k, p.zn[k])

    def mine(self, j, fn):
        pl.when(self.p.c == j % 2)(fn)

    def start(self, j):
        pl.when(self.p.c != j % 2)(lambda: self.pair_copy(j).start())

    def sum_pair(self, j):
        def do():
            self.pair_copy(j).wait_recv()
            if j >= 2:
                self.x_copy(j).wait_recv()

            def one(i, _):
                w, d = i // 8, i % 8
                at = (w, d // 2, d % 2)
                a = self.gt[(j,) + at].astype(F32) + self.hp[(j // 2,) + at].astype(F32)
                if j >= 2:
                    a = a + self.hx[at].astype(F32)
                self.gt[(j,) + at] = a.astype(BF)
                return 0

            lax.fori_loop(0, 24, one, 0)
            if j < 2:
                self.x_copy(j).start()
            else:
                self.y_copy(j).start()

        self.mine(j, do)

    def sum_y(self, j):
        def do():
            p = self.p
            self.y_copy(j).wait_recv()
            for i in range(3):
                for k in (1, 2, 3):
                    zt = (p.z + k) % 4
                    a = self.gt[j, i, zt, p.y].astype(F32) + self.hy[i, zt].astype(F32)
                    self.gt[j, i, zt, p.y] = a.astype(BF)
            for k in (1, 2, 3):
                self.z_copy(j, k).start()

        self.mine(j, do)

    def finish(self, j):
        def do():
            p = self.p
            for k in (1, 2, 3):
                self.z_copy(j, k).wait_recv()
            for i in range(3):
                a = self.gt[j, i, p.z, p.y].astype(F32) + self.hy[i, p.z].astype(F32)
                for k in range(3):
                    a = a + self.hz[k, i].astype(F32)
                self.out[i] = a

        self.mine(j, do)

    def drain(self):
        for j in range(4):
            pl.when(self.p.c != j % 2)(lambda j=j: self.pair_copy(j).wait_send())

        def sent(j):
            self.x_copy(j).wait_send()
            self.y_copy(j + 2).wait_send()
            for k in (1, 2, 3):
                self.z_copy(j + 2, k).wait_send()

        for j in (0, 1):
            self.mine(j, lambda j=j: sent(j))


def row_steps(count, one):
    def body(i, _):
        one(pl.ds(pl.multiple_of(i * CH, CH), CH))
        return 0

    lax.fori_loop(0, count // CH, body, 0)


def head_half(shape, axis, h):
    return (lax.broadcasted_iota(jnp.int32, shape, axis) // HEAD) == h


def keep_half(value, axis, h):
    return jnp.where(head_half(value.shape, axis, h), value.astype(F32), 0.0).astype(BF)


def run_hooks(hooks, step, half):
    for (at, part), hook in hooks.items():
        if part == half:
            pl.when(step == at)(hook)


def attend(qt, k, vt, bias, ot, lse, temp, hooks):
    def ready(p, h):
        lanes = pl.ds(pl.multiple_of(p * 128, 128), 128)
        return k[:, lanes], keep_half(qt[lanes, :], 0, h)

    def score(kp, qm, h, i, top):
        s = nn(kp[i * 512 : i * 512 + 512], qm) * SCALE
        if bias is not None:
            s = s + bias[i * 512 : i * 512 + 512, :]
        temp[h * 1024 + i * 512 : h * 1024 + i * 512 + 512, :] = s
        m = jnp.max(s, axis=0, keepdims=True)
        return m if top is None else jnp.maximum(top, m)

    def mix(vh, h, i, top, total, mixed):
        e = jnp.exp2(temp[h * 1024 + i * 512 : h * 1024 + i * 512 + 512, :] - top)
        part = jnp.sum(e, axis=0, keepdims=True)
        o = nn(vh[:, i * 512 : i * 512 + 512], e.astype(BF))
        return (part, o) if total is None else (total + part, mixed + o)

    def pair(p, top):
        for h in (0, 1):
            kp, qm = ready(p if h == 0 else (p + 1) % 4, 1 - h)
            vh = vt[pl.ds(pl.multiple_of(p * 128 + h * 64, 64), 64), :]
            total = mixed = later = None
            for i in range(2):
                later = score(kp, qm, 1 - h, i, later)
                total, mixed = mix(vh, h, i, top, total, mixed)
            ot[pl.ds(pl.multiple_of(p * 128 + h * 64, 64), 64), :] = mixed * (1.0 / total)
            lse[pl.ds(p * 2 + h, 1), :] = top + jnp.log2(total)
            top = later
            run_hooks(hooks, p, h)
        return top

    kp, qm = ready(0, 0)
    top = None
    for i in range(2):
        top = score(kp, qm, 0, i, top)
    lax.fori_loop(0, 4, pair, top)


def attend_back(q, qt, k, kt, v, do, dot_, ot, bias, lse, dqt, dk_own, dv_own, dkv_send, order, hooks):
    def pair(step, _):
        p = order(step)
        lanes = pl.ds(pl.multiple_of(p * 128, 128), 128)
        kp, vp = k[:, lanes], v[:, lanes]
        qp, dop = qt[lanes, :], dot_[lanes, :]
        inner = dop.astype(F32) * ot[lanes, :]
        qms = [keep_half(qp, 0, h) for h in (0, 1)]
        doms = [keep_half(dop, 0, h) for h in (0, 1)]
        qr = jnp.concatenate([keep_half(q[:, lanes], 1, h) for h in (0, 1)], axis=0)
        dor = jnp.concatenate([keep_half(do[:, lanes], 1, h) for h in (0, 1)], axis=0)
        ds_sum = [jnp.sum(inner[h * 64 : h * 64 + 64], axis=0, keepdims=True) for h in (0, 1)]
        logs = [lse[pl.ds(p * 2 + h, 1), :] for h in (0, 1)]
        shares, grads = {}, {}
        dq = [None, None]
        dvs, dks = {}, {}

        def one(h, i):
            rows = slice(i * 256, i * 256 + 256)
            s = nn(kp[rows], qms[h]) * SCALE
            if bias is not None:
                s = s + bias[rows, :]
            e = jnp.exp2(s - logs[h])
            dp = nn(vp[rows], doms[h])
            shares[h, i] = e.astype(BF)
            grads[h, i] = (e * (dp - ds_sum[h])).astype(BF)

        def two(h, i):
            rows = slice(i * 256, i * 256 + 256)
            kh = kt[pl.ds(pl.multiple_of(p * 128 + h * 64, 64), 64), rows]
            part = nn(kh, grads[h, i])
            dq[h] = part if dq[h] is None else dq[h] + part
            dv = nn(shares[h, i], dor[h * 512 : h * 512 + 512])
            dk = nn(grads[h, i], qr[h * 512 : h * 512 + 512])
            dvs[i] = dv if i not in dvs else dvs[i] + dv
            dks[i] = dk if i not in dks else dks[i] + dk

        def out(i):
            rows = slice(i * 256, i * 256 + 256)
            if i < 2:
                dk_own[rows, lanes] = dks[i] * 0.125
                dv_own[rows, lanes] = dvs[i]
            else:
                back = slice(i * 256 - 512, i * 256 - 256)
                dkv_send[0, back, lanes] = (dks[i] * 0.125).astype(BF)
                dkv_send[1, back, lanes] = dvs[i].astype(BF)

        for i in range(4):
            one(0, i)
        for i in range(4):
            one(1, i)
            two(0, i)
        run_hooks(hooks, step, 0)
        for i in range(4):
            two(1, i)
            out(i)
        for h in (0, 1):
            dqt[pl.ds(pl.multiple_of(p * 128 + h * 64, 64), 64), :] = (dq[h] * 0.125).astype(BF)
        run_hooks(hooks, step, 1)
        return 0

    lax.fori_loop(0, 4, pair, 0)


def norm_rows(z):
    mean = jnp.mean(z, axis=-1, keepdims=True)
    centred = z - mean
    r = lax.rsqrt(jnp.mean(centred * centred, axis=-1, keepdims=True) + norm_eps)
    return centred * r, r


def norm_back_rows(e, n, r, gain):
    s = e * gain
    a = jnp.mean(s, axis=-1, keepdims=True)
    b = jnp.mean(s * n, axis=-1, keepdims=True)
    return r * (s - a - n * b)


def fast_kernel(
    x_i, enc_i, og_i, valid, seg, rank,
    sq, sk, sv, so, cq, ck, cv, co, up, down,
    g1, b1, g2, b2, g3, b3,
    y_o, dx_o, eg_o, ga_o, gb_o, gf_o, ns_o, vs_o,
    x, enc, og, codes, wa, wb, wf, gt,
    q1, qt1, k1, v1, vt1, o1, ot1, l1,
    q2, qt2, k2, v2, vt2, o2, ot2, l2,
    bias, n1, n2, h1b, h2b, u, gp, dg, dz, low, lowt, do, dot_,
    kvs, kvr1, kvr2, tt, yb, row, st,
    hc, hq, hu, hd, c1, c2, c3, p1, p2, p3, u1, u2, u3, d1, d2, d3, hp, hx, hy, hz,
    st_r, gss, grs, rss, rrs, aas, ars, ess, ers, tss, trs, ls,
):
    dqt, dq = h2b, q2
    dkv = [v2.at[pl.ds(0, 512)], v2.at[pl.ds(512, 512)]]
    p = Place()
    loads = []
    for i, (src, w, j, cols) in enumerate(
        (
            (sq, wa, 0, 128), (sk, wa, 1, 128), (sv, wa, 2, 128),
            (so, wb, 0, 128), (co, wb, 1, 128), (cq, wb, 2, 128), (ck, wb, 3, 128), (cv, wb, 4, 128),
            (up, wf, 0, 512), (down, wf, 1, 512),
        )
    ):
        col = pl.ds(pl.multiple_of(p.t * cols, 128), cols)
        loads.append(pltpu.make_async_copy(src, w.at[j, p.z, p.y, :, col], ls.at[i]))
    for i, (src, dst) in enumerate(((x_i, x), (enc_i, enc), (og_i, og))):
        loads.append(pltpu.make_async_copy(src, dst, ls.at[10 + i]))
    for cp in loads:
        cp.start()
    p.barrier()
    GA, GB, GU, GD = G = [
        Gather(p, w, cols, gss.at[i], grs.at[i])
        for i, (w, cols) in enumerate(
            ((wa, 128), (wb, 128), (wf.at[pl.ds(0, 1)], 512), (wf.at[pl.ds(1, 1)], 512))
        )
    ]
    for cp in loads[:3]:
        cp.wait()
    GA.zs()
    GA.oxy()
    for cp in loads[3:]:
        cp.wait()
    GB.oxy()

    def mat(w, j):
        return w[j].reshape(512, w.shape[4])

    st[...] = jnp.zeros_like(st)
    row[...] = jnp.broadcast_to(valid[...].astype(F32), (128, 512)).T
    own = pl.ds(pl.multiple_of(p.c * 512, 128), 512)
    other = pl.ds(pl.multiple_of((1 - p.c) * 512, 128), 512)
    sx = pl.ds(p.x, 1)
    ranks = rank[sx, :]
    codes[1:2, :] = seg[sx, :] * 8
    codes[0:1, :] = seg[sx, :] * 8 + jnp.concatenate(
        [jnp.broadcast_to(ranks[:, b : b + 1], (1, 128)) for b in range(8)], axis=1
    )
    base, high = codes[1:2, own], codes[0:1, own]
    for i, half in enumerate((own, other)):
        code = jnp.broadcast_to(codes[0:1, half], (128, 512)).T
        for j in range(4):
            c = code[j * 128 : j * 128 + 128, :1]
            ok = (c >= base) & (c <= high)
            bias[i * 512 + j * 128 : i * 512 + j * 128 + 128, :] = jnp.where(ok, 0.0, -2.0e9)
    tt[...] = turn(x[...])

    GA.plane(GB.zs)
    GU.oxy()
    GA.corner()
    GU.zs()
    GD.oxy()
    GA.cross()
    GB.plane()
    GA.finish()
    GD.zs()

    xv = x[...]
    k1[0:512, :] = nn(xv, mat(wa, 1)).astype(BF)
    v1[0:512, :] = nn(xv, mat(wa, 2)).astype(BF)

    def swap(buf, i):
        return remote(buf.at[pl.ds(0, 512)], buf.at[pl.ds(512, 512)], ess.at[i], ers.at[i], p.pair)

    swap(k1, 0).start()
    swap(v1, 1).start()
    qv = nn(xv, mat(wa, 0)).astype(BF)
    q1[...] = qv
    qt1[...] = turn(qv)
    swap(k1, 0).wait_recv()
    swap(v1, 1).wait_recv()
    vt1[...] = turn(v1[...])
    attend(qt1, k1, vt1, bias, ot1, l1, gp, {(0, 0): GB.corner, (1, 0): GU.plane, (2, 0): GB.cross, (3, 0): GD.plane})
    o1[...] = turn(ot1[...].astype(BF))
    GB.finish()
    ev = enc[...]
    k2[0:512, :] = nn(ev, mat(wb, 3)).astype(BF)
    v2[0:512, :] = nn(ev, mat(wb, 4)).astype(BF)
    swap(k2, 2).start()
    swap(v2, 3).start()
    yb[...] = nt(o1[...], mat(wb, 0))
    GU.corner()

    def first(r):
        n, s = norm_rows(x[r, :].astype(F32) + yb[r, :])
        n1[r, :] = n
        row[r, 0:1] = s
        h1b[r, :] = (n * g1[...] + b1[...]).astype(BF)

    row_steps(512, first)
    qv = nn(h1b[...], mat(wb, 2)).astype(BF)
    q2[...] = qv
    qt2[...] = turn(qv)
    swap(k2, 2).wait_recv()
    swap(v2, 3).wait_recv()
    vt2[...] = turn(v2[...])
    attend(qt2, k2, vt2, None, ot2, l2, gp, {(0, 1): GD.corner, (2, 1): GU.cross})
    o2[...] = turn(ot2[...].astype(BF))
    yb[...] = nt(o2[...], mat(wb, 1))

    def second(r):
        n, s = norm_rows(n1[r, :] * g1[...] + b1[...] + yb[r, :])
        n2[r, :] = n
        row[r, 1:2] = s
        h2b[r, :] = (n * g2[...] + b2[...]).astype(BF)

    row_steps(512, second)
    hv = h2b[...]
    blocks = [p.t, p.pair[1], p.xt, (1 - p.x) * 2 + 1 - p.c]
    waits = [None, GU.p_recv(0).wait_recv, GD.cross, GU.p_recv(1).wait_recv]
    for t, wait in zip(blocks, waits):
        if wait is not None:
            wait()
        cols = pl.ds(pl.multiple_of(t * 512, 512), 512)
        gp[cols, :] = nn(hv, wf[0, :, :, :, cols].reshape(512, 512))

        def gelu(r, cols=cols, t=t):
            at = pl.ds(pl.multiple_of(r.start + t * 512, CH), CH)
            v = gp[at, :]
            cdf = 0.5 * (1.0 + lax.erf(v * 0.7071067811865476))
            u[r, cols] = (v * cdf).astype(BF)
            gp[at, :] = cdf + v * (jnp.exp2(v * v * (-0.5 * LOG2E)) * 0.3989422804014327)

        row_steps(512, gelu)
    waits = [None, GD.p_recv(0).wait_recv, None, GD.p_recv(1).wait_recv]
    for i, (t, wait) in enumerate(zip(blocks, waits)):
        if wait is not None:
            wait()
        cols = pl.ds(pl.multiple_of(t * 512, 512), 512)
        part = nt(u[:, cols], wf[1, :, :, :, cols].reshape(512, 512))
        yb[...] = part if i == 0 else yb[...] + part

    def third(r):
        n, s = norm_rows(n2[r, :] * g2[...] + b2[...] + yb[r, :])
        out = n * g3[...] + b3[...]
        vc = row[r, 2:3]
        yb[r, :] = out
        e = og[r, :].astype(F32) * vc
        st[4:5, :] += jnp.sum(e * n, axis=0, keepdims=True)
        st[5:6, :] += jnp.sum(e, axis=0, keepdims=True)
        st[6:7, :] += jnp.sum(vc * out * out, axis=0, keepdims=True)
        back = norm_back_rows(e, n, s, g3[...])
        dz[r, :] = back
        low[r, :] = back.astype(BF)

    row_steps(512, third)
    y_copy = pltpu.make_async_copy(yb, y_o, ls.at[0])
    y_copy.start()
    lv = low[...]
    lowt[...] = turn(lv)
    for j in range(4):
        cols = slice(j * 512, j * 512 + 512)
        dg[:, cols] = (nn(lv, wf[1, :, :, :, cols].reshape(512, 512)) * gp[cols, :]).astype(BF)
    for g in G:
        g.drain()
    RC, RP, RU, RD = R = [
        Reduce(p, w.at[pl.ds(at, n)], cols, *bufs, out.at[pl.ds(at, n)], rss.at[i], rrs.at[i])
        for i, (w, at, n, cols, bufs, out) in enumerate(
            (
                (wb, 0, 2, 128, (hc, c1, c2, c3), gb_o),
                (wb, 2, 3, 128, (hq, p1, p2, p3), gb_o),
                (wf, 0, 1, 512, (hu, u1, u2, u3), gf_o),
                (wf, 1, 1, 512, (hd, d1, d2, d3), gf_o),
            )
        )
    ]
    for j in range(4):
        cols = slice(j * 512, j * 512 + 512)
        wf[1, :, :, :, cols] = nn(lowt[...], u[:, cols]).astype(BF).reshape(4, 2, 64, 512)
    RD.start()
    dz[...] += nt(dg[...], mat(wf, 0))
    tt[...] = turn(h2b[...])
    for j in range(4):
        cols = slice(j * 512, j * 512 + 512)
        wf[0, :, :, :, cols] = nn(tt[...], dg[:, cols]).astype(BF).reshape(4, 2, 64, 512)
    RU.start()
    RD.corner()

    def back2(r):
        e = dz[r, :]
        n = n2[r, :]
        st[2:3, :] += jnp.sum(e * n, axis=0, keepdims=True)
        st[3:4, :] += jnp.sum(e, axis=0, keepdims=True)
        back = norm_back_rows(e, n, row[r, 1:2], g2[...])
        dz[r, :] = back
        low[r, :] = back.astype(BF)

    row_steps(512, back2)
    dov = nn(low[...], mat(wb, 1)).astype(BF)
    do[...] = dov
    dot_[...] = turn(dov)
    lowt[...] = turn(low[...])
    wb[1] = nn(lowt[...], o2[...]).astype(BF).reshape(4, 2, 64, 512)
    vt2[...] = turn(k2[...])
    RU.corner()
    attend_back(
        q2, qt2, k2, vt2, v2, do, dot_, ot2, None, l2, dqt,
        gp.at[pl.ds(0, 512)], gp.at[pl.ds(512, 512)], kvs, lambda step: step,
        {(0, 0): RD.plane, (1, 0): RU.plane, (3, 0): RD.along},
    )

    def swap_back(buf, i):
        return remote(kvs, buf, ess.at[i], ers.at[i], p.pair)

    swap_back(kvr2, 4).start()
    dqv = turn(dqt[...])
    dz[...] += nt(dqv, mat(wb, 2))
    tt[...] = turn(h1b[...])
    wb[2] = nn(tt[...], dqv).astype(BF).reshape(4, 2, 64, 512)
    tt[...] = turn(enc[...])
    swap_back(kvr2, 4).wait()
    for i in range(4):
        swap((k1, v1, k2, v2)[i], i).wait_send()

    def join(recv, at):
        def one(r):
            for i in (0, 1):
                own_rows = pl.ds(pl.multiple_of(r.start + at + i * 512, CH), CH)
                dkv[i][r, :] = (gp[own_rows, :] + recv[i, r, :].astype(F32)).astype(BF)

        row_steps(512, one)

    join(kvr2, 0)
    y_copy.wait()
    yb[...] = nt(dkv[0][...], mat(wb, 3)) + nt(dkv[1][...], mat(wb, 4))
    e_copy = pltpu.make_async_copy(yb, eg_o, ls.at[0])
    e_copy.start()
    wb[3] = nn(tt[...], dkv[0][...]).astype(BF).reshape(4, 2, 64, 512)
    wb[4] = nn(tt[...], dkv[1][...]).astype(BF).reshape(4, 2, 64, 512)
    RP.start()

    def back1(r):
        e = dz[r, :]
        n = n1[r, :]
        st[0:1, :] += jnp.sum(e * n, axis=0, keepdims=True)
        st[1:2, :] += jnp.sum(e, axis=0, keepdims=True)
        back = norm_back_rows(e, n, row[r, 0:1], g1[...])
        dz[r, :] = back
        low[r, :] = back.astype(BF)

    row_steps(512, back1)
    RU.along()
    dov = nn(low[...], mat(wb, 0)).astype(BF)
    do[...] = dov
    dot_[...] = turn(dov)
    lowt[...] = turn(low[...])
    wb[0] = nn(lowt[...], o1[...]).astype(BF).reshape(4, 2, 64, 512)
    RC.start()
    RP.corner()
    vt1[...] = turn(k1[...])
    tt[...] = turn(x[...])
    T = Tail(p, gt, hp, hx, hy, hz, ga_o, aas, ars)

    def order(step):
        far = (step // 2) * p.x + (1 - step // 2) * (1 - p.x)
        return 2 * far + step % 2

    def lanes_of(step):
        return pl.ds(pl.multiple_of(order(step) * 128, 128), 128)

    def part_back(step):
        at = lanes_of(step)
        return remote(
            kvs.at[:, :, at], kvr1.at[:, :, at], ess.at[5 + step], ers.at[5 + step], p.pair
        )

    def grads(step):
        at = lanes_of(step)
        part_back(step).wait_recv()

        def one(r):
            for i in (0, 1):
                rows = pl.ds(pl.multiple_of(r.start + 1024 + i * 512, CH), CH)
                dkv[i][r, at] = (gp[rows, at] + kvr1[i, r, at].astype(F32)).astype(BF)

        row_steps(512, one)
        dqv = turn(dqt[at, :])
        dq[:, at] = dqv
        gt[step, 0] = nn(tt[...], dqv).astype(BF).reshape(4, 2, 64, 128)
        gt[step, 1] = nn(tt[...], dkv[0][:, at]).astype(BF).reshape(4, 2, 64, 128)
        gt[step, 2] = nn(tt[...], dkv[1][:, at]).astype(BF).reshape(4, 2, 64, 128)
        T.start(step)

    def both(*fns):
        def run():
            for fn in fns:
                fn()

        return run

    attend_back(
        q1, qt1, k1, vt1, v1, do, dot_, ot1, bias, l1, dqt,
        gp.at[pl.ds(1024, 512)], gp.at[pl.ds(1536, 512)], kvs, order,
        {
            (0, 0): RC.corner,
            (0, 1): both(lambda: part_back(0).start(), RP.plane),
            (1, 0): lambda: grads(0),
            (1, 1): both(lambda: part_back(1).start(), RC.plane, RD.finish),
            (2, 0): both(lambda: grads(1), lambda: T.sum_pair(0)),
            (2, 1): both(lambda: part_back(2).start(), RP.along, RU.finish),
            (3, 0): both(lambda: grads(2), lambda: T.sum_pair(1)),
            (3, 1): both(lambda: part_back(3).start(), RC.along),
        },
    )
    T.sum_pair(2)
    grads(3)
    T.sum_pair(3)
    T.sum_y(2)
    dz[...] += nt(dq[...], mat(wa, 0)) + nt(dkv[0][...], mat(wa, 1)) + nt(dkv[1][...], mat(wa, 2))
    x_copy = pltpu.make_async_copy(dz, dx_o, ls.at[1])
    x_copy.start()

    def squares(r):
        st[7:8, :] += jnp.sum(row[r, 2:3] * dz[r, :] * dz[r, :], axis=0, keepdims=True)

    row_steps(512, squares)

    def stat(i, src, dev):
        return remote(src, st_r.at[i], tss.at[i], trs.at[i], dev)

    stat(0, st, p.pair).start()
    T.sum_y(3)
    stat(0, st, p.pair).wait()
    st_r[6] = st[...] + st_r[0]
    stat(1, st_r.at[6], p.xn).start()
    T.finish(2)
    RP.finish()
    RC.finish()
    stat(1, st_r.at[6], p.xn).wait()
    st_r[7] = st_r[6] + st_r[1]
    stat(2, st_r.at[7], p.yn).start()
    stat(2, st_r.at[7], p.yn).wait()
    st_r[8] = st_r[7] + st_r[2]
    for k in (1, 2, 3):
        stat(2 + k, st_r.at[8], p.zn[k]).start()
    T.finish(3)
    for k in (1, 2, 3):
        stat(2 + k, st_r.at[8], p.zn[k]).wait()
    total = None
    for zs in range(4):
        part = None
        for k in range(4):
            got = st_r[8] if k == 0 else st_r[2 + k]
            got = jnp.where((p.z - k + 4) % 4 == zs, got, 0.0)
            part = got if part is None else part + got
        total = part if total is None else total + part
    ns_o[...] = total[0:6]
    vs_o[...] = jnp.sqrt(total[6:8] * (1.0 / 16384.0))
    for step in range(4):
        part_back(step).wait_send()
    for r in R:
        r.drain()
    T.drain()
    e_copy.wait()
    x_copy.wait()


def place_kernel(*refs):
    srcs, outs, held, sems = refs[:8], refs[8:23], refs[23:31], refs[31]
    parts = [held[0], held[1], held[2]] + [held[3].at[i] for i in range(3)]
    parts += [held[4].at[i] for i in range(5)] + [held[5].at[i] for i in range(2)] + [held[6], held[7]]
    first = [pltpu.make_async_copy(a, b, sems.at[i]) for i, (a, b) in enumerate(zip(srcs, held))]
    last = [pltpu.make_async_copy(a, b, sems.at[8 + i]) for i, (a, b) in enumerate(zip(parts, outs))]
    ends = [(0, 1), (1, 2), (2, 3), (3, 6), (6, 11), (11, 13), (13, 14), (14, 15)]
    order = (6, 7, 3, 4, 5, 0, 1, 2)
    for i in order:
        first[i].start()
    for i in order:
        first[i].wait()
        for cp in last[ends[i][0] : ends[i][1]]:
            cp.start()
    for cp in last:
        cp.wait()


def fast_shards(
    tokens, encoder_states, output_grad, valid_mask, segment_ids, context_ranks,
    self_query, self_key, self_value, self_output,
    cross_query, cross_key, cross_value, cross_output, hidden_up, hidden_down,
    norm1_gain, norm1_bias, norm2_gain, norm2_bias, norm3_gain, norm3_bias,
):
    vm = pl.BlockSpec(memory_space=pltpu.VMEM)
    hbm = pl.BlockSpec(memory_space=pl.ANY)
    rows = [
        v.reshape(1, 512)
        for v in (norm1_gain, norm1_bias, norm2_gain, norm2_bias, norm3_gain, norm3_bias)
    ]

    def V(*shape, dtype=BF):
        return pltpu.VMEM(shape, dtype)

    def S(*shape):
        return pltpu.SemaphoreType.DMA(shape)

    def group(n, cols):
        return [
            V(2, n, 4, 2, 64, cols),
            [V(2, n, 2, 64, cols), V(2, n, 4, 64, cols), V(3, n, 64, cols)],
        ]

    rc, rp, ru, rd = group(2, 128), group(3, 128), group(1, 512), group(1, 512)

    def attention():
        return [
            V(512, 512), V(512, 512), V(1024, 512), V(1024, 512), V(512, 1024), V(512, 512),
            V(512, 512, dtype=F32), V(8, 512, dtype=F32),
        ]

    scratch = (
        [V(512, 512)] * 3
        + [V(8, 1024, dtype=jnp.int32)]
        + [V(3, 4, 2, 64, 512), V(5, 4, 2, 64, 512), V(2, 4, 2, 64, 2048), V(4, 3, 4, 2, 64, 128)]
        + attention()
        + attention()
        + [V(1024, 512, dtype=F32), V(512, 512, dtype=F32), V(512, 512, dtype=F32)]
        + [V(512, 512), V(512, 512)]
        + [V(512, 2048), V(2048, 512, dtype=F32), V(512, 2048), V(512, 512, dtype=F32)]
        + [V(512, 512)] * 4
        + [V(2, 512, 512), V(2, 512, 512), V(2, 512, 512)]
        + [V(512, 512), V(512, 512, dtype=F32), V(512, 128, dtype=F32), V(8, 512, dtype=F32)]
        + [rc[0], rp[0], ru[0], rd[0]]
        + rc[1] + rp[1] + ru[1] + rd[1]
        + [V(2, 3, 4, 2, 64, 128), V(3, 4, 2, 64, 128), V(3, 4, 64, 128), V(3, 3, 64, 128)]
        + [V(9, 8, 512, dtype=F32)]
        + [S(4, 19), S(4, 19), S(4, 9), S(4, 9), S(9), S(9), S(9), S(9), S(6), S(6), S(13)]
    )
    big = jax.ShapeDtypeStruct((512, 512), F32)
    outs = pl.pallas_call(
        fast_kernel,
        out_shape=[big, big, big]
        + [jax.ShapeDtypeStruct(s, F32) for s in ((3, 64, 128), (5, 64, 128), (2, 64, 512), (6, 512), (2, 512))],
        in_specs=[hbm] * 3 + [vm] * 3 + [hbm] * 10 + [vm] * 6,
        out_specs=[hbm] * 3 + [vm] * 5,
        scratch_shapes=scratch,
        compiler_params=pltpu.CompilerParams(
            collective_id=0, has_side_effects=True, vmem_limit_bytes=63 << 20
        ),
        name="layer",
    )(
        tokens, encoder_states, output_grad, valid_mask.reshape(1, 512), segment_ids, context_ranks,
        self_query, self_key, self_value, self_output.T,
        cross_query, cross_key, cross_value, cross_output.T, hidden_up, hidden_down.T, *rows,
    )
    ends = [big, big, big] + [jax.ShapeDtypeStruct((64, 128), F32)] * 8
    ends += [jax.ShapeDtypeStruct((64, 512), F32)] * 2
    ends += [jax.ShapeDtypeStruct(v, F32) for v in ((6, 512), (2, 512))]
    y, dx, eg, dsq, dsk, dsv, dso, dco, dcq, dck, dcv, dup, ddown, ns, vs = pl.pallas_call(
        place_kernel,
        out_shape=ends,
        in_specs=[hbm] * 8,
        out_specs=[hbm] * 15,
        scratch_shapes=[pltpu.VMEM(o.shape, F32) for o in outs] + [S(23)],
        name="place",
    )(*outs)
    return (
        y, dx, eg, dsq, dsk, dsv, dso.T, dcq, dck, dcv, dco.T, dup, ddown.T, ns, vs,
    )


def solution(mesh):
    in_specs = (
        P(("dp", "tensor"), None),
        P(("dp", "tensor"), None),
        P(("dp", "tensor"), None),
        P(("dp", "tensor")),
        P("dp", None),
        P("dp", None),
        P("dp", "tensor"),
        P("dp", "tensor"),
        P("dp", "tensor"),
        P("tensor", "dp"),
        P("dp", "tensor"),
        P("dp", "tensor"),
        P("dp", "tensor"),
        P("tensor", "dp"),
        P("dp", "tensor"),
        P("tensor", "dp"),
        P(),
        P(),
        P(),
        P(),
        P(),
        P(),
    )
    out_specs = (
        P(("dp", "tensor"), None),
        P(("dp", "tensor"), None),
        P(("dp", "tensor"), None),
        P("dp", "tensor"),
        P("dp", "tensor"),
        P("dp", "tensor"),
        P("tensor", "dp"),
        P("dp", "tensor"),
        P("dp", "tensor"),
        P("dp", "tensor"),
        P("tensor", "dp"),
        P("dp", "tensor"),
        P("tensor", "dp"),
        P(),
        P(),
    )
    body = fast_shards if dict(mesh.shape) == {"dp": 8, "tensor": 4} else shards
    return jax.shard_map(body, mesh=mesh, in_specs=in_specs, out_specs=out_specs, check_vma=False)
```

```python
import jax
import jax.numpy as jnp
from jax import lax
from jax.experimental import pallas as pl
from jax.experimental.pallas import tpu as pltpu
from jax.sharding import PartitionSpec as P

HEAD = 64
LEN = 1024
BLK = 128


norm_eps = 1e-05
mask_fill = -1000000000.0


def gelu_exact(value):
    return jax.nn.gelu(value, approximate=False)


def gelu_back(preact, upstream):
    return jax.vjp(gelu_exact, preact)[1](upstream)[0]


def layer_norm(value, gain, bias):
    mean = jnp.mean(value, axis=-1, keepdims=True)
    centred = value - mean
    scale = lax.rsqrt(jnp.mean(centred * centred, axis=-1, keepdims=True) + norm_eps)
    normal = centred * scale
    return (normal * gain + bias, normal, scale)


def norm_back(upstream, normal, scale, gain):
    scaled = upstream * gain
    mean_grad = jnp.mean(scaled, axis=-1, keepdims=True)
    mean_cross = jnp.mean(scaled * normal, axis=-1, keepdims=True)
    inward = scale * (scaled - mean_grad - normal * mean_cross)
    return (inward, jnp.sum(upstream * normal, axis=0), jnp.sum(upstream, axis=0))


def context_allowed(segments, ranks, first, count):
    length = segments.shape[0]
    key_block = jnp.arange(length, dtype=jnp.int32) // BLK
    key_rank = jnp.broadcast_to(ranks[:, None], (ranks.shape[0], BLK)).reshape(length)
    query_segment = lax.dynamic_slice_in_dim(segments, first, count)
    query_rank = lax.dynamic_slice_in_dim(key_rank, first, count)
    query_block = (first + jnp.arange(count, dtype=jnp.int32)) // BLK
    same_doc = query_segment[:, None] == segments[None, :]
    earlier = key_rank[None, :] < query_rank[:, None]
    same_block = query_block[:, None] == key_block[None, :]
    return same_doc & (earlier | same_block)


def full_rows(value):
    return lax.all_gather(value, "tensor", axis=0, tiled=True)


def grad_rows(value):
    return lax.all_gather(value, "tensor", axis=0, tiled=True)


def branch_sum(mixed, weight):
    return lax.psum_scatter(
        jnp.dot(mixed, weight, preferred_element_type=jnp.float32),
        "tensor",
        scatter_dimension=0,
        tiled=True,
    )


def back_product(left, weight):
    return lax.dot_general(
        left, weight, (((1,), (1,)), ((), ())), preferred_element_type=jnp.float32
    )


def row_product(left, right):
    return lax.dot_general(
        left, right, (((0,), (0,)), ((), ())), preferred_element_type=jnp.float32
    )


def input_sum(pairs):
    total = None
    for left, weight in pairs:
        portion = back_product(left, weight)
        total = portion if total is None else total + portion
    return lax.psum_scatter(total, "tensor", scatter_dimension=0, tiled=True)


def split_heads(value, count):
    return value.reshape(count, LEN, value.shape[1] // HEAD, HEAD)


def attend_sequence(query, keys, values, segments, ranks, masked):
    length = query.shape[0]
    width = min(length, 512)

    def one_block(index):
        first = index * width
        piece = lax.dynamic_slice_in_dim(query, first, width, 0)
        scores = jnp.einsum("qhd,khd->hqk", piece, keys, preferred_element_type=jnp.float32) * 0.125
        if masked:
            scores = jnp.where(
                context_allowed(segments, ranks, first, width)[None], scores, mask_fill
            )
        top = jnp.max(scores, axis=-1, keepdims=True)
        raised = jnp.exp(scores - top)
        total = jnp.sum(raised, axis=-1, keepdims=True)
        shares = (raised / total).astype(jnp.bfloat16)
        mixed = jnp.einsum("hqk,khd->qhd", shares, values, preferred_element_type=jnp.float32)
        return (mixed.astype(jnp.bfloat16), (top + jnp.log(total))[..., 0])

    mixed, log_total = lax.map(one_block, jnp.arange(length // width, dtype=jnp.int32))
    return (mixed.reshape(query.shape), log_total)


def attend_sequence_back(query, keys, values, segments, ranks, masked, log_total, grad_mixed):
    length = query.shape[0]
    width = min(length, 512)

    def one_block(carry, index):
        key_sum, value_sum = carry
        first = index * width
        piece = lax.dynamic_slice_in_dim(query, first, width, 0)
        grad_piece = lax.dynamic_slice_in_dim(grad_mixed, first, width, 0)
        scores = jnp.einsum("qhd,khd->hqk", piece, keys, preferred_element_type=jnp.float32) * 0.125
        if masked:
            scores = jnp.where(
                context_allowed(segments, ranks, first, width)[None], scores, mask_fill
            )
        shares = jnp.exp(scores - log_total[index][..., None])
        grad_shares = jnp.einsum(
            "qhd,khd->hqk", grad_piece, values, preferred_element_type=jnp.float32
        )
        inner = jnp.sum(shares * grad_shares, axis=-1, keepdims=True)
        grad_scores = (shares * (grad_shares - inner)).astype(jnp.bfloat16)
        grad_query = (
            jnp.einsum("hqk,khd->qhd", grad_scores, keys, preferred_element_type=jnp.float32)
            * 0.125
        )
        key_sum = (
            key_sum
            + jnp.einsum("hqk,qhd->khd", grad_scores, piece, preferred_element_type=jnp.float32)
            * 0.125
        )
        value_sum = value_sum + jnp.einsum(
            "hqk,qhd->khd",
            shares.astype(jnp.bfloat16),
            grad_piece,
            preferred_element_type=jnp.float32,
        )
        return ((key_sum, value_sum), grad_query.astype(jnp.bfloat16))

    zeros = jnp.zeros(keys.shape, jnp.float32)
    (key_sum, value_sum), grad_query = lax.scan(
        one_block, (zeros, zeros), jnp.arange(length // width, dtype=jnp.int32)
    )
    return (
        grad_query.reshape(query.shape),
        key_sum.astype(jnp.bfloat16),
        value_sum.astype(jnp.bfloat16),
    )


def attend_all(query, keys, values, segments, ranks, masked):
    count = query.shape[0] // LEN

    def one_sequence(items):
        return attend_sequence(items[0], items[1], items[2], items[3], items[4], masked)

    mixed, log_total = lax.map(
        one_sequence,
        (
            split_heads(query, count),
            split_heads(keys, count),
            split_heads(values, count),
            segments,
            ranks,
        ),
    )
    return (mixed.reshape(query.shape), log_total)


def attend_back_all(query, keys, values, segments, ranks, masked, log_total, grad_mixed):
    count = query.shape[0] // LEN

    def one_sequence(items):
        return attend_sequence_back(
            items[0], items[1], items[2], items[3], items[4], masked, items[5], items[6]
        )

    grad_query, grad_keys, grad_values = lax.map(
        one_sequence,
        (
            split_heads(query, count),
            split_heads(keys, count),
            split_heads(values, count),
            segments,
            ranks,
            log_total,
            split_heads(grad_mixed, count),
        ),
    )
    return (
        grad_query.reshape(query.shape),
        grad_keys.reshape(keys.shape),
        grad_values.reshape(values.shape),
    )


def shards(
    tokens,
    encoder_states,
    output_grad,
    valid_mask,
    segment_ids,
    context_ranks,
    self_query,
    self_key,
    self_value,
    self_output,
    cross_query,
    cross_key,
    cross_value,
    cross_output,
    hidden_up,
    hidden_down,
    norm1_gain,
    norm1_bias,
    norm2_gain,
    norm2_bias,
    norm3_gain,
    norm3_bias,
):
    (
        self_query,
        self_key,
        self_value,
        self_output,
        cross_query,
        cross_key,
        cross_value,
        cross_output,
        hidden_up,
        hidden_down,
    ) = (
        lax.all_gather(self_query, "dp", axis=0, tiled=True),
        lax.all_gather(self_key, "dp", axis=0, tiled=True),
        lax.all_gather(self_value, "dp", axis=0, tiled=True),
        lax.all_gather(self_output, "dp", axis=1, tiled=True),
        lax.all_gather(cross_query, "dp", axis=0, tiled=True),
        lax.all_gather(cross_key, "dp", axis=0, tiled=True),
        lax.all_gather(cross_value, "dp", axis=0, tiled=True),
        lax.all_gather(cross_output, "dp", axis=1, tiled=True),
        lax.all_gather(hidden_up, "dp", axis=0, tiled=True),
        lax.all_gather(hidden_down, "dp", axis=1, tiled=True),
    )
    tokens_full = full_rows(tokens)
    query = jnp.dot(tokens_full, self_query, preferred_element_type=jnp.float32).astype(
        jnp.bfloat16
    )
    keys = jnp.dot(tokens_full, self_key, preferred_element_type=jnp.float32).astype(jnp.bfloat16)
    values = jnp.dot(tokens_full, self_value, preferred_element_type=jnp.float32).astype(
        jnp.bfloat16
    )
    self_mixed, self_log = attend_all(query, keys, values, segment_ids, context_ranks, True)
    attended = branch_sum(self_mixed, self_output)
    first_out, first_normal, first_scale = layer_norm(
        tokens.astype(jnp.float32) + attended, norm1_gain, norm1_bias
    )
    first_full = full_rows(first_out.astype(jnp.bfloat16))
    encoder_full = full_rows(encoder_states)
    second_query = jnp.dot(first_full, cross_query, preferred_element_type=jnp.float32).astype(
        jnp.bfloat16
    )
    encoder_keys = jnp.dot(encoder_full, cross_key, preferred_element_type=jnp.float32).astype(
        jnp.bfloat16
    )
    encoder_values = jnp.dot(encoder_full, cross_value, preferred_element_type=jnp.float32).astype(
        jnp.bfloat16
    )
    cross_mixed, cross_log = attend_all(
        second_query, encoder_keys, encoder_values, segment_ids, context_ranks, False
    )
    crossed = branch_sum(cross_mixed, cross_output)
    second_out, second_normal, second_scale = layer_norm(
        first_out + crossed, norm2_gain, norm2_bias
    )
    second_low = second_out.astype(jnp.bfloat16)
    feed_input = full_rows(second_low)
    preact = jnp.dot(feed_input, hidden_up, preferred_element_type=jnp.float32)
    activated = gelu_exact(preact).astype(jnp.bfloat16)
    feed_out = branch_sum(activated, hidden_down)
    third_out, third_normal, third_scale = layer_norm(second_out + feed_out, norm3_gain, norm3_bias)
    valid_rows = valid_mask.astype(jnp.float32)[:, None]
    grad_layer = output_grad.astype(jnp.float32) * valid_rows
    grad_third, gain3_grad, bias3_grad = norm_back(
        grad_layer, third_normal, third_scale, norm3_gain
    )
    grad_third_low = grad_third.astype(jnp.bfloat16)
    grad_feed = grad_rows(grad_third_low)
    grad_active = back_product(grad_feed, hidden_down)
    grad_preact = gelu_back(preact, grad_active).astype(jnp.bfloat16)
    up_grad = row_product(feed_input, grad_preact)
    down_grad = row_product(activated, grad_feed)
    grad_second = grad_third + input_sum([(grad_preact, hidden_up)])
    grad_second_in, gain2_grad, bias2_grad = norm_back(
        grad_second, second_normal, second_scale, norm2_gain
    )
    grad_crossed = grad_rows(grad_second_in.astype(jnp.bfloat16))
    cross_output_grad = row_product(cross_mixed, grad_crossed)
    grad_cross_mixed = back_product(grad_crossed, cross_output).astype(jnp.bfloat16)
    grad_second_query, grad_encoder_keys, grad_encoder_values = attend_back_all(
        second_query,
        encoder_keys,
        encoder_values,
        segment_ids,
        context_ranks,
        False,
        cross_log,
        grad_cross_mixed,
    )
    cross_query_grad = row_product(first_full, grad_second_query)
    cross_key_grad = row_product(encoder_full, grad_encoder_keys)
    cross_value_grad = row_product(encoder_full, grad_encoder_values)
    grad_first = grad_second_in + input_sum([(grad_second_query, cross_query)])
    encoder_grad = input_sum([(grad_encoder_keys, cross_key), (grad_encoder_values, cross_value)])
    grad_first_in, gain1_grad, bias1_grad = norm_back(
        grad_first, first_normal, first_scale, norm1_gain
    )
    grad_attended = grad_rows(grad_first_in.astype(jnp.bfloat16))
    self_output_grad = row_product(self_mixed, grad_attended)
    grad_self_mixed = back_product(grad_attended, self_output).astype(jnp.bfloat16)
    grad_query, grad_keys, grad_values = attend_back_all(
        query, keys, values, segment_ids, context_ranks, True, self_log, grad_self_mixed
    )
    self_query_grad = row_product(tokens_full, grad_query)
    self_key_grad = row_product(tokens_full, grad_keys)
    self_value_grad = row_product(tokens_full, grad_values)
    tokens_grad = grad_first_in + input_sum(
        [(grad_query, self_query), (grad_keys, self_key), (grad_values, self_value)]
    )
    (
        self_query_grad,
        self_key_grad,
        self_value_grad,
        self_output_grad,
        cross_query_grad,
        cross_key_grad,
        cross_value_grad,
        cross_output_grad,
        up_grad,
        down_grad,
    ) = (
        lax.psum_scatter(self_query_grad, "dp", scatter_dimension=0, tiled=True),
        lax.psum_scatter(self_key_grad, "dp", scatter_dimension=0, tiled=True),
        lax.psum_scatter(self_value_grad, "dp", scatter_dimension=0, tiled=True),
        lax.psum_scatter(self_output_grad, "dp", scatter_dimension=1, tiled=True),
        lax.psum_scatter(cross_query_grad, "dp", scatter_dimension=0, tiled=True),
        lax.psum_scatter(cross_key_grad, "dp", scatter_dimension=0, tiled=True),
        lax.psum_scatter(cross_value_grad, "dp", scatter_dimension=0, tiled=True),
        lax.psum_scatter(cross_output_grad, "dp", scatter_dimension=1, tiled=True),
        lax.psum_scatter(up_grad, "dp", scatter_dimension=0, tiled=True),
        lax.psum_scatter(down_grad, "dp", scatter_dimension=1, tiled=True),
    )
    norm_sums, square_sums = lax.psum(
        (
            jnp.stack([gain1_grad, bias1_grad, gain2_grad, bias2_grad, gain3_grad, bias3_grad]),
            jnp.stack(
                [
                    jnp.sum(valid_rows * third_out * third_out, axis=0),
                    jnp.sum(valid_rows * tokens_grad * tokens_grad, axis=0),
                ]
            ),
        ),
        ("dp", "tensor"),
    )
    total_tokens = tokens.shape[0] * lax.axis_size("dp") * lax.axis_size("tensor")
    valid_scales = jnp.sqrt(square_sums / total_tokens)
    return (
        third_out,
        tokens_grad,
        encoder_grad,
        self_query_grad,
        self_key_grad,
        self_value_grad,
        self_output_grad,
        cross_query_grad,
        cross_key_grad,
        cross_value_grad,
        cross_output_grad,
        up_grad,
        down_grad,
        norm_sums,
        valid_scales,
    )


MESH = pl.DeviceIdType.MESH
BF = jnp.bfloat16
F32 = jnp.float32
LOG2E = 1.4426950408889634
SCALE = 0.125 * LOG2E
CH = 256


def nn(a, b):
    return lax.dot_general(a, b, (((1,), (0,)), ((), ())), preferred_element_type=F32)


def nt(a, b):
    return lax.dot_general(a, b, (((1,), (1,)), ((), ())), preferred_element_type=F32)


def turn(x):
    return x.T


class Place:
    def __init__(self):
        self.d = lax.axis_index("dp")
        self.t = lax.axis_index("tensor")
        self.z, self.y = self.d // 2, self.d % 2
        self.x, self.c = self.t // 2, self.t % 2
        self.xt = (1 - self.x) * 2 + self.c
        self.xn = (self.d, self.xt)
        self.yn = (self.z * 2 + 1 - self.y, self.t)
        self.pair = (self.d, self.x * 2 + 1 - self.c)
        self.zn = [None] + [((((self.z + k) % 4) * 2 + self.y), self.t) for k in (1, 2, 3)]
        top = self.z // 2
        self.near = [self.z, top * (5 - self.z) + (1 - top) * (1 - self.z), 2 - top, 3 * (1 - top)]

    def plane_peer(self, i):
        x, y, c = (self.x + i // 4) % 2, (self.y + i // 2) % 2, (self.c + i) % 2
        return (self.z * 2 + y, x * 2 + c)

    def barrier(self):
        sem = pltpu.get_barrier_semaphore()
        for dev in [self.plane_peer(i) for i in range(1, 8)] + self.zn[1:]:
            pl.semaphore_signal(sem, inc=1, device_id=dev, device_id_type=MESH)
        pl.semaphore_wait(sem, 10)


def remote(src, dst, send, recv, dev):
    return pltpu.make_async_remote_copy(
        src_ref=src, dst_ref=dst, send_sem=send, recv_sem=recv, device_id=dev, device_id_type=MESH
    )


class Gather:
    def __init__(self, p, w, cols, ss, rs):
        self.p, self.w, self.cols, self.ss, self.rs = p, w, cols, ss, rs

    def col(self, t):
        return pl.ds(pl.multiple_of(t * self.cols, 128), self.cols)

    def blk(self, k, y, t):
        return self.w.at[:, self.p.near[k], y, :, self.col(t)]

    def cp(self, ref, i, dev, send=None):
        return remote(ref, ref, self.ss.at[i if send is None else send], self.rs.at[i], dev)

    def own(self):
        return self.blk(0, self.p.y, self.p.t)

    def z_send(self, k):
        p = self.p
        dev = (p.near[k] * 2 + p.y, p.t)
        return self.cp(self.own(), 15 + p.z, dev, k - 1)

    def z_recv(self, k):
        p = self.p
        ref = self.blk(k, p.y, p.t)
        return self.cp(ref, 15 + p.near[k], (p.near[k] * 2 + p.y, p.t), k - 1)

    def x_send(self, k):
        return self.cp(self.blk(k, self.p.y, self.p.t), 3 + k, self.p.xn)

    def x_recv(self, k):
        return self.cp(self.blk(k, self.p.y, self.p.xt), 3 + k, self.p.xn)

    def y_send(self, k):
        return self.cp(self.blk(k, self.p.y, self.p.t), 7 + k, self.p.yn)

    def y_recv(self, k):
        return self.cp(self.blk(k, 1 - self.p.y, self.p.t), 7 + k, self.p.yn)

    def q_send(self, k):
        if k < 2:
            return self.cp(self.blk(k, self.p.y, self.p.xt), 11 + k, self.p.yn)
        return self.cp(self.blk(k, 1 - self.p.y, self.p.t), 11 + k, self.p.xn)

    def q_recv(self, k):
        return self.cp(self.blk(k, 1 - self.p.y, self.p.xt), 11 + k, self.p.xn)

    def rail(self, i, core):
        x = self.p.x if i == 0 else 1 - self.p.x
        return self.w.at[:, :, :, :, self.col(x * 2 + core)]

    def p_send(self, i):
        return self.cp(self.rail(i, self.p.c), 1 + i, self.p.pair, 17 + i)

    def p_recv(self, i):
        return self.cp(self.rail(i, 1 - self.p.c), 1 + i, self.p.pair, 17 + i)

    def zs(self):
        for k in (1, 2, 3):
            self.z_send(k).start()

    def oxy(self):
        self.x_send(0).start()
        self.y_send(0).start()

    def plane(self, *between):
        for k in (1, 2, 3):
            self.z_recv(k).wait_recv()
            if k == 1:
                for fn in between:
                    fn()
            self.x_send(k).start()
            self.y_send(k).start()

    def corner(self):
        for k in range(4):
            self.x_recv(k).wait_recv()
            if k < 2:
                self.q_send(k).start()
            self.y_recv(k).wait_recv()
            if k >= 2:
                self.q_send(k).start()
        self.p_send(0).start()

    def cross(self):
        for k in range(4):
            self.q_recv(k).wait_recv()
        self.p_send(1).start()

    def finish(self):
        self.p_recv(0).wait_recv()
        self.p_recv(1).wait_recv()

    def drain(self):
        for k in (1, 2, 3):
            self.z_send(k).wait_send()
        for k in range(4):
            self.x_send(k).wait_send()
            self.y_send(k).wait_send()
            self.q_send(k).wait_send()
        self.p_send(0).wait_send()
        self.p_send(1).wait_send()


class Reduce:
    def __init__(self, p, g, cols, held, r1, r2, r3, out, ss, rs):
        self.p, self.g, self.cols, self.held = p, g, cols, held
        self.r1, self.r2, self.r3, self.out, self.ss, self.rs = r1, r2, r3, out, ss, rs
        self.n = g.shape[0]

    def col(self, t):
        return pl.ds(pl.multiple_of(t * self.cols, 128), self.cols)

    def cp(self, src, dst, i, dev):
        return remote(src, dst, self.ss.at[i], self.rs.at[i], dev)

    def pair_copy(self, x):
        src = self.g.at[:, :, :, :, self.col(x * 2 + 1 - self.p.c)]
        return self.cp(src, self.held.at[x], x, self.p.pair)

    def corner_copy(self, i):
        p = self.p
        src = self.held.at[1 - p.x, :, pl.ds(2 * i, 2), 1 - p.y]
        return self.cp(src, self.r1.at[i], 2 + i, p.yn if i == 0 else p.xn)

    def plane_copy(self, i):
        p = self.p
        src = self.held.at[1 - p.x, :, :, p.y] if i == 0 else self.held.at[p.x, :, :, 1 - p.y]
        return self.cp(src, self.r2.at[i], 4 + i, p.xn if i == 0 else p.yn)

    def z_copy(self, k):
        p = self.p
        src = self.held.at[p.x, :, (p.z + k) % 4, p.y]
        return self.cp(src, self.r3.at[k - 1], 5 + k, p.zn[k])

    def start(self):
        self.pair_copy(0).start()
        self.pair_copy(1).start()

    def corner(self):
        for x in (0, 1):
            self.pair_copy(x).wait_recv()
        for x in (0, 1):
            col = self.col(x * 2 + self.p.c)

            def one(j, _, x=x, col=col):
                i, z = j // 4, j % 4
                a = self.g[i, z, :, :, col].astype(F32) + self.held[x, i, z].astype(F32)
                self.held[x, i, z] = a.astype(BF)
                return 0

            def whole(i, _, x=x, col=col):
                a = self.g[i, :, :, :, col].astype(F32) + self.held[x, i].astype(F32)
                self.held[x, i] = a.astype(BF)
                return 0

            if self.cols > 128:
                lax.fori_loop(0, self.n * 4, one, 0)
            else:
                lax.fori_loop(0, self.n, whole, 0)
        self.corner_copy(0).start()
        self.corner_copy(1).start()

    def plane(self):
        p = self.p
        self.corner_copy(0).wait_recv()
        self.corner_copy(1).wait_recv()
        for i in range(self.n):
            for j in range(2):
                a = self.held[1 - p.x, i, j, p.y].astype(F32) + self.r1[0, i, j].astype(F32)
                self.held[1 - p.x, i, j, p.y] = a.astype(BF)
                b = self.held[p.x, i, 2 + j, 1 - p.y].astype(F32) + self.r1[1, i, j].astype(F32)
                self.held[p.x, i, 2 + j, 1 - p.y] = b.astype(BF)
        self.plane_copy(0).start()
        self.plane_copy(1).start()

    def along(self):
        p = self.p
        self.plane_copy(0).wait_recv()
        self.plane_copy(1).wait_recv()
        for k in (1, 2, 3):
            zt = (p.z + k) % 4
            for i in range(self.n):
                a = (
                    self.held[p.x, i, zt, p.y].astype(F32)
                    + self.r2[0, i, zt].astype(F32)
                    + self.r2[1, i, zt].astype(F32)
                )
                self.held[p.x, i, zt, p.y] = a.astype(BF)
            self.z_copy(k).start()

    def finish(self):
        p = self.p
        for k in (1, 2, 3):
            self.z_copy(k).wait_recv()
        for i in range(self.n):
            a = (
                self.held[p.x, i, p.z, p.y].astype(F32)
                + self.r2[0, i, p.z].astype(F32)
                + self.r2[1, i, p.z].astype(F32)
            )
            for k in range(3):
                a = a + self.r3[k, i].astype(F32)
            self.out[i] = a

    def drain(self):
        for i in (0, 1):
            self.pair_copy(i).wait_send()
            self.corner_copy(i).wait_send()
            self.plane_copy(i).wait_send()
        for k in (1, 2, 3):
            self.z_copy(k).wait_send()


class Tail:
    def __init__(self, p, gt, hp, hx, hy, hz, hc, out, ss, rs):
        self.p, self.gt, self.hp, self.hx, self.hy, self.hz, self.hc = p, gt, hp, hx, hy, hz, hc
        self.out, self.ss, self.rs = out, ss, rs

    def cp(self, src, dst, i, dev):
        return remote(src, dst, self.ss.at[i], self.rs.at[i], dev)

    def pair_copy(self, j):
        return self.cp(self.gt.at[j], self.hp.at[j // 2], j, self.p.pair)

    def x_copy(self, j):
        if j == 1:
            return self.cp(self.gt.at[1, :, :, self.p.y], self.hx.at[:, :, 0], 4, self.p.xn)
        return self.cp(self.gt.at[0], self.hx, 4, self.p.xn)

    def corner_copy(self):
        return self.cp(self.gt.at[1, :, :, 1 - self.p.y], self.hc, 9, self.p.yn)

    def y_copy(self, j):
        return self.cp(self.gt.at[j, :, :, 1 - self.p.y], self.hy, 5, self.p.yn)

    def z_copy(self, j, k):
        p = self.p
        return self.cp(self.gt.at[j, :, (p.z + k) % 4, p.y], self.hz.at[k - 1], 5 + k, p.zn[k])

    def mine(self, j, fn):
        pl.when(self.p.c == j % 2)(fn)

    def start(self, j):
        pl.when(self.p.c != j % 2)(lambda: self.pair_copy(j).start())

    def sum_pair(self, j):
        def do():
            self.pair_copy(j).wait_recv()
            if j == 2:
                self.x_copy(0).wait_recv()
            for w in range(3):
                a = self.gt[j, w].astype(F32) + self.hp[j // 2, w].astype(F32)
                if j == 2:
                    a = a + self.hx[w].astype(F32)
                self.gt[j, w] = a.astype(BF)
            if j == 0:
                self.x_copy(0).start()
            elif j == 1:
                self.corner_copy().start()
            else:
                self.y_copy(j).start()

        self.mine(j, do)

    def corner(self):
        def do():
            self.corner_copy().wait_recv()
            y = self.p.y
            for w in range(3):
                a = self.gt[1, w, :, y].astype(F32) + self.hc[w].astype(F32)
                self.gt[1, w, :, y] = a.astype(BF)
            self.x_copy(1).start()

        self.mine(1, do)

    def sum_y(self, j):
        def do():
            p = self.p
            self.y_copy(j).wait_recv()
            if j == 3:
                self.x_copy(1).wait_recv()
            for i in range(3):
                for k in (1, 2, 3):
                    zt = (p.z + k) % 4
                    a = self.gt[j, i, zt, p.y].astype(F32) + self.hy[i, zt].astype(F32)
                    if j == 3:
                        a = a + self.hx[i, zt, 0].astype(F32)
                    self.gt[j, i, zt, p.y] = a.astype(BF)
            for k in (1, 2, 3):
                self.z_copy(j, k).start()

        self.mine(j, do)

    def finish(self, j):
        def do():
            p = self.p
            for k in (1, 2, 3):
                self.z_copy(j, k).wait_recv()
            for i in range(3):
                a = self.gt[j, i, p.z, p.y].astype(F32) + self.hy[i, p.z].astype(F32)
                if j == 3:
                    a = a + self.hx[i, p.z, 0].astype(F32)
                for k in range(3):
                    a = a + self.hz[k, i].astype(F32)
                self.out[i] = a

        self.mine(j, do)

    def drain(self):
        for j in range(4):
            pl.when(self.p.c != j % 2)(lambda j=j: self.pair_copy(j).wait_send())

        def sent(j):
            self.x_copy(j).wait_send()
            if j == 1:
                self.corner_copy().wait_send()
            self.y_copy(j + 2).wait_send()
            for k in (1, 2, 3):
                self.z_copy(j + 2, k).wait_send()

        for j in (0, 1):
            self.mine(j, lambda j=j: sent(j))


def row_steps(count, one):
    def body(i, _):
        one(pl.ds(pl.multiple_of(i * CH, CH), CH))
        return 0

    lax.fori_loop(0, count // CH, body, 0)


def head_half(shape, axis, h):
    return (lax.broadcasted_iota(jnp.int32, shape, axis) // HEAD) == h


def keep_half(value, axis, h):
    return jnp.where(head_half(value.shape, axis, h), value.astype(F32), 0.0).astype(BF)


def run_hooks(hooks, step, half):
    for (at, part), hook in hooks.items():
        if part == half:
            pl.when(step == at)(hook)


def attend(qt, k, vt, bias, ot, lse, temp, hooks):
    def ready(p, h):
        lanes = pl.ds(pl.multiple_of(p * 128, 128), 128)
        return k[:, lanes], keep_half(qt[lanes, :], 0, h)

    def score(kp, qm, h, i, top):
        s = nn(kp[i * 512 : i * 512 + 512], qm) * SCALE
        if bias is not None:
            s = s + bias[i * 512 : i * 512 + 512, :]
        temp[h * 1024 + i * 512 : h * 1024 + i * 512 + 512, :] = s
        m = jnp.max(s, axis=0, keepdims=True)
        return m if top is None else jnp.maximum(top, m)

    def mix(vh, h, i, top, total, mixed):
        e = jnp.exp2(temp[h * 1024 + i * 512 : h * 1024 + i * 512 + 512, :] - top)
        part = jnp.sum(e, axis=0, keepdims=True)
        o = nn(vh[:, i * 512 : i * 512 + 512], e.astype(BF))
        return (part, o) if total is None else (total + part, mixed + o)

    def pair(p, top):
        for h in (0, 1):
            kp, qm = ready(p if h == 0 else (p + 1) % 4, 1 - h)
            vh = vt[pl.ds(pl.multiple_of(p * 128 + h * 64, 64), 64), :]
            total = mixed = later = None
            for i in range(2):
                later = score(kp, qm, 1 - h, i, later)
                total, mixed = mix(vh, h, i, top, total, mixed)
            ot[pl.ds(pl.multiple_of(p * 128 + h * 64, 64), 64), :] = mixed * (1.0 / total)
            lse[pl.ds(p * 2 + h, 1), :] = top + jnp.log2(total)
            top = later
            run_hooks(hooks, p, h)
        return top

    kp, qm = ready(0, 0)
    top = None
    for i in range(2):
        top = score(kp, qm, 0, i, top)
    lax.fori_loop(0, 4, pair, top)


def attend_back(q, qt, k, kt, v, do, dot_, ot, bias, lse, dqt, dk_own, dv_own, dkv_send, order, hooks):
    def pair(step, _):
        p = order(step)
        lanes = pl.ds(pl.multiple_of(p * 128, 128), 128)
        kp, vp = k[:, lanes], v[:, lanes]
        qp, dop = qt[lanes, :], dot_[lanes, :]
        inner = dop.astype(F32) * ot[lanes, :]
        qms = [keep_half(qp, 0, h) for h in (0, 1)]
        doms = [keep_half(dop, 0, h) for h in (0, 1)]
        qr = jnp.concatenate([keep_half(q[:, lanes], 1, h) for h in (0, 1)], axis=0)
        dor = jnp.concatenate([keep_half(do[:, lanes], 1, h) for h in (0, 1)], axis=0)
        ds_sum = [jnp.sum(inner[h * 64 : h * 64 + 64], axis=0, keepdims=True) for h in (0, 1)]
        logs = [lse[pl.ds(p * 2 + h, 1), :] for h in (0, 1)]
        shares, grads = {}, {}
        dq = [None, None]
        dvs, dks = {}, {}

        def one(h, i):
            rows = slice(i * 256, i * 256 + 256)
            s = nn(kp[rows], qms[h]) * SCALE
            if bias is not None:
                s = s + bias[rows, :]
            e = jnp.exp2(s - logs[h])
            dp = nn(vp[rows], doms[h])
            shares[h, i] = e.astype(BF)
            grads[h, i] = (e * (dp - ds_sum[h])).astype(BF)

        def two(h, i):
            rows = slice(i * 256, i * 256 + 256)
            kh = kt[pl.ds(pl.multiple_of(p * 128 + h * 64, 64), 64), rows]
            part = nn(kh, grads[h, i])
            dq[h] = part if dq[h] is None else dq[h] + part
            dv = nn(shares[h, i], dor[h * 512 : h * 512 + 512])
            dk = nn(grads[h, i], qr[h * 512 : h * 512 + 512])
            dvs[i] = dv if i not in dvs else dvs[i] + dv
            dks[i] = dk if i not in dks else dks[i] + dk

        def out(i):
            rows = slice(i * 256, i * 256 + 256)
            if i < 2:
                dk_own[rows, lanes] = (dks[i] * 0.125).astype(dk_own.dtype)
                dv_own[rows, lanes] = dvs[i].astype(dv_own.dtype)
            else:
                back = slice(i * 256 - 512, i * 256 - 256)
                dkv_send[0, back, lanes] = (dks[i] * 0.125).astype(BF)
                dkv_send[1, back, lanes] = dvs[i].astype(BF)

        for i in range(4):
            one(0, i)
        for i in range(4):
            one(1, i)
            two(0, i)
        run_hooks(hooks, step, 0)
        for i in range(4):
            two(1, i)
            out(i)
        for h in (0, 1):
            dqt[pl.ds(pl.multiple_of(p * 128 + h * 64, 64), 64), :] = (dq[h] * 0.125).astype(BF)
        run_hooks(hooks, step, 1)
        return 0

    lax.fori_loop(0, 4, pair, 0)


def norm_rows(z):
    mean = jnp.mean(z, axis=-1, keepdims=True)
    centred = z - mean
    r = lax.rsqrt(jnp.mean(centred * centred, axis=-1, keepdims=True) + norm_eps)
    return centred * r, r


def norm_back_rows(e, n, r, gain):
    s = e * gain
    a = jnp.mean(s, axis=-1, keepdims=True)
    b = jnp.mean(s * n, axis=-1, keepdims=True)
    return r * (s - a - n * b)


def fast_kernel(
    x_i, enc_i, og_i, valid, seg, rank,
    sq, sk, sv, so, cq, ck, cv, co, up, down,
    g1, b1, g2, b2, g3, b3,
    y_o, dx_o, eg_o, ga_o, gb_o, gf_o, ns_o, vs_o,
    xs, enc, og, codes, wa, wb, wf, gt,
    q1, qt1, k1, v1, vt1, o1, ot1, l1,
    q2, qt2, k2, v2, vt2, o2, ot2, l2,
    bias, n1, n2, h1b, h2b, u, gp, dg, dz, low, lowt, do, dot_,
    kvs, kvr1, kvr2, tt, yb, row, st,
    hc, hq, hu, hd, c1, c2, c3, p1, p2, p3, u1, u2, u3, d1, d2, d3, hp, hx, hy, hz, hcn,
    st_r, gss, grs, rss, rrs, aas, ars, ess, ers, tss, trs, ls,
):
    dqt, dq = h2b, q2
    x = xs.at[pl.ds(0, 512)]
    dkv = [v2.at[pl.ds(0, 512)], v2.at[pl.ds(512, 512)]]
    p = Place()
    loads = []
    for i, (src, w, j, cols) in enumerate(
        (
            (sq, wa, 0, 128), (sk, wa, 1, 128), (sv, wa, 2, 128),
            (so, wb, 0, 128), (co, wb, 1, 128), (cq, wb, 2, 128), (ck, wb, 3, 128), (cv, wb, 4, 128),
            (up, wf, 0, 512), (down, wf, 1, 512),
        )
    ):
        col = pl.ds(pl.multiple_of(p.t * cols, 128), cols)
        loads.append(pltpu.make_async_copy(src, w.at[j, p.z, p.y, :, col], ls.at[i]))
    for i, (src, dst) in enumerate(((x_i, x), (enc_i, enc), (og_i, og))):
        loads.append(pltpu.make_async_copy(src, dst, ls.at[10 + i]))
    for cp in loads:
        cp.start()
    p.barrier()
    GA, GB, GU, GD = G = [
        Gather(p, w, cols, gss.at[i], grs.at[i])
        for i, (w, cols) in enumerate(
            ((wa, 128), (wb, 128), (wf.at[pl.ds(0, 1)], 512), (wf.at[pl.ds(1, 1)], 512))
        )
    ]
    for cp in loads[:3]:
        cp.wait()
    GA.zs()
    GA.oxy()
    for cp in loads[3:]:
        cp.wait()
    halves = remote(
        xs.at[pl.ds(0, 512)], xs.at[pl.ds(512, 512)], ess.at[9], ers.at[9], p.pair
    )
    halves.start()
    GB.oxy()

    def mat(w, j):
        return w[j].reshape(512, w.shape[4])

    st[...] = jnp.zeros_like(st)
    row[...] = jnp.broadcast_to(valid[...].astype(F32), (128, 512)).T
    own = pl.ds(pl.multiple_of(p.c * 512, 128), 512)
    other = pl.ds(pl.multiple_of((1 - p.c) * 512, 128), 512)
    sx = pl.ds(p.x, 1)
    ranks = rank[sx, :]
    codes[1:2, :] = seg[sx, :] * 8
    codes[0:1, :] = seg[sx, :] * 8 + jnp.concatenate(
        [jnp.broadcast_to(ranks[:, b : b + 1], (1, 128)) for b in range(8)], axis=1
    )
    base, high = codes[1:2, own], codes[0:1, own]
    for i, half in enumerate((own, other)):
        code = jnp.broadcast_to(codes[0:1, half], (128, 512)).T
        for j in range(4):
            c = code[j * 128 : j * 128 + 128, :1]
            ok = (c >= base) & (c <= high)
            bias[i * 512 + j * 128 : i * 512 + j * 128 + 128, :] = jnp.where(ok, 0.0, -2.0e9)

    GA.plane(GB.zs)
    GU.oxy()
    GA.corner()
    GU.zs()
    GD.oxy()
    GA.cross()
    GB.plane()
    GA.finish()
    GD.zs()

    def swap(buf, i):
        return remote(buf.at[pl.ds(0, 512)], buf.at[pl.ds(512, 512)], ess.at[i], ers.at[i], p.pair)

    halves.wait()
    xv = xs[...]
    k1[...] = nn(xv, mat(wa, 1)).astype(BF)
    vv = nn(xv, mat(wa, 2)).astype(BF)
    v1[...] = vv
    vt1[...] = turn(vv)
    xv = x[...]
    qv = nn(xv, mat(wa, 0)).astype(BF)
    q1[...] = qv
    qt1[...] = turn(qv)
    attend(qt1, k1, vt1, bias, ot1, l1, gp, {(0, 0): GB.corner, (1, 0): GU.plane, (2, 0): GB.cross, (3, 0): GD.plane})
    o1[...] = turn(ot1[...].astype(BF))
    GB.finish()
    ev = enc[...]
    k2[0:512, :] = nn(ev, mat(wb, 3)).astype(BF)
    v2[0:512, :] = nn(ev, mat(wb, 4)).astype(BF)
    swap(k2, 2).start()
    swap(v2, 3).start()
    yb[...] = nt(o1[...], mat(wb, 0))
    GU.corner()

    def first(r):
        n, s = norm_rows(x[r, :].astype(F32) + yb[r, :])
        n1[r, :] = n
        row[r, 0:1] = s
        h1b[r, :] = (n * g1[...] + b1[...]).astype(BF)

    row_steps(512, first)
    qv = nn(h1b[...], mat(wb, 2)).astype(BF)
    q2[...] = qv
    qt2[...] = turn(qv)
    swap(k2, 2).wait_recv()
    swap(v2, 3).wait_recv()
    vt2[...] = turn(v2[...])
    attend(qt2, k2, vt2, None, ot2, l2, gp, {(0, 1): GD.corner, (2, 1): GU.cross})
    o2[...] = turn(ot2[...].astype(BF))
    yb[...] = nt(o2[...], mat(wb, 1))

    def second(r):
        n, s = norm_rows(n1[r, :] * g1[...] + b1[...] + yb[r, :])
        n2[r, :] = n
        row[r, 1:2] = s
        h2b[r, :] = (n * g2[...] + b2[...]).astype(BF)

    row_steps(512, second)
    hv = h2b[...]
    blocks = [p.t, p.pair[1], p.xt, (1 - p.x) * 2 + 1 - p.c]
    waits = [None, GU.p_recv(0).wait_recv, GD.cross, GU.p_recv(1).wait_recv]
    for t, wait in zip(blocks, waits):
        if wait is not None:
            wait()
        cols = pl.ds(pl.multiple_of(t * 512, 512), 512)
        gp[cols, :] = nn(hv, wf[0, :, :, :, cols].reshape(512, 512))

        def gelu(r, cols=cols, t=t):
            at = pl.ds(pl.multiple_of(r.start + t * 512, CH), CH)
            v = gp[at, :]
            cdf = 0.5 * (1.0 + lax.erf(v * 0.7071067811865476))
            u[r, cols] = (v * cdf).astype(BF)
            gp[at, :] = cdf + v * (jnp.exp2(v * v * (-0.5 * LOG2E)) * 0.3989422804014327)

        row_steps(512, gelu)
    waits = [None, GD.p_recv(0).wait_recv, None, GD.p_recv(1).wait_recv]
    for i, (t, wait) in enumerate(zip(blocks, waits)):
        if wait is not None:
            wait()
        cols = pl.ds(pl.multiple_of(t * 512, 512), 512)
        part = nt(u[:, cols], wf[1, :, :, :, cols].reshape(512, 512))
        yb[...] = part if i == 0 else yb[...] + part

    def third(r):
        n, s = norm_rows(n2[r, :] * g2[...] + b2[...] + yb[r, :])
        out = n * g3[...] + b3[...]
        vc = row[r, 2:3]
        yb[r, :] = out
        e = og[r, :].astype(F32) * vc
        st[4:5, :] += jnp.sum(e * n, axis=0, keepdims=True)
        st[5:6, :] += jnp.sum(e, axis=0, keepdims=True)
        st[6:7, :] += jnp.sum(vc * out * out, axis=0, keepdims=True)
        back = norm_back_rows(e, n, s, g3[...])
        dz[r, :] = back
        low[r, :] = back.astype(BF)

    row_steps(512, third)
    y_copy = pltpu.make_async_copy(yb, y_o, ls.at[0])
    y_copy.start()
    lv = low[...]
    lowt[...] = turn(lv)
    for j in range(4):
        cols = slice(j * 512, j * 512 + 512)
        dg[:, cols] = (nn(lv, wf[1, :, :, :, cols].reshape(512, 512)) * gp[cols, :]).astype(BF)
    for g in G:
        g.drain()
    RC, RP, RU, RD = R = [
        Reduce(p, w.at[pl.ds(at, n)], cols, *bufs, out.at[pl.ds(at, n)], rss.at[i], rrs.at[i])
        for i, (w, at, n, cols, bufs, out) in enumerate(
            (
                (wb, 0, 2, 128, (hc, c1, c2, c3), gb_o),
                (wb, 2, 3, 128, (hq, p1, p2, p3), gb_o),
                (wf, 0, 1, 512, (hu, u1, u2, u3), gf_o),
                (wf, 1, 1, 512, (hd, d1, d2, d3), gf_o),
            )
        )
    ]
    for j in range(4):
        cols = slice(j * 512, j * 512 + 512)
        wf[1, :, :, :, cols] = nn(lowt[...], u[:, cols]).astype(BF).reshape(4, 2, 64, 512)
    RD.start()
    dz[...] += nt(dg[...], mat(wf, 0))
    tt[...] = turn(h2b[...])
    for j in range(4):
        cols = slice(j * 512, j * 512 + 512)
        wf[0, :, :, :, cols] = nn(tt[...], dg[:, cols]).astype(BF).reshape(4, 2, 64, 512)
    RU.start()
    RD.corner()

    def back2(r):
        e = dz[r, :]
        n = n2[r, :]
        st[2:3, :] += jnp.sum(e * n, axis=0, keepdims=True)
        st[3:4, :] += jnp.sum(e, axis=0, keepdims=True)
        back = norm_back_rows(e, n, row[r, 1:2], g2[...])
        dz[r, :] = back
        low[r, :] = back.astype(BF)

    row_steps(512, back2)
    dov = nn(low[...], mat(wb, 1)).astype(BF)
    do[...] = dov
    dot_[...] = turn(dov)
    lowt[...] = turn(low[...])
    wb[1] = nn(lowt[...], o2[...]).astype(BF).reshape(4, 2, 64, 512)
    vt2[...] = turn(k2[...])
    RU.corner()
    attend_back(
        q2, qt2, k2, vt2, v2, do, dot_, ot2, None, l2, dqt,
        gp.at[pl.ds(0, 512)], gp.at[pl.ds(512, 512)], kvs.at[:, pl.ds(512, 512)], lambda step: step,
        {(0, 0): RD.plane, (1, 0): RU.plane, (3, 0): RD.along},
    )

    def swap_back(buf, i):
        return remote(kvs.at[:, pl.ds(512, 512)], buf, ess.at[i], ers.at[i], p.pair)

    swap_back(kvr2, 4).start()
    dqv = turn(dqt[...])
    dz[...] += nt(dqv, mat(wb, 2))
    tt[...] = turn(h1b[...])
    wb[2] = nn(tt[...], dqv).astype(BF).reshape(4, 2, 64, 512)
    tt[...] = turn(enc[...])
    swap_back(kvr2, 4).wait()
    for i in (2, 3):
        swap((k1, v1, k2, v2)[i], i).wait_send()

    def join(recv, at):
        def one(r):
            for i in (0, 1):
                own_rows = pl.ds(pl.multiple_of(r.start + at + i * 512, CH), CH)
                dkv[i][r, :] = (gp[own_rows, :] + recv[i, r, :].astype(F32)).astype(BF)

        row_steps(512, one)

    join(kvr2, 0)
    y_copy.wait()
    yb[...] = nt(dkv[0][...], mat(wb, 3)) + nt(dkv[1][...], mat(wb, 4))
    e_copy = pltpu.make_async_copy(yb, eg_o, ls.at[0])
    e_copy.start()
    wb[3] = nn(tt[...], dkv[0][...]).astype(BF).reshape(4, 2, 64, 512)
    wb[4] = nn(tt[...], dkv[1][...]).astype(BF).reshape(4, 2, 64, 512)
    RP.start()

    def back1(r):
        e = dz[r, :]
        n = n1[r, :]
        st[0:1, :] += jnp.sum(e * n, axis=0, keepdims=True)
        st[1:2, :] += jnp.sum(e, axis=0, keepdims=True)
        back = norm_back_rows(e, n, row[r, 0:1], g1[...])
        dz[r, :] = back
        low[r, :] = back.astype(BF)

    row_steps(512, back1)
    RU.along()
    dov = nn(low[...], mat(wb, 0)).astype(BF)
    do[...] = dov
    dot_[...] = turn(dov)
    lowt[...] = turn(low[...])
    wb[0] = nn(lowt[...], o1[...]).astype(BF).reshape(4, 2, 64, 512)
    RC.start()
    RP.corner()
    vt1[...] = turn(k1[...])
    vt2[...] = turn(xs[...])
    T = Tail(p, gt, hp, hx, hy, hz, hcn, ga_o, aas, ars)

    def order(step):
        far = (step // 2) * p.x + (1 - step // 2) * (1 - p.x)
        return 2 * far + step % 2

    def lanes_of(step):
        return pl.ds(pl.multiple_of(order(step) * 128, 128), 128)

    def part_back(step):
        at = lanes_of(step)
        return remote(
            kvs.at[:, pl.ds(512, 512), at], kvr1.at[:, :, at], ess.at[5 + step], ers.at[5 + step], p.pair
        )

    def grads(step):
        at = lanes_of(step)
        dqv = turn(dqt[at, :])
        dq[:, at] = dqv
        gt[step, 0] = nn(vt2[:, 0:512], dqv).astype(BF).reshape(4, 2, 64, 128)
        gt[step, 1] = nn(vt2[...], kvs[0, :, at]).astype(BF).reshape(4, 2, 64, 128)
        gt[step, 2] = nn(vt2[...], kvs[1, :, at]).astype(BF).reshape(4, 2, 64, 128)
        T.start(step)

    def both(*fns):
        def run():
            for fn in fns:
                fn()

        return run

    attend_back(
        q1, qt1, k1, vt1, v1, do, dot_, ot1, bias, l1, dqt,
        kvs.at[0, pl.ds(0, 512)], kvs.at[1, pl.ds(0, 512)], kvs.at[:, pl.ds(512, 512)], order,
        {
            (0, 0): RC.corner,
            (0, 1): both(lambda: part_back(0).start(), lambda: grads(0), RP.plane),
            (1, 0): lambda: T.sum_pair(0),
            (1, 1): both(lambda: part_back(1).start(), lambda: grads(1), RC.plane, RD.finish),
            (2, 0): lambda: T.sum_pair(1),
            (2, 1): both(lambda: part_back(2).start(), lambda: grads(2), RP.along, RU.finish),
            (3, 0): lambda: T.sum_pair(2),
            (3, 1): both(lambda: part_back(3).start(), T.corner, RC.along),
        },
    )
    grads(3)
    T.sum_y(2)
    dz[...] += nt(dq[...], mat(wa, 0))
    for step in range(4):
        part_back(step).wait_recv()

    def join_last(r):
        for i in (0, 1):
            dkv[i][r, :] = (kvs[i, r, :].astype(F32) + kvr1[i, r, :].astype(F32)).astype(BF)

    row_steps(512, join_last)
    T.sum_pair(3)
    dz[...] += nt(dkv[0][...], mat(wa, 1)) + nt(dkv[1][...], mat(wa, 2))
    x_copy = pltpu.make_async_copy(dz, dx_o, ls.at[1])
    x_copy.start()

    def squares(r):
        st[7:8, :] += jnp.sum(row[r, 2:3] * dz[r, :] * dz[r, :], axis=0, keepdims=True)

    row_steps(512, squares)

    stats = []
    st_r[0] = st[...]
    for i in range(1, 8):
        stats.append(remote(st, st_r.at[i], tss.at[i], trs.at[i], p.plane_peer(i)))
    for cp in stats:
        cp.start()
    T.sum_y(3)
    for cp in stats:
        cp.wait()
    total = None
    for i in range(8):
        x, y, c = (p.x + i // 4) % 2, (p.y + i // 2) % 2, (p.c + i) % 2
        part = st_r[x * 4 + y * 2 + c]
        total = part if total is None else total + part
    st_r[8 + p.z] = total
    stats = []
    for k in (1, 2, 3):
        at = st_r.at[8 + p.z]
        stats.append((remote(at, at, tss.at[7 + k], trs.at[7 + k], p.zn[k]), k))
    for cp, _ in stats:
        cp.start()
    RP.finish()
    RC.finish()
    T.finish(2)
    for cp, k in stats:
        cp.wait_send()
        back = st_r.at[8 + (p.z - k + 4) % 4]
        remote(back, back, tss.at[7 + k], trs.at[7 + k], p.zn[k]).wait_recv()
    T.finish(3)
    total = st_r[8] + st_r[9] + st_r[10] + st_r[11]
    ns_o[...] = total[0:6]
    vs_o[...] = jnp.sqrt(total[6:8] * (1.0 / 16384.0))
    for step in range(4):
        part_back(step).wait_send()
    for r in R:
        r.drain()
    T.drain()
    e_copy.wait()
    x_copy.wait()


def place_kernel(*refs):
    srcs, outs, held, sems = refs[:8], refs[8:23], refs[23:31], refs[31]
    parts = [held[0], held[1], held[2]] + [held[3].at[i] for i in range(3)]
    parts += [held[4].at[i] for i in range(5)] + [held[5].at[i] for i in range(2)] + [held[6], held[7]]
    first = [pltpu.make_async_copy(a, b, sems.at[i]) for i, (a, b) in enumerate(zip(srcs, held))]
    last = [pltpu.make_async_copy(a, b, sems.at[8 + i]) for i, (a, b) in enumerate(zip(parts, outs))]
    ends = [(0, 1), (1, 2), (2, 3), (3, 6), (6, 11), (11, 13), (13, 14), (14, 15)]
    order = (6, 7, 3, 4, 5, 0, 1, 2)
    for i in order:
        first[i].start()
    for i in order:
        first[i].wait()
        for cp in last[ends[i][0] : ends[i][1]]:
            cp.start()
    for cp in last:
        cp.wait()


def fast_shards(
    tokens, encoder_states, output_grad, valid_mask, segment_ids, context_ranks,
    self_query, self_key, self_value, self_output,
    cross_query, cross_key, cross_value, cross_output, hidden_up, hidden_down,
    norm1_gain, norm1_bias, norm2_gain, norm2_bias, norm3_gain, norm3_bias,
):
    vm = pl.BlockSpec(memory_space=pltpu.VMEM)
    hbm = pl.BlockSpec(memory_space=pl.ANY)
    rows = [
        v.reshape(1, 512)
        for v in (norm1_gain, norm1_bias, norm2_gain, norm2_bias, norm3_gain, norm3_bias)
    ]

    def V(*shape, dtype=BF):
        return pltpu.VMEM(shape, dtype)

    def S(*shape):
        return pltpu.SemaphoreType.DMA(shape)

    def group(n, cols):
        return [
            V(2, n, 4, 2, 64, cols),
            [V(2, n, 2, 64, cols), V(2, n, 4, 64, cols), V(3, n, 64, cols)],
        ]

    rc, rp, ru, rd = group(2, 128), group(3, 128), group(1, 512), group(1, 512)

    def attention():
        return [
            V(512, 512), V(512, 512), V(1024, 512), V(1024, 512), V(512, 1024), V(512, 512),
            V(512, 512, dtype=F32), V(8, 512, dtype=F32),
        ]

    scratch = (
        [V(1024, 512), V(512, 512), V(512, 512)]
        + [V(8, 1024, dtype=jnp.int32)]
        + [V(3, 4, 2, 64, 512), V(5, 4, 2, 64, 512), V(2, 4, 2, 64, 2048), V(4, 3, 4, 2, 64, 128)]
        + attention()
        + attention()
        + [V(1024, 512, dtype=F32), V(512, 512, dtype=F32), V(512, 512, dtype=F32)]
        + [V(512, 512), V(512, 512)]
        + [V(512, 2048), V(2048, 512, dtype=F32), V(512, 2048), V(512, 512, dtype=F32)]
        + [V(512, 512)] * 4
        + [V(2, 1024, 512), V(2, 512, 512), V(2, 512, 512)]
        + [V(512, 512), V(512, 512, dtype=F32), V(512, 128, dtype=F32), V(8, 512, dtype=F32)]
        + [rc[0], rp[0], ru[0], rd[0]]
        + rc[1] + rp[1] + ru[1] + rd[1]
        + [V(2, 3, 4, 2, 64, 128), V(3, 4, 2, 64, 128), V(3, 4, 64, 128), V(3, 3, 64, 128), V(3, 4, 64, 128)]
        + [V(12, 8, 512, dtype=F32)]
        + [S(4, 19), S(4, 19), S(4, 9), S(4, 9), S(10), S(10), S(10), S(10), S(11), S(11), S(13)]
    )
    big = jax.ShapeDtypeStruct((512, 512), F32)
    outs = pl.pallas_call(
        fast_kernel,
        out_shape=[big, big, big]
        + [jax.ShapeDtypeStruct(s, F32) for s in ((3, 64, 128), (5, 64, 128), (2, 64, 512), (6, 512), (2, 512))],
        in_specs=[hbm] * 3 + [vm] * 3 + [hbm] * 10 + [vm] * 6,
        out_specs=[hbm] * 3 + [vm] * 5,
        scratch_shapes=scratch,
        compiler_params=pltpu.CompilerParams(
            collective_id=0, has_side_effects=True, vmem_limit_bytes=63 << 20
        ),
        name="layer",
    )(
        tokens, encoder_states, output_grad, valid_mask.reshape(1, 512), segment_ids, context_ranks,
        self_query, self_key, self_value, self_output.T,
        cross_query, cross_key, cross_value, cross_output.T, hidden_up, hidden_down.T, *rows,
    )
    ends = [big, big, big] + [jax.ShapeDtypeStruct((64, 128), F32)] * 8
    ends += [jax.ShapeDtypeStruct((64, 512), F32)] * 2
    ends += [jax.ShapeDtypeStruct(v, F32) for v in ((6, 512), (2, 512))]
    y, dx, eg, dsq, dsk, dsv, dso, dco, dcq, dck, dcv, dup, ddown, ns, vs = pl.pallas_call(
        place_kernel,
        out_shape=ends,
        in_specs=[hbm] * 8,
        out_specs=[hbm] * 15,
        scratch_shapes=[pltpu.VMEM(o.shape, F32) for o in outs] + [S(23)],
        name="place",
    )(*outs)
    return (
        y, dx, eg, dsq, dsk, dsv, dso.T, dcq, dck, dcv, dco.T, dup, ddown.T, ns, vs,
    )


def solution(mesh):
    in_specs = (
        P(("dp", "tensor"), None),
        P(("dp", "tensor"), None),
        P(("dp", "tensor"), None),
        P(("dp", "tensor")),
        P("dp", None),
        P("dp", None),
        P("dp", "tensor"),
        P("dp", "tensor"),
        P("dp", "tensor"),
        P("tensor", "dp"),
        P("dp", "tensor"),
        P("dp", "tensor"),
        P("dp", "tensor"),
        P("tensor", "dp"),
        P("dp", "tensor"),
        P("tensor", "dp"),
        P(),
        P(),
        P(),
        P(),
        P(),
        P(),
    )
    out_specs = (
        P(("dp", "tensor"), None),
        P(("dp", "tensor"), None),
        P(("dp", "tensor"), None),
        P("dp", "tensor"),
        P("dp", "tensor"),
        P("dp", "tensor"),
        P("tensor", "dp"),
        P("dp", "tensor"),
        P("dp", "tensor"),
        P("dp", "tensor"),
        P("tensor", "dp"),
        P("dp", "tensor"),
        P("tensor", "dp"),
        P(),
        P(),
    )
    body = fast_shards if dict(mesh.shape) == {"dp": 8, "tensor": 4} else shards
    return jax.shard_map(body, mesh=mesh, in_specs=in_specs, out_specs=out_specs, check_vma=False)
```

```python
import jax
import jax.numpy as jnp
from jax import lax
from jax.experimental import pallas as pl
from jax.experimental.pallas import tpu as pltpu
from jax.sharding import PartitionSpec as P

HEAD = 64
LEN = 1024
BLK = 128


norm_eps = 1e-05
mask_fill = -1000000000.0


def gelu_exact(value):
    return jax.nn.gelu(value, approximate=False)


def gelu_back(preact, upstream):
    return jax.vjp(gelu_exact, preact)[1](upstream)[0]


def layer_norm(value, gain, bias):
    mean = jnp.mean(value, axis=-1, keepdims=True)
    centred = value - mean
    scale = lax.rsqrt(jnp.mean(centred * centred, axis=-1, keepdims=True) + norm_eps)
    normal = centred * scale
    return (normal * gain + bias, normal, scale)


def norm_back(upstream, normal, scale, gain):
    scaled = upstream * gain
    mean_grad = jnp.mean(scaled, axis=-1, keepdims=True)
    mean_cross = jnp.mean(scaled * normal, axis=-1, keepdims=True)
    inward = scale * (scaled - mean_grad - normal * mean_cross)
    return (inward, jnp.sum(upstream * normal, axis=0), jnp.sum(upstream, axis=0))


def context_allowed(segments, ranks, first, count):
    length = segments.shape[0]
    key_block = jnp.arange(length, dtype=jnp.int32) // BLK
    key_rank = jnp.broadcast_to(ranks[:, None], (ranks.shape[0], BLK)).reshape(length)
    query_segment = lax.dynamic_slice_in_dim(segments, first, count)
    query_rank = lax.dynamic_slice_in_dim(key_rank, first, count)
    query_block = (first + jnp.arange(count, dtype=jnp.int32)) // BLK
    same_doc = query_segment[:, None] == segments[None, :]
    earlier = key_rank[None, :] < query_rank[:, None]
    same_block = query_block[:, None] == key_block[None, :]
    return same_doc & (earlier | same_block)


def full_rows(value):
    return lax.all_gather(value, "tensor", axis=0, tiled=True)


def grad_rows(value):
    return lax.all_gather(value, "tensor", axis=0, tiled=True)


def branch_sum(mixed, weight):
    return lax.psum_scatter(
        jnp.dot(mixed, weight, preferred_element_type=jnp.float32),
        "tensor",
        scatter_dimension=0,
        tiled=True,
    )


def back_product(left, weight):
    return lax.dot_general(
        left, weight, (((1,), (1,)), ((), ())), preferred_element_type=jnp.float32
    )


def row_product(left, right):
    return lax.dot_general(
        left, right, (((0,), (0,)), ((), ())), preferred_element_type=jnp.float32
    )


def input_sum(pairs):
    total = None
    for left, weight in pairs:
        portion = back_product(left, weight)
        total = portion if total is None else total + portion
    return lax.psum_scatter(total, "tensor", scatter_dimension=0, tiled=True)


def split_heads(value, count):
    return value.reshape(count, LEN, value.shape[1] // HEAD, HEAD)


def attend_sequence(query, keys, values, segments, ranks, masked):
    length = query.shape[0]
    width = min(length, 512)

    def one_block(index):
        first = index * width
        piece = lax.dynamic_slice_in_dim(query, first, width, 0)
        scores = jnp.einsum("qhd,khd->hqk", piece, keys, preferred_element_type=jnp.float32) * 0.125
        if masked:
            scores = jnp.where(
                context_allowed(segments, ranks, first, width)[None], scores, mask_fill
            )
        top = jnp.max(scores, axis=-1, keepdims=True)
        raised = jnp.exp(scores - top)
        total = jnp.sum(raised, axis=-1, keepdims=True)
        shares = (raised / total).astype(jnp.bfloat16)
        mixed = jnp.einsum("hqk,khd->qhd", shares, values, preferred_element_type=jnp.float32)
        return (mixed.astype(jnp.bfloat16), (top + jnp.log(total))[..., 0])

    mixed, log_total = lax.map(one_block, jnp.arange(length // width, dtype=jnp.int32))
    return (mixed.reshape(query.shape), log_total)


def attend_sequence_back(query, keys, values, segments, ranks, masked, log_total, grad_mixed):
    length = query.shape[0]
    width = min(length, 512)

    def one_block(carry, index):
        key_sum, value_sum = carry
        first = index * width
        piece = lax.dynamic_slice_in_dim(query, first, width, 0)
        grad_piece = lax.dynamic_slice_in_dim(grad_mixed, first, width, 0)
        scores = jnp.einsum("qhd,khd->hqk", piece, keys, preferred_element_type=jnp.float32) * 0.125
        if masked:
            scores = jnp.where(
                context_allowed(segments, ranks, first, width)[None], scores, mask_fill
            )
        shares = jnp.exp(scores - log_total[index][..., None])
        grad_shares = jnp.einsum(
            "qhd,khd->hqk", grad_piece, values, preferred_element_type=jnp.float32
        )
        inner = jnp.sum(shares * grad_shares, axis=-1, keepdims=True)
        grad_scores = (shares * (grad_shares - inner)).astype(jnp.bfloat16)
        grad_query = (
            jnp.einsum("hqk,khd->qhd", grad_scores, keys, preferred_element_type=jnp.float32)
            * 0.125
        )
        key_sum = (
            key_sum
            + jnp.einsum("hqk,qhd->khd", grad_scores, piece, preferred_element_type=jnp.float32)
            * 0.125
        )
        value_sum = value_sum + jnp.einsum(
            "hqk,qhd->khd",
            shares.astype(jnp.bfloat16),
            grad_piece,
            preferred_element_type=jnp.float32,
        )
        return ((key_sum, value_sum), grad_query.astype(jnp.bfloat16))

    zeros = jnp.zeros(keys.shape, jnp.float32)
    (key_sum, value_sum), grad_query = lax.scan(
        one_block, (zeros, zeros), jnp.arange(length // width, dtype=jnp.int32)
    )
    return (
        grad_query.reshape(query.shape),
        key_sum.astype(jnp.bfloat16),
        value_sum.astype(jnp.bfloat16),
    )


def attend_all(query, keys, values, segments, ranks, masked):
    count = query.shape[0] // LEN

    def one_sequence(items):
        return attend_sequence(items[0], items[1], items[2], items[3], items[4], masked)

    mixed, log_total = lax.map(
        one_sequence,
        (
            split_heads(query, count),
            split_heads(keys, count),
            split_heads(values, count),
            segments,
            ranks,
        ),
    )
    return (mixed.reshape(query.shape), log_total)


def attend_back_all(query, keys, values, segments, ranks, masked, log_total, grad_mixed):
    count = query.shape[0] // LEN

    def one_sequence(items):
        return attend_sequence_back(
            items[0], items[1], items[2], items[3], items[4], masked, items[5], items[6]
        )

    grad_query, grad_keys, grad_values = lax.map(
        one_sequence,
        (
            split_heads(query, count),
            split_heads(keys, count),
            split_heads(values, count),
            segments,
            ranks,
            log_total,
            split_heads(grad_mixed, count),
        ),
    )
    return (
        grad_query.reshape(query.shape),
        grad_keys.reshape(keys.shape),
        grad_values.reshape(values.shape),
    )


def shards(
    tokens,
    encoder_states,
    output_grad,
    valid_mask,
    segment_ids,
    context_ranks,
    self_query,
    self_key,
    self_value,
    self_output,
    cross_query,
    cross_key,
    cross_value,
    cross_output,
    hidden_up,
    hidden_down,
    norm1_gain,
    norm1_bias,
    norm2_gain,
    norm2_bias,
    norm3_gain,
    norm3_bias,
):
    (
        self_query,
        self_key,
        self_value,
        self_output,
        cross_query,
        cross_key,
        cross_value,
        cross_output,
        hidden_up,
        hidden_down,
    ) = (
        lax.all_gather(self_query, "dp", axis=0, tiled=True),
        lax.all_gather(self_key, "dp", axis=0, tiled=True),
        lax.all_gather(self_value, "dp", axis=0, tiled=True),
        lax.all_gather(self_output, "dp", axis=1, tiled=True),
        lax.all_gather(cross_query, "dp", axis=0, tiled=True),
        lax.all_gather(cross_key, "dp", axis=0, tiled=True),
        lax.all_gather(cross_value, "dp", axis=0, tiled=True),
        lax.all_gather(cross_output, "dp", axis=1, tiled=True),
        lax.all_gather(hidden_up, "dp", axis=0, tiled=True),
        lax.all_gather(hidden_down, "dp", axis=1, tiled=True),
    )
    tokens_full = full_rows(tokens)
    query = jnp.dot(tokens_full, self_query, preferred_element_type=jnp.float32).astype(
        jnp.bfloat16
    )
    keys = jnp.dot(tokens_full, self_key, preferred_element_type=jnp.float32).astype(jnp.bfloat16)
    values = jnp.dot(tokens_full, self_value, preferred_element_type=jnp.float32).astype(
        jnp.bfloat16
    )
    self_mixed, self_log = attend_all(query, keys, values, segment_ids, context_ranks, True)
    attended = branch_sum(self_mixed, self_output)
    first_out, first_normal, first_scale = layer_norm(
        tokens.astype(jnp.float32) + attended, norm1_gain, norm1_bias
    )
    first_full = full_rows(first_out.astype(jnp.bfloat16))
    encoder_full = full_rows(encoder_states)
    second_query = jnp.dot(first_full, cross_query, preferred_element_type=jnp.float32).astype(
        jnp.bfloat16
    )
    encoder_keys = jnp.dot(encoder_full, cross_key, preferred_element_type=jnp.float32).astype(
        jnp.bfloat16
    )
    encoder_values = jnp.dot(encoder_full, cross_value, preferred_element_type=jnp.float32).astype(
        jnp.bfloat16
    )
    cross_mixed, cross_log = attend_all(
        second_query, encoder_keys, encoder_values, segment_ids, context_ranks, False
    )
    crossed = branch_sum(cross_mixed, cross_output)
    second_out, second_normal, second_scale = layer_norm(
        first_out + crossed, norm2_gain, norm2_bias
    )
    second_low = second_out.astype(jnp.bfloat16)
    feed_input = full_rows(second_low)
    preact = jnp.dot(feed_input, hidden_up, preferred_element_type=jnp.float32)
    activated = gelu_exact(preact).astype(jnp.bfloat16)
    feed_out = branch_sum(activated, hidden_down)
    third_out, third_normal, third_scale = layer_norm(second_out + feed_out, norm3_gain, norm3_bias)
    valid_rows = valid_mask.astype(jnp.float32)[:, None]
    grad_layer = output_grad.astype(jnp.float32) * valid_rows
    grad_third, gain3_grad, bias3_grad = norm_back(
        grad_layer, third_normal, third_scale, norm3_gain
    )
    grad_third_low = grad_third.astype(jnp.bfloat16)
    grad_feed = grad_rows(grad_third_low)
    grad_active = back_product(grad_feed, hidden_down)
    grad_preact = gelu_back(preact, grad_active).astype(jnp.bfloat16)
    up_grad = row_product(feed_input, grad_preact)
    down_grad = row_product(activated, grad_feed)
    grad_second = grad_third + input_sum([(grad_preact, hidden_up)])
    grad_second_in, gain2_grad, bias2_grad = norm_back(
        grad_second, second_normal, second_scale, norm2_gain
    )
    grad_crossed = grad_rows(grad_second_in.astype(jnp.bfloat16))
    cross_output_grad = row_product(cross_mixed, grad_crossed)
    grad_cross_mixed = back_product(grad_crossed, cross_output).astype(jnp.bfloat16)
    grad_second_query, grad_encoder_keys, grad_encoder_values = attend_back_all(
        second_query,
        encoder_keys,
        encoder_values,
        segment_ids,
        context_ranks,
        False,
        cross_log,
        grad_cross_mixed,
    )
    cross_query_grad = row_product(first_full, grad_second_query)
    cross_key_grad = row_product(encoder_full, grad_encoder_keys)
    cross_value_grad = row_product(encoder_full, grad_encoder_values)
    grad_first = grad_second_in + input_sum([(grad_second_query, cross_query)])
    encoder_grad = input_sum([(grad_encoder_keys, cross_key), (grad_encoder_values, cross_value)])
    grad_first_in, gain1_grad, bias1_grad = norm_back(
        grad_first, first_normal, first_scale, norm1_gain
    )
    grad_attended = grad_rows(grad_first_in.astype(jnp.bfloat16))
    self_output_grad = row_product(self_mixed, grad_attended)
    grad_self_mixed = back_product(grad_attended, self_output).astype(jnp.bfloat16)
    grad_query, grad_keys, grad_values = attend_back_all(
        query, keys, values, segment_ids, context_ranks, True, self_log, grad_self_mixed
    )
    self_query_grad = row_product(tokens_full, grad_query)
    self_key_grad = row_product(tokens_full, grad_keys)
    self_value_grad = row_product(tokens_full, grad_values)
    tokens_grad = grad_first_in + input_sum(
        [(grad_query, self_query), (grad_keys, self_key), (grad_values, self_value)]
    )
    (
        self_query_grad,
        self_key_grad,
        self_value_grad,
        self_output_grad,
        cross_query_grad,
        cross_key_grad,
        cross_value_grad,
        cross_output_grad,
        up_grad,
        down_grad,
    ) = (
        lax.psum_scatter(self_query_grad, "dp", scatter_dimension=0, tiled=True),
        lax.psum_scatter(self_key_grad, "dp", scatter_dimension=0, tiled=True),
        lax.psum_scatter(self_value_grad, "dp", scatter_dimension=0, tiled=True),
        lax.psum_scatter(self_output_grad, "dp", scatter_dimension=1, tiled=True),
        lax.psum_scatter(cross_query_grad, "dp", scatter_dimension=0, tiled=True),
        lax.psum_scatter(cross_key_grad, "dp", scatter_dimension=0, tiled=True),
        lax.psum_scatter(cross_value_grad, "dp", scatter_dimension=0, tiled=True),
        lax.psum_scatter(cross_output_grad, "dp", scatter_dimension=1, tiled=True),
        lax.psum_scatter(up_grad, "dp", scatter_dimension=0, tiled=True),
        lax.psum_scatter(down_grad, "dp", scatter_dimension=1, tiled=True),
    )
    norm_sums, square_sums = lax.psum(
        (
            jnp.stack([gain1_grad, bias1_grad, gain2_grad, bias2_grad, gain3_grad, bias3_grad]),
            jnp.stack(
                [
                    jnp.sum(valid_rows * third_out * third_out, axis=0),
                    jnp.sum(valid_rows * tokens_grad * tokens_grad, axis=0),
                ]
            ),
        ),
        ("dp", "tensor"),
    )
    total_tokens = tokens.shape[0] * lax.axis_size("dp") * lax.axis_size("tensor")
    valid_scales = jnp.sqrt(square_sums / total_tokens)
    return (
        third_out,
        tokens_grad,
        encoder_grad,
        self_query_grad,
        self_key_grad,
        self_value_grad,
        self_output_grad,
        cross_query_grad,
        cross_key_grad,
        cross_value_grad,
        cross_output_grad,
        up_grad,
        down_grad,
        norm_sums,
        valid_scales,
    )


MESH = pl.DeviceIdType.MESH
BF = jnp.bfloat16
F32 = jnp.float32
LOG2E = 1.4426950408889634
SCALE = 0.125 * LOG2E
CH = 512


def nn(a, b):
    return lax.dot_general(a, b, (((1,), (0,)), ((), ())), preferred_element_type=F32)


def nt(a, b):
    return lax.dot_general(a, b, (((1,), (1,)), ((), ())), preferred_element_type=F32)


def turn(x):
    return x.T


class Place:
    def __init__(self):
        self.d = lax.axis_index("dp")
        self.t = lax.axis_index("tensor")
        self.z, self.y = self.d // 2, self.d % 2
        self.x, self.c = self.t // 2, self.t % 2
        self.xt = (1 - self.x) * 2 + self.c
        self.xn = (self.d, self.xt)
        self.yn = (self.z * 2 + 1 - self.y, self.t)
        self.pair = (self.d, self.x * 2 + 1 - self.c)
        self.zn = [None] + [((((self.z + k) % 4) * 2 + self.y), self.t) for k in (1, 2, 3)]
        top = self.z // 2
        self.near = [self.z, top * (5 - self.z) + (1 - top) * (1 - self.z), 2 - top, 3 * (1 - top)]

    def plane_peer(self, i):
        x, y, c = (self.x + i // 4) % 2, (self.y + i // 2) % 2, (self.c + i) % 2
        return (self.z * 2 + y, x * 2 + c)

    def barrier(self):
        sem = pltpu.get_barrier_semaphore()
        for dev in [self.plane_peer(i) for i in range(1, 8)] + self.zn[1:]:
            pl.semaphore_signal(sem, inc=1, device_id=dev, device_id_type=MESH)
        pl.semaphore_wait(sem, 10)


def remote(src, dst, send, recv, dev):
    return pltpu.make_async_remote_copy(
        src_ref=src, dst_ref=dst, send_sem=send, recv_sem=recv, device_id=dev, device_id_type=MESH
    )


class Gather:
    def __init__(self, p, w, cols, ss, rs):
        self.p, self.w, self.cols, self.ss, self.rs = p, w, cols, ss, rs

    def col(self, t):
        return pl.ds(pl.multiple_of(t * self.cols, 128), self.cols)

    def blk(self, k, y, t):
        return self.w.at[:, self.p.near[k], y, :, self.col(t)]

    def cp(self, ref, i, dev, send=None):
        return remote(ref, ref, self.ss.at[i if send is None else send], self.rs.at[i], dev)

    def own(self):
        return self.blk(0, self.p.y, self.p.t)

    def z_send(self, k):
        p = self.p
        dev = (p.near[k] * 2 + p.y, p.t)
        return self.cp(self.own(), 15 + p.z, dev, k - 1)

    def z_recv(self, k):
        p = self.p
        ref = self.blk(k, p.y, p.t)
        return self.cp(ref, 15 + p.near[k], (p.near[k] * 2 + p.y, p.t), k - 1)

    def x_send(self, k):
        return self.cp(self.blk(k, self.p.y, self.p.t), 3 + k, self.p.xn)

    def x_recv(self, k):
        return self.cp(self.blk(k, self.p.y, self.p.xt), 3 + k, self.p.xn)

    def y_send(self, k):
        return self.cp(self.blk(k, self.p.y, self.p.t), 7 + k, self.p.yn)

    def y_recv(self, k):
        return self.cp(self.blk(k, 1 - self.p.y, self.p.t), 7 + k, self.p.yn)

    def q_send(self, k):
        if k < 2:
            return self.cp(self.blk(k, self.p.y, self.p.xt), 11 + k, self.p.yn)
        return self.cp(self.blk(k, 1 - self.p.y, self.p.t), 11 + k, self.p.xn)

    def q_recv(self, k):
        return self.cp(self.blk(k, 1 - self.p.y, self.p.xt), 11 + k, self.p.xn)

    def rail(self, i, core):
        x = self.p.x if i == 0 else 1 - self.p.x
        return self.w.at[:, :, :, :, self.col(x * 2 + core)]

    def p_send(self, i):
        return self.cp(self.rail(i, self.p.c), 1 + i, self.p.pair, 17 + i)

    def p_recv(self, i):
        return self.cp(self.rail(i, 1 - self.p.c), 1 + i, self.p.pair, 17 + i)

    def zs(self):
        for k in (1, 2, 3):
            self.z_send(k).start()

    def oxy(self):
        self.x_send(0).start()
        self.y_send(0).start()

    def plane(self, *between):
        for k in (1, 2, 3):
            self.z_recv(k).wait_recv()
            if k == 1:
                for fn in between:
                    fn()
            self.x_send(k).start()
            self.y_send(k).start()

    def corner(self):
        for k in range(4):
            self.x_recv(k).wait_recv()
            if k < 2:
                self.q_send(k).start()
            self.y_recv(k).wait_recv()
            if k >= 2:
                self.q_send(k).start()
        self.p_send(0).start()

    def cross(self):
        for k in range(4):
            self.q_recv(k).wait_recv()
        self.p_send(1).start()

    def finish(self):
        self.p_recv(0).wait_recv()
        self.p_recv(1).wait_recv()

    def drain(self):
        for k in (1, 2, 3):
            self.z_send(k).wait_send()
        for k in range(4):
            self.x_send(k).wait_send()
            self.y_send(k).wait_send()
            self.q_send(k).wait_send()
        self.p_send(0).wait_send()
        self.p_send(1).wait_send()


class Reduce:
    def __init__(self, p, g, cols, held, r1, r2, r3, out, ss, rs):
        self.p, self.g, self.cols, self.held = p, g, cols, held
        self.r1, self.r2, self.r3, self.out, self.ss, self.rs = r1, r2, r3, out, ss, rs
        self.n = g.shape[0]

    def col(self, t):
        return pl.ds(pl.multiple_of(t * self.cols, 128), self.cols)

    def cp(self, src, dst, i, dev):
        return remote(src, dst, self.ss.at[i], self.rs.at[i], dev)

    def pair_copy(self, x):
        src = self.g.at[:, :, :, :, self.col(x * 2 + 1 - self.p.c)]
        return self.cp(src, self.held.at[x], x, self.p.pair)

    def corner_copy(self, i):
        p = self.p
        src = self.held.at[1 - p.x, :, pl.ds(2 * i, 2), 1 - p.y]
        return self.cp(src, self.r1.at[i], 2 + i, p.yn if i == 0 else p.xn)

    def plane_copy(self, i):
        p = self.p
        src = self.held.at[1 - p.x, :, :, p.y] if i == 0 else self.held.at[p.x, :, :, 1 - p.y]
        return self.cp(src, self.r2.at[i], 4 + i, p.xn if i == 0 else p.yn)

    def z_copy(self, k):
        p = self.p
        src = self.held.at[p.x, :, (p.z + k) % 4, p.y]
        return self.cp(src, self.r3.at[k - 1], 5 + k, p.zn[k])

    def start(self):
        self.pair_copy(0).start()
        self.pair_copy(1).start()

    def corner(self):
        for x in (0, 1):
            self.pair_copy(x).wait_recv()
        for x in (0, 1):
            col = self.col(x * 2 + self.p.c)

            def one(j, _, x=x, col=col):
                i, z = j // 4, j % 4
                a = self.g[i, z, :, :, col].astype(F32) + self.held[x, i, z].astype(F32)
                self.held[x, i, z] = a.astype(BF)
                return 0

            def whole(i, _, x=x, col=col):
                a = self.g[i, :, :, :, col].astype(F32) + self.held[x, i].astype(F32)
                self.held[x, i] = a.astype(BF)
                return 0

            if self.cols > 128:
                lax.fori_loop(0, self.n * 4, one, 0)
            else:
                lax.fori_loop(0, self.n, whole, 0)
        self.corner_copy(0).start()
        self.corner_copy(1).start()

    def plane(self):
        p = self.p
        self.corner_copy(0).wait_recv()
        self.corner_copy(1).wait_recv()
        for i in range(self.n):
            for j in range(2):
                a = self.held[1 - p.x, i, j, p.y].astype(F32) + self.r1[0, i, j].astype(F32)
                self.held[1 - p.x, i, j, p.y] = a.astype(BF)
                b = self.held[p.x, i, 2 + j, 1 - p.y].astype(F32) + self.r1[1, i, j].astype(F32)
                self.held[p.x, i, 2 + j, 1 - p.y] = b.astype(BF)
        self.plane_copy(0).start()
        self.plane_copy(1).start()

    def along(self):
        p = self.p
        self.plane_copy(0).wait_recv()
        self.plane_copy(1).wait_recv()
        for k in (1, 2, 3):
            zt = (p.z + k) % 4
            for i in range(self.n):
                a = (
                    self.held[p.x, i, zt, p.y].astype(F32)
                    + self.r2[0, i, zt].astype(F32)
                    + self.r2[1, i, zt].astype(F32)
                )
                self.held[p.x, i, zt, p.y] = a.astype(BF)
            self.z_copy(k).start()

    def finish(self):
        p = self.p
        for k in (1, 2, 3):
            self.z_copy(k).wait_recv()
        for i in range(self.n):
            a = (
                self.held[p.x, i, p.z, p.y].astype(F32)
                + self.r2[0, i, p.z].astype(F32)
                + self.r2[1, i, p.z].astype(F32)
            )
            for k in range(3):
                a = a + self.r3[k, i].astype(F32)
            self.out[i] = a

    def drain(self):
        for i in (0, 1):
            self.pair_copy(i).wait_send()
            self.corner_copy(i).wait_send()
            self.plane_copy(i).wait_send()
        for k in (1, 2, 3):
            self.z_copy(k).wait_send()


class Tail:
    def __init__(self, p, gt, hp, hx, hy, hz, hc, out, ss, rs):
        self.p, self.gt, self.hp, self.hx, self.hy, self.hz, self.hc = p, gt, hp, hx, hy, hz, hc
        self.out, self.ss, self.rs = out, ss, rs

    def cp(self, src, dst, i, dev):
        return remote(src, dst, self.ss.at[i], self.rs.at[i], dev)

    def pair_copy(self, j):
        return self.cp(self.gt.at[j], self.hp.at[j // 2], j, self.p.pair)

    def x_copy(self, j):
        if j == 1:
            return self.cp(self.gt.at[1, :, :, self.p.y], self.hx.at[:, :, 0], 4, self.p.xn)
        return self.cp(self.gt.at[0], self.hx, 4, self.p.xn)

    def corner_copy(self):
        return self.cp(self.gt.at[1, :, :, 1 - self.p.y], self.hc, 9, self.p.yn)

    def y_copy(self, j):
        return self.cp(self.gt.at[j, :, :, 1 - self.p.y], self.hy, 5, self.p.yn)

    def z_copy(self, j, k):
        p = self.p
        return self.cp(self.gt.at[j, :, (p.z + k) % 4, p.y], self.hz.at[k - 1], 5 + k, p.zn[k])

    def mine(self, j, fn):
        pl.when(self.p.c == j % 2)(fn)

    def start(self, j):
        pl.when(self.p.c != j % 2)(lambda: self.pair_copy(j).start())

    def sum_pair(self, j):
        def do():
            self.pair_copy(j).wait_recv()
            if j == 2:
                self.x_copy(0).wait_recv()
            for w in range(3):
                a = self.gt[j, w].astype(F32) + self.hp[j // 2, w].astype(F32)
                if j == 2:
                    a = a + self.hx[w].astype(F32)
                self.gt[j, w] = a.astype(BF)
            if j == 0:
                self.x_copy(0).start()
            elif j == 1:
                self.corner_copy().start()
            else:
                self.y_copy(j).start()

        self.mine(j, do)

    def corner(self):
        def do():
            self.corner_copy().wait_recv()
            y = self.p.y
            for w in range(3):
                a = self.gt[1, w, :, y].astype(F32) + self.hc[w].astype(F32)
                self.gt[1, w, :, y] = a.astype(BF)
            self.x_copy(1).start()

        self.mine(1, do)

    def sum_y(self, j):
        def do():
            p = self.p
            self.y_copy(j).wait_recv()
            if j == 3:
                self.x_copy(1).wait_recv()
            for i in range(3):
                for k in (1, 2, 3):
                    zt = (p.z + k) % 4
                    a = self.gt[j, i, zt, p.y].astype(F32) + self.hy[i, zt].astype(F32)
                    if j == 3:
                        a = a + self.hx[i, zt, 0].astype(F32)
                    self.gt[j, i, zt, p.y] = a.astype(BF)
            for k in (1, 2, 3):
                self.z_copy(j, k).start()

        self.mine(j, do)

    def finish(self, j):
        def do():
            p = self.p
            for k in (1, 2, 3):
                self.z_copy(j, k).wait_recv()
            for i in range(3):
                a = self.gt[j, i, p.z, p.y].astype(F32) + self.hy[i, p.z].astype(F32)
                if j == 3:
                    a = a + self.hx[i, p.z, 0].astype(F32)
                for k in range(3):
                    a = a + self.hz[k, i].astype(F32)
                self.out[i] = a

        self.mine(j, do)

    def drain(self):
        for j in range(4):
            pl.when(self.p.c != j % 2)(lambda j=j: self.pair_copy(j).wait_send())

        def sent(j):
            self.x_copy(j).wait_send()
            if j == 1:
                self.corner_copy().wait_send()
            self.y_copy(j + 2).wait_send()
            for k in (1, 2, 3):
                self.z_copy(j + 2, k).wait_send()

        for j in (0, 1):
            self.mine(j, lambda j=j: sent(j))


def row_steps(count, one):
    def body(i, _):
        one(pl.ds(pl.multiple_of(i * CH, CH), CH))
        return 0

    lax.fori_loop(0, count // CH, body, 0)


def head_half(shape, axis, h):
    return (lax.broadcasted_iota(jnp.int32, shape, axis) // HEAD) == h


def keep_half(value, axis, h):
    return jnp.where(head_half(value.shape, axis, h), value.astype(F32), 0.0).astype(BF)


def run_hooks(hooks, step, half):
    for (at, part), hook in hooks.items():
        if part == half:
            pl.when(step == at)(hook)


def attend(qt, k, vt, bias, ot, lse, temp, hooks):
    def ready(p, h):
        lanes = pl.ds(pl.multiple_of(p * 128, 128), 128)
        return k[:, lanes], keep_half(qt[lanes, :], 0, h)

    def score(kp, qm, h, i, top):
        s = nn(kp[i * 512 : i * 512 + 512], qm) * SCALE
        if bias is not None:
            s = s + bias[i * 512 : i * 512 + 512, :]
        temp[h * 1024 + i * 512 : h * 1024 + i * 512 + 512, :] = s
        m = jnp.max(s, axis=0, keepdims=True)
        return m if top is None else jnp.maximum(top, m)

    def mix(vh, h, i, top, total, mixed):
        e = jnp.exp2(temp[h * 1024 + i * 512 : h * 1024 + i * 512 + 512, :] - top)
        part = jnp.sum(e, axis=0, keepdims=True)
        o = nn(vh[:, i * 512 : i * 512 + 512], e.astype(BF))
        return (part, o) if total is None else (total + part, mixed + o)

    def pair(p, top):
        for h in (0, 1):
            kp, qm = ready(p if h == 0 else (p + 1) % 4, 1 - h)
            vh = vt[pl.ds(pl.multiple_of(p * 128 + h * 64, 64), 64), :]
            total = mixed = later = None
            for i in range(2):
                later = score(kp, qm, 1 - h, i, later)
                total, mixed = mix(vh, h, i, top, total, mixed)
            ot[pl.ds(pl.multiple_of(p * 128 + h * 64, 64), 64), :] = mixed * (1.0 / total)
            lse[pl.ds(p * 2 + h, 1), :] = top + jnp.log2(total)
            top = later
            run_hooks(hooks, p, h)
        return top

    kp, qm = ready(0, 0)
    top = None
    for i in range(2):
        top = score(kp, qm, 0, i, top)
    lax.fori_loop(0, 4, pair, top)


def attend_back(q, qt, k, kt, v, do, dot_, ot, bias, lse, dqt, dk_own, dv_own, dkv_send, order, hooks):
    def pair(step, _):
        p = order(step)
        lanes = pl.ds(pl.multiple_of(p * 128, 128), 128)
        kp, vp = k[:, lanes], v[:, lanes]
        qp, dop = qt[lanes, :], dot_[lanes, :]
        inner = dop.astype(F32) * ot[lanes, :]
        qms = [keep_half(qp, 0, h) for h in (0, 1)]
        doms = [keep_half(dop, 0, h) for h in (0, 1)]
        qr = jnp.concatenate([keep_half(q[:, lanes], 1, h) for h in (0, 1)], axis=0)
        dor = jnp.concatenate([keep_half(do[:, lanes], 1, h) for h in (0, 1)], axis=0)
        ds_sum = [jnp.sum(inner[h * 64 : h * 64 + 64], axis=0, keepdims=True) for h in (0, 1)]
        logs = [lse[pl.ds(p * 2 + h, 1), :] for h in (0, 1)]
        shares, grads = {}, {}
        dq = [None, None]
        dvs, dks = {}, {}

        def one(h, i):
            rows = slice(i * 256, i * 256 + 256)
            s = nn(kp[rows], qms[h]) * SCALE
            if bias is not None:
                s = s + bias[rows, :]
            e = jnp.exp2(s - logs[h])
            dp = nn(vp[rows], doms[h])
            shares[h, i] = e.astype(BF)
            grads[h, i] = (e * (dp - ds_sum[h])).astype(BF)

        def two(h, i):
            rows = slice(i * 256, i * 256 + 256)
            kh = kt[pl.ds(pl.multiple_of(p * 128 + h * 64, 64), 64), rows]
            part = nn(kh, grads[h, i])
            dq[h] = part if dq[h] is None else dq[h] + part
            dv = nn(shares[h, i], dor[h * 512 : h * 512 + 512])
            dk = nn(grads[h, i], qr[h * 512 : h * 512 + 512])
            dvs[i] = dv if i not in dvs else dvs[i] + dv
            dks[i] = dk if i not in dks else dks[i] + dk

        def out(i):
            rows = slice(i * 256, i * 256 + 256)
            if i < 2:
                dk_own[rows, lanes] = (dks[i] * 0.125).astype(dk_own.dtype)
                dv_own[rows, lanes] = dvs[i].astype(dv_own.dtype)
            else:
                back = slice(i * 256 - 512, i * 256 - 256)
                dkv_send[0, back, lanes] = (dks[i] * 0.125).astype(BF)
                dkv_send[1, back, lanes] = dvs[i].astype(BF)

        for i in range(4):
            one(0, i)
        for i in range(4):
            one(1, i)
            two(0, i)
        run_hooks(hooks, step, 0)
        for i in range(4):
            two(1, i)
            out(i)
        for h in (0, 1):
            dqt[pl.ds(pl.multiple_of(p * 128 + h * 64, 64), 64), :] = (dq[h] * 0.125).astype(BF)
        run_hooks(hooks, step, 1)
        return 0

    lax.fori_loop(0, 4, pair, 0)


def norm_rows(z):
    mean = jnp.mean(z, axis=-1, keepdims=True)
    centred = z - mean
    r = lax.rsqrt(jnp.mean(centred * centred, axis=-1, keepdims=True) + norm_eps)
    return centred * r, r


def norm_back_rows(e, n, r, gain):
    s = e * gain
    a = jnp.mean(s, axis=-1, keepdims=True)
    b = jnp.mean(s * n, axis=-1, keepdims=True)
    return r * (s - a - n * b)


def fast_kernel(
    x_i, enc_i, og_i, valid, seg, rank,
    sq, sk, sv, so, cq, ck, cv, co, up, down,
    g1, b1, g2, b2, g3, b3,
    y_o, dx_o, eg_o, ga_o, gb_o, gf_o, ns_o, vs_o,
    xs, enc, og, codes, wa, wb, wf, gt,
    q1, qt1, k1, v1, vt1, o1, ot1, l1,
    q2, qt2, k2, v2, vt2, o2, ot2, l2,
    bias, n1, n2, h1b, h2b, u, gp, dg, dz, low, lowt, do, dot_,
    kvs, kvr1, kvr2, tt, yb, row, st,
    hc, hq, hu, hd, c1, c2, c3, p1, p2, p3, u1, u2, u3, d1, d2, d3, hp, hx, hy, hz, hcn,
    st_r, gss, grs, rss, rrs, aas, ars, ess, ers, tss, trs, ls,
):
    dqt, dq = h2b, q2
    x = xs.at[pl.ds(0, 512)]
    dkv = [v2.at[pl.ds(0, 512)], v2.at[pl.ds(512, 512)]]
    p = Place()
    loads = []
    for i, (src, w, j, cols) in enumerate(
        (
            (sq, wa, 0, 128), (sk, wa, 1, 128), (sv, wa, 2, 128),
            (so, wb, 0, 128), (co, wb, 1, 128), (cq, wb, 2, 128), (ck, wb, 3, 128), (cv, wb, 4, 128),
            (up, wf, 0, 512), (down, wf, 1, 512),
        )
    ):
        col = pl.ds(pl.multiple_of(p.t * cols, 128), cols)
        loads.append(pltpu.make_async_copy(src, w.at[j, p.z, p.y, :, col], ls.at[i]))
    for i, (src, dst) in enumerate(((x_i, x), (enc_i, enc), (og_i, og))):
        loads.append(pltpu.make_async_copy(src, dst, ls.at[10 + i]))
    for cp in loads:
        cp.start()
    p.barrier()
    GA, GB, GU, GD = G = [
        Gather(p, w, cols, gss.at[i], grs.at[i])
        for i, (w, cols) in enumerate(
            ((wa, 128), (wb, 128), (wf.at[pl.ds(0, 1)], 512), (wf.at[pl.ds(1, 1)], 512))
        )
    ]
    for cp in loads[:3]:
        cp.wait()
    GA.zs()
    GA.oxy()
    for cp in loads[3:]:
        cp.wait()
    halves = remote(
        xs.at[pl.ds(0, 512)], xs.at[pl.ds(512, 512)], ess.at[9], ers.at[9], p.pair
    )
    halves.start()
    GB.oxy()

    def mat(w, j):
        return w[j].reshape(512, w.shape[4])

    st[...] = jnp.zeros_like(st)
    row[...] = jnp.broadcast_to(valid[...].astype(F32), (128, 512)).T
    own = pl.ds(pl.multiple_of(p.c * 512, 128), 512)
    other = pl.ds(pl.multiple_of((1 - p.c) * 512, 128), 512)
    sx = pl.ds(p.x, 1)
    ranks = rank[sx, :]
    codes[1:2, :] = seg[sx, :] * 8
    codes[0:1, :] = seg[sx, :] * 8 + jnp.concatenate(
        [jnp.broadcast_to(ranks[:, b : b + 1], (1, 128)) for b in range(8)], axis=1
    )
    base, high = codes[1:2, own], codes[0:1, own]
    for i, half in enumerate((own, other)):
        code = jnp.broadcast_to(codes[0:1, half], (128, 512)).T
        for j in range(4):
            c = code[j * 128 : j * 128 + 128, :1]
            ok = (c >= base) & (c <= high)
            bias[i * 512 + j * 128 : i * 512 + j * 128 + 128, :] = jnp.where(ok, 0.0, -2.0e9)

    GA.plane(GB.zs)
    GU.oxy()
    GA.corner()
    GU.zs()
    GD.oxy()
    GA.cross()
    GB.plane()
    GA.finish()
    GD.zs()

    def swap(buf, i):
        return remote(buf.at[pl.ds(0, 512)], buf.at[pl.ds(512, 512)], ess.at[i], ers.at[i], p.pair)

    halves.wait()
    xv = xs[...]
    k1[...] = nn(xv, mat(wa, 1)).astype(BF)
    vv = nn(xv, mat(wa, 2)).astype(BF)
    v1[...] = vv
    vt1[...] = turn(vv)
    xv = x[...]
    qv = nn(xv, mat(wa, 0)).astype(BF)
    q1[...] = qv
    qt1[...] = turn(qv)
    attend(qt1, k1, vt1, bias, ot1, l1, gp, {(0, 0): GB.corner, (1, 0): GU.plane, (2, 0): GB.cross, (3, 0): GD.plane})
    o1[...] = turn(ot1[...].astype(BF))
    GB.finish()
    ev = enc[...]
    k2[0:512, :] = nn(ev, mat(wb, 3)).astype(BF)
    v2[0:512, :] = nn(ev, mat(wb, 4)).astype(BF)
    swap(k2, 2).start()
    swap(v2, 3).start()
    yb[...] = nt(o1[...], mat(wb, 0))
    GU.corner()

    def first(r):
        n, s = norm_rows(x[r, :].astype(F32) + yb[r, :])
        n1[r, :] = n
        row[r, 0:1] = s
        h1b[r, :] = (n * g1[...] + b1[...]).astype(BF)

    row_steps(512, first)
    qv = nn(h1b[...], mat(wb, 2)).astype(BF)
    q2[...] = qv
    qt2[...] = turn(qv)
    swap(k2, 2).wait_recv()
    swap(v2, 3).wait_recv()
    vt2[...] = turn(v2[...])
    attend(qt2, k2, vt2, None, ot2, l2, gp, {(0, 1): GD.corner, (2, 1): GU.cross})
    o2[...] = turn(ot2[...].astype(BF))
    yb[...] = nt(o2[...], mat(wb, 1))

    def second(r):
        n, s = norm_rows(n1[r, :] * g1[...] + b1[...] + yb[r, :])
        n2[r, :] = n
        row[r, 1:2] = s
        h2b[r, :] = (n * g2[...] + b2[...]).astype(BF)

    row_steps(512, second)
    hv = h2b[...]
    blocks = [p.t, p.pair[1], p.xt, (1 - p.x) * 2 + 1 - p.c]
    waits = [None, GU.p_recv(0).wait_recv, GD.cross, GU.p_recv(1).wait_recv]
    for t, wait in zip(blocks, waits):
        if wait is not None:
            wait()
        cols = pl.ds(pl.multiple_of(t * 512, 512), 512)
        gp[cols, :] = nn(hv, wf[0, :, :, :, cols].reshape(512, 512))

        def gelu(r, cols=cols, t=t):
            at = pl.ds(pl.multiple_of(r.start + t * 512, CH), CH)
            v = gp[at, :]
            cdf = 0.5 * (1.0 + lax.erf(v * 0.7071067811865476))
            u[r, cols] = (v * cdf).astype(BF)
            gp[at, :] = cdf + v * (jnp.exp2(v * v * (-0.5 * LOG2E)) * 0.3989422804014327)

        row_steps(512, gelu)
    waits = [None, GD.p_recv(0).wait_recv, None, GD.p_recv(1).wait_recv]
    for i, (t, wait) in enumerate(zip(blocks, waits)):
        if wait is not None:
            wait()
        cols = pl.ds(pl.multiple_of(t * 512, 512), 512)
        part = nt(u[:, cols], wf[1, :, :, :, cols].reshape(512, 512))
        yb[...] = part if i == 0 else yb[...] + part

    def third(r):
        n, s = norm_rows(n2[r, :] * g2[...] + b2[...] + yb[r, :])
        out = n * g3[...] + b3[...]
        vc = row[r, 2:3]
        yb[r, :] = out
        e = og[r, :].astype(F32) * vc
        st[4:5, :] += jnp.sum(e * n, axis=0, keepdims=True)
        st[5:6, :] += jnp.sum(e, axis=0, keepdims=True)
        st[6:7, :] += jnp.sum(vc * out * out, axis=0, keepdims=True)
        back = norm_back_rows(e, n, s, g3[...])
        dz[r, :] = back
        low[r, :] = back.astype(BF)

    row_steps(512, third)
    y_copy = pltpu.make_async_copy(yb, y_o, ls.at[0])
    y_copy.start()
    lv = low[...]
    lowt[...] = turn(lv)
    for g in G:
        g.drain()
    RC, RP, RU, RD = R = [
        Reduce(p, w.at[pl.ds(at, n)], cols, *bufs, out.at[pl.ds(at, n)], rss.at[i], rrs.at[i])
        for i, (w, at, n, cols, bufs, out) in enumerate(
            (
                (wb, 0, 2, 128, (hc, c1, c2, c3), gb_o),
                (wb, 2, 3, 128, (hq, p1, p2, p3), gb_o),
                (wf, 0, 1, 512, (hu, u1, u2, u3), gf_o),
                (wf, 1, 1, 512, (hd, d1, d2, d3), gf_o),
            )
        )
    ]
    for j in range(4):
        cols = slice(j * 512, j * 512 + 512)
        dg[:, cols] = (nn(lv, wf[1, :, :, :, cols].reshape(512, 512)) * gp[cols, :]).astype(BF)
        wf[1, :, :, :, cols] = nn(lowt[...], u[:, cols]).astype(BF).reshape(4, 2, 64, 512)
        if j % 2 == 1:
            RD.pair_copy(j // 2).start()
    dz[...] += nt(dg[...], mat(wf, 0))
    tt[...] = turn(h2b[...])
    for j in range(4):
        cols = slice(j * 512, j * 512 + 512)
        wf[0, :, :, :, cols] = nn(tt[...], dg[:, cols]).astype(BF).reshape(4, 2, 64, 512)
    RU.start()
    RD.corner()

    def back2(r):
        e = dz[r, :]
        n = n2[r, :]
        st[2:3, :] += jnp.sum(e * n, axis=0, keepdims=True)
        st[3:4, :] += jnp.sum(e, axis=0, keepdims=True)
        back = norm_back_rows(e, n, row[r, 1:2], g2[...])
        dz[r, :] = back
        low[r, :] = back.astype(BF)

    row_steps(512, back2)
    dov = nn(low[...], mat(wb, 1)).astype(BF)
    do[...] = dov
    dot_[...] = turn(dov)
    lowt[...] = turn(low[...])
    wb[1] = nn(lowt[...], o2[...]).astype(BF).reshape(4, 2, 64, 512)
    vt2[...] = turn(k2[...])
    RU.corner()
    attend_back(
        q2, qt2, k2, vt2, v2, do, dot_, ot2, None, l2, dqt,
        gp.at[pl.ds(0, 512)], gp.at[pl.ds(512, 512)], kvs.at[:, pl.ds(512, 512)], lambda step: step,
        {(0, 0): RD.plane, (1, 0): RU.plane, (3, 0): RD.along},
    )

    def swap_back(buf, i):
        return remote(kvs.at[:, pl.ds(512, 512)], buf, ess.at[i], ers.at[i], p.pair)

    swap_back(kvr2, 4).start()
    dqv = turn(dqt[...])
    dz[...] += nt(dqv, mat(wb, 2))
    tt[...] = turn(h1b[...])
    wb[2] = nn(tt[...], dqv).astype(BF).reshape(4, 2, 64, 512)
    tt[...] = turn(enc[...])
    swap_back(kvr2, 4).wait()
    for i in (2, 3):
        swap((k1, v1, k2, v2)[i], i).wait_send()

    def join(recv, at):
        def one(r):
            for i in (0, 1):
                own_rows = pl.ds(pl.multiple_of(r.start + at + i * 512, CH), CH)
                dkv[i][r, :] = (gp[own_rows, :] + recv[i, r, :].astype(F32)).astype(BF)

        row_steps(512, one)

    join(kvr2, 0)
    y_copy.wait()
    yb[...] = nt(dkv[0][...], mat(wb, 3)) + nt(dkv[1][...], mat(wb, 4))
    e_copy = pltpu.make_async_copy(yb, eg_o, ls.at[0])
    e_copy.start()
    wb[3] = nn(tt[...], dkv[0][...]).astype(BF).reshape(4, 2, 64, 512)
    wb[4] = nn(tt[...], dkv[1][...]).astype(BF).reshape(4, 2, 64, 512)
    RP.start()

    def back1(r):
        e = dz[r, :]
        n = n1[r, :]
        st[0:1, :] += jnp.sum(e * n, axis=0, keepdims=True)
        st[1:2, :] += jnp.sum(e, axis=0, keepdims=True)
        back = norm_back_rows(e, n, row[r, 0:1], g1[...])
        dz[r, :] = back
        low[r, :] = back.astype(BF)

    row_steps(512, back1)
    RU.along()
    dov = nn(low[...], mat(wb, 0)).astype(BF)
    do[...] = dov
    dot_[...] = turn(dov)
    lowt[...] = turn(low[...])
    wb[0] = nn(lowt[...], o1[...]).astype(BF).reshape(4, 2, 64, 512)
    RC.start()
    RP.corner()
    vt1[...] = turn(k1[...])
    vt2[...] = turn(xs[...])
    T = Tail(p, gt, hp, hx, hy, hz, hcn, ga_o, aas, ars)

    def order(step):
        far = (step // 2) * p.x + (1 - step // 2) * (1 - p.x)
        return 2 * far + step % 2

    def lanes_of(step):
        return pl.ds(pl.multiple_of(order(step) * 128, 128), 128)

    def part_back(step):
        at = lanes_of(step)
        return remote(
            kvs.at[:, pl.ds(512, 512), at], kvr1.at[:, :, at], ess.at[5 + step], ers.at[5 + step], p.pair
        )

    def grads(step):
        at = lanes_of(step)
        dqv = turn(dqt[at, :])
        dq[:, at] = dqv
        gt[step, 0] = nn(vt2[:, 0:512], dqv).astype(BF).reshape(4, 2, 64, 128)
        gt[step, 1] = nn(vt2[...], kvs[0, :, at]).astype(BF).reshape(4, 2, 64, 128)
        gt[step, 2] = nn(vt2[...], kvs[1, :, at]).astype(BF).reshape(4, 2, 64, 128)
        T.start(step)

    def both(*fns):
        def run():
            for fn in fns:
                fn()

        return run

    attend_back(
        q1, qt1, k1, vt1, v1, do, dot_, ot1, bias, l1, dqt,
        kvs.at[0, pl.ds(0, 512)], kvs.at[1, pl.ds(0, 512)], kvs.at[:, pl.ds(512, 512)], order,
        {
            (0, 0): RC.corner,
            (0, 1): both(lambda: part_back(0).start(), lambda: grads(0), RP.plane),
            (1, 0): lambda: T.sum_pair(0),
            (1, 1): both(lambda: part_back(1).start(), lambda: grads(1), RC.plane, RD.finish),
            (2, 0): lambda: T.sum_pair(1),
            (2, 1): both(lambda: part_back(2).start(), lambda: grads(2), RP.along, RU.finish),
            (3, 0): lambda: T.sum_pair(2),
            (3, 1): both(lambda: part_back(3).start(), T.corner, RC.along),
        },
    )
    grads(3)
    T.sum_y(2)
    dz[...] += nt(dq[...], mat(wa, 0))
    for step in range(4):
        part_back(step).wait_recv()

    def join_last(r):
        for i in (0, 1):
            dkv[i][r, :] = (kvs[i, r, :].astype(F32) + kvr1[i, r, :].astype(F32)).astype(BF)

    row_steps(512, join_last)
    T.sum_pair(3)
    dz[...] += nt(dkv[0][...], mat(wa, 1)) + nt(dkv[1][...], mat(wa, 2))
    x_copy = pltpu.make_async_copy(dz, dx_o, ls.at[1])
    x_copy.start()

    def squares(r):
        st[7:8, :] += jnp.sum(row[r, 2:3] * dz[r, :] * dz[r, :], axis=0, keepdims=True)

    row_steps(512, squares)

    stats = []
    st_r[0] = st[...]
    for i in range(1, 8):
        stats.append(remote(st, st_r.at[i], tss.at[i], trs.at[i], p.plane_peer(i)))
    for cp in stats:
        cp.start()
    T.sum_y(3)
    for cp in stats:
        cp.wait()
    total = None
    for i in range(8):
        x, y, c = (p.x + i // 4) % 2, (p.y + i // 2) % 2, (p.c + i) % 2
        part = st_r[x * 4 + y * 2 + c]
        total = part if total is None else total + part
    st_r[8 + p.z] = total
    stats = []
    for k in (1, 2, 3):
        at = st_r.at[8 + p.z]
        stats.append((remote(at, at, tss.at[7 + k], trs.at[7 + k], p.zn[k]), k))
    for cp, _ in stats:
        cp.start()
    RP.finish()
    RC.finish()
    T.finish(2)
    for cp, k in stats:
        cp.wait_send()
        back = st_r.at[8 + (p.z - k + 4) % 4]
        remote(back, back, tss.at[7 + k], trs.at[7 + k], p.zn[k]).wait_recv()
    T.finish(3)
    total = st_r[8] + st_r[9] + st_r[10] + st_r[11]
    ns_o[...] = total[0:6]
    vs_o[...] = jnp.sqrt(total[6:8] * (1.0 / 16384.0))
    for step in range(4):
        part_back(step).wait_send()
    for r in R:
        r.drain()
    T.drain()
    e_copy.wait()
    x_copy.wait()


def place_kernel(*refs):
    srcs, outs, held, sems = refs[:8], refs[8:23], refs[23:31], refs[31]
    parts = [held[0], held[1], held[2]] + [held[3].at[i] for i in range(3)]
    parts += [held[4].at[i] for i in range(5)] + [held[5].at[i] for i in range(2)] + [held[6], held[7]]
    first = [pltpu.make_async_copy(a, b, sems.at[i]) for i, (a, b) in enumerate(zip(srcs, held))]
    last = [pltpu.make_async_copy(a, b, sems.at[8 + i]) for i, (a, b) in enumerate(zip(parts, outs))]
    ends = [(0, 1), (1, 2), (2, 3), (3, 6), (6, 11), (11, 13), (13, 14), (14, 15)]
    order = (6, 7, 3, 4, 5, 0, 1, 2)
    for i in order:
        first[i].start()
    for i in order:
        first[i].wait()
        for cp in last[ends[i][0] : ends[i][1]]:
            cp.start()
    for cp in last:
        cp.wait()


def fast_shards(
    tokens, encoder_states, output_grad, valid_mask, segment_ids, context_ranks,
    self_query, self_key, self_value, self_output,
    cross_query, cross_key, cross_value, cross_output, hidden_up, hidden_down,
    norm1_gain, norm1_bias, norm2_gain, norm2_bias, norm3_gain, norm3_bias,
):
    vm = pl.BlockSpec(memory_space=pltpu.VMEM)
    hbm = pl.BlockSpec(memory_space=pl.ANY)
    rows = [
        v.reshape(1, 512)
        for v in (norm1_gain, norm1_bias, norm2_gain, norm2_bias, norm3_gain, norm3_bias)
    ]

    def V(*shape, dtype=BF):
        return pltpu.VMEM(shape, dtype)

    def S(*shape):
        return pltpu.SemaphoreType.DMA(shape)

    def group(n, cols):
        return [
            V(2, n, 4, 2, 64, cols),
            [V(2, n, 2, 64, cols), V(2, n, 4, 64, cols), V(3, n, 64, cols)],
        ]

    rc, rp, ru, rd = group(2, 128), group(3, 128), group(1, 512), group(1, 512)

    def attention():
        return [
            V(512, 512), V(512, 512), V(1024, 512), V(1024, 512), V(512, 1024), V(512, 512),
            V(512, 512, dtype=F32), V(8, 512, dtype=F32),
        ]

    scratch = (
        [V(1024, 512), V(512, 512), V(512, 512)]
        + [V(8, 1024, dtype=jnp.int32)]
        + [V(3, 4, 2, 64, 512), V(5, 4, 2, 64, 512), V(2, 4, 2, 64, 2048), V(4, 3, 4, 2, 64, 128)]
        + attention()
        + attention()
        + [V(1024, 512, dtype=F32), V(512, 512, dtype=F32), V(512, 512, dtype=F32)]
        + [V(512, 512), V(512, 512)]
        + [V(512, 2048), V(2048, 512, dtype=F32), V(512, 2048), V(512, 512, dtype=F32)]
        + [V(512, 512)] * 4
        + [V(2, 1024, 512), V(2, 512, 512), V(2, 512, 512)]
        + [V(512, 512), V(512, 512, dtype=F32), V(512, 128, dtype=F32), V(8, 512, dtype=F32)]
        + [rc[0], rp[0], ru[0], rd[0]]
        + rc[1] + rp[1] + ru[1] + rd[1]
        + [V(2, 3, 4, 2, 64, 128), V(3, 4, 2, 64, 128), V(3, 4, 64, 128), V(3, 3, 64, 128), V(3, 4, 64, 128)]
        + [V(12, 8, 512, dtype=F32)]
        + [S(4, 19), S(4, 19), S(4, 9), S(4, 9), S(10), S(10), S(10), S(10), S(11), S(11), S(13)]
    )
    big = jax.ShapeDtypeStruct((512, 512), F32)
    outs = pl.pallas_call(
        fast_kernel,
        out_shape=[big, big, big]
        + [jax.ShapeDtypeStruct(s, F32) for s in ((3, 64, 128), (5, 64, 128), (2, 64, 512), (6, 512), (2, 512))],
        in_specs=[hbm] * 3 + [vm] * 3 + [hbm] * 10 + [vm] * 6,
        out_specs=[hbm] * 3 + [vm] * 5,
        scratch_shapes=scratch,
        compiler_params=pltpu.CompilerParams(
            collective_id=0, has_side_effects=True, vmem_limit_bytes=63 << 20
        ),
        name="layer",
    )(
        tokens, encoder_states, output_grad, valid_mask.reshape(1, 512), segment_ids, context_ranks,
        self_query, self_key, self_value, self_output.T,
        cross_query, cross_key, cross_value, cross_output.T, hidden_up, hidden_down.T, *rows,
    )
    ends = [big, big, big] + [jax.ShapeDtypeStruct((64, 128), F32)] * 8
    ends += [jax.ShapeDtypeStruct((64, 512), F32)] * 2
    ends += [jax.ShapeDtypeStruct(v, F32) for v in ((6, 512), (2, 512))]
    y, dx, eg, dsq, dsk, dsv, dso, dco, dcq, dck, dcv, dup, ddown, ns, vs = pl.pallas_call(
        place_kernel,
        out_shape=ends,
        in_specs=[hbm] * 8,
        out_specs=[hbm] * 15,
        scratch_shapes=[pltpu.VMEM(o.shape, F32) for o in outs] + [S(23)],
        name="place",
    )(*outs)
    return (
        y, dx, eg, dsq, dsk, dsv, dso.T, dcq, dck, dcv, dco.T, dup, ddown.T, ns, vs,
    )


def solution(mesh):
    in_specs = (
        P(("dp", "tensor"), None),
        P(("dp", "tensor"), None),
        P(("dp", "tensor"), None),
        P(("dp", "tensor")),
        P("dp", None),
        P("dp", None),
        P("dp", "tensor"),
        P("dp", "tensor"),
        P("dp", "tensor"),
        P("tensor", "dp"),
        P("dp", "tensor"),
        P("dp", "tensor"),
        P("dp", "tensor"),
        P("tensor", "dp"),
        P("dp", "tensor"),
        P("tensor", "dp"),
        P(),
        P(),
        P(),
        P(),
        P(),
        P(),
    )
    out_specs = (
        P(("dp", "tensor"), None),
        P(("dp", "tensor"), None),
        P(("dp", "tensor"), None),
        P("dp", "tensor"),
        P("dp", "tensor"),
        P("dp", "tensor"),
        P("tensor", "dp"),
        P("dp", "tensor"),
        P("dp", "tensor"),
        P("dp", "tensor"),
        P("tensor", "dp"),
        P("dp", "tensor"),
        P("tensor", "dp"),
        P(),
        P(),
    )
    body = fast_shards if dict(mesh.shape) == {"dp": 8, "tensor": 4} else shards
    return jax.shard_map(body, mesh=mesh, in_specs=in_specs, out_specs=out_specs, check_vma=False)
```

```python
import jax
import jax.numpy as jnp
from jax import lax
from jax.experimental import pallas as pl
from jax.experimental.pallas import tpu as pltpu
from jax.sharding import PartitionSpec as P

HEAD = 64
LEN = 1024
BLK = 128


norm_eps = 1e-05
mask_fill = -1000000000.0


def gelu_exact(value):
    return jax.nn.gelu(value, approximate=False)


def gelu_back(preact, upstream):
    return jax.vjp(gelu_exact, preact)[1](upstream)[0]


def layer_norm(value, gain, bias):
    mean = jnp.mean(value, axis=-1, keepdims=True)
    centred = value - mean
    scale = lax.rsqrt(jnp.mean(centred * centred, axis=-1, keepdims=True) + norm_eps)
    normal = centred * scale
    return (normal * gain + bias, normal, scale)


def norm_back(upstream, normal, scale, gain):
    scaled = upstream * gain
    mean_grad = jnp.mean(scaled, axis=-1, keepdims=True)
    mean_cross = jnp.mean(scaled * normal, axis=-1, keepdims=True)
    inward = scale * (scaled - mean_grad - normal * mean_cross)
    return (inward, jnp.sum(upstream * normal, axis=0), jnp.sum(upstream, axis=0))


def context_allowed(segments, ranks, first, count):
    length = segments.shape[0]
    key_block = jnp.arange(length, dtype=jnp.int32) // BLK
    key_rank = jnp.broadcast_to(ranks[:, None], (ranks.shape[0], BLK)).reshape(length)
    query_segment = lax.dynamic_slice_in_dim(segments, first, count)
    query_rank = lax.dynamic_slice_in_dim(key_rank, first, count)
    query_block = (first + jnp.arange(count, dtype=jnp.int32)) // BLK
    same_doc = query_segment[:, None] == segments[None, :]
    earlier = key_rank[None, :] < query_rank[:, None]
    same_block = query_block[:, None] == key_block[None, :]
    return same_doc & (earlier | same_block)


def full_rows(value):
    return lax.all_gather(value, "tensor", axis=0, tiled=True)


def grad_rows(value):
    return lax.all_gather(value, "tensor", axis=0, tiled=True)


def branch_sum(mixed, weight):
    return lax.psum_scatter(
        jnp.dot(mixed, weight, preferred_element_type=jnp.float32),
        "tensor",
        scatter_dimension=0,
        tiled=True,
    )


def back_product(left, weight):
    return lax.dot_general(
        left, weight, (((1,), (1,)), ((), ())), preferred_element_type=jnp.float32
    )


def row_product(left, right):
    return lax.dot_general(
        left, right, (((0,), (0,)), ((), ())), preferred_element_type=jnp.float32
    )


def input_sum(pairs):
    total = None
    for left, weight in pairs:
        portion = back_product(left, weight)
        total = portion if total is None else total + portion
    return lax.psum_scatter(total, "tensor", scatter_dimension=0, tiled=True)


def split_heads(value, count):
    return value.reshape(count, LEN, value.shape[1] // HEAD, HEAD)


def attend_sequence(query, keys, values, segments, ranks, masked):
    length = query.shape[0]
    width = min(length, 512)

    def one_block(index):
        first = index * width
        piece = lax.dynamic_slice_in_dim(query, first, width, 0)
        scores = jnp.einsum("qhd,khd->hqk", piece, keys, preferred_element_type=jnp.float32) * 0.125
        if masked:
            scores = jnp.where(
                context_allowed(segments, ranks, first, width)[None], scores, mask_fill
            )
        top = jnp.max(scores, axis=-1, keepdims=True)
        raised = jnp.exp(scores - top)
        total = jnp.sum(raised, axis=-1, keepdims=True)
        shares = (raised / total).astype(jnp.bfloat16)
        mixed = jnp.einsum("hqk,khd->qhd", shares, values, preferred_element_type=jnp.float32)
        return (mixed.astype(jnp.bfloat16), (top + jnp.log(total))[..., 0])

    mixed, log_total = lax.map(one_block, jnp.arange(length // width, dtype=jnp.int32))
    return (mixed.reshape(query.shape), log_total)


def attend_sequence_back(query, keys, values, segments, ranks, masked, log_total, grad_mixed):
    length = query.shape[0]
    width = min(length, 512)

    def one_block(carry, index):
        key_sum, value_sum = carry
        first = index * width
        piece = lax.dynamic_slice_in_dim(query, first, width, 0)
        grad_piece = lax.dynamic_slice_in_dim(grad_mixed, first, width, 0)
        scores = jnp.einsum("qhd,khd->hqk", piece, keys, preferred_element_type=jnp.float32) * 0.125
        if masked:
            scores = jnp.where(
                context_allowed(segments, ranks, first, width)[None], scores, mask_fill
            )
        shares = jnp.exp(scores - log_total[index][..., None])
        grad_shares = jnp.einsum(
            "qhd,khd->hqk", grad_piece, values, preferred_element_type=jnp.float32
        )
        inner = jnp.sum(shares * grad_shares, axis=-1, keepdims=True)
        grad_scores = (shares * (grad_shares - inner)).astype(jnp.bfloat16)
        grad_query = (
            jnp.einsum("hqk,khd->qhd", grad_scores, keys, preferred_element_type=jnp.float32)
            * 0.125
        )
        key_sum = (
            key_sum
            + jnp.einsum("hqk,qhd->khd", grad_scores, piece, preferred_element_type=jnp.float32)
            * 0.125
        )
        value_sum = value_sum + jnp.einsum(
            "hqk,qhd->khd",
            shares.astype(jnp.bfloat16),
            grad_piece,
            preferred_element_type=jnp.float32,
        )
        return ((key_sum, value_sum), grad_query.astype(jnp.bfloat16))

    zeros = jnp.zeros(keys.shape, jnp.float32)
    (key_sum, value_sum), grad_query = lax.scan(
        one_block, (zeros, zeros), jnp.arange(length // width, dtype=jnp.int32)
    )
    return (
        grad_query.reshape(query.shape),
        key_sum.astype(jnp.bfloat16),
        value_sum.astype(jnp.bfloat16),
    )


def attend_all(query, keys, values, segments, ranks, masked):
    count = query.shape[0] // LEN

    def one_sequence(items):
        return attend_sequence(items[0], items[1], items[2], items[3], items[4], masked)

    mixed, log_total = lax.map(
        one_sequence,
        (
            split_heads(query, count),
            split_heads(keys, count),
            split_heads(values, count),
            segments,
            ranks,
        ),
    )
    return (mixed.reshape(query.shape), log_total)


def attend_back_all(query, keys, values, segments, ranks, masked, log_total, grad_mixed):
    count = query.shape[0] // LEN

    def one_sequence(items):
        return attend_sequence_back(
            items[0], items[1], items[2], items[3], items[4], masked, items[5], items[6]
        )

    grad_query, grad_keys, grad_values = lax.map(
        one_sequence,
        (
            split_heads(query, count),
            split_heads(keys, count),
            split_heads(values, count),
            segments,
            ranks,
            log_total,
            split_heads(grad_mixed, count),
        ),
    )
    return (
        grad_query.reshape(query.shape),
        grad_keys.reshape(keys.shape),
        grad_values.reshape(values.shape),
    )


def shards(
    tokens,
    encoder_states,
    output_grad,
    valid_mask,
    segment_ids,
    context_ranks,
    self_query,
    self_key,
    self_value,
    self_output,
    cross_query,
    cross_key,
    cross_value,
    cross_output,
    hidden_up,
    hidden_down,
    norm1_gain,
    norm1_bias,
    norm2_gain,
    norm2_bias,
    norm3_gain,
    norm3_bias,
):
    (
        self_query,
        self_key,
        self_value,
        self_output,
        cross_query,
        cross_key,
        cross_value,
        cross_output,
        hidden_up,
        hidden_down,
    ) = (
        lax.all_gather(self_query, "dp", axis=0, tiled=True),
        lax.all_gather(self_key, "dp", axis=0, tiled=True),
        lax.all_gather(self_value, "dp", axis=0, tiled=True),
        lax.all_gather(self_output, "dp", axis=1, tiled=True),
        lax.all_gather(cross_query, "dp", axis=0, tiled=True),
        lax.all_gather(cross_key, "dp", axis=0, tiled=True),
        lax.all_gather(cross_value, "dp", axis=0, tiled=True),
        lax.all_gather(cross_output, "dp", axis=1, tiled=True),
        lax.all_gather(hidden_up, "dp", axis=0, tiled=True),
        lax.all_gather(hidden_down, "dp", axis=1, tiled=True),
    )
    tokens_full = full_rows(tokens)
    query = jnp.dot(tokens_full, self_query, preferred_element_type=jnp.float32).astype(
        jnp.bfloat16
    )
    keys = jnp.dot(tokens_full, self_key, preferred_element_type=jnp.float32).astype(jnp.bfloat16)
    values = jnp.dot(tokens_full, self_value, preferred_element_type=jnp.float32).astype(
        jnp.bfloat16
    )
    self_mixed, self_log = attend_all(query, keys, values, segment_ids, context_ranks, True)
    attended = branch_sum(self_mixed, self_output)
    first_out, first_normal, first_scale = layer_norm(
        tokens.astype(jnp.float32) + attended, norm1_gain, norm1_bias
    )
    first_full = full_rows(first_out.astype(jnp.bfloat16))
    encoder_full = full_rows(encoder_states)
    second_query = jnp.dot(first_full, cross_query, preferred_element_type=jnp.float32).astype(
        jnp.bfloat16
    )
    encoder_keys = jnp.dot(encoder_full, cross_key, preferred_element_type=jnp.float32).astype(
        jnp.bfloat16
    )
    encoder_values = jnp.dot(encoder_full, cross_value, preferred_element_type=jnp.float32).astype(
        jnp.bfloat16
    )
    cross_mixed, cross_log = attend_all(
        second_query, encoder_keys, encoder_values, segment_ids, context_ranks, False
    )
    crossed = branch_sum(cross_mixed, cross_output)
    second_out, second_normal, second_scale = layer_norm(
        first_out + crossed, norm2_gain, norm2_bias
    )
    second_low = second_out.astype(jnp.bfloat16)
    feed_input = full_rows(second_low)
    preact = jnp.dot(feed_input, hidden_up, preferred_element_type=jnp.float32)
    activated = gelu_exact(preact).astype(jnp.bfloat16)
    feed_out = branch_sum(activated, hidden_down)
    third_out, third_normal, third_scale = layer_norm(second_out + feed_out, norm3_gain, norm3_bias)
    valid_rows = valid_mask.astype(jnp.float32)[:, None]
    grad_layer = output_grad.astype(jnp.float32) * valid_rows
    grad_third, gain3_grad, bias3_grad = norm_back(
        grad_layer, third_normal, third_scale, norm3_gain
    )
    grad_third_low = grad_third.astype(jnp.bfloat16)
    grad_feed = grad_rows(grad_third_low)
    grad_active = back_product(grad_feed, hidden_down)
    grad_preact = gelu_back(preact, grad_active).astype(jnp.bfloat16)
    up_grad = row_product(feed_input, grad_preact)
    down_grad = row_product(activated, grad_feed)
    grad_second = grad_third + input_sum([(grad_preact, hidden_up)])
    grad_second_in, gain2_grad, bias2_grad = norm_back(
        grad_second, second_normal, second_scale, norm2_gain
    )
    grad_crossed = grad_rows(grad_second_in.astype(jnp.bfloat16))
    cross_output_grad = row_product(cross_mixed, grad_crossed)
    grad_cross_mixed = back_product(grad_crossed, cross_output).astype(jnp.bfloat16)
    grad_second_query, grad_encoder_keys, grad_encoder_values = attend_back_all(
        second_query,
        encoder_keys,
        encoder_values,
        segment_ids,
        context_ranks,
        False,
        cross_log,
        grad_cross_mixed,
    )
    cross_query_grad = row_product(first_full, grad_second_query)
    cross_key_grad = row_product(encoder_full, grad_encoder_keys)
    cross_value_grad = row_product(encoder_full, grad_encoder_values)
    grad_first = grad_second_in + input_sum([(grad_second_query, cross_query)])
    encoder_grad = input_sum([(grad_encoder_keys, cross_key), (grad_encoder_values, cross_value)])
    grad_first_in, gain1_grad, bias1_grad = norm_back(
        grad_first, first_normal, first_scale, norm1_gain
    )
    grad_attended = grad_rows(grad_first_in.astype(jnp.bfloat16))
    self_output_grad = row_product(self_mixed, grad_attended)
    grad_self_mixed = back_product(grad_attended, self_output).astype(jnp.bfloat16)
    grad_query, grad_keys, grad_values = attend_back_all(
        query, keys, values, segment_ids, context_ranks, True, self_log, grad_self_mixed
    )
    self_query_grad = row_product(tokens_full, grad_query)
    self_key_grad = row_product(tokens_full, grad_keys)
    self_value_grad = row_product(tokens_full, grad_values)
    tokens_grad = grad_first_in + input_sum(
        [(grad_query, self_query), (grad_keys, self_key), (grad_values, self_value)]
    )
    (
        self_query_grad,
        self_key_grad,
        self_value_grad,
        self_output_grad,
        cross_query_grad,
        cross_key_grad,
        cross_value_grad,
        cross_output_grad,
        up_grad,
        down_grad,
    ) = (
        lax.psum_scatter(self_query_grad, "dp", scatter_dimension=0, tiled=True),
        lax.psum_scatter(self_key_grad, "dp", scatter_dimension=0, tiled=True),
        lax.psum_scatter(self_value_grad, "dp", scatter_dimension=0, tiled=True),
        lax.psum_scatter(self_output_grad, "dp", scatter_dimension=1, tiled=True),
        lax.psum_scatter(cross_query_grad, "dp", scatter_dimension=0, tiled=True),
        lax.psum_scatter(cross_key_grad, "dp", scatter_dimension=0, tiled=True),
        lax.psum_scatter(cross_value_grad, "dp", scatter_dimension=0, tiled=True),
        lax.psum_scatter(cross_output_grad, "dp", scatter_dimension=1, tiled=True),
        lax.psum_scatter(up_grad, "dp", scatter_dimension=0, tiled=True),
        lax.psum_scatter(down_grad, "dp", scatter_dimension=1, tiled=True),
    )
    norm_sums, square_sums = lax.psum(
        (
            jnp.stack([gain1_grad, bias1_grad, gain2_grad, bias2_grad, gain3_grad, bias3_grad]),
            jnp.stack(
                [
                    jnp.sum(valid_rows * third_out * third_out, axis=0),
                    jnp.sum(valid_rows * tokens_grad * tokens_grad, axis=0),
                ]
            ),
        ),
        ("dp", "tensor"),
    )
    total_tokens = tokens.shape[0] * lax.axis_size("dp") * lax.axis_size("tensor")
    valid_scales = jnp.sqrt(square_sums / total_tokens)
    return (
        third_out,
        tokens_grad,
        encoder_grad,
        self_query_grad,
        self_key_grad,
        self_value_grad,
        self_output_grad,
        cross_query_grad,
        cross_key_grad,
        cross_value_grad,
        cross_output_grad,
        up_grad,
        down_grad,
        norm_sums,
        valid_scales,
    )


MESH = pl.DeviceIdType.MESH
BF = jnp.bfloat16
F32 = jnp.float32
LOG2E = 1.4426950408889634
SCALE = 0.125 * LOG2E
CH = 512


def nn(a, b):
    return lax.dot_general(a, b, (((1,), (0,)), ((), ())), preferred_element_type=F32)


def nt(a, b):
    return lax.dot_general(a, b, (((1,), (1,)), ((), ())), preferred_element_type=F32)


def turn(x):
    return x.T


class Place:
    def __init__(self):
        self.d = lax.axis_index("dp")
        self.t = lax.axis_index("tensor")
        self.z, self.y = self.d // 2, self.d % 2
        self.x, self.c = self.t // 2, self.t % 2
        self.xt = (1 - self.x) * 2 + self.c
        self.xn = (self.d, self.xt)
        self.yn = (self.z * 2 + 1 - self.y, self.t)
        self.pair = (self.d, self.x * 2 + 1 - self.c)
        self.zn = [None] + [((((self.z + k) % 4) * 2 + self.y), self.t) for k in (1, 2, 3)]
        top = self.z // 2
        self.near = [self.z, top * (5 - self.z) + (1 - top) * (1 - self.z), 2 - top, 3 * (1 - top)]

    def plane_peer(self, i):
        x, y, c = (self.x + i // 4) % 2, (self.y + i // 2) % 2, (self.c + i) % 2
        return (self.z * 2 + y, x * 2 + c)

    def barrier(self):
        sem = pltpu.get_barrier_semaphore()
        for dev in [self.plane_peer(i) for i in range(1, 8)] + self.zn[1:]:
            pl.semaphore_signal(sem, inc=1, device_id=dev, device_id_type=MESH)
        pl.semaphore_wait(sem, 10)


def remote(src, dst, send, recv, dev):
    return pltpu.make_async_remote_copy(
        src_ref=src, dst_ref=dst, send_sem=send, recv_sem=recv, device_id=dev, device_id_type=MESH
    )


class Gather:
    def __init__(self, p, w, cols, ss, rs):
        self.p, self.w, self.cols, self.ss, self.rs = p, w, cols, ss, rs

    def col(self, t):
        return pl.ds(pl.multiple_of(t * self.cols, 128), self.cols)

    def blk(self, k, y, t):
        return self.w.at[:, self.p.near[k], y, :, self.col(t)]

    def cp(self, ref, i, dev, send=None):
        return remote(ref, ref, self.ss.at[i if send is None else send], self.rs.at[i], dev)

    def own(self):
        return self.blk(0, self.p.y, self.p.t)

    def z_send(self, k):
        p = self.p
        dev = (p.near[k] * 2 + p.y, p.t)
        return self.cp(self.own(), 15 + p.z, dev, k - 1)

    def z_recv(self, k):
        p = self.p
        ref = self.blk(k, p.y, p.t)
        return self.cp(ref, 15 + p.near[k], (p.near[k] * 2 + p.y, p.t), k - 1)

    def x_send(self, k):
        return self.cp(self.blk(k, self.p.y, self.p.t), 3 + k, self.p.xn)

    def x_recv(self, k):
        return self.cp(self.blk(k, self.p.y, self.p.xt), 3 + k, self.p.xn)

    def y_send(self, k):
        return self.cp(self.blk(k, self.p.y, self.p.t), 7 + k, self.p.yn)

    def y_recv(self, k):
        return self.cp(self.blk(k, 1 - self.p.y, self.p.t), 7 + k, self.p.yn)

    def q_send(self, k):
        if k < 2:
            return self.cp(self.blk(k, self.p.y, self.p.xt), 11 + k, self.p.yn)
        return self.cp(self.blk(k, 1 - self.p.y, self.p.t), 11 + k, self.p.xn)

    def q_recv(self, k):
        return self.cp(self.blk(k, 1 - self.p.y, self.p.xt), 11 + k, self.p.xn)

    def rail(self, i, core):
        x = self.p.x if i == 0 else 1 - self.p.x
        return self.w.at[:, :, :, :, self.col(x * 2 + core)]

    def p_send(self, i):
        return self.cp(self.rail(i, self.p.c), 1 + i, self.p.pair, 17 + i)

    def p_recv(self, i):
        return self.cp(self.rail(i, 1 - self.p.c), 1 + i, self.p.pair, 17 + i)

    def zs(self):
        for k in (1, 2, 3):
            self.z_send(k).start()

    def oxy(self):
        self.x_send(0).start()
        self.y_send(0).start()

    def plane(self, *between):
        for k in (1, 2, 3):
            self.z_recv(k).wait_recv()
            if k == 1:
                for fn in between:
                    fn()
            self.x_send(k).start()
            self.y_send(k).start()

    def corner(self):
        for k in range(4):
            self.x_recv(k).wait_recv()
            if k < 2:
                self.q_send(k).start()
            self.y_recv(k).wait_recv()
            if k >= 2:
                self.q_send(k).start()
        self.p_send(0).start()

    def cross(self):
        for k in range(4):
            self.q_recv(k).wait_recv()
        self.p_send(1).start()

    def finish(self):
        self.p_recv(0).wait_recv()
        self.p_recv(1).wait_recv()

    def drain(self):
        for k in (1, 2, 3):
            self.z_send(k).wait_send()
        for k in range(4):
            self.x_send(k).wait_send()
            self.y_send(k).wait_send()
            self.q_send(k).wait_send()
        self.p_send(0).wait_send()
        self.p_send(1).wait_send()


class Reduce:
    def __init__(self, p, g, cols, held, r1, r2, r3, out, ss, rs):
        self.p, self.g, self.cols, self.held = p, g, cols, held
        self.r1, self.r2, self.r3, self.out, self.ss, self.rs = r1, r2, r3, out, ss, rs
        self.n = g.shape[0]

    def col(self, t):
        return pl.ds(pl.multiple_of(t * self.cols, 128), self.cols)

    def cp(self, src, dst, i, dev):
        return remote(src, dst, self.ss.at[i], self.rs.at[i], dev)

    def pair_copy(self, x):
        src = self.g.at[:, :, :, :, self.col(x * 2 + 1 - self.p.c)]
        return self.cp(src, self.held.at[x], x, self.p.pair)

    def corner_copy(self, i):
        p = self.p
        src = self.held.at[1 - p.x, :, pl.ds(2 * i, 2), 1 - p.y]
        return self.cp(src, self.r1.at[i], 2 + i, p.yn if i == 0 else p.xn)

    def plane_copy(self, i):
        p = self.p
        src = self.held.at[1 - p.x, :, :, p.y] if i == 0 else self.held.at[p.x, :, :, 1 - p.y]
        return self.cp(src, self.r2.at[i], 4 + i, p.xn if i == 0 else p.yn)

    def z_copy(self, k):
        p = self.p
        src = self.held.at[p.x, :, (p.z + k) % 4, p.y]
        return self.cp(src, self.r3.at[k - 1], 5 + k, p.zn[k])

    def start(self):
        self.pair_copy(0).start()
        self.pair_copy(1).start()

    def corner(self):
        for x in (0, 1):
            self.pair_copy(x).wait_recv()
        for x in (0, 1):
            col = self.col(x * 2 + self.p.c)

            def one(j, _, x=x, col=col):
                i, z = j // 4, j % 4
                a = self.g[i, z, :, :, col].astype(F32) + self.held[x, i, z].astype(F32)
                self.held[x, i, z] = a.astype(BF)
                return 0

            def whole(i, _, x=x, col=col):
                a = self.g[i, :, :, :, col].astype(F32) + self.held[x, i].astype(F32)
                self.held[x, i] = a.astype(BF)
                return 0

            if self.cols > 128:
                lax.fori_loop(0, self.n * 4, one, 0)
            else:
                lax.fori_loop(0, self.n, whole, 0)
        self.corner_copy(0).start()
        self.corner_copy(1).start()

    def plane(self):
        p = self.p
        self.corner_copy(0).wait_recv()
        self.corner_copy(1).wait_recv()
        for i in range(self.n):
            for j in range(2):
                a = self.held[1 - p.x, i, j, p.y].astype(F32) + self.r1[0, i, j].astype(F32)
                self.held[1 - p.x, i, j, p.y] = a.astype(BF)
                b = self.held[p.x, i, 2 + j, 1 - p.y].astype(F32) + self.r1[1, i, j].astype(F32)
                self.held[p.x, i, 2 + j, 1 - p.y] = b.astype(BF)
        self.plane_copy(0).start()
        self.plane_copy(1).start()

    def along(self):
        p = self.p
        self.plane_copy(0).wait_recv()
        self.plane_copy(1).wait_recv()
        for k in (1, 2, 3):
            zt = (p.z + k) % 4
            for i in range(self.n):
                a = (
                    self.held[p.x, i, zt, p.y].astype(F32)
                    + self.r2[0, i, zt].astype(F32)
                    + self.r2[1, i, zt].astype(F32)
                )
                self.held[p.x, i, zt, p.y] = a.astype(BF)
            self.z_copy(k).start()

    def finish(self):
        p = self.p
        for k in (1, 2, 3):
            self.z_copy(k).wait_recv()
        for i in range(self.n):
            a = (
                self.held[p.x, i, p.z, p.y].astype(F32)
                + self.r2[0, i, p.z].astype(F32)
                + self.r2[1, i, p.z].astype(F32)
            )
            for k in range(3):
                a = a + self.r3[k, i].astype(F32)
            self.out[i] = a

    def drain(self):
        for i in (0, 1):
            self.pair_copy(i).wait_send()
            self.corner_copy(i).wait_send()
            self.plane_copy(i).wait_send()
        for k in (1, 2, 3):
            self.z_copy(k).wait_send()


class Tail:
    def __init__(self, p, gt, hp, hx, hy, hz, hc, out, ss, rs):
        self.p, self.gt, self.hp, self.hx, self.hy, self.hz, self.hc = p, gt, hp, hx, hy, hz, hc
        self.out, self.ss, self.rs = out, ss, rs

    def cp(self, src, dst, i, dev):
        return remote(src, dst, self.ss.at[i], self.rs.at[i], dev)

    def pair_copy(self, j):
        return self.cp(self.gt.at[j], self.hp.at[j // 2], j, self.p.pair)

    def x_copy(self, j):
        if j == 1:
            return self.cp(self.gt.at[1, :, :, self.p.y], self.hx.at[:, :, 0], 4, self.p.xn)
        return self.cp(self.gt.at[0], self.hx, 4, self.p.xn)

    def corner_copy(self):
        return self.cp(self.gt.at[1, :, :, 1 - self.p.y], self.hc, 9, self.p.yn)

    def y_copy(self, j):
        return self.cp(self.gt.at[j, :, :, 1 - self.p.y], self.hy, 5, self.p.yn)

    def z_copy(self, j, k):
        p = self.p
        return self.cp(self.gt.at[j, :, (p.z + k) % 4, p.y], self.hz.at[k - 1], 5 + k, p.zn[k])

    def mine(self, j, fn):
        pl.when(self.p.c == j % 2)(fn)

    def start(self, j):
        pl.when(self.p.c != j % 2)(lambda: self.pair_copy(j).start())

    def sum_pair(self, j):
        def do():
            self.pair_copy(j).wait_recv()
            if j == 2:
                self.x_copy(0).wait_recv()
            for w in range(3):
                a = self.gt[j, w].astype(F32) + self.hp[j // 2, w].astype(F32)
                if j == 2:
                    a = a + self.hx[w].astype(F32)
                self.gt[j, w] = a.astype(BF)
            if j == 0:
                self.x_copy(0).start()
            elif j == 1:
                self.corner_copy().start()
            else:
                self.y_copy(j).start()

        self.mine(j, do)

    def corner(self):
        def do():
            self.corner_copy().wait_recv()
            y = self.p.y
            for w in range(3):
                a = self.gt[1, w, :, y].astype(F32) + self.hc[w].astype(F32)
                self.gt[1, w, :, y] = a.astype(BF)
            self.x_copy(1).start()

        self.mine(1, do)

    def sum_y(self, j):
        def do():
            p = self.p
            self.y_copy(j).wait_recv()
            if j == 3:
                self.x_copy(1).wait_recv()
            for i in range(3):
                for k in (1, 2, 3):
                    zt = (p.z + k) % 4
                    a = self.gt[j, i, zt, p.y].astype(F32) + self.hy[i, zt].astype(F32)
                    if j == 3:
                        a = a + self.hx[i, zt, 0].astype(F32)
                    self.gt[j, i, zt, p.y] = a.astype(BF)
            for k in (1, 2, 3):
                self.z_copy(j, k).start()

        self.mine(j, do)

    def finish(self, j):
        def do():
            p = self.p
            for k in (1, 2, 3):
                self.z_copy(j, k).wait_recv()
            for i in range(3):
                a = self.gt[j, i, p.z, p.y].astype(F32) + self.hy[i, p.z].astype(F32)
                if j == 3:
                    a = a + self.hx[i, p.z, 0].astype(F32)
                for k in range(3):
                    a = a + self.hz[k, i].astype(F32)
                self.out[i] = a

        self.mine(j, do)

    def drain(self):
        for j in range(4):
            pl.when(self.p.c != j % 2)(lambda j=j: self.pair_copy(j).wait_send())

        def sent(j):
            self.x_copy(j).wait_send()
            if j == 1:
                self.corner_copy().wait_send()
            self.y_copy(j + 2).wait_send()
            for k in (1, 2, 3):
                self.z_copy(j + 2, k).wait_send()

        for j in (0, 1):
            self.mine(j, lambda j=j: sent(j))


def row_steps(count, one):
    def body(i, _):
        one(pl.ds(pl.multiple_of(i * CH, CH), CH))
        return 0

    lax.fori_loop(0, count // CH, body, 0)


def head_half(shape, axis, h):
    return (lax.broadcasted_iota(jnp.int32, shape, axis) // HEAD) == h


def keep_half(value, axis, h):
    return jnp.where(head_half(value.shape, axis, h), value.astype(F32), 0.0).astype(BF)


def run_hooks(hooks, step, half):
    for (at, part), hook in hooks.items():
        if part == half:
            pl.when(step == at)(hook)


def attend(qt, k, vt, bias, ot, lse, temp, hooks):
    def ready(p, h):
        lanes = pl.ds(pl.multiple_of(p * 128, 128), 128)
        return k[:, lanes], keep_half(qt[lanes, :], 0, h)

    def score(kp, qm, h, i, top):
        s = nn(kp[i * 512 : i * 512 + 512], qm) * SCALE
        if bias is not None:
            s = s + bias[i * 512 : i * 512 + 512, :]
        temp[h * 1024 + i * 512 : h * 1024 + i * 512 + 512, :] = s
        m = jnp.max(s, axis=0, keepdims=True)
        return m if top is None else jnp.maximum(top, m)

    def mix(vh, h, i, top, total, mixed):
        e = jnp.exp2(temp[h * 1024 + i * 512 : h * 1024 + i * 512 + 512, :] - top)
        part = jnp.sum(e, axis=0, keepdims=True)
        o = nn(vh[:, i * 512 : i * 512 + 512], e.astype(BF))
        return (part, o) if total is None else (total + part, mixed + o)

    def pair(p, top):
        for h in (0, 1):
            kp, qm = ready(p if h == 0 else (p + 1) % 4, 1 - h)
            vh = vt[pl.ds(pl.multiple_of(p * 128 + h * 64, 64), 64), :]
            total = mixed = later = None
            for i in range(2):
                later = score(kp, qm, 1 - h, i, later)
                total, mixed = mix(vh, h, i, top, total, mixed)
            ot[pl.ds(pl.multiple_of(p * 128 + h * 64, 64), 64), :] = mixed * (1.0 / total)
            lse[pl.ds(p * 2 + h, 1), :] = top + jnp.log2(total)
            top = later
            run_hooks(hooks, p, h)
        return top

    kp, qm = ready(0, 0)
    top = None
    for i in range(2):
        top = score(kp, qm, 0, i, top)
    lax.fori_loop(0, 4, pair, top)


def attend_back(q, qt, k, kt, v, do, dot_, ot, bias, lse, dqt, dk_own, dv_own, dkv_send, order, hooks):
    def pair(step, _):
        p = order(step)
        lanes = pl.ds(pl.multiple_of(p * 128, 128), 128)
        kp, vp = k[:, lanes], v[:, lanes]
        qp, dop = qt[lanes, :], dot_[lanes, :]
        inner = dop.astype(F32) * ot[lanes, :]
        qms = [keep_half(qp, 0, h) for h in (0, 1)]
        doms = [keep_half(dop, 0, h) for h in (0, 1)]
        qr = jnp.concatenate([keep_half(q[:, lanes], 1, h) for h in (0, 1)], axis=0)
        dor = jnp.concatenate([keep_half(do[:, lanes], 1, h) for h in (0, 1)], axis=0)
        ds_sum = [jnp.sum(inner[h * 64 : h * 64 + 64], axis=0, keepdims=True) for h in (0, 1)]
        logs = [lse[pl.ds(p * 2 + h, 1), :] for h in (0, 1)]
        shares, grads = {}, {}
        dq = [None, None]
        dvs, dks = {}, {}

        def one(h, i):
            rows = slice(i * 256, i * 256 + 256)
            s = nn(kp[rows], qms[h]) * SCALE
            if bias is not None:
                s = s + bias[rows, :]
            e = jnp.exp2(s - logs[h])
            dp = nn(vp[rows], doms[h])
            shares[h, i] = e.astype(BF)
            grads[h, i] = (e * (dp - ds_sum[h])).astype(BF)

        def two(h, i):
            rows = slice(i * 256, i * 256 + 256)
            kh = kt[pl.ds(pl.multiple_of(p * 128 + h * 64, 64), 64), rows]
            part = nn(kh, grads[h, i])
            dq[h] = part if dq[h] is None else dq[h] + part
            dv = nn(shares[h, i], dor[h * 512 : h * 512 + 512])
            dk = nn(grads[h, i], qr[h * 512 : h * 512 + 512])
            dvs[i] = dv if i not in dvs else dvs[i] + dv
            dks[i] = dk if i not in dks else dks[i] + dk

        def out(i):
            rows = slice(i * 256, i * 256 + 256)
            if i < 2:
                dk_own[rows, lanes] = (dks[i] * 0.125).astype(dk_own.dtype)
                dv_own[rows, lanes] = dvs[i].astype(dv_own.dtype)
            else:
                back = slice(i * 256 - 512, i * 256 - 256)
                dkv_send[0, back, lanes] = (dks[i] * 0.125).astype(BF)
                dkv_send[1, back, lanes] = dvs[i].astype(BF)

        for i in range(4):
            one(0, i)
        for i in range(4):
            one(1, i)
            two(0, i)
        run_hooks(hooks, step, 0)
        for i in range(4):
            two(1, i)
            out(i)
        for h in (0, 1):
            dqt[pl.ds(pl.multiple_of(p * 128 + h * 64, 64), 64), :] = (dq[h] * 0.125).astype(BF)
        run_hooks(hooks, step, 1)
        return 0

    lax.fori_loop(0, 4, pair, 0)


def norm_rows(z):
    mean = jnp.mean(z, axis=-1, keepdims=True)
    centred = z - mean
    r = lax.rsqrt(jnp.mean(centred * centred, axis=-1, keepdims=True) + norm_eps)
    return centred * r, r


def norm_back_rows(e, n, r, gain):
    s = e * gain
    a = jnp.mean(s, axis=-1, keepdims=True)
    b = jnp.mean(s * n, axis=-1, keepdims=True)
    return r * (s - a - n * b)


def fast_kernel(
    x_i, enc_i, og_i, valid, seg, rank,
    sq, sk, sv, so, cq, ck, cv, co, up, down,
    g1, b1, g2, b2, g3, b3,
    y_o, dx_o, eg_o, ga_o, gb_o, gf_o, ns_o, vs_o,
    xs, enc, og, codes, wa, wb, wf, gt,
    q1, qt1, k1, v1, vt1, o1, ot1, l1,
    q2, qt2, k2, v2, vt2, o2, ot2, l2,
    bias, n1, n2, h1b, h2b, u, gp, dg, dz, low, lowt, do, dot_,
    kvs, kvr1, kvr2, tt, yb, row, st,
    hc, hq, hu, hd, c1, c2, c3, p1, p2, p3, u1, u2, u3, d1, d2, d3, hp, hx, hy, hz, hcn,
    st_r, gss, grs, rss, rrs, aas, ars, ess, ers, tss, trs, ls,
):
    dqt, dq = h2b, q2
    x = xs.at[pl.ds(0, 512)]
    dkv = [v2.at[pl.ds(0, 512)], v2.at[pl.ds(512, 512)]]
    p = Place()
    loads = []
    for i, (src, w, j, cols) in enumerate(
        (
            (sq, wa, 0, 128), (sk, wa, 1, 128), (sv, wa, 2, 128),
            (so, wb, 0, 128), (co, wb, 1, 128), (cq, wb, 2, 128), (ck, wb, 3, 128), (cv, wb, 4, 128),
            (up, wf, 0, 512), (down, wf, 1, 512),
        )
    ):
        col = pl.ds(pl.multiple_of(p.t * cols, 128), cols)
        loads.append(pltpu.make_async_copy(src, w.at[j, p.z, p.y, :, col], ls.at[i]))
    for i, (src, dst) in enumerate(((x_i, x), (enc_i, enc), (og_i, og))):
        loads.append(pltpu.make_async_copy(src, dst, ls.at[10 + i]))
    for cp in loads:
        cp.start()
    p.barrier()
    GA, GB, GU, GD = G = [
        Gather(p, w, cols, gss.at[i], grs.at[i])
        for i, (w, cols) in enumerate(
            ((wa, 128), (wb, 128), (wf.at[pl.ds(0, 1)], 512), (wf.at[pl.ds(1, 1)], 512))
        )
    ]
    for cp in loads[:3]:
        cp.wait()
    GA.zs()
    GA.oxy()
    for cp in loads[3:]:
        cp.wait()
    halves = remote(
        xs.at[pl.ds(0, 512)], xs.at[pl.ds(512, 512)], ess.at[9], ers.at[9], p.pair
    )
    halves.start()
    GB.oxy()

    def mat(w, j):
        return w[j].reshape(512, w.shape[4])

    st[...] = jnp.zeros_like(st)
    row[...] = jnp.broadcast_to(valid[...].astype(F32), (128, 512)).T
    own = pl.ds(pl.multiple_of(p.c * 512, 128), 512)
    other = pl.ds(pl.multiple_of((1 - p.c) * 512, 128), 512)
    sx = pl.ds(p.x, 1)
    ranks = rank[sx, :]
    codes[1:2, :] = seg[sx, :] * 8
    codes[0:1, :] = seg[sx, :] * 8 + jnp.concatenate(
        [jnp.broadcast_to(ranks[:, b : b + 1], (1, 128)) for b in range(8)], axis=1
    )
    base, high = codes[1:2, own], codes[0:1, own]
    for i, half in enumerate((own, other)):
        code = jnp.broadcast_to(codes[0:1, half], (128, 512)).T
        for j in range(4):
            c = code[j * 128 : j * 128 + 128, :1]
            ok = (c >= base) & (c <= high)
            bias[i * 512 + j * 128 : i * 512 + j * 128 + 128, :] = jnp.where(ok, 0.0, -2.0e9)

    GA.plane(GB.zs)
    GU.oxy()
    GA.corner()
    GU.zs()
    GD.oxy()
    GA.cross()
    GB.plane()
    GA.finish()
    GD.zs()

    def swap(buf, i):
        return remote(buf.at[pl.ds(0, 512)], buf.at[pl.ds(512, 512)], ess.at[i], ers.at[i], p.pair)

    halves.wait()
    xv = xs[...]
    k1[...] = nn(xv, mat(wa, 1)).astype(BF)
    vv = nn(xv, mat(wa, 2)).astype(BF)
    v1[...] = vv
    vt1[...] = turn(vv)
    xv = x[...]
    qv = nn(xv, mat(wa, 0)).astype(BF)
    q1[...] = qv
    qt1[...] = turn(qv)
    attend(qt1, k1, vt1, bias, ot1, l1, gp, {(0, 0): GB.corner, (1, 0): GU.plane, (2, 0): GB.cross, (3, 0): GD.plane})
    o1[...] = turn(ot1[...].astype(BF))
    vt1[...] = turn(k1[...])
    GB.finish()
    ev = enc[...]
    k2[0:512, :] = nn(ev, mat(wb, 3)).astype(BF)
    v2[0:512, :] = nn(ev, mat(wb, 4)).astype(BF)
    swap(k2, 2).start()
    swap(v2, 3).start()
    yb[...] = nt(o1[...], mat(wb, 0))
    GU.corner()

    def first(r):
        n, s = norm_rows(x[r, :].astype(F32) + yb[r, :])
        n1[r, :] = n
        row[r, 0:1] = s
        h1b[r, :] = (n * g1[...] + b1[...]).astype(BF)

    row_steps(512, first)
    qv = nn(h1b[...], mat(wb, 2)).astype(BF)
    q2[...] = qv
    qt2[...] = turn(qv)
    swap(k2, 2).wait_recv()
    swap(v2, 3).wait_recv()
    vt2[...] = turn(v2[...])
    attend(qt2, k2, vt2, None, ot2, l2, gp, {(0, 1): GD.corner, (2, 1): GU.cross})
    o2[...] = turn(ot2[...].astype(BF))
    vt2[...] = turn(k2[...])
    yb[...] = nt(o2[...], mat(wb, 1))

    def second(r):
        n, s = norm_rows(n1[r, :] * g1[...] + b1[...] + yb[r, :])
        n2[r, :] = n
        row[r, 1:2] = s
        h2b[r, :] = (n * g2[...] + b2[...]).astype(BF)

    row_steps(512, second)
    tt[...] = turn(h2b[...])
    hv = h2b[...]
    blocks = [p.t, p.pair[1], p.xt, (1 - p.x) * 2 + 1 - p.c]
    waits = [None, GU.p_recv(0).wait_recv, GD.cross, GU.p_recv(1).wait_recv]
    for t, wait in zip(blocks, waits):
        if wait is not None:
            wait()
        cols = pl.ds(pl.multiple_of(t * 512, 512), 512)
        gp[cols, :] = nn(hv, wf[0, :, :, :, cols].reshape(512, 512))

        def gelu(r, cols=cols, t=t):
            at = pl.ds(pl.multiple_of(r.start + t * 512, CH), CH)
            v = gp[at, :]
            cdf = 0.5 * (1.0 + lax.erf(v * 0.7071067811865476))
            u[r, cols] = (v * cdf).astype(BF)
            gp[at, :] = cdf + v * (jnp.exp2(v * v * (-0.5 * LOG2E)) * 0.3989422804014327)

        row_steps(512, gelu)
    waits = [None, GD.p_recv(0).wait_recv, None, GD.p_recv(1).wait_recv]
    for i, (t, wait) in enumerate(zip(blocks, waits)):
        if wait is not None:
            wait()
        cols = pl.ds(pl.multiple_of(t * 512, 512), 512)
        part = nt(u[:, cols], wf[1, :, :, :, cols].reshape(512, 512))
        yb[...] = part if i == 0 else yb[...] + part

    def third(r):
        n, s = norm_rows(n2[r, :] * g2[...] + b2[...] + yb[r, :])
        out = n * g3[...] + b3[...]
        vc = row[r, 2:3]
        yb[r, :] = out
        e = og[r, :].astype(F32) * vc
        st[4:5, :] += jnp.sum(e * n, axis=0, keepdims=True)
        st[5:6, :] += jnp.sum(e, axis=0, keepdims=True)
        st[6:7, :] += jnp.sum(vc * out * out, axis=0, keepdims=True)
        back = norm_back_rows(e, n, s, g3[...])
        dz[r, :] = back
        low[r, :] = back.astype(BF)

    row_steps(512, third)
    y_copy = pltpu.make_async_copy(yb, y_o, ls.at[0])
    y_copy.start()
    lv = low[...]
    lowt[...] = turn(lv)
    for g in G:
        g.drain()
    RC, RP, RU, RD = R = [
        Reduce(p, w.at[pl.ds(at, n)], cols, *bufs, out.at[pl.ds(at, n)], rss.at[i], rrs.at[i])
        for i, (w, at, n, cols, bufs, out) in enumerate(
            (
                (wb, 0, 2, 128, (hc, c1, c2, c3), gb_o),
                (wb, 2, 3, 128, (hq, p1, p2, p3), gb_o),
                (wf, 0, 1, 512, (hu, u1, u2, u3), gf_o),
                (wf, 1, 1, 512, (hd, d1, d2, d3), gf_o),
            )
        )
    ]
    for j in range(4):
        cols = slice(j * 512, j * 512 + 512)
        dg[:, cols] = (nn(lv, wf[1, :, :, :, cols].reshape(512, 512)) * gp[cols, :]).astype(BF)
        wf[1, :, :, :, cols] = nn(lowt[...], u[:, cols]).astype(BF).reshape(4, 2, 64, 512)
        if j % 2 == 1:
            RD.pair_copy(j // 2).start()
    dz[...] += nt(dg[...], mat(wf, 0))
    for j in range(4):
        cols = slice(j * 512, j * 512 + 512)
        wf[0, :, :, :, cols] = nn(tt[...], dg[:, cols]).astype(BF).reshape(4, 2, 64, 512)
    RU.start()
    RD.corner()

    def back2(r):
        e = dz[r, :]
        n = n2[r, :]
        st[2:3, :] += jnp.sum(e * n, axis=0, keepdims=True)
        st[3:4, :] += jnp.sum(e, axis=0, keepdims=True)
        back = norm_back_rows(e, n, row[r, 1:2], g2[...])
        dz[r, :] = back
        low[r, :] = back.astype(BF)

    row_steps(512, back2)
    dov = nn(low[...], mat(wb, 1)).astype(BF)
    do[...] = dov
    dot_[...] = turn(dov)
    lowt[...] = turn(low[...])
    wb[1] = nn(lowt[...], o2[...]).astype(BF).reshape(4, 2, 64, 512)
    RU.corner()
    attend_back(
        q2, qt2, k2, vt2, v2, do, dot_, ot2, None, l2, dqt,
        gp.at[pl.ds(0, 512)], gp.at[pl.ds(512, 512)], kvs.at[:, pl.ds(512, 512)], lambda step: step,
        {(0, 0): RD.plane, (1, 0): RU.plane, (3, 0): RD.along},
    )

    def swap_back(buf, i):
        return remote(kvs.at[:, pl.ds(512, 512)], buf, ess.at[i], ers.at[i], p.pair)

    swap_back(kvr2, 4).start()
    dqv = turn(dqt[...])
    dz[...] += nt(dqv, mat(wb, 2))
    tt[...] = turn(h1b[...])
    wb[2] = nn(tt[...], dqv).astype(BF).reshape(4, 2, 64, 512)
    tt[...] = turn(enc[...])
    swap_back(kvr2, 4).wait()
    for i in (2, 3):
        swap((k1, v1, k2, v2)[i], i).wait_send()

    def join(recv, at):
        def one(r):
            for i in (0, 1):
                own_rows = pl.ds(pl.multiple_of(r.start + at + i * 512, CH), CH)
                dkv[i][r, :] = (gp[own_rows, :] + recv[i, r, :].astype(F32)).astype(BF)

        row_steps(512, one)

    join(kvr2, 0)
    y_copy.wait()
    yb[...] = nt(dkv[0][...], mat(wb, 3)) + nt(dkv[1][...], mat(wb, 4))
    e_copy = pltpu.make_async_copy(yb, eg_o, ls.at[0])
    e_copy.start()
    wb[3] = nn(tt[...], dkv[0][...]).astype(BF).reshape(4, 2, 64, 512)
    wb[4] = nn(tt[...], dkv[1][...]).astype(BF).reshape(4, 2, 64, 512)
    RP.start()

    def back1(r):
        e = dz[r, :]
        n = n1[r, :]
        st[0:1, :] += jnp.sum(e * n, axis=0, keepdims=True)
        st[1:2, :] += jnp.sum(e, axis=0, keepdims=True)
        back = norm_back_rows(e, n, row[r, 0:1], g1[...])
        dz[r, :] = back
        low[r, :] = back.astype(BF)

    row_steps(512, back1)
    RU.along()
    dov = nn(low[...], mat(wb, 0)).astype(BF)
    do[...] = dov
    dot_[...] = turn(dov)
    lowt[...] = turn(low[...])
    wb[0] = nn(lowt[...], o1[...]).astype(BF).reshape(4, 2, 64, 512)
    RC.start()
    RP.corner()
    vt2[...] = turn(xs[...])
    T = Tail(p, gt, hp, hx, hy, hz, hcn, ga_o, aas, ars)

    def order(step):
        far = (step // 2) * p.x + (1 - step // 2) * (1 - p.x)
        return 2 * far + step % 2

    def lanes_of(step):
        return pl.ds(pl.multiple_of(order(step) * 128, 128), 128)

    def part_back(step):
        at = lanes_of(step)
        return remote(
            kvs.at[:, pl.ds(512, 512), at], kvr1.at[:, :, at], ess.at[5 + step], ers.at[5 + step], p.pair
        )

    def grads(step):
        at = lanes_of(step)
        dqv = turn(dqt[at, :])
        dq[:, at] = dqv
        gt[step, 0] = nn(vt2[:, 0:512], dqv).astype(BF).reshape(4, 2, 64, 128)
        gt[step, 1] = nn(vt2[...], kvs[0, :, at]).astype(BF).reshape(4, 2, 64, 128)
        gt[step, 2] = nn(vt2[...], kvs[1, :, at]).astype(BF).reshape(4, 2, 64, 128)
        T.start(step)

    def both(*fns):
        def run():
            for fn in fns:
                fn()

        return run

    attend_back(
        q1, qt1, k1, vt1, v1, do, dot_, ot1, bias, l1, dqt,
        kvs.at[0, pl.ds(0, 512)], kvs.at[1, pl.ds(0, 512)], kvs.at[:, pl.ds(512, 512)], order,
        {
            (0, 0): RC.corner,
            (0, 1): both(lambda: part_back(0).start(), lambda: grads(0), RP.plane),
            (1, 0): lambda: T.sum_pair(0),
            (1, 1): both(lambda: part_back(1).start(), lambda: grads(1), RC.plane, RD.finish),
            (2, 0): lambda: T.sum_pair(1),
            (2, 1): both(lambda: part_back(2).start(), lambda: grads(2), RP.along, RU.finish),
            (3, 0): lambda: T.sum_pair(2),
            (3, 1): both(lambda: part_back(3).start(), T.corner, RC.along),
        },
    )
    grads(3)
    T.sum_y(2)
    dz[...] += nt(dq[...], mat(wa, 0))
    for step in range(4):
        part_back(step).wait_recv()

    def join_last(r):
        for i in (0, 1):
            dkv[i][r, :] = (kvs[i, r, :].astype(F32) + kvr1[i, r, :].astype(F32)).astype(BF)

    row_steps(512, join_last)
    T.sum_pair(3)
    dz[...] += nt(dkv[0][...], mat(wa, 1)) + nt(dkv[1][...], mat(wa, 2))
    x_copy = pltpu.make_async_copy(dz, dx_o, ls.at[1])
    x_copy.start()

    def squares(r):
        st[7:8, :] += jnp.sum(row[r, 2:3] * dz[r, :] * dz[r, :], axis=0, keepdims=True)

    row_steps(512, squares)

    stats = []
    st_r[0] = st[...]
    for i in range(1, 8):
        stats.append(remote(st, st_r.at[i], tss.at[i], trs.at[i], p.plane_peer(i)))
    for cp in stats:
        cp.start()
    T.sum_y(3)
    for cp in stats:
        cp.wait()
    total = None
    for i in range(8):
        x, y, c = (p.x + i // 4) % 2, (p.y + i // 2) % 2, (p.c + i) % 2
        part = st_r[x * 4 + y * 2 + c]
        total = part if total is None else total + part
    st_r[8 + p.z] = total
    stats = []
    for k in (1, 2, 3):
        at = st_r.at[8 + p.z]
        stats.append((remote(at, at, tss.at[7 + k], trs.at[7 + k], p.zn[k]), k))
    for cp, _ in stats:
        cp.start()
    RP.finish()
    RC.finish()
    T.finish(2)
    for cp, k in stats:
        cp.wait_send()
        back = st_r.at[8 + (p.z - k + 4) % 4]
        remote(back, back, tss.at[7 + k], trs.at[7 + k], p.zn[k]).wait_recv()
    T.finish(3)
    total = st_r[8] + st_r[9] + st_r[10] + st_r[11]
    ns_o[...] = total[0:6]
    vs_o[...] = jnp.sqrt(total[6:8] * (1.0 / 16384.0))
    for step in range(4):
        part_back(step).wait_send()
    for r in R:
        r.drain()
    T.drain()
    e_copy.wait()
    x_copy.wait()


def place_kernel(*refs):
    srcs, outs, held, sems = refs[:8], refs[8:23], refs[23:31], refs[31]
    parts = [held[0], held[1], held[2]] + [held[3].at[i] for i in range(3)]
    parts += [held[4].at[i] for i in range(5)] + [held[5].at[i] for i in range(2)] + [held[6], held[7]]
    first = [pltpu.make_async_copy(a, b, sems.at[i]) for i, (a, b) in enumerate(zip(srcs, held))]
    last = [pltpu.make_async_copy(a, b, sems.at[8 + i]) for i, (a, b) in enumerate(zip(parts, outs))]
    ends = [(0, 1), (1, 2), (2, 3), (3, 6), (6, 11), (11, 13), (13, 14), (14, 15)]
    order = (6, 7, 3, 4, 5, 0, 1, 2)
    for i in order:
        first[i].start()
    for i in order:
        first[i].wait()
        for cp in last[ends[i][0] : ends[i][1]]:
            cp.start()
    for cp in last:
        cp.wait()


def fast_shards(
    tokens, encoder_states, output_grad, valid_mask, segment_ids, context_ranks,
    self_query, self_key, self_value, self_output,
    cross_query, cross_key, cross_value, cross_output, hidden_up, hidden_down,
    norm1_gain, norm1_bias, norm2_gain, norm2_bias, norm3_gain, norm3_bias,
):
    vm = pl.BlockSpec(memory_space=pltpu.VMEM)
    hbm = pl.BlockSpec(memory_space=pl.ANY)
    rows = [
        v.reshape(1, 512)
        for v in (norm1_gain, norm1_bias, norm2_gain, norm2_bias, norm3_gain, norm3_bias)
    ]

    def V(*shape, dtype=BF):
        return pltpu.VMEM(shape, dtype)

    def S(*shape):
        return pltpu.SemaphoreType.DMA(shape)

    def group(n, cols):
        return [
            V(2, n, 4, 2, 64, cols),
            [V(2, n, 2, 64, cols), V(2, n, 4, 64, cols), V(3, n, 64, cols)],
        ]

    rc, rp, ru, rd = group(2, 128), group(3, 128), group(1, 512), group(1, 512)

    def attention():
        return [
            V(512, 512), V(512, 512), V(1024, 512), V(1024, 512), V(512, 1024), V(512, 512),
            V(512, 512, dtype=F32), V(8, 512, dtype=F32),
        ]

    scratch = (
        [V(1024, 512), V(512, 512), V(512, 512)]
        + [V(8, 1024, dtype=jnp.int32)]
        + [V(3, 4, 2, 64, 512), V(5, 4, 2, 64, 512), V(2, 4, 2, 64, 2048), V(4, 3, 4, 2, 64, 128)]
        + attention()
        + attention()
        + [V(1024, 512, dtype=F32), V(512, 512, dtype=F32), V(512, 512, dtype=F32)]
        + [V(512, 512), V(512, 512)]
        + [V(512, 2048), V(2048, 512, dtype=F32), V(512, 2048), V(512, 512, dtype=F32)]
        + [V(512, 512)] * 4
        + [V(2, 1024, 512), V(2, 512, 512), V(2, 512, 512)]
        + [V(512, 512), V(512, 512, dtype=F32), V(512, 128, dtype=F32), V(8, 512, dtype=F32)]
        + [rc[0], rp[0], ru[0], rd[0]]
        + rc[1] + rp[1] + ru[1] + rd[1]
        + [V(2, 3, 4, 2, 64, 128), V(3, 4, 2, 64, 128), V(3, 4, 64, 128), V(3, 3, 64, 128), V(3, 4, 64, 128)]
        + [V(12, 8, 512, dtype=F32)]
        + [S(4, 19), S(4, 19), S(4, 9), S(4, 9), S(10), S(10), S(10), S(10), S(11), S(11), S(13)]
    )
    big = jax.ShapeDtypeStruct((512, 512), F32)
    outs = pl.pallas_call(
        fast_kernel,
        out_shape=[big, big, big]
        + [jax.ShapeDtypeStruct(s, F32) for s in ((3, 64, 128), (5, 64, 128), (2, 64, 512), (6, 512), (2, 512))],
        in_specs=[hbm] * 3 + [vm] * 3 + [hbm] * 10 + [vm] * 6,
        out_specs=[hbm] * 3 + [vm] * 5,
        scratch_shapes=scratch,
        compiler_params=pltpu.CompilerParams(
            collective_id=0, has_side_effects=True, vmem_limit_bytes=63 << 20
        ),
        name="layer",
    )(
        tokens, encoder_states, output_grad, valid_mask.reshape(1, 512), segment_ids, context_ranks,
        self_query, self_key, self_value, self_output.T,
        cross_query, cross_key, cross_value, cross_output.T, hidden_up, hidden_down.T, *rows,
    )
    ends = [big, big, big] + [jax.ShapeDtypeStruct((64, 128), F32)] * 8
    ends += [jax.ShapeDtypeStruct((64, 512), F32)] * 2
    ends += [jax.ShapeDtypeStruct(v, F32) for v in ((6, 512), (2, 512))]
    y, dx, eg, dsq, dsk, dsv, dso, dco, dcq, dck, dcv, dup, ddown, ns, vs = pl.pallas_call(
        place_kernel,
        out_shape=ends,
        in_specs=[hbm] * 8,
        out_specs=[hbm] * 15,
        scratch_shapes=[pltpu.VMEM(o.shape, F32) for o in outs] + [S(23)],
        name="place",
    )(*outs)
    return (
        y, dx, eg, dsq, dsk, dsv, dso.T, dcq, dck, dcv, dco.T, dup, ddown.T, ns, vs,
    )


def solution(mesh):
    in_specs = (
        P(("dp", "tensor"), None),
        P(("dp", "tensor"), None),
        P(("dp", "tensor"), None),
        P(("dp", "tensor")),
        P("dp", None),
        P("dp", None),
        P("dp", "tensor"),
        P("dp", "tensor"),
        P("dp", "tensor"),
        P("tensor", "dp"),
        P("dp", "tensor"),
        P("dp", "tensor"),
        P("dp", "tensor"),
        P("tensor", "dp"),
        P("dp", "tensor"),
        P("tensor", "dp"),
        P(),
        P(),
        P(),
        P(),
        P(),
        P(),
    )
    out_specs = (
        P(("dp", "tensor"), None),
        P(("dp", "tensor"), None),
        P(("dp", "tensor"), None),
        P("dp", "tensor"),
        P("dp", "tensor"),
        P("dp", "tensor"),
        P("tensor", "dp"),
        P("dp", "tensor"),
        P("dp", "tensor"),
        P("dp", "tensor"),
        P("tensor", "dp"),
        P("dp", "tensor"),
        P("tensor", "dp"),
        P(),
        P(),
    )
    body = fast_shards if dict(mesh.shape) == {"dp": 8, "tensor": 4} else shards
    return jax.shard_map(body, mesh=mesh, in_specs=in_specs, out_specs=out_specs, check_vma=False)
```

```python
import jax
import jax.numpy as jnp
from jax import lax
from jax.experimental import pallas as pl
from jax.experimental.pallas import tpu as pltpu
from jax.sharding import PartitionSpec as P

HEAD = 64
LEN = 1024
BLK = 128


norm_eps = 1e-05
mask_fill = -1000000000.0


def gelu_exact(value):
    return jax.nn.gelu(value, approximate=False)


def gelu_back(preact, upstream):
    return jax.vjp(gelu_exact, preact)[1](upstream)[0]


def layer_norm(value, gain, bias):
    mean = jnp.mean(value, axis=-1, keepdims=True)
    centred = value - mean
    scale = lax.rsqrt(jnp.mean(centred * centred, axis=-1, keepdims=True) + norm_eps)
    normal = centred * scale
    return (normal * gain + bias, normal, scale)


def norm_back(upstream, normal, scale, gain):
    scaled = upstream * gain
    mean_grad = jnp.mean(scaled, axis=-1, keepdims=True)
    mean_cross = jnp.mean(scaled * normal, axis=-1, keepdims=True)
    inward = scale * (scaled - mean_grad - normal * mean_cross)
    return (inward, jnp.sum(upstream * normal, axis=0), jnp.sum(upstream, axis=0))


def context_allowed(segments, ranks, first, count):
    length = segments.shape[0]
    key_block = jnp.arange(length, dtype=jnp.int32) // BLK
    key_rank = jnp.broadcast_to(ranks[:, None], (ranks.shape[0], BLK)).reshape(length)
    query_segment = lax.dynamic_slice_in_dim(segments, first, count)
    query_rank = lax.dynamic_slice_in_dim(key_rank, first, count)
    query_block = (first + jnp.arange(count, dtype=jnp.int32)) // BLK
    same_doc = query_segment[:, None] == segments[None, :]
    earlier = key_rank[None, :] < query_rank[:, None]
    same_block = query_block[:, None] == key_block[None, :]
    return same_doc & (earlier | same_block)


def full_rows(value):
    return lax.all_gather(value, "tensor", axis=0, tiled=True)


def grad_rows(value):
    return lax.all_gather(value, "tensor", axis=0, tiled=True)


def branch_sum(mixed, weight):
    return lax.psum_scatter(
        jnp.dot(mixed, weight, preferred_element_type=jnp.float32),
        "tensor",
        scatter_dimension=0,
        tiled=True,
    )


def back_product(left, weight):
    return lax.dot_general(
        left, weight, (((1,), (1,)), ((), ())), preferred_element_type=jnp.float32
    )


def row_product(left, right):
    return lax.dot_general(
        left, right, (((0,), (0,)), ((), ())), preferred_element_type=jnp.float32
    )


def input_sum(pairs):
    total = None
    for left, weight in pairs:
        portion = back_product(left, weight)
        total = portion if total is None else total + portion
    return lax.psum_scatter(total, "tensor", scatter_dimension=0, tiled=True)


def split_heads(value, count):
    return value.reshape(count, LEN, value.shape[1] // HEAD, HEAD)


def attend_sequence(query, keys, values, segments, ranks, masked):
    length = query.shape[0]
    width = min(length, 512)

    def one_block(index):
        first = index * width
        piece = lax.dynamic_slice_in_dim(query, first, width, 0)
        scores = jnp.einsum("qhd,khd->hqk", piece, keys, preferred_element_type=jnp.float32) * 0.125
        if masked:
            scores = jnp.where(
                context_allowed(segments, ranks, first, width)[None], scores, mask_fill
            )
        top = jnp.max(scores, axis=-1, keepdims=True)
        raised = jnp.exp(scores - top)
        total = jnp.sum(raised, axis=-1, keepdims=True)
        shares = (raised / total).astype(jnp.bfloat16)
        mixed = jnp.einsum("hqk,khd->qhd", shares, values, preferred_element_type=jnp.float32)
        return (mixed.astype(jnp.bfloat16), (top + jnp.log(total))[..., 0])

    mixed, log_total = lax.map(one_block, jnp.arange(length // width, dtype=jnp.int32))
    return (mixed.reshape(query.shape), log_total)


def attend_sequence_back(query, keys, values, segments, ranks, masked, log_total, grad_mixed):
    length = query.shape[0]
    width = min(length, 512)

    def one_block(carry, index):
        key_sum, value_sum = carry
        first = index * width
        piece = lax.dynamic_slice_in_dim(query, first, width, 0)
        grad_piece = lax.dynamic_slice_in_dim(grad_mixed, first, width, 0)
        scores = jnp.einsum("qhd,khd->hqk", piece, keys, preferred_element_type=jnp.float32) * 0.125
        if masked:
            scores = jnp.where(
                context_allowed(segments, ranks, first, width)[None], scores, mask_fill
            )
        shares = jnp.exp(scores - log_total[index][..., None])
        grad_shares = jnp.einsum(
            "qhd,khd->hqk", grad_piece, values, preferred_element_type=jnp.float32
        )
        inner = jnp.sum(shares * grad_shares, axis=-1, keepdims=True)
        grad_scores = (shares * (grad_shares - inner)).astype(jnp.bfloat16)
        grad_query = (
            jnp.einsum("hqk,khd->qhd", grad_scores, keys, preferred_element_type=jnp.float32)
            * 0.125
        )
        key_sum = (
            key_sum
            + jnp.einsum("hqk,qhd->khd", grad_scores, piece, preferred_element_type=jnp.float32)
            * 0.125
        )
        value_sum = value_sum + jnp.einsum(
            "hqk,qhd->khd",
            shares.astype(jnp.bfloat16),
            grad_piece,
            preferred_element_type=jnp.float32,
        )
        return ((key_sum, value_sum), grad_query.astype(jnp.bfloat16))

    zeros = jnp.zeros(keys.shape, jnp.float32)
    (key_sum, value_sum), grad_query = lax.scan(
        one_block, (zeros, zeros), jnp.arange(length // width, dtype=jnp.int32)
    )
    return (
        grad_query.reshape(query.shape),
        key_sum.astype(jnp.bfloat16),
        value_sum.astype(jnp.bfloat16),
    )


def attend_all(query, keys, values, segments, ranks, masked):
    count = query.shape[0] // LEN

    def one_sequence(items):
        return attend_sequence(items[0], items[1], items[2], items[3], items[4], masked)

    mixed, log_total = lax.map(
        one_sequence,
        (
            split_heads(query, count),
            split_heads(keys, count),
            split_heads(values, count),
            segments,
            ranks,
        ),
    )
    return (mixed.reshape(query.shape), log_total)


def attend_back_all(query, keys, values, segments, ranks, masked, log_total, grad_mixed):
    count = query.shape[0] // LEN

    def one_sequence(items):
        return attend_sequence_back(
            items[0], items[1], items[2], items[3], items[4], masked, items[5], items[6]
        )

    grad_query, grad_keys, grad_values = lax.map(
        one_sequence,
        (
            split_heads(query, count),
            split_heads(keys, count),
            split_heads(values, count),
            segments,
            ranks,
            log_total,
            split_heads(grad_mixed, count),
        ),
    )
    return (
        grad_query.reshape(query.shape),
        grad_keys.reshape(keys.shape),
        grad_values.reshape(values.shape),
    )


def shards(
    tokens,
    encoder_states,
    output_grad,
    valid_mask,
    segment_ids,
    context_ranks,
    self_query,
    self_key,
    self_value,
    self_output,
    cross_query,
    cross_key,
    cross_value,
    cross_output,
    hidden_up,
    hidden_down,
    norm1_gain,
    norm1_bias,
    norm2_gain,
    norm2_bias,
    norm3_gain,
    norm3_bias,
):
    (
        self_query,
        self_key,
        self_value,
        self_output,
        cross_query,
        cross_key,
        cross_value,
        cross_output,
        hidden_up,
        hidden_down,
    ) = (
        lax.all_gather(self_query, "dp", axis=0, tiled=True),
        lax.all_gather(self_key, "dp", axis=0, tiled=True),
        lax.all_gather(self_value, "dp", axis=0, tiled=True),
        lax.all_gather(self_output, "dp", axis=1, tiled=True),
        lax.all_gather(cross_query, "dp", axis=0, tiled=True),
        lax.all_gather(cross_key, "dp", axis=0, tiled=True),
        lax.all_gather(cross_value, "dp", axis=0, tiled=True),
        lax.all_gather(cross_output, "dp", axis=1, tiled=True),
        lax.all_gather(hidden_up, "dp", axis=0, tiled=True),
        lax.all_gather(hidden_down, "dp", axis=1, tiled=True),
    )
    tokens_full = full_rows(tokens)
    query = jnp.dot(tokens_full, self_query, preferred_element_type=jnp.float32).astype(
        jnp.bfloat16
    )
    keys = jnp.dot(tokens_full, self_key, preferred_element_type=jnp.float32).astype(jnp.bfloat16)
    values = jnp.dot(tokens_full, self_value, preferred_element_type=jnp.float32).astype(
        jnp.bfloat16
    )
    self_mixed, self_log = attend_all(query, keys, values, segment_ids, context_ranks, True)
    attended = branch_sum(self_mixed, self_output)
    first_out, first_normal, first_scale = layer_norm(
        tokens.astype(jnp.float32) + attended, norm1_gain, norm1_bias
    )
    first_full = full_rows(first_out.astype(jnp.bfloat16))
    encoder_full = full_rows(encoder_states)
    second_query = jnp.dot(first_full, cross_query, preferred_element_type=jnp.float32).astype(
        jnp.bfloat16
    )
    encoder_keys = jnp.dot(encoder_full, cross_key, preferred_element_type=jnp.float32).astype(
        jnp.bfloat16
    )
    encoder_values = jnp.dot(encoder_full, cross_value, preferred_element_type=jnp.float32).astype(
        jnp.bfloat16
    )
    cross_mixed, cross_log = attend_all(
        second_query, encoder_keys, encoder_values, segment_ids, context_ranks, False
    )
    crossed = branch_sum(cross_mixed, cross_output)
    second_out, second_normal, second_scale = layer_norm(
        first_out + crossed, norm2_gain, norm2_bias
    )
    second_low = second_out.astype(jnp.bfloat16)
    feed_input = full_rows(second_low)
    preact = jnp.dot(feed_input, hidden_up, preferred_element_type=jnp.float32)
    activated = gelu_exact(preact).astype(jnp.bfloat16)
    feed_out = branch_sum(activated, hidden_down)
    third_out, third_normal, third_scale = layer_norm(second_out + feed_out, norm3_gain, norm3_bias)
    valid_rows = valid_mask.astype(jnp.float32)[:, None]
    grad_layer = output_grad.astype(jnp.float32) * valid_rows
    grad_third, gain3_grad, bias3_grad = norm_back(
        grad_layer, third_normal, third_scale, norm3_gain
    )
    grad_third_low = grad_third.astype(jnp.bfloat16)
    grad_feed = grad_rows(grad_third_low)
    grad_active = back_product(grad_feed, hidden_down)
    grad_preact = gelu_back(preact, grad_active).astype(jnp.bfloat16)
    up_grad = row_product(feed_input, grad_preact)
    down_grad = row_product(activated, grad_feed)
    grad_second = grad_third + input_sum([(grad_preact, hidden_up)])
    grad_second_in, gain2_grad, bias2_grad = norm_back(
        grad_second, second_normal, second_scale, norm2_gain
    )
    grad_crossed = grad_rows(grad_second_in.astype(jnp.bfloat16))
    cross_output_grad = row_product(cross_mixed, grad_crossed)
    grad_cross_mixed = back_product(grad_crossed, cross_output).astype(jnp.bfloat16)
    grad_second_query, grad_encoder_keys, grad_encoder_values = attend_back_all(
        second_query,
        encoder_keys,
        encoder_values,
        segment_ids,
        context_ranks,
        False,
        cross_log,
        grad_cross_mixed,
    )
    cross_query_grad = row_product(first_full, grad_second_query)
    cross_key_grad = row_product(encoder_full, grad_encoder_keys)
    cross_value_grad = row_product(encoder_full, grad_encoder_values)
    grad_first = grad_second_in + input_sum([(grad_second_query, cross_query)])
    encoder_grad = input_sum([(grad_encoder_keys, cross_key), (grad_encoder_values, cross_value)])
    grad_first_in, gain1_grad, bias1_grad = norm_back(
        grad_first, first_normal, first_scale, norm1_gain
    )
    grad_attended = grad_rows(grad_first_in.astype(jnp.bfloat16))
    self_output_grad = row_product(self_mixed, grad_attended)
    grad_self_mixed = back_product(grad_attended, self_output).astype(jnp.bfloat16)
    grad_query, grad_keys, grad_values = attend_back_all(
        query, keys, values, segment_ids, context_ranks, True, self_log, grad_self_mixed
    )
    self_query_grad = row_product(tokens_full, grad_query)
    self_key_grad = row_product(tokens_full, grad_keys)
    self_value_grad = row_product(tokens_full, grad_values)
    tokens_grad = grad_first_in + input_sum(
        [(grad_query, self_query), (grad_keys, self_key), (grad_values, self_value)]
    )
    (
        self_query_grad,
        self_key_grad,
        self_value_grad,
        self_output_grad,
        cross_query_grad,
        cross_key_grad,
        cross_value_grad,
        cross_output_grad,
        up_grad,
        down_grad,
    ) = (
        lax.psum_scatter(self_query_grad, "dp", scatter_dimension=0, tiled=True),
        lax.psum_scatter(self_key_grad, "dp", scatter_dimension=0, tiled=True),
        lax.psum_scatter(self_value_grad, "dp", scatter_dimension=0, tiled=True),
        lax.psum_scatter(self_output_grad, "dp", scatter_dimension=1, tiled=True),
        lax.psum_scatter(cross_query_grad, "dp", scatter_dimension=0, tiled=True),
        lax.psum_scatter(cross_key_grad, "dp", scatter_dimension=0, tiled=True),
        lax.psum_scatter(cross_value_grad, "dp", scatter_dimension=0, tiled=True),
        lax.psum_scatter(cross_output_grad, "dp", scatter_dimension=1, tiled=True),
        lax.psum_scatter(up_grad, "dp", scatter_dimension=0, tiled=True),
        lax.psum_scatter(down_grad, "dp", scatter_dimension=1, tiled=True),
    )
    norm_sums, square_sums = lax.psum(
        (
            jnp.stack([gain1_grad, bias1_grad, gain2_grad, bias2_grad, gain3_grad, bias3_grad]),
            jnp.stack(
                [
                    jnp.sum(valid_rows * third_out * third_out, axis=0),
                    jnp.sum(valid_rows * tokens_grad * tokens_grad, axis=0),
                ]
            ),
        ),
        ("dp", "tensor"),
    )
    total_tokens = tokens.shape[0] * lax.axis_size("dp") * lax.axis_size("tensor")
    valid_scales = jnp.sqrt(square_sums / total_tokens)
    return (
        third_out,
        tokens_grad,
        encoder_grad,
        self_query_grad,
        self_key_grad,
        self_value_grad,
        self_output_grad,
        cross_query_grad,
        cross_key_grad,
        cross_value_grad,
        cross_output_grad,
        up_grad,
        down_grad,
        norm_sums,
        valid_scales,
    )


MESH = pl.DeviceIdType.MESH
BF = jnp.bfloat16
F32 = jnp.float32
LOG2E = 1.4426950408889634
SCALE = 0.125 * LOG2E
CH = 512


def nn(a, b):
    return lax.dot_general(a, b, (((1,), (0,)), ((), ())), preferred_element_type=F32)


def nt(a, b):
    return lax.dot_general(a, b, (((1,), (1,)), ((), ())), preferred_element_type=F32)


def turn(x):
    return x.T


class Place:
    def __init__(self):
        self.d = lax.axis_index("dp")
        self.t = lax.axis_index("tensor")
        self.z, self.y = self.d // 2, self.d % 2
        self.x, self.c = self.t // 2, self.t % 2
        self.xt = (1 - self.x) * 2 + self.c
        self.xn = (self.d, self.xt)
        self.yn = (self.z * 2 + 1 - self.y, self.t)
        self.pair = (self.d, self.x * 2 + 1 - self.c)
        self.zn = [None] + [((((self.z + k) % 4) * 2 + self.y), self.t) for k in (1, 2, 3)]
        top = self.z // 2
        self.near = [self.z, top * (5 - self.z) + (1 - top) * (1 - self.z), 2 - top, 3 * (1 - top)]

    def plane_peer(self, i):
        x, y, c = (self.x + i // 4) % 2, (self.y + i // 2) % 2, (self.c + i) % 2
        return (self.z * 2 + y, x * 2 + c)

    def barrier(self):
        sem = pltpu.get_barrier_semaphore()
        for dev in [self.plane_peer(i) for i in range(1, 8)] + self.zn[1:]:
            pl.semaphore_signal(sem, inc=1, device_id=dev, device_id_type=MESH)
        pl.semaphore_wait(sem, 10)


def remote(src, dst, send, recv, dev):
    return pltpu.make_async_remote_copy(
        src_ref=src, dst_ref=dst, send_sem=send, recv_sem=recv, device_id=dev, device_id_type=MESH
    )


class Gather:
    def __init__(self, p, w, cols, ss, rs):
        self.p, self.w, self.cols, self.ss, self.rs = p, w, cols, ss, rs

    def col(self, t):
        return pl.ds(pl.multiple_of(t * self.cols, 128), self.cols)

    def blk(self, k, y, t):
        return self.w.at[:, self.p.near[k], y, :, self.col(t)]

    def cp(self, ref, i, dev, send=None):
        return remote(ref, ref, self.ss.at[i if send is None else send], self.rs.at[i], dev)

    def own(self):
        return self.blk(0, self.p.y, self.p.t)

    def z_send(self, k):
        p = self.p
        dev = (p.near[k] * 2 + p.y, p.t)
        return self.cp(self.own(), 15 + p.z, dev, k - 1)

    def z_recv(self, k):
        p = self.p
        ref = self.blk(k, p.y, p.t)
        return self.cp(ref, 15 + p.near[k], (p.near[k] * 2 + p.y, p.t), k - 1)

    def x_send(self, k):
        return self.cp(self.blk(k, self.p.y, self.p.t), 3 + k, self.p.xn)

    def x_recv(self, k):
        return self.cp(self.blk(k, self.p.y, self.p.xt), 3 + k, self.p.xn)

    def y_send(self, k):
        return self.cp(self.blk(k, self.p.y, self.p.t), 7 + k, self.p.yn)

    def y_recv(self, k):
        return self.cp(self.blk(k, 1 - self.p.y, self.p.t), 7 + k, self.p.yn)

    def q_send(self, k):
        if k < 2:
            return self.cp(self.blk(k, self.p.y, self.p.xt), 11 + k, self.p.yn)
        return self.cp(self.blk(k, 1 - self.p.y, self.p.t), 11 + k, self.p.xn)

    def q_recv(self, k):
        return self.cp(self.blk(k, 1 - self.p.y, self.p.xt), 11 + k, self.p.xn)

    def rail(self, i, core):
        x = self.p.x if i == 0 else 1 - self.p.x
        return self.w.at[:, :, :, :, self.col(x * 2 + core)]

    def p_send(self, i):
        return self.cp(self.rail(i, self.p.c), 1 + i, self.p.pair, 17 + i)

    def p_recv(self, i):
        return self.cp(self.rail(i, 1 - self.p.c), 1 + i, self.p.pair, 17 + i)

    def zs(self):
        for k in (1, 2, 3):
            self.z_send(k).start()

    def oxy(self):
        self.x_send(0).start()
        self.y_send(0).start()

    def plane(self, *between):
        for k in (1, 2, 3):
            self.z_recv(k).wait_recv()
            if k == 1:
                for fn in between:
                    fn()
            self.x_send(k).start()
            self.y_send(k).start()

    def corner(self):
        for k in range(4):
            self.x_recv(k).wait_recv()
            if k < 2:
                self.q_send(k).start()
            self.y_recv(k).wait_recv()
            if k >= 2:
                self.q_send(k).start()
        self.p_send(0).start()

    def cross(self):
        for k in range(4):
            self.q_recv(k).wait_recv()
        self.p_send(1).start()

    def finish(self):
        self.p_recv(0).wait_recv()
        self.p_recv(1).wait_recv()

    def drain(self):
        for k in (1, 2, 3):
            self.z_send(k).wait_send()
        for k in range(4):
            self.x_send(k).wait_send()
            self.y_send(k).wait_send()
            self.q_send(k).wait_send()
        self.p_send(0).wait_send()
        self.p_send(1).wait_send()


class Reduce:
    def __init__(self, p, g, cols, held, r1, r2, r3, out, ss, rs):
        self.p, self.g, self.cols, self.held = p, g, cols, held
        self.r1, self.r2, self.r3, self.out, self.ss, self.rs = r1, r2, r3, out, ss, rs
        self.n = g.shape[0]

    def col(self, t):
        return pl.ds(pl.multiple_of(t * self.cols, 128), self.cols)

    def cp(self, src, dst, i, dev):
        return remote(src, dst, self.ss.at[i], self.rs.at[i], dev)

    def pair_copy(self, x):
        src = self.g.at[:, :, :, :, self.col(x * 2 + 1 - self.p.c)]
        return self.cp(src, self.held.at[x], x, self.p.pair)

    def corner_copy(self, i):
        p = self.p
        src = self.held.at[1 - p.x, :, pl.ds(2 * i, 2), 1 - p.y]
        return self.cp(src, self.r1.at[i], 2 + i, p.yn if i == 0 else p.xn)

    def plane_copy(self, i):
        p = self.p
        src = self.held.at[1 - p.x, :, :, p.y] if i == 0 else self.held.at[p.x, :, :, 1 - p.y]
        return self.cp(src, self.r2.at[i], 4 + i, p.xn if i == 0 else p.yn)

    def z_copy(self, k):
        p = self.p
        src = self.held.at[p.x, :, (p.z + k) % 4, p.y]
        return self.cp(src, self.r3.at[k - 1], 5 + k, p.zn[k])

    def start(self):
        self.pair_copy(0).start()
        self.pair_copy(1).start()

    def corner(self):
        for x in (0, 1):
            self.pair_copy(x).wait_recv()
        for x in (0, 1):
            col = self.col(x * 2 + self.p.c)

            def one(j, _, x=x, col=col):
                i, z = j // 4, j % 4
                a = self.g[i, z, :, :, col].astype(F32) + self.held[x, i, z].astype(F32)
                self.held[x, i, z] = a.astype(BF)
                return 0

            def whole(i, _, x=x, col=col):
                a = self.g[i, :, :, :, col].astype(F32) + self.held[x, i].astype(F32)
                self.held[x, i] = a.astype(BF)
                return 0

            if self.cols > 128:
                lax.fori_loop(0, self.n * 4, one, 0)
            else:
                lax.fori_loop(0, self.n, whole, 0)
        self.corner_copy(0).start()
        self.corner_copy(1).start()

    def plane(self):
        p = self.p
        self.corner_copy(0).wait_recv()
        self.corner_copy(1).wait_recv()
        for i in range(self.n):
            for j in range(2):
                a = self.held[1 - p.x, i, j, p.y].astype(F32) + self.r1[0, i, j].astype(F32)
                self.held[1 - p.x, i, j, p.y] = a.astype(BF)
                b = self.held[p.x, i, 2 + j, 1 - p.y].astype(F32) + self.r1[1, i, j].astype(F32)
                self.held[p.x, i, 2 + j, 1 - p.y] = b.astype(BF)
        self.plane_copy(0).start()
        self.plane_copy(1).start()

    def along(self):
        p = self.p
        self.plane_copy(0).wait_recv()
        self.plane_copy(1).wait_recv()
        for k in (1, 2, 3):
            zt = (p.z + k) % 4
            for i in range(self.n):
                a = (
                    self.held[p.x, i, zt, p.y].astype(F32)
                    + self.r2[0, i, zt].astype(F32)
                    + self.r2[1, i, zt].astype(F32)
                )
                self.held[p.x, i, zt, p.y] = a.astype(BF)
            self.z_copy(k).start()

    def finish(self):
        p = self.p
        for k in (1, 2, 3):
            self.z_copy(k).wait_recv()
        for i in range(self.n):
            a = (
                self.held[p.x, i, p.z, p.y].astype(F32)
                + self.r2[0, i, p.z].astype(F32)
                + self.r2[1, i, p.z].astype(F32)
            )
            for k in range(3):
                a = a + self.r3[k, i].astype(F32)
            self.out[i] = a

    def drain(self):
        for i in (0, 1):
            self.pair_copy(i).wait_send()
            self.corner_copy(i).wait_send()
            self.plane_copy(i).wait_send()
        for k in (1, 2, 3):
            self.z_copy(k).wait_send()


class Tail:
    def __init__(self, p, gt, hp, hx, hy, hz, hc, out, ss, rs):
        self.p, self.gt, self.hp, self.hx, self.hy, self.hz, self.hc = p, gt, hp, hx, hy, hz, hc
        self.out, self.ss, self.rs = out, ss, rs

    def cp(self, src, dst, i, dev):
        return remote(src, dst, self.ss.at[i], self.rs.at[i], dev)

    def pair_copy(self, j):
        return self.cp(self.gt.at[j], self.hp.at[j // 2], j, self.p.pair)

    def x_copy(self, j):
        if j == 1:
            return self.cp(self.gt.at[1, :, :, self.p.y], self.hx.at[:, :, 0], 4, self.p.xn)
        return self.cp(self.gt.at[0], self.hx, 4, self.p.xn)

    def corner_copy(self):
        return self.cp(self.gt.at[1, :, :, 1 - self.p.y], self.hc, 9, self.p.yn)

    def y_copy(self, j):
        return self.cp(self.gt.at[j, :, :, 1 - self.p.y], self.hy, 5, self.p.yn)

    def z_copy(self, j, k):
        p = self.p
        return self.cp(self.gt.at[j, :, (p.z + k) % 4, p.y], self.hz.at[k - 1], 5 + k, p.zn[k])

    def mine(self, j, fn):
        pl.when(self.p.c == j % 2)(fn)

    def start(self, j):
        pl.when(self.p.c != j % 2)(lambda: self.pair_copy(j).start())

    def sum_pair(self, j):
        def do():
            self.pair_copy(j).wait_recv()
            if j == 2:
                self.x_copy(0).wait_recv()
            for w in range(3):
                a = self.gt[j, w].astype(F32) + self.hp[j // 2, w].astype(F32)
                if j == 2:
                    a = a + self.hx[w].astype(F32)
                self.gt[j, w] = a.astype(BF)
            if j == 0:
                self.x_copy(0).start()
            elif j == 1:
                self.corner_copy().start()
            else:
                self.y_copy(j).start()

        self.mine(j, do)

    def corner(self):
        def do():
            self.corner_copy().wait_recv()
            y = self.p.y
            for w in range(3):
                a = self.gt[1, w, :, y].astype(F32) + self.hc[w].astype(F32)
                self.gt[1, w, :, y] = a.astype(BF)
            self.x_copy(1).start()

        self.mine(1, do)

    def sum_y(self, j):
        def do():
            p = self.p
            self.y_copy(j).wait_recv()
            if j == 3:
                self.x_copy(1).wait_recv()
            for i in range(3):
                for k in (1, 2, 3):
                    zt = (p.z + k) % 4
                    a = self.gt[j, i, zt, p.y].astype(F32) + self.hy[i, zt].astype(F32)
                    if j == 3:
                        a = a + self.hx[i, zt, 0].astype(F32)
                    self.gt[j, i, zt, p.y] = a.astype(BF)
            for k in (1, 2, 3):
                self.z_copy(j, k).start()

        self.mine(j, do)

    def finish(self, j):
        def do():
            p = self.p
            for k in (1, 2, 3):
                self.z_copy(j, k).wait_recv()
            for i in range(3):
                a = self.gt[j, i, p.z, p.y].astype(F32) + self.hy[i, p.z].astype(F32)
                if j == 3:
                    a = a + self.hx[i, p.z, 0].astype(F32)
                for k in range(3):
                    a = a + self.hz[k, i].astype(F32)
                self.out[i] = a

        self.mine(j, do)

    def drain(self):
        for j in range(4):
            pl.when(self.p.c != j % 2)(lambda j=j: self.pair_copy(j).wait_send())

        def sent(j):
            self.x_copy(j).wait_send()
            if j == 1:
                self.corner_copy().wait_send()
            self.y_copy(j + 2).wait_send()
            for k in (1, 2, 3):
                self.z_copy(j + 2, k).wait_send()

        for j in (0, 1):
            self.mine(j, lambda j=j: sent(j))


def row_steps(count, one):
    def body(i, _):
        one(pl.ds(pl.multiple_of(i * CH, CH), CH))
        return 0

    lax.fori_loop(0, count // CH, body, 0)


def head_half(shape, axis, h):
    return (lax.broadcasted_iota(jnp.int32, shape, axis) // HEAD) == h


def keep_half(value, axis, h):
    return jnp.where(head_half(value.shape, axis, h), value.astype(F32), 0.0).astype(BF)


def run_hooks(hooks, step, half):
    for (at, part), hook in hooks.items():
        if part == half:
            pl.when(step == at)(hook)


def attend(qt, k, vt, bias, ot, lse, temp, hooks):
    def ready(p, h):
        lanes = pl.ds(pl.multiple_of(p * 128, 128), 128)
        return k[:, lanes], keep_half(qt[lanes, :], 0, h)

    def score(kp, qm, h, i, top):
        s = nn(kp[i * 512 : i * 512 + 512], qm) * SCALE
        if bias is not None:
            s = s + bias[i * 512 : i * 512 + 512, :]
        temp[h * 1024 + i * 512 : h * 1024 + i * 512 + 512, :] = s
        m = jnp.max(s, axis=0, keepdims=True)
        return m if top is None else jnp.maximum(top, m)

    def mix(vh, h, i, top, total, mixed):
        e = jnp.exp2(temp[h * 1024 + i * 512 : h * 1024 + i * 512 + 512, :] - top)
        part = jnp.sum(e, axis=0, keepdims=True)
        o = nn(vh[:, i * 512 : i * 512 + 512], e.astype(BF))
        return (part, o) if total is None else (total + part, mixed + o)

    def pair(p, top):
        for h in (0, 1):
            kp, qm = ready(p if h == 0 else (p + 1) % 4, 1 - h)
            vh = vt[pl.ds(pl.multiple_of(p * 128 + h * 64, 64), 64), :]
            total = mixed = later = None
            for i in range(2):
                later = score(kp, qm, 1 - h, i, later)
                total, mixed = mix(vh, h, i, top, total, mixed)
            ot[pl.ds(pl.multiple_of(p * 128 + h * 64, 64), 64), :] = mixed * (1.0 / total)
            lse[pl.ds(p * 2 + h, 1), :] = top + jnp.log2(total)
            top = later
            run_hooks(hooks, p, h)
        return top

    kp, qm = ready(0, 0)
    top = None
    for i in range(2):
        top = score(kp, qm, 0, i, top)
    lax.fori_loop(0, 4, pair, top)


def attend_back(q, qt, k, kt, v, do, dot_, ot, bias, lse, dqt, dk_own, dv_own, dkv_send, order, hooks):
    def pair(step, _):
        p = order(step)
        lanes = pl.ds(pl.multiple_of(p * 128, 128), 128)
        kp, vp = k[:, lanes], v[:, lanes]
        qp, dop = qt[lanes, :], dot_[lanes, :]
        inner = dop.astype(F32) * ot[lanes, :]
        qms = [keep_half(qp, 0, h) for h in (0, 1)]
        doms = [keep_half(dop, 0, h) for h in (0, 1)]
        qr = jnp.concatenate([keep_half(q[:, lanes], 1, h) for h in (0, 1)], axis=0)
        dor = jnp.concatenate([keep_half(do[:, lanes], 1, h) for h in (0, 1)], axis=0)
        ds_sum = [jnp.sum(inner[h * 64 : h * 64 + 64], axis=0, keepdims=True) for h in (0, 1)]
        logs = [lse[pl.ds(p * 2 + h, 1), :] for h in (0, 1)]
        shares, grads = {}, {}
        dq = [None, None]
        dvs, dks = {}, {}

        def one(h, i):
            rows = slice(i * 256, i * 256 + 256)
            s = nn(kp[rows], qms[h]) * SCALE
            if bias is not None:
                s = s + bias[rows, :]
            e = jnp.exp2(s - logs[h])
            dp = nn(vp[rows], doms[h])
            shares[h, i] = e.astype(BF)
            grads[h, i] = (e * (dp - ds_sum[h])).astype(BF)

        def two(h, i):
            rows = slice(i * 256, i * 256 + 256)
            kh = kt[pl.ds(pl.multiple_of(p * 128 + h * 64, 64), 64), rows]
            part = nn(kh, grads[h, i])
            dq[h] = part if dq[h] is None else dq[h] + part
            dv = nn(shares[h, i], dor[h * 512 : h * 512 + 512])
            dk = nn(grads[h, i], qr[h * 512 : h * 512 + 512])
            dvs[i] = dv if i not in dvs else dvs[i] + dv
            dks[i] = dk if i not in dks else dks[i] + dk

        def out(i):
            rows = slice(i * 256, i * 256 + 256)
            if i < 2:
                dk_own[rows, lanes] = (dks[i] * 0.125).astype(dk_own.dtype)
                dv_own[rows, lanes] = dvs[i].astype(dv_own.dtype)
            else:
                back = slice(i * 256 - 512, i * 256 - 256)
                dkv_send[0, back, lanes] = (dks[i] * 0.125).astype(BF)
                dkv_send[1, back, lanes] = dvs[i].astype(BF)

        for i in range(4):
            one(0, i)
        for i in range(4):
            one(1, i)
            two(0, i)
        run_hooks(hooks, step, 0)
        for i in range(4):
            two(1, i)
            out(i)
        for h in (0, 1):
            dqt[pl.ds(pl.multiple_of(p * 128 + h * 64, 64), 64), :] = (dq[h] * 0.125).astype(BF)
        run_hooks(hooks, step, 1)
        return 0

    lax.fori_loop(0, 4, pair, 0)


def norm_rows(z):
    mean = jnp.mean(z, axis=-1, keepdims=True)
    centred = z - mean
    r = lax.rsqrt(jnp.mean(centred * centred, axis=-1, keepdims=True) + norm_eps)
    return centred * r, r


def norm_back_rows(e, n, r, gain):
    s = e * gain
    a = jnp.mean(s, axis=-1, keepdims=True)
    b = jnp.mean(s * n, axis=-1, keepdims=True)
    return r * (s - a - n * b)


def fast_kernel(
    x_i, enc_i, og_i, valid, seg, rank,
    sq, sk, sv, so, cq, ck, cv, co, up, down,
    g1, b1, g2, b2, g3, b3,
    y_o, dx_o, eg_o, ga_o, gb_o, gf_o, ns_o, vs_o,
    xs, enc, og, codes, wa, wb, wf, gt,
    q1, qt1, k1, v1, vt1, o1, ot1, l1,
    q2, qt2, k2, v2, vt2, o2, ot2, l2,
    bias, n1, n2, h1b, h2b, u, gp, dg, dz, low, lowt, do, dot_,
    kvs, kvr1, kvr2, tt, yb, row, st,
    hc, hq, hu, hd, c1, c2, c3, p1, p2, p3, u1, u2, u3, d1, d2, d3, hp, hx, hy, hz, hcn,
    st_r, gss, grs, rss, rrs, aas, ars, ess, ers, tss, trs, ls,
):
    dqt, dq = h2b, q2
    x = xs.at[pl.ds(0, 512)]
    dkv = [v2.at[pl.ds(0, 512)], v2.at[pl.ds(512, 512)]]
    p = Place()
    loads = []
    for i, (src, w, j, cols) in enumerate(
        (
            (sq, wa, 0, 128), (sk, wa, 1, 128), (sv, wa, 2, 128),
            (so, wb, 0, 128), (co, wb, 1, 128), (cq, wb, 2, 128), (ck, wb, 3, 128), (cv, wb, 4, 128),
            (up, wf, 0, 512), (down, wf, 1, 512),
        )
    ):
        col = pl.ds(pl.multiple_of(p.t * cols, 128), cols)
        loads.append(pltpu.make_async_copy(src, w.at[j, p.z, p.y, :, col], ls.at[i]))
    for i, (src, dst) in enumerate(((x_i, x), (enc_i, enc), (og_i, og))):
        loads.append(pltpu.make_async_copy(src, dst, ls.at[10 + i]))
    for cp in loads:
        cp.start()
    p.barrier()
    GA, GB, GU, GD = G = [
        Gather(p, w, cols, gss.at[i], grs.at[i])
        for i, (w, cols) in enumerate(
            ((wa, 128), (wb, 128), (wf.at[pl.ds(0, 1)], 512), (wf.at[pl.ds(1, 1)], 512))
        )
    ]
    for cp in loads[:3]:
        cp.wait()
    GA.zs()
    GA.oxy()
    for cp in loads[3:]:
        cp.wait()
    halves = remote(
        xs.at[pl.ds(0, 512)], xs.at[pl.ds(512, 512)], ess.at[9], ers.at[9], p.pair
    )
    halves.start()
    GB.oxy()

    def mat(w, j):
        return w[j].reshape(512, w.shape[4])

    st[...] = jnp.zeros_like(st)
    row[...] = jnp.broadcast_to(valid[...].astype(F32), (128, 512)).T
    own = pl.ds(pl.multiple_of(p.c * 512, 128), 512)
    other = pl.ds(pl.multiple_of((1 - p.c) * 512, 128), 512)
    sx = pl.ds(p.x, 1)
    ranks = rank[sx, :]
    codes[1:2, :] = seg[sx, :] * 8
    codes[0:1, :] = seg[sx, :] * 8 + jnp.concatenate(
        [jnp.broadcast_to(ranks[:, b : b + 1], (1, 128)) for b in range(8)], axis=1
    )
    base, high = codes[1:2, own], codes[0:1, own]
    for i, half in enumerate((own, other)):
        code = jnp.broadcast_to(codes[0:1, half], (128, 512)).T
        for j in range(4):
            c = code[j * 128 : j * 128 + 128, :1]
            ok = (c >= base) & (c <= high)
            bias[i * 512 + j * 128 : i * 512 + j * 128 + 128, :] = jnp.where(ok, 0.0, -2.0e9)

    GA.plane(GB.zs)
    GU.oxy()
    GA.corner()
    GU.zs()
    GD.oxy()
    GA.cross()
    GB.plane()
    GA.finish()
    GD.zs()

    def swap(buf, i):
        return remote(buf.at[pl.ds(0, 512)], buf.at[pl.ds(512, 512)], ess.at[i], ers.at[i], p.pair)

    halves.wait()
    xv = xs[...]
    k1[...] = nn(xv, mat(wa, 1)).astype(BF)
    vv = nn(xv, mat(wa, 2)).astype(BF)
    v1[...] = vv
    vt1[...] = turn(vv)
    xv = x[...]
    qv = nn(xv, mat(wa, 0)).astype(BF)
    q1[...] = qv
    qt1[...] = turn(qv)
    attend(qt1, k1, vt1, bias, ot1, l1, gp, {(0, 0): GB.corner, (1, 0): GU.plane, (2, 0): GB.cross, (3, 0): GD.plane})
    o1[...] = turn(ot1[...].astype(BF))
    vt1[...] = turn(k1[...])
    GB.finish()
    ev = enc[...]
    k2[0:512, :] = nn(ev, mat(wb, 3)).astype(BF)
    v2[0:512, :] = nn(ev, mat(wb, 4)).astype(BF)
    swap(k2, 2).start()
    swap(v2, 3).start()
    yb[...] = nt(o1[...], mat(wb, 0))
    GU.corner()

    def first(r):
        n, s = norm_rows(x[r, :].astype(F32) + yb[r, :])
        n1[r, :] = n
        row[r, 0:1] = s
        h1b[r, :] = (n * g1[...] + b1[...]).astype(BF)

    row_steps(512, first)
    qv = nn(h1b[...], mat(wb, 2)).astype(BF)
    q2[...] = qv
    qt2[...] = turn(qv)
    swap(k2, 2).wait_recv()
    swap(v2, 3).wait_recv()
    vt2[...] = turn(v2[...])
    attend(qt2, k2, vt2, None, ot2, l2, gp, {(0, 1): GD.corner, (2, 1): GU.cross})
    o2[...] = turn(ot2[...].astype(BF))
    vt2[...] = turn(k2[...])
    yb[...] = nt(o2[...], mat(wb, 1))

    def second(r):
        n, s = norm_rows(n1[r, :] * g1[...] + b1[...] + yb[r, :])
        n2[r, :] = n
        row[r, 1:2] = s
        h2b[r, :] = (n * g2[...] + b2[...]).astype(BF)

    row_steps(512, second)
    tt[...] = turn(h2b[...])
    hv = h2b[...]
    blocks = [p.t, p.pair[1], p.xt, (1 - p.x) * 2 + 1 - p.c]
    waits = [None, GU.p_recv(0).wait_recv, GD.cross, GU.p_recv(1).wait_recv]
    for t, wait in zip(blocks, waits):
        if wait is not None:
            wait()
        cols = pl.ds(pl.multiple_of(t * 512, 512), 512)
        gp[cols, :] = nn(hv, wf[0, :, :, :, cols].reshape(512, 512))

        def gelu(r, cols=cols, t=t):
            at = pl.ds(pl.multiple_of(r.start + t * 512, CH), CH)
            v = gp[at, :]
            cdf = 0.5 * (1.0 + lax.erf(v * 0.7071067811865476))
            u[r, cols] = (v * cdf).astype(BF)
            gp[at, :] = cdf + v * (jnp.exp2(v * v * (-0.5 * LOG2E)) * 0.3989422804014327)

        row_steps(512, gelu)
    waits = [None, GD.p_recv(0).wait_recv, None, GD.p_recv(1).wait_recv]
    for i, (t, wait) in enumerate(zip(blocks, waits)):
        if wait is not None:
            wait()
        cols = pl.ds(pl.multiple_of(t * 512, 512), 512)
        part = nt(u[:, cols], wf[1, :, :, :, cols].reshape(512, 512))
        yb[...] = part if i == 0 else yb[...] + part

    def third(r):
        n, s = norm_rows(n2[r, :] * g2[...] + b2[...] + yb[r, :])
        out = n * g3[...] + b3[...]
        vc = row[r, 2:3]
        yb[r, :] = out
        e = og[r, :].astype(F32) * vc
        st[4:5, :] += jnp.sum(e * n, axis=0, keepdims=True)
        st[5:6, :] += jnp.sum(e, axis=0, keepdims=True)
        st[6:7, :] += jnp.sum(vc * out * out, axis=0, keepdims=True)
        back = norm_back_rows(e, n, s, g3[...])
        dz[r, :] = back
        low[r, :] = back.astype(BF)

    row_steps(512, third)
    y_copy = pltpu.make_async_copy(yb, y_o, ls.at[0])
    y_copy.start()
    lv = low[...]
    lowt[...] = turn(lv)
    for g in G:
        g.drain()
    RC, RP, RU, RD = R = [
        Reduce(p, w.at[pl.ds(at, n)], cols, *bufs, out.at[pl.ds(at, n)], rss.at[i], rrs.at[i])
        for i, (w, at, n, cols, bufs, out) in enumerate(
            (
                (wb, 0, 2, 128, (hc, c1, c2, c3), gb_o),
                (wb, 2, 3, 128, (hq, p1, p2, p3), gb_o),
                (wf, 0, 1, 512, (hu, u1, u2, u3), gf_o),
                (wf, 1, 1, 512, (hd, d1, d2, d3), gf_o),
            )
        )
    ]
    for j in range(4):
        cols = slice(j * 512, j * 512 + 512)
        dg[:, cols] = (nn(lv, wf[1, :, :, :, cols].reshape(512, 512)) * gp[cols, :]).astype(BF)
        wf[1, :, :, :, cols] = nn(lowt[...], u[:, cols]).astype(BF).reshape(4, 2, 64, 512)
        if j % 2 == 1:
            RD.pair_copy(j // 2).start()
    dz[...] += nt(dg[...], mat(wf, 0))
    for j in range(4):
        cols = slice(j * 512, j * 512 + 512)
        wf[0, :, :, :, cols] = nn(tt[...], dg[:, cols]).astype(BF).reshape(4, 2, 64, 512)
    RU.start()
    RD.corner()

    def back2(r):
        e = dz[r, :]
        n = n2[r, :]
        st[2:3, :] += jnp.sum(e * n, axis=0, keepdims=True)
        st[3:4, :] += jnp.sum(e, axis=0, keepdims=True)
        back = norm_back_rows(e, n, row[r, 1:2], g2[...])
        dz[r, :] = back
        low[r, :] = back.astype(BF)

    row_steps(512, back2)
    dov = nn(low[...], mat(wb, 1)).astype(BF)
    do[...] = dov
    dot_[...] = turn(dov)
    lowt[...] = turn(low[...])
    wb[1] = nn(lowt[...], o2[...]).astype(BF).reshape(4, 2, 64, 512)
    RU.corner()
    attend_back(
        q2, qt2, k2, vt2, v2, do, dot_, ot2, None, l2, dqt,
        gp.at[pl.ds(0, 512)], gp.at[pl.ds(512, 512)], kvs.at[:, pl.ds(512, 512)], lambda step: step,
        {(0, 0): RD.plane, (1, 0): RU.plane, (3, 0): RD.along},
    )

    def swap_back(buf, i):
        return remote(kvs.at[:, pl.ds(512, 512)], buf, ess.at[i], ers.at[i], p.pair)

    swap_back(kvr2, 4).start()
    dqv = turn(dqt[...])
    dz[...] += nt(dqv, mat(wb, 2))
    tt[...] = turn(h1b[...])
    wb[2] = nn(tt[...], dqv).astype(BF).reshape(4, 2, 64, 512)
    tt[...] = turn(enc[...])
    swap_back(kvr2, 4).wait()
    for i in (2, 3):
        swap((k1, v1, k2, v2)[i], i).wait_send()

    def join(recv, at):
        def one(r):
            for i in (0, 1):
                own_rows = pl.ds(pl.multiple_of(r.start + at + i * 512, CH), CH)
                dkv[i][r, :] = (gp[own_rows, :] + recv[i, r, :].astype(F32)).astype(BF)

        row_steps(512, one)

    join(kvr2, 0)
    y_copy.wait()
    yb[...] = nt(dkv[0][...], mat(wb, 3)) + nt(dkv[1][...], mat(wb, 4))
    e_copy = pltpu.make_async_copy(yb, eg_o, ls.at[0])
    e_copy.start()
    wb[3] = nn(tt[...], dkv[0][...]).astype(BF).reshape(4, 2, 64, 512)
    wb[4] = nn(tt[...], dkv[1][...]).astype(BF).reshape(4, 2, 64, 512)
    RP.start()

    def back1(r):
        e = dz[r, :]
        n = n1[r, :]
        st[0:1, :] += jnp.sum(e * n, axis=0, keepdims=True)
        st[1:2, :] += jnp.sum(e, axis=0, keepdims=True)
        back = norm_back_rows(e, n, row[r, 0:1], g1[...])
        dz[r, :] = back
        low[r, :] = back.astype(BF)

    row_steps(512, back1)
    RU.along()
    dov = nn(low[...], mat(wb, 0)).astype(BF)
    do[...] = dov
    dot_[...] = turn(dov)
    lowt[...] = turn(low[...])
    wb[0] = nn(lowt[...], o1[...]).astype(BF).reshape(4, 2, 64, 512)
    RC.start()
    RP.corner()
    vt2[...] = turn(xs[...])
    T = Tail(p, gt, hp, hx, hy, hz, hcn, ga_o, aas, ars)

    def order(step):
        far = (step // 2) * p.x + (1 - step // 2) * (1 - p.x)
        return 2 * far + step % 2

    def lanes_of(step):
        return pl.ds(pl.multiple_of(order(step) * 128, 128), 128)

    def part_back(step):
        at = lanes_of(step)
        return remote(
            kvs.at[:, pl.ds(512, 512), at], kvr1.at[:, :, at], ess.at[5 + step], ers.at[5 + step], p.pair
        )

    def grads(step):
        at = lanes_of(step)
        dqv = turn(dqt[at, :])
        dq[:, at] = dqv
        gt[step, 0] = nn(vt2[:, 0:512], dqv).astype(BF).reshape(4, 2, 64, 128)
        gt[step, 1] = nn(vt2[...], kvs[0, :, at]).astype(BF).reshape(4, 2, 64, 128)
        gt[step, 2] = nn(vt2[...], kvs[1, :, at]).astype(BF).reshape(4, 2, 64, 128)
        T.start(step)

    def both(*fns):
        def run():
            for fn in fns:
                fn()

        return run

    attend_back(
        q1, qt1, k1, vt1, v1, do, dot_, ot1, bias, l1, dqt,
        kvs.at[0, pl.ds(0, 512)], kvs.at[1, pl.ds(0, 512)], kvs.at[:, pl.ds(512, 512)], order,
        {
            (0, 0): RC.corner,
            (0, 1): both(lambda: part_back(0).start(), lambda: grads(0), RP.plane),
            (1, 0): lambda: T.sum_pair(0),
            (1, 1): both(lambda: part_back(1).start(), lambda: grads(1), RC.plane, RD.finish),
            (2, 0): lambda: T.sum_pair(1),
            (2, 1): both(lambda: part_back(2).start(), lambda: grads(2), RP.along, RU.finish),
            (3, 0): lambda: T.sum_pair(2),
            (3, 1): both(lambda: part_back(3).start(), T.corner, RC.along),
        },
    )
    grads(3)
    T.sum_y(2)
    dz[...] += nt(dq[...], mat(wa, 0))
    T.sum_pair(3)
    for step in range(4):
        part_back(step).wait_recv()

    def join_last(r):
        for i in (0, 1):
            dkv[i][r, :] = (kvs[i, r, :].astype(F32) + kvr1[i, r, :].astype(F32)).astype(BF)

    row_steps(512, join_last)
    dz[...] += nt(dkv[0][...], mat(wa, 1)) + nt(dkv[1][...], mat(wa, 2))
    x_copy = pltpu.make_async_copy(dz, dx_o, ls.at[1])
    x_copy.start()

    def squares(r):
        st[7:8, :] += jnp.sum(row[r, 2:3] * dz[r, :] * dz[r, :], axis=0, keepdims=True)

    row_steps(512, squares)

    stats = []
    st_r[0] = st[...]
    for i in range(1, 8):
        stats.append(remote(st, st_r.at[i], tss.at[i], trs.at[i], p.plane_peer(i)))
    for cp in stats:
        cp.start()
    T.sum_y(3)
    for cp in stats:
        cp.wait()
    total = None
    for i in range(8):
        x, y, c = (p.x + i // 4) % 2, (p.y + i // 2) % 2, (p.c + i) % 2
        part = st_r[x * 4 + y * 2 + c]
        total = part if total is None else total + part
    st_r[8 + p.z] = total
    stats = []
    for k in (1, 2, 3):
        at = st_r.at[8 + p.z]
        stats.append((remote(at, at, tss.at[7 + k], trs.at[7 + k], p.zn[k]), k))
    for cp, _ in stats:
        cp.start()
    RP.finish()
    RC.finish()
    T.finish(2)
    for cp, k in stats:
        cp.wait_send()
        back = st_r.at[8 + (p.z - k + 4) % 4]
        remote(back, back, tss.at[7 + k], trs.at[7 + k], p.zn[k]).wait_recv()
    T.finish(3)
    total = st_r[8] + st_r[9] + st_r[10] + st_r[11]
    ns_o[...] = total[0:6]
    vs_o[...] = jnp.sqrt(total[6:8] * (1.0 / 16384.0))
    for step in range(4):
        part_back(step).wait_send()
    for r in R:
        r.drain()
    T.drain()
    e_copy.wait()
    x_copy.wait()


def place_kernel(*refs):
    srcs, outs, held, sems = refs[:8], refs[8:23], refs[23:31], refs[31]
    parts = [held[0], held[1], held[2]] + [held[3].at[i] for i in range(3)]
    parts += [held[4].at[i] for i in range(5)] + [held[5].at[i] for i in range(2)] + [held[6], held[7]]
    first = [pltpu.make_async_copy(a, b, sems.at[i]) for i, (a, b) in enumerate(zip(srcs, held))]
    last = [pltpu.make_async_copy(a, b, sems.at[8 + i]) for i, (a, b) in enumerate(zip(parts, outs))]
    ends = [(0, 1), (1, 2), (2, 3), (3, 6), (6, 11), (11, 13), (13, 14), (14, 15)]
    order = (6, 7, 3, 4, 5, 0, 1, 2)
    for i in order:
        first[i].start()
    for i in order:
        first[i].wait()
        for cp in last[ends[i][0] : ends[i][1]]:
            cp.start()
    for cp in last:
        cp.wait()


def fast_shards(
    tokens, encoder_states, output_grad, valid_mask, segment_ids, context_ranks,
    self_query, self_key, self_value, self_output,
    cross_query, cross_key, cross_value, cross_output, hidden_up, hidden_down,
    norm1_gain, norm1_bias, norm2_gain, norm2_bias, norm3_gain, norm3_bias,
):
    vm = pl.BlockSpec(memory_space=pltpu.VMEM)
    hbm = pl.BlockSpec(memory_space=pl.ANY)
    rows = [
        v.reshape(1, 512)
        for v in (norm1_gain, norm1_bias, norm2_gain, norm2_bias, norm3_gain, norm3_bias)
    ]

    def V(*shape, dtype=BF):
        return pltpu.VMEM(shape, dtype)

    def S(*shape):
        return pltpu.SemaphoreType.DMA(shape)

    def group(n, cols):
        return [
            V(2, n, 4, 2, 64, cols),
            [V(2, n, 2, 64, cols), V(2, n, 4, 64, cols), V(3, n, 64, cols)],
        ]

    rc, rp, ru, rd = group(2, 128), group(3, 128), group(1, 512), group(1, 512)

    def attention():
        return [
            V(512, 512), V(512, 512), V(1024, 512), V(1024, 512), V(512, 1024), V(512, 512),
            V(512, 512, dtype=F32), V(8, 512, dtype=F32),
        ]

    scratch = (
        [V(1024, 512), V(512, 512), V(512, 512)]
        + [V(8, 1024, dtype=jnp.int32)]
        + [V(3, 4, 2, 64, 512), V(5, 4, 2, 64, 512), V(2, 4, 2, 64, 2048), V(4, 3, 4, 2, 64, 128)]
        + attention()
        + attention()
        + [V(1024, 512, dtype=F32), V(512, 512, dtype=F32), V(512, 512, dtype=F32)]
        + [V(512, 512), V(512, 512)]
        + [V(512, 2048), V(2048, 512, dtype=F32), V(512, 2048), V(512, 512, dtype=F32)]
        + [V(512, 512)] * 4
        + [V(2, 1024, 512), V(2, 512, 512), V(2, 512, 512)]
        + [V(512, 512), V(512, 512, dtype=F32), V(512, 128, dtype=F32), V(8, 512, dtype=F32)]
        + [rc[0], rp[0], ru[0], rd[0]]
        + rc[1] + rp[1] + ru[1] + rd[1]
        + [V(2, 3, 4, 2, 64, 128), V(3, 4, 2, 64, 128), V(3, 4, 64, 128), V(3, 3, 64, 128), V(3, 4, 64, 128)]
        + [V(12, 8, 512, dtype=F32)]
        + [S(4, 19), S(4, 19), S(4, 9), S(4, 9), S(10), S(10), S(10), S(10), S(11), S(11), S(13)]
    )
    big = jax.ShapeDtypeStruct((512, 512), F32)
    outs = pl.pallas_call(
        fast_kernel,
        out_shape=[big, big, big]
        + [jax.ShapeDtypeStruct(s, F32) for s in ((3, 64, 128), (5, 64, 128), (2, 64, 512), (6, 512), (2, 512))],
        in_specs=[hbm] * 3 + [vm] * 3 + [hbm] * 10 + [vm] * 6,
        out_specs=[hbm] * 3 + [vm] * 5,
        scratch_shapes=scratch,
        compiler_params=pltpu.CompilerParams(
            collective_id=0, has_side_effects=True, vmem_limit_bytes=63 << 20
        ),
        name="layer",
    )(
        tokens, encoder_states, output_grad, valid_mask.reshape(1, 512), segment_ids, context_ranks,
        self_query, self_key, self_value, self_output.T,
        cross_query, cross_key, cross_value, cross_output.T, hidden_up, hidden_down.T, *rows,
    )
    ends = [big, big, big] + [jax.ShapeDtypeStruct((64, 128), F32)] * 8
    ends += [jax.ShapeDtypeStruct((64, 512), F32)] * 2
    ends += [jax.ShapeDtypeStruct(v, F32) for v in ((6, 512), (2, 512))]
    y, dx, eg, dsq, dsk, dsv, dso, dco, dcq, dck, dcv, dup, ddown, ns, vs = pl.pallas_call(
        place_kernel,
        out_shape=ends,
        in_specs=[hbm] * 8,
        out_specs=[hbm] * 15,
        scratch_shapes=[pltpu.VMEM(o.shape, F32) for o in outs] + [S(23)],
        name="place",
    )(*outs)
    return (
        y, dx, eg, dsq, dsk, dsv, dso.T, dcq, dck, dcv, dco.T, dup, ddown.T, ns, vs,
    )


def solution(mesh):
    in_specs = (
        P(("dp", "tensor"), None),
        P(("dp", "tensor"), None),
        P(("dp", "tensor"), None),
        P(("dp", "tensor")),
        P("dp", None),
        P("dp", None),
        P("dp", "tensor"),
        P("dp", "tensor"),
        P("dp", "tensor"),
        P("tensor", "dp"),
        P("dp", "tensor"),
        P("dp", "tensor"),
        P("dp", "tensor"),
        P("tensor", "dp"),
        P("dp", "tensor"),
        P("tensor", "dp"),
        P(),
        P(),
        P(),
        P(),
        P(),
        P(),
    )
    out_specs = (
        P(("dp", "tensor"), None),
        P(("dp", "tensor"), None),
        P(("dp", "tensor"), None),
        P("dp", "tensor"),
        P("dp", "tensor"),
        P("dp", "tensor"),
        P("tensor", "dp"),
        P("dp", "tensor"),
        P("dp", "tensor"),
        P("dp", "tensor"),
        P("tensor", "dp"),
        P("dp", "tensor"),
        P("tensor", "dp"),
        P(),
        P(),
    )
    body = fast_shards if dict(mesh.shape) == {"dp": 8, "tensor": 4} else shards
    return jax.shard_map(body, mesh=mesh, in_specs=in_specs, out_specs=out_specs, check_vma=False)
```
